32 devices in a mesh: dp: 16 (over z, y, x), seq: 2 (over core).
Axes of the slice: x: 2, y: 2, z: 4, core: 2. Of those that a mesh axis runs over, the one named last changes fastest.
Arguments:
- hidden_in: bfloat16 [16384, 768], P(('dp', 'seq')), may hold values from -6 to 6
- prefix: int32 [16], P('dp'), may hold values from 102 to 512
- w_qkv: bfloat16 [768, 2304], P(('dp', 'seq')), may hold values from -0.21875 to 0.21875
- q_bias: bfloat16 [768], P(('dp', 'seq')), may hold values from -3 to 3
- v_bias: bfloat16 [768], P(('dp', 'seq')), may hold values from -3 to 3
- rel_table: bfloat16 [512, 768], P(('dp', 'seq')), may hold values from -6 to 6
- w_posk: bfloat16 [768, 768], P(('dp', 'seq')), may hold values from -0.21875 to 0.21875
- w_posq: bfloat16 [768, 768], P(('dp', 'seq')), may hold values from -0.21875 to 0.21875
- posq_bias: bfloat16 [768], P(('dp', 'seq')), may hold values from -3 to 3
- w_out: bfloat16 [768, 768], P(('dp', 'seq')), may hold values from -0.875 to 0.875
- out_bias: bfloat16 [768], P(('dp', 'seq')), may hold values from -3 to 3
- norm1_gain: bfloat16 [768], P(('dp', 'seq')), may hold values from 0.5 to 1.5
- norm1_bias: bfloat16 [768], P(('dp', 'seq')), may hold values from -3 to 3
- w_up: bfloat16 [768, 3072], P(('dp', 'seq')), may hold values from -0.21875 to 0.21875
- up_bias: bfloat16 [3072], P(('dp', 'seq')), may hold values from -3 to 3
- w_down: bfloat16 [3072, 768], P(('dp', 'seq')), may hold values from -0.109375 to 0.109375
- down_bias: bfloat16 [768], P(('dp', 'seq')), may hold values from -3 to 3
- norm2_gain: bfloat16 [768], P(('dp', 'seq')), may hold values from 0.5 to 1.5
- norm2_bias: bfloat16 [768], P(('dp', 'seq')), may hold values from -3 to 3
- out_grad: bfloat16 [16384, 768], P(('dp', 'seq')), may hold values from -6 to 6
Outputs:
- hidden_out: bfloat16 [16384, 768], P(('dp', 'seq'))
- in_grad: float32 [16384, 768], P(('dp', 'seq'))
- w_qkv_grad: float32 [768, 2304], P(('dp', 'seq'))
- q_bias_grad: float32 [768], P(('dp', 'seq'))
- v_bias_grad: float32 [768], P(('dp', 'seq'))
- rel_table_grad: float32 [512, 768], P(('dp', 'seq'))
- w_posk_grad: float32 [768, 768], P(('dp', 'seq'))
- w_posq_grad: float32 [768, 768], P(('dp', 'seq'))
- posq_bias_grad: float32 [768], P(('dp', 'seq'))
- w_out_grad: float32 [768, 768], P(('dp', 'seq'))
- out_bias_grad: float32 [768], P(('dp', 'seq'))
- norm1_gain_grad: float32 [768], P(('dp', 'seq'))
- norm1_bias_grad: float32 [768], P(('dp', 'seq'))
- w_up_grad: float32 [768, 3072], P(('dp', 'seq'))
- up_bias_grad: float32 [3072], P(('dp', 'seq'))
- w_down_grad: float32 [3072, 768], P(('dp', 'seq'))
- down_bias_grad: float32 [768], P(('dp', 'seq'))
- norm2_gain_grad: float32 [768], P(('dp', 'seq'))
- norm2_bias_grad: float32 [768], P(('dp', 'seq'))
The draws below stay inside these ranges and needn't reach their ends.
All inputs are finite; a program needn't handle non-finite values.
Results may differ from the reference program's by a relative error of at most 0.023.
Values may be sent and summed in bfloat16 or wider, within the bound.
No kernel may reach another device: no remote copies, remote signals or barrier semaphores. Data moves between devices by JAX's collectives and lax.ppermute only.
A program may use at most 192 MiB of HBM per device.

```python
import math
import jax
import jax.numpy as jnp
from jax import lax

D = 768
HEADS = 12
HEAD_DIM = 64
FF = 3072
SPAN = 256
SEQ_LEN = 1024
ROWS = 512
SEQS = 16
TOKENS = 16384
N_SEQ = 2


def place_ends(drawn, stream_key, low, high):
    dims = drawn.shape
    spot = [jax.random.randint(jax.random.fold_in(stream_key, axis), (), 0, dims[axis]) for axis in range(len(dims))]
    drawn = drawn.at[tuple(spot)].set(low)
    longest = dims.index(max(dims))
    spot[longest] = (spot[longest] + 1) % dims[longest]
    return drawn.at[tuple(spot)].set(high)


def raised(entries, key, source, target, blocks, factor):
    def block_of(dim):
        return (jnp.arange(entries.shape[dim]) // (entries.shape[dim] // blocks)).reshape((-1,) + (1,) * (entries.ndim - 1 - dim))

    near = jax.random.permutation(key, blocks)[block_of(target)]
    second = (block_of(target) + blocks // 2) % blocks
    return jnp.where((block_of(source) == near) | (block_of(source) == second), factor * entries, entries)


def level_of(own_key, extent, pieces, low, top_value):
    level, own = 1.0, jax.random.fold_in(own_key, 6)
    for position, parts in pieces:
        heights = jnp.exp(jax.random.uniform(jax.random.fold_in(own, position), (parts,), jnp.float32, low / len(pieces), top_value / len(pieces)))
        level = level * jnp.repeat(heights, extent[position] // parts).reshape([-1 if axis == position else 1 for axis in range(len(extent))])
    return level


def scatter_about(rng, extent, deviation, most, shards=(), kind=jnp.bfloat16):
    drawn = jax.random.normal(rng, extent, jnp.float32) * deviation
    if len(shards) > 0:
        drawn = level_of(rng, extent, shards, -0.22, 0.18) * drawn
    return jnp.clip(drawn, min=-most, max=most).astype(kind)


def noise_with(stream_key, dims, spread, reach, split, heavy, held_as=jnp.bfloat16):
    drawn = spread * jax.random.normal(stream_key, dims, jnp.float32)
    if split:
        drawn = drawn * level_of(stream_key, dims, split, -0.22, 0.18)
    return jnp.clip(raised(drawn, jax.random.fold_in(stream_key, 3), *heavy), -reach, reach).astype(held_as)


def setup_inputs(seed: int = 0) -> dict:
    arg_keys = jax.random.split(jax.random.key(seed), 21)
    return {
        "hidden_in": noise_with(arg_keys[0], (TOKENS, D), 1.0, 6.0, ((0, 32),), (0, 1, 32, 2.75)),
        "prefix": place_ends(jax.random.randint(arg_keys[1], (SEQS,), SEQ_LEN // 10, SEQ_LEN // 2 + 1), jax.random.fold_in(arg_keys[1], 1), SEQ_LEN // 10, (SEQ_LEN // 2 + 1) - 1).astype(jnp.int32),
        "w_qkv": scatter_about(arg_keys[2], (D, 3 * D), D ** -0.5, 0.21875, ((0, 32),)),
        "q_bias": scatter_about(arg_keys[3], (D,), 0.5, 3.0, ((0, 32),)),
        "v_bias": scatter_about(arg_keys[4], (D,), 0.5, 3.0, ((0, 32),)),
        "rel_table": scatter_about(arg_keys[5], (2 * SPAN, D), 1.0, 6.0, ((0, 32),)),
        "w_posk": scatter_about(arg_keys[6], (D, D), D ** -0.5, 0.21875, ((0, 32),)),
        "w_posq": scatter_about(arg_keys[7], (D, D), D ** -0.5, 0.21875, ((0, 32),)),
        "posq_bias": scatter_about(arg_keys[8], (D,), 0.5, 3.0, ((0, 32),)),
        "w_out": scatter_about(arg_keys[9], (D, D), (D // 16) ** -0.5, 0.875, ((0, 32),)),
        "out_bias": scatter_about(arg_keys[10], (D,), 0.5, 3.0, ((0, 32),)),
        "norm1_gain": jnp.clip(1.0 + 0.1 * jax.random.normal(arg_keys[11], (D,), jnp.float32), 0.5, 1.5).astype(jnp.bfloat16),
        "norm1_bias": scatter_about(arg_keys[12], (D,), 0.5, 3.0, ((0, 32),)),
        "w_up": scatter_about(arg_keys[13], (D, FF), D ** -0.5, 0.21875, ((0, 32),)),
        "up_bias": scatter_about(arg_keys[14], (FF,), 0.5, 3.0, ((0, 32),)),
        "w_down": scatter_about(arg_keys[15], (FF, D), FF ** -0.5, 0.109375, ((0, 32),)),
        "down_bias": scatter_about(arg_keys[16], (D,), 0.5, 3.0, ((0, 32),)),
        "norm2_gain": jnp.clip(1.0 + 0.1 * jax.random.normal(arg_keys[17], (D,), jnp.float32), 0.5, 1.5).astype(jnp.bfloat16),
        "norm2_bias": scatter_about(arg_keys[18], (D,), 0.5, 3.0, ((0, 32),)),
        "out_grad": noise_with(arg_keys[19], (TOKENS, D), 1.0, 6.0, ((0, 32),), (0, 1, 32, 2.75)),
    }


@jax.custom_vjp
def low(v):
    return lax.optimization_barrier(v.astype(jnp.bfloat16)).astype(jnp.float32)

@jax.custom_vjp
def low_back(v):
    return v

def low_keep(v):
    return (low(v), None)

def low_pass(kept, grad):
    return (grad,)

def back_keep(v):
    return (v, None)

def back_low(kept, grad):
    return (low(grad),)
low.defvjp(low_keep, low_pass)
low_back.defvjp(back_keep, back_low)
eps_norm = 1e-07

def matmul(left, right):
    return jnp.dot(left, right, precision=lax.Precision.HIGHEST, preferred_element_type=jnp.float32)

def normalize(value, gain, shift):
    average = lax.optimization_barrier(jnp.mean(value, axis=-1, keepdims=True))
    centred = value - average
    variance = lax.optimization_barrier(jnp.mean(centred * centred, axis=-1, keepdims=True))
    return centred * lax.rsqrt(variance + eps_norm) * gain + shift

def split_heads(matrix):
    return matrix.reshape(matrix.shape[0], HEADS, HEAD_DIM).transpose(1, 0, 2)

def block_context(start, query_heads, key_heads, value_heads, posk_heads, posq_heads, prefix_len):
    block_query = lax.dynamic_slice_in_dim(query_heads, start, ROWS, 1)
    query_pos = start + jnp.arange(ROWS, dtype=jnp.int32)
    key_pos = jnp.arange(SEQ_LEN, dtype=jnp.int32)
    content = jnp.einsum('hid,hjd->hij', block_query, key_heads, precision=lax.Precision.HIGHEST)
    table_a = low_back(jnp.einsum('hid,hrd->hir', block_query, posk_heads, precision=lax.Precision.HIGHEST))
    table_b = low_back(jnp.einsum('hjd,hrd->hjr', key_heads, posq_heads, precision=lax.Precision.HIGHEST))
    index_a = jnp.clip(query_pos[:, None] - key_pos[None, :] + SPAN, 0, 2 * SPAN - 1).astype(jnp.int32)
    index_b = jnp.clip(key_pos[:, None] - query_pos[None, :] + SPAN, 0, 2 * SPAN - 1).astype(jnp.int32)
    term_a = jnp.take_along_axis(table_a, jnp.broadcast_to(index_a[None, :, :], (HEADS, ROWS, SEQ_LEN)), axis=2)
    term_b = jnp.take_along_axis(table_b, jnp.broadcast_to(index_b[None, :, :], (HEADS, SEQ_LEN, ROWS)), axis=2)
    raw = content + term_a + jnp.swapaxes(term_b, 1, 2)
    visible = (key_pos[None, :] < prefix_len) | (key_pos[None, :] <= query_pos[:, None])
    scores = jnp.where(visible[None, :, :], low_back(raw) / math.sqrt(3 * HEAD_DIM), -jnp.inf)
    probs = jax.nn.softmax(scores, axis=-1)
    return jnp.einsum('hij,hjd->hid', low(probs), value_heads, precision=lax.Precision.HIGHEST)

def layer_sequence(hidden, prefix_len, params, posk_heads, posq_heads):
    w_qkv, q_bias, v_bias, w_out, out_bias, norm1_gain, norm1_bias, w_up, up_bias, w_down, down_bias, norm2_gain, norm2_bias = params
    merged = matmul(hidden, w_qkv)
    queries = low(low_back(merged[:, :D] + q_bias))
    keys = low(low_back(merged[:, D:2 * D]))
    values = low(low_back(merged[:, 2 * D:] + v_bias))
    query_heads = split_heads(queries)
    key_heads = split_heads(keys)
    value_heads = split_heads(values)

    def one_block(start):
        return block_context(start, query_heads, key_heads, value_heads, posk_heads, posq_heads, prefix_len)
    starts = jnp.arange(N_SEQ, dtype=jnp.int32) * ROWS
    blocks = lax.map(jax.checkpoint(one_block), starts)
    context = blocks.transpose(0, 2, 1, 3).reshape(SEQ_LEN, D)
    context = low(low_back(context))
    attended = low_back(matmul(context, w_out) + out_bias)
    normed = normalize(hidden + attended, norm1_gain, norm1_bias)
    expanded = low_back(matmul(low(normed), w_up) + up_bias)
    activated = low(jax.nn.gelu(expanded, approximate=False))
    reduced = low_back(matmul(activated, w_down) + down_bias)
    return normalize(normed + reduced, norm2_gain, norm2_bias)

def whole_layer(hidden, prefix, w_qkv, q_bias, v_bias, rel_table, w_posk, w_posq, posq_bias, w_out, out_bias, norm1_gain, norm1_bias, w_up, up_bias, w_down, down_bias, norm2_gain, norm2_bias):
    pos_keys = low(low_back(matmul(rel_table, w_posk)))
    pos_queries = low(low_back(matmul(rel_table, w_posq) + posq_bias))
    posk_heads = split_heads(pos_keys)
    posq_heads = split_heads(pos_queries)
    params = (w_qkv, q_bias, v_bias, w_out, out_bias, norm1_gain, norm1_bias, w_up, up_bias, w_down, down_bias, norm2_gain, norm2_bias)

    def one_sequence(item):
        return layer_sequence(item[0], item[1], params, posk_heads, posq_heads)
    outputs = lax.map(jax.checkpoint(one_sequence), (hidden.reshape(SEQS, SEQ_LEN, D), prefix))
    return outputs.reshape(TOKENS, D)

def reference(hidden_in, prefix, w_qkv, q_bias, v_bias, rel_table, w_posk, w_posq, posq_bias, w_out, out_bias, norm1_gain, norm1_bias, w_up, up_bias, w_down, down_bias, norm2_gain, norm2_bias, out_grad):
    floats = tuple((item.astype(jnp.float32) for item in (hidden_in, w_qkv, q_bias, v_bias, rel_table, w_posk, w_posq, posq_bias, w_out, out_bias, norm1_gain, norm1_bias, w_up, up_bias, w_down, down_bias, norm2_gain, norm2_bias)))

    def forward(hidden, *weights):
        return whole_layer(hidden, prefix, *weights)
    result, pullback = jax.vjp(forward, *floats)
    grads = pullback(out_grad.astype(jnp.float32))
    return (result.astype(jnp.bfloat16), grads[0], grads[1], grads[2], grads[3], grads[4], grads[5], grads[6], grads[7], grads[8], grads[9], grads[10], grads[11], grads[12], grads[13], grads[14], grads[15], grads[16], grads[17])
```

```python
import math

import jax
import jax.numpy as jnp
from jax import lax
from jax.experimental import pallas as pl
from jax.experimental.pallas import tpu as pltpu
from jax.sharding import PartitionSpec as P

D = 768
HEADS = 12
HEAD_DIM = 64
SPAN = 256
TILE = 128
BLOCK = 256
BAND = 768
PAIR = 2 * HEAD_DIM


eps_norm = 1e-07


def normalize(value, gain, shift):
    average = jnp.mean(value, axis=-1, keepdims=True)
    centred = value - average
    variance = jnp.mean(centred * centred, axis=-1, keepdims=True)
    return centred * lax.rsqrt(variance + eps_norm) * gain + shift


def gelu_exact(value):
    return jax.nn.gelu(value, approximate=False)


def product(left, right):
    return jnp.dot(left, right, preferred_element_type=jnp.float32)


def inner_first(left, right):
    return lax.dot_general(
        left, right, (((0,), (0,)), ((), ())), preferred_element_type=jnp.float32
    )


def inner_last(left, right):
    return lax.dot_general(
        left, right, (((1,), (1,)), ((), ())), preferred_element_type=jnp.float32
    )


def split_heads(matrix):
    return matrix.reshape(matrix.shape[0], HEADS, HEAD_DIM).transpose(1, 0, 2)


def join_heads(stacked):
    return stacked.transpose(1, 0, 2).reshape(stacked.shape[1], D)


def column_sums(matrix):
    return jnp.sum(matrix.astype(jnp.float32), axis=0)


def nn(left, right):
    return lax.dot_general(
        left, right, (((1,), (0,)), ((), ())), preferred_element_type=jnp.float32
    )


def nt(left, right):
    return lax.dot_general(
        left, right, (((1,), (1,)), ((), ())), preferred_element_type=jnp.float32
    )


def unit_matrix(size, reverse=False):
    rows = lax.broadcasted_iota(jnp.int32, (size, size), 0)
    cols = lax.broadcasted_iota(jnp.int32, (size, size), 1)
    if reverse:
        cols = size - 1 - cols
    return jnp.where(rows == cols, 1.0, 0.0).astype(jnp.bfloat16)


def head_lanes(head):
    lanes = lax.broadcasted_iota(jnp.int32, (1, PAIR), 1)
    return lanes // HEAD_DIM == head


def head_rows(head):
    rows = lax.broadcasted_iota(jnp.int32, (HEAD_DIM, PAIR), 0)
    cols = lax.broadcasted_iota(jnp.int32, (HEAD_DIM, PAIR), 1)
    return jnp.where(cols == rows + head * HEAD_DIM, 1.0, 0.0).astype(jnp.bfloat16)


def key_tiles(block, length):
    return max(length // 2, (block + 1) * BLOCK) // TILE


def tile_seen(query_tile, key_tile, length):
    return key_tile < key_tiles(query_tile * TILE // BLOCK, length)


def skewed(window):
    return pltpu.roll(window, 0, 1, stride=1, stride_axis=0)


def forward_body(prefix_ref, q_ref, k_ref, v_ref, pk_ref, pq_ref, ctx_ref, p_ref, wb_ref, far_ref, s_ref):
    length = q_ref.shape[0]
    head = pl.program_id(1)
    mine = head_lanes(head)
    prefix = prefix_ref[0]
    eye = unit_matrix(TILE)
    eye_block = unit_matrix(BLOCK)
    zero = jnp.zeros((), jnp.bfloat16)
    scale = math.log2(math.e) / math.sqrt(3 * HEAD_DIM)
    for tile in range(length // TILE):
        rows = slice(tile * TILE, (tile + 1) * TILE)
        table = nt(jnp.where(mine, k_ref[rows, :], zero), pq_ref[...])
        wb_ref[rows, :] = skewed(table)
        wb_ref[rows, 0:TILE] = table[:, BAND - TILE :]
        far_ref[rows, :] = table[:, 0:TILE]
    v_cols = nt(jnp.where(lax.broadcasted_iota(jnp.int32, (PAIR, PAIR), 0) // HEAD_DIM == head, unit_matrix(PAIR), zero), v_ref[...]).astype(jnp.bfloat16)
    for block in range(length // BLOCK):
        cols = slice(block * BLOCK, (block + 1) * BLOCK)
        q_own = jnp.where(mine, q_ref[cols, :], zero)
        skews, highs, lows = [], [], []
        for sub in range(2):
            table = nt(q_own[sub * TILE : (sub + 1) * TILE], pk_ref[...])
            skews.append(skewed(table).astype(jnp.bfloat16))
            highs.append(table[:, 0:TILE].astype(jnp.bfloat16))
            lows.append(table[:, BAND - TILE :].astype(jnp.bfloat16))
        count = key_tiles(block, length)
        highest = None
        for tile in range(count):
            rows = slice(tile * TILE, (tile + 1) * TILE)
            parts_a, parts_b = [], []
            for sub in range(2):
                step = 2 * block + sub - tile
                if step >= 3:
                    parts_a.append(highs[sub])
                    parts_b.append(wb_ref[rows, 0:TILE])
                elif step <= -3:
                    parts_a.append(lows[sub])
                    parts_b.append(far_ref[rows, :])
                else:
                    at = 384 - TILE * step
                    parts_a.append(skews[sub][:, at : at + TILE])
                    at = 384 + TILE * step
                    parts_b.append(wb_ref[rows, at : at + TILE])
            right = jnp.concatenate([jnp.concatenate(parts_a, axis=0), q_own], axis=1)
            left = jnp.concatenate([eye, k_ref[rows, :]], axis=1)
            raw = nt(left, right) + jnp.concatenate(parts_b, axis=1)
            if (tile + 1) * TILE > block * BLOCK + 1:
                keys = tile * TILE + lax.broadcasted_iota(jnp.int32, (TILE, BLOCK), 0)
                queries = block * BLOCK + lax.broadcasted_iota(jnp.int32, (TILE, BLOCK), 1)
                raw = jnp.where((keys < prefix) | (keys <= queries), raw, -jnp.inf)
            s_ref[rows, :] = raw
            top = jnp.max(raw, axis=0, keepdims=True)
            highest = top if highest is None else jnp.maximum(highest, top)
        total = jnp.zeros((1, BLOCK), jnp.float32)
        for tile in range(count):
            rows = slice(tile * TILE, (tile + 1) * TILE)
            expo = jnp.exp2((s_ref[rows, :] - highest) * scale)
            s_ref[rows, :] = expo
            total = total + jnp.sum(expo, axis=0, keepdims=True)
        inverse = 1.0 / total
        for tile in range(count):
            rows = slice(tile * TILE, (tile + 1) * TILE)
            p_ref[rows, cols] = (s_ref[rows, :] * inverse).astype(jnp.bfloat16)
        seen = count * TILE
        ctx_cols = nn(v_cols[:, :seen], p_ref[0:seen, cols]).astype(jnp.bfloat16)
        ctx = nt(eye_block, ctx_cols).astype(jnp.bfloat16)

        @pl.when(head == 0)
        def _():
            ctx_ref[cols, :] = ctx

        @pl.when(head == 1)
        def _():
            ctx_ref[cols, :] = ctx_ref[cols, :] + ctx


def attention_forward(prefix, q, k, v, pk, pq):
    length, width = q.shape
    pairs = width // PAIR
    tall = pl.BlockSpec((length, PAIR), lambda p, h: (0, p))
    band = pl.BlockSpec((BAND, PAIR), lambda p, h: (0, p))
    return pl.pallas_call(
        forward_body,
        grid=(pairs, 2),
        in_specs=[pl.BlockSpec(memory_space=pltpu.SMEM), tall, tall, tall, band, band],
        out_specs=[tall, pl.BlockSpec((None, length, length), lambda p, h: (2 * p + h, 0, 0))],
        out_shape=[
            jax.ShapeDtypeStruct((length, width), jnp.bfloat16),
            jax.ShapeDtypeStruct((2 * pairs, length, length), jnp.bfloat16),
        ],
        scratch_shapes=[
            pltpu.VMEM((length, BAND), jnp.float32),
            pltpu.VMEM((length, TILE), jnp.float32),
            pltpu.VMEM((length, BLOCK), jnp.float32),
        ],
        compiler_params=pltpu.CompilerParams(dimension_semantics=("arbitrary", "arbitrary"), vmem_limit_bytes=48 << 20),
        name="attention_forward",
    )(prefix, q, k, v, pk, pq)


def backward_body(q_ref, k_ref, v_ref, dctx_ref, p_ref, pk_ref, pq_ref, dq_ref, dk_ref, dv_ref, dpk_ref, dpq_ref, dr_ref, dk_acc, dv_acc):
    length = q_ref.shape[0]
    head = pl.program_id(1)
    mine = head_lanes(head)
    flip = unit_matrix(TILE, reverse=True)
    pick = head_rows(head)
    bf = jnp.bfloat16
    zero = jnp.zeros((), bf)
    scale = 1.0 / math.sqrt(3 * HEAD_DIM)
    back = BAND - (TILE - 1)
    blank = jnp.zeros((TILE, TILE), bf)
    dk_acc[...] = jnp.zeros_like(dk_acc)
    dv_acc[...] = jnp.zeros_like(dv_acc)
    dpk_ref[...] = jnp.zeros_like(dpk_ref)
    dpq_ref[...] = jnp.zeros_like(dpq_ref)

    def put(ref, rows, value):
        @pl.when(head == 0)
        def _():
            ref[rows, :] = jnp.where(mine, value, 0.0).astype(bf)

        @pl.when(head == 1)
        def _():
            ref[rows, :] = jnp.where(mine, value.astype(bf), ref[rows, :])

    for block in range(length // BLOCK):
        cols = slice(block * BLOCK, (block + 1) * BLOCK)
        count = key_tiles(block, length)
        seen = count * TILE
        dctx = dctx_ref[cols, :]
        v_own = jnp.where(mine, v_ref[0:seen, :], zero)
        probs_low = p_ref[0:seen, cols]
        probs = probs_low.astype(jnp.float32)
        d_probs = nt(v_own, dctx)
        row_dot = jnp.sum(probs * d_probs, axis=0, keepdims=True)
        d_raw = (probs * ((d_probs - row_dot) * scale)).astype(bf)
        dr_ref[0:seen, cols] = d_raw
        dv_acc[0:seen, :] += nn(probs_low, dctx)
        dk_acc[0:seen, :] += nn(d_raw, q_ref[cols, :])
        for sub in range(2):
            tile = 2 * block + sub
            own = slice(tile * TILE, (tile + 1) * TILE)
            turned_f = nt(flip, dr_ref[0:seen, own])
            turned = turned_f.astype(bf)
            dq = nn(turned, k_ref[0:seen, :])

            def piece(key_tile):
                return turned[:, key_tile * TILE : (key_tile + 1) * TILE]

            band = [blank]
            for step in (2, 1, 0, -1, -2):
                key_tile = tile - step
                band.append(piece(key_tile) if 0 <= key_tile < count else blank)
            spread = pltpu.roll(jnp.concatenate(band, axis=1), back, 1, stride=1, stride_axis=0)
            near = [turned_f[:, t * TILE : (t + 1) * TILE] for t in range(count) if tile - t >= 3]
            far = [turned_f[:, t * TILE : (t + 1) * TILE] for t in range(count) if tile - t <= -3]
            spread = add_edges(spread, near, far)
            dq = dq + nn(spread, pk_ref[...])
            put(dq_ref, own, nn(flip, dq.astype(bf)))
            q_turned = nn(flip, q_ref[own, :]).astype(bf)
            q_cols = nt(pick, q_turned).astype(bf)
            dpk_ref[...] += nn(q_cols, spread)
    tiles = length // TILE
    for key_tile in range(tiles):
        rows = slice(key_tile * TILE, (key_tile + 1) * TILE)

        def held(query_tile):
            return dr_ref[rows, query_tile * TILE : (query_tile + 1) * TILE]

        seen_by = [t for t in range(tiles) if tile_seen(t, key_tile, length)]
        band = [blank]
        for step in (-2, -1, 0, 1, 2):
            query_tile = key_tile + step
            band.append(held(query_tile) if query_tile in seen_by else blank)
        later = [held(t).astype(jnp.float32) for t in seen_by if t - key_tile >= 3]
        earlier = [held(t).astype(jnp.float32) for t in seen_by if t - key_tile <= -3]
        spread = pltpu.roll(nn(flip, jnp.concatenate(band, axis=1)).astype(bf), back, 1, stride=1, stride_axis=0)
        flat = lambda parts: [nn(flip, sum(parts[1:], parts[0]).astype(bf))] if parts else []
        spread = add_edges(spread, flat(earlier), flat(later))
        d_key = nn(flip, nn(spread, pq_ref[...]).astype(bf))
        put(dk_ref, rows, dk_acc[rows, :] + d_key)
        k_turned = nn(flip, k_ref[rows, :]).astype(bf)
        k_cols = nt(pick, k_turned).astype(bf)
        dpq_ref[...] += nn(k_cols, spread)
        put(dv_ref, rows, dv_acc[rows, :])


def add_edges(spread, first, last):
    parts = [spread[:, 0:TILE], spread[:, TILE : BAND - TILE], spread[:, BAND - TILE :]]
    for place, tiles in ((0, first), (2, last)):
        if tiles:
            total = parts[place].astype(jnp.float32)
            for tile in tiles:
                total = total + tile
            parts[place] = total.astype(jnp.bfloat16)
    return jnp.concatenate(parts, axis=1)


def attention_backward(q, k, v, dctx, probs, pk, pq):
    length, width = q.shape
    pairs = width // PAIR
    tall = pl.BlockSpec((length, PAIR), lambda p, h: (0, p))
    band = pl.BlockSpec((BAND, PAIR), lambda p, h: (0, p))
    table = pl.BlockSpec((HEAD_DIM, BAND), lambda p, h: (2 * p + h, 0))
    flat = jax.ShapeDtypeStruct((length, width), jnp.bfloat16)
    wide = jax.ShapeDtypeStruct((width, BAND), jnp.float32)
    return pl.pallas_call(
        backward_body,
        grid=(pairs, 2),
        in_specs=[tall, tall, tall, tall, pl.BlockSpec((None, length, length), lambda p, h: (2 * p + h, 0, 0)), band, band],
        out_specs=[tall, tall, tall, table, table],
        out_shape=[flat, flat, flat, wide, wide],
        scratch_shapes=[
            pltpu.VMEM((length, length), jnp.bfloat16),
            pltpu.VMEM((length, PAIR), jnp.float32),
            pltpu.VMEM((length, PAIR), jnp.float32),
        ],
        compiler_params=pltpu.CompilerParams(dimension_semantics=("arbitrary", "arbitrary"), vmem_limit_bytes=48 << 20),
        name="attention_backward",
    )(q, k, v, dctx, probs, pk, pq)


CORES = [(0, 1), (1, 0)]


def swap(value):
    return lax.ppermute(value, "seq", CORES)


def ordered(core, own, other, axis=0):
    return jnp.concatenate(
        [jnp.where(core == 0, own, other), jnp.where(core == 0, other, own)], axis=axis
    )


def half_of(core, matrix, axis):
    size = matrix.shape[axis] // 2
    return lax.dynamic_slice_in_dim(matrix, core * size, size, axis)


def gather_pair(value, bit, mask):
    other = lax.ppermute(value, "dp", [(i, i ^ mask) for i in range(16)])
    return jnp.stack([jnp.where(bit == 0, value, other), jnp.where(bit == 0, other, value)])


def gather_line(value, place):
    below, above = [value], [value]
    for step in range(1, 4):
        up = [(i, i + 4) for i in range(12) if i // 4 >= step - 1]
        down = [(i + 4, i) for i in range(12) if i // 4 <= 3 - step]
        below.append(lax.ppermute(below[-1], "dp", up))
        above.append(lax.ppermute(above[-1], "dp", down))
    blocks = []
    for block in range(4):
        options = [below[z - block] if z >= block else above[block - z] for z in range(4)]
        blocks.append(lax.select_n(place, *options))
    return jnp.stack(blocks)


def scatter_pair(value, bit, mask):
    keep = jnp.where(bit == 0, value[0], value[1])
    give = jnp.where(bit == 0, value[1], value[0])
    other = lax.ppermute(give, "dp", [(i, i ^ mask) for i in range(16)])
    return (keep.astype(jnp.float32) + other.astype(jnp.float32)).astype(value.dtype)


def scatter_line(value, place):
    def block(offset):
        options = [value[min(max(z + offset, 0), 3)] for z in range(4)]
        return lax.select_n(place, *options).astype(jnp.float32)

    up = down = None
    for step in range(3, 0, -1):
        to_above, to_below = block(step), block(-step)
        if up is not None:
            to_above = to_above + up.astype(jnp.float32)
            to_below = to_below + down.astype(jnp.float32)
        ups = [(i, i + 4) for i in range(12) if i // 4 + step <= 3]
        downs = [(i + 4, i) for i in range(12) if i // 4 + 1 - step >= 0]
        up = lax.ppermute(to_above.astype(value.dtype), "dp", ups)
        down = lax.ppermute(to_below.astype(value.dtype), "dp", downs)
    return block(0) + up.astype(jnp.float32) + down.astype(jnp.float32)


def gather_chips(value, first):
    chip = lax.axis_index("dp")
    z, y, x = chip // 4, (chip // 2) % 2, chip % 2
    line = gather_line(value, z)
    if first == "x":
        grid = gather_pair(gather_pair(line, x, 1), y, 2)
        grid = jnp.moveaxis(grid, (0, 1, 2), (1, 2, 0))
    else:
        grid = gather_pair(gather_pair(line, y, 2), x, 1)
        grid = jnp.moveaxis(grid, (0, 1, 2), (2, 1, 0))
    return grid.reshape((16,) + value.shape)


def scatter_chips(value, first):
    chip = lax.axis_index("dp")
    z, y, x = chip // 4, (chip // 2) % 2, chip % 2
    grid = value.reshape((4, 2, 2) + value.shape[1:])
    if first == "x":
        grid = jnp.moveaxis(grid, (0, 1, 2), (2, 1, 0))
        line = scatter_pair(scatter_pair(grid, x, 1), y, 2)
    else:
        grid = jnp.moveaxis(grid, (0, 1, 2), (2, 0, 1))
        line = scatter_pair(scatter_pair(grid, y, 2), x, 1)
    return scatter_line(line, z)


def norm_parts(value):
    average = jnp.mean(value, axis=-1, keepdims=True)
    centred = value - average
    variance = jnp.mean(centred * centred, axis=-1, keepdims=True)
    inverse = lax.rsqrt(variance + eps_norm)
    return centred * inverse, inverse


def norm_back(unit, inverse, gain, grad):
    scaled = grad * gain
    mean_grad = jnp.mean(scaled, axis=-1, keepdims=True)
    mean_along = jnp.mean(scaled * unit, axis=-1, keepdims=True)
    return inverse * (scaled - mean_grad - unit * mean_along)


def head_split(
    hidden_in, prefix, w_qkv, q_bias, v_bias, rel_table, w_posk, w_posq, posq_bias, w_out, out_bias,
    norm1_gain, norm1_bias, w_up, up_bias, w_down, down_bias, norm2_gain, norm2_bias, out_grad,
):
    bf = jnp.bfloat16
    f32 = jnp.float32
    core = lax.axis_index("seq")
    rows = w_qkv.shape[0]
    units = w_down.shape[0]
    table_rows = rel_table.shape[0]
    chips = 16
    half = D // 2
    ff_half = chips * units
    buckets = 2 * SPAN

    small = jnp.concatenate(
        [q_bias, v_bias, posq_bias, out_bias, norm1_gain, norm1_bias, down_bias, norm2_gain, norm2_bias, up_bias]
    )
    small = jnp.pad(small, (0, half - small.shape[0]))[None, :]
    last_rows = rows - table_rows - 1

    def columns(side):
        qkv = w_qkv.reshape(rows, 3, 2, half)[:, :, side].reshape(rows, 3 * half)
        corner = jnp.concatenate(
            [rel_table[:, side * half : (side + 1) * half], small, jnp.zeros((last_rows, half), bf)], axis=0
        )
        cut = slice(side * half, (side + 1) * half)
        up = w_up.reshape(rows, chips, 2, units)[:, :, side].reshape(rows, ff_half)
        return (
            jnp.concatenate([qkv, w_posk[:, cut], w_posq[:, cut], corner], axis=1),
            jnp.concatenate([w_out[:, cut], up], axis=1),
        )

    early0, late0 = columns(0)
    early1, late1 = columns(1)
    early_own = jnp.where(core == 0, early0, early1)
    early_got = swap(jnp.where(core == 0, early1, early0))
    late_own = jnp.where(core == 0, late0, late1)
    late_got = swap(jnp.where(core == 0, late1, late0))

    def both_cores(own, got):
        first = gather_chips(jnp.where(core == 0, own, got), "x")
        second = gather_chips(jnp.where(core == 0, got, own), "y")
        return jnp.stack([first, second], axis=1).reshape(chips * 2 * rows, own.shape[1])

    hidden_all = ordered(core, hidden_in, swap(hidden_in))
    early = both_cores(early_own, early_got)
    w_qkv_own = early[:, : 3 * half]
    w_pos_own = early[:, 3 * half : 5 * half]
    corner = early[:, 5 * half :].reshape(2 * chips, rows, half)
    table_half = corner[:, :table_rows].reshape(buckets, half)
    table = ordered(core, table_half, swap(table_half), axis=1)
    vectors = corner[:, table_rows].astype(f32)
    lists = vectors[:, : 9 * rows].reshape(2 * chips, 9, rows).transpose(1, 0, 2).reshape(9, D)
    qb, vb, pqb, ob, gain1, shift1, db, gain2, shift2 = [lists[i] for i in range(9)]
    up_lists = vectors[:, 9 * rows : 9 * rows + units].reshape(chips, 2, units)
    ub = jnp.where(core == 0, up_lists[:, 0], up_lists[:, 1]).reshape(ff_half)

    late = both_cores(late_own, late_got)
    down_left = gather_chips(w_down[:, :half], "x").reshape(ff_half, half)
    down_right = gather_chips(w_down[:, half:], "y").reshape(ff_half, half)
    w_down_own = jnp.concatenate([down_left, down_right], axis=1)
    out_columns = late[:, :half]
    w_out_own = ordered(
        core, half_of(core, out_columns, 0), swap(half_of(1 - core, out_columns, 0)), axis=1
    )
    w_up_own = late[:, half:]

    band = lax.broadcasted_iota(jnp.int32, (BAND, buckets), 0)
    bucket = lax.broadcasted_iota(jnp.int32, (BAND, buckets), 1)
    chosen = (jnp.clip(SPAN + 384 - band, 0, buckets - 1) == bucket).astype(bf)
    pos_shift = jnp.concatenate([jnp.zeros((half,), f32), half_of(core, pqb, 0)])
    pos = (product(table, w_pos_own) + pos_shift).astype(bf)
    pos_band = product(chosen, pos).astype(bf)
    pk, pq = pos_band[:, :half], pos_band[:, half:]

    qkv_shift = jnp.concatenate([half_of(core, qb, 0), jnp.zeros((half,), f32), half_of(core, vb, 0)])
    merged = (product(hidden_all, w_qkv_own) + qkv_shift).astype(bf)
    q, k, v = merged[:, :half], merged[:, half : 2 * half], merged[:, 2 * half :]
    context, probs = attention_forward(prefix, q, k, v, pk, pq)

    def summed_rows(left, multiply):
        given = swap(multiply(half_of(1 - core, left, 0)))
        return multiply(half_of(core, left, 0)) + given

    hidden_f = hidden_in.astype(f32)
    residual1 = hidden_f + summed_rows(context, lambda part: product(part, w_out_own)) + ob
    unit1, inverse1 = norm_parts(residual1)
    normed = unit1 * gain1 + shift1
    normed_low = normed.astype(bf)
    normed_all = ordered(core, normed_low, swap(normed_low))
    expanded = product(normed_all, w_up_own) + ub
    normal_cdf = 0.5 * lax.erfc(-expanded * math.sqrt(0.5))
    activated = (expanded * normal_cdf).astype(bf)
    slope = (
        normal_cdf + expanded * jnp.exp(-0.5 * expanded * expanded) * (1.0 / math.sqrt(2.0 * math.pi))
    ).astype(bf)
    residual2 = normed + summed_rows(activated, lambda part: product(part, w_down_own)) + db
    unit2, inverse2 = norm_parts(residual2)
    hidden_out = (unit2 * gain2 + shift2).astype(bf)

    grad = out_grad.astype(f32)
    d_res2 = norm_back(unit2, inverse2, gain2, grad)
    d_gain2 = jnp.sum(grad * unit2, axis=0)
    d_shift2 = jnp.sum(grad, axis=0)
    d_reduced = d_res2.astype(bf)
    d_down_bias = column_sums(d_reduced)
    reduced_all = ordered(core, d_reduced, swap(d_reduced))
    d_expanded = (inner_last(reduced_all, w_down_own) * slope.astype(f32)).astype(bf)
    d_normed = summed_rows(d_expanded, lambda part: inner_last(part, w_up_own)) + d_res2
    d_wdown = inner_first(activated, reduced_all).astype(bf)
    d_wup = inner_first(normed_all, d_expanded).astype(bf)
    d_up_bias = column_sums(d_expanded)
    d_res1 = norm_back(unit1, inverse1, gain1, d_normed)
    d_gain1 = jnp.sum(d_normed * unit1, axis=0)
    d_shift1 = jnp.sum(d_normed, axis=0)
    d_attended = d_res1.astype(bf)
    d_out_bias = column_sums(d_attended)
    attended_all = ordered(core, d_attended, swap(d_attended))
    d_context = inner_last(attended_all, w_out_own).astype(bf)
    d_wout_rows = inner_first(context, attended_all).astype(bf)
    d_wout = ordered(
        core, half_of(core, d_wout_rows, 1), swap(half_of(1 - core, d_wout_rows, 1)), axis=0
    )

    def spread_cores(matrix):
        split = matrix.reshape(chips, 2, rows, matrix.shape[1])
        return scatter_chips(split[:, 0], "x"), scatter_chips(split[:, 1], "y")

    def rejoin(first, second):
        own = jnp.where(core == 0, first, second)
        got = swap(jnp.where(core == 0, second, first))
        return jnp.where(core == 0, own, got), jnp.where(core == 0, got, own)

    late_grads = spread_cores(jnp.concatenate([d_wout, d_wup], axis=1))
    down_parts = d_wdown.reshape(chips, units, D)
    g_wdown = jnp.concatenate(
        [scatter_chips(down_parts[:, :, :half], "x"), scatter_chips(down_parts[:, :, half:], "y")], axis=1
    )

    d_q, d_k, d_v, d_pk, d_pq = attention_backward(q, k, v, d_context, probs, pk, pq)
    d_merged = jnp.concatenate([d_q, d_k, d_v], axis=1)
    in_grad = d_res1 + summed_rows(d_merged, lambda part: inner_last(part, w_qkv_own))
    d_wqkv = inner_first(hidden_all, d_merged).astype(bf)
    d_q_bias = column_sums(d_q)
    d_v_bias = column_sums(d_v)
    d_band = jnp.concatenate([d_pk, d_pq], axis=0).astype(bf)
    d_pos = lax.dot_general(
        chosen, d_band, (((0,), (1,)), ((), ())), preferred_element_type=f32
    )
    d_posq_bias = jnp.sum(d_pos[:, half:], axis=0)
    d_pos_low = d_pos.astype(bf)
    d_wpos = inner_first(table, d_pos_low).astype(bf)
    d_table_all = inner_last(d_pos_low, w_pos_own).astype(bf)
    d_table = (
        half_of(core, d_table_all, 1).astype(f32)
        + swap(half_of(1 - core, d_table_all, 1)).astype(f32)
    ).astype(bf)

    def whole(part):
        blank = jnp.zeros_like(part)
        return ordered(core, part, blank)

    lists_grad = jnp.stack(
        [
            whole(d_q_bias), whole(d_v_bias), whole(d_posq_bias), d_out_bias, d_gain1, d_shift1,
            d_down_bias, d_gain2, d_shift2,
        ]
    ).reshape(9, chips, 2, rows).transpose(2, 1, 0, 3).reshape(2, chips, 9 * rows)
    vector_own = jnp.where(core == 0, lists_grad[0], lists_grad[1])
    vector_got = swap(jnp.where(core == 0, lists_grad[1], lists_grad[0]))
    vector = jnp.concatenate(
        [vector_own + vector_got, d_up_bias.reshape(chips, units), jnp.zeros((chips, half - 9 * rows - units), f32)],
        axis=1,
    ).astype(bf)
    vector = jnp.broadcast_to(vector[:, None, None, :], (chips, 2, 1, half))
    corner_grad = jnp.concatenate(
        [d_table.reshape(chips, 2, table_rows, half), vector, jnp.zeros((chips, 2, last_rows, half), bf)], axis=2
    ).reshape(chips * 2 * rows, half)
    early_grads = spread_cores(jnp.concatenate([d_wqkv, d_wpos, corner_grad], axis=1))
    vector_sum = jnp.where(core == 0, early_grads[0], early_grads[1])[table_rows, 5 * half :]
    early_left, early_right = rejoin(*early_grads)
    late_left, late_right = rejoin(*late_grads)

    def side_by_side(left, right, at, count):
        pieces = []
        for index in range(count):
            cut = slice((at + index) * half, (at + index + 1) * half)
            pieces += [left[:, cut], right[:, cut]]
        return jnp.concatenate(pieces, axis=1)

    g_wqkv = side_by_side(early_left, early_right, 0, 3)
    g_wposk = side_by_side(early_left, early_right, 3, 1)
    g_wposq = side_by_side(early_left, early_right, 4, 1)
    g_table = side_by_side(early_left, early_right, 5, 1)[:table_rows]
    g_wout = side_by_side(late_left, late_right, 0, 1)
    g_wup = jnp.stack(
        [late_left[:, half:].reshape(rows, chips, units), late_right[:, half:].reshape(rows, chips, units)], axis=2
    ).reshape(rows, 2 * ff_half)
    g = [vector_sum[i * rows : (i + 1) * rows] for i in range(9)]
    g_up_bias = vector_sum[9 * rows : 9 * rows + units]
    return (
        hidden_out, in_grad, g_wqkv, g[0], g[1], g_table, g_wposk, g_wposq, g[2], g_wout, g[3], g[4], g[5],
        g_wup, g_up_bias, g_wdown, g[6], g[7], g[8],
    )


def row_split(
    hidden_in,
    prefix,
    w_qkv,
    q_bias,
    v_bias,
    rel_table,
    w_posk,
    w_posq,
    posq_bias,
    w_out,
    out_bias,
    norm1_gain,
    norm1_bias,
    w_up,
    up_bias,
    w_down,
    down_bias,
    norm2_gain,
    norm2_bias,
    out_grad,
):
    gathered = (
        lax.all_gather(w_qkv, ("dp", "seq"), axis=0, tiled=True),
        lax.all_gather(q_bias, ("dp", "seq"), axis=0, tiled=True),
        lax.all_gather(v_bias, ("dp", "seq"), axis=0, tiled=True),
        lax.all_gather(rel_table, ("dp", "seq"), axis=0, tiled=True),
        lax.all_gather(w_posk, ("dp", "seq"), axis=0, tiled=True),
        lax.all_gather(w_posq, ("dp", "seq"), axis=0, tiled=True),
        lax.all_gather(posq_bias, ("dp", "seq"), axis=0, tiled=True),
        lax.all_gather(w_out, ("dp", "seq"), axis=0, tiled=True),
        lax.all_gather(out_bias, ("dp", "seq"), axis=0, tiled=True),
        lax.all_gather(norm1_gain, ("dp", "seq"), axis=0, tiled=True),
        lax.all_gather(norm1_bias, ("dp", "seq"), axis=0, tiled=True),
        lax.all_gather(w_up, ("dp", "seq"), axis=0, tiled=True),
        lax.all_gather(up_bias, ("dp", "seq"), axis=0, tiled=True),
        lax.all_gather(w_down, ("dp", "seq"), axis=0, tiled=True),
        lax.all_gather(down_bias, ("dp", "seq"), axis=0, tiled=True),
        lax.all_gather(norm2_gain, ("dp", "seq"), axis=0, tiled=True),
        lax.all_gather(norm2_bias, ("dp", "seq"), axis=0, tiled=True),
    )
    (
        full_qkv,
        full_qb,
        full_vb,
        full_table,
        full_posk,
        full_posq,
        full_pqb,
        full_out,
        full_ob,
        full_g1,
        full_b1,
        full_up,
        full_ub,
        full_down,
        full_db,
        full_g2,
        full_b2,
    ) = gathered
    row_count = hidden_in.shape[0]
    groups = lax.axis_size("seq")
    seq_length = row_count * groups
    seq_rank = lax.axis_index("seq")
    prefix_len = prefix[0]
    score_scale = 1.0 / math.sqrt(3 * HEAD_DIM)
    buckets = 2 * SPAN
    window = row_count + buckets
    first_row = seq_rank * row_count
    query_pos = first_row + jnp.arange(row_count, dtype=jnp.int32)
    key_pos = jnp.arange(seq_length, dtype=jnp.int32)
    visible = (key_pos[None, :] < prefix_len) | (key_pos[None, :] <= query_pos[:, None])
    padded_cols = jnp.arange(seq_length + buckets, dtype=jnp.int32)
    below_window = padded_cols[None, :] < first_row

    def skew_table(table, row_total, offset, col_total):
        shifted = jnp.pad(
            jnp.flip(table, axis=1), ((0, 0), (row_count, row_count - 1)), mode="edge"
        )
        stride = shifted.shape[1] - 1
        flattened = shifted.reshape(-1)
        picked = lax.slice_in_dim(flattened, offset, offset + row_total * stride)
        return picked.reshape(row_total, stride)[:, :col_total]

    def pos_terms(table_a, table_w, edge_terms):
        band_terms = (
            skew_table(table_a, row_count, row_count - 1, window)
            + skew_table(table_w, window, window - 1, row_count).T
        )
        low_side = table_a[:, buckets - 1 : buckets] + jnp.pad(edge_terms[0], (SPAN, SPAN))[None, :]
        high_side = table_a[:, 0:1] + jnp.pad(edge_terms[1], (SPAN, SPAN))[None, :]
        backdrop = jnp.where(below_window, low_side, high_side)
        placed = lax.dynamic_update_slice(
            backdrop, band_terms, (jnp.zeros((), jnp.int32), first_row)
        )
        return placed[:, SPAN : SPAN + seq_length]

    pos_keys = product(full_table, full_posk).astype(jnp.bfloat16)
    pos_queries = (product(full_table, full_posq) + full_pqb.astype(jnp.float32)).astype(
        jnp.bfloat16
    )
    merged = product(hidden_in, full_qkv)
    queries = (merged[:, :D] + full_qb.astype(jnp.float32)).astype(jnp.bfloat16)
    keys_local = merged[:, D : 2 * D].astype(jnp.bfloat16)
    values_local = (merged[:, 2 * D :] + full_vb.astype(jnp.float32)).astype(jnp.bfloat16)
    keys_all, values_all = (
        lax.all_gather(keys_local, "seq", axis=0, tiled=True),
        lax.all_gather(values_local, "seq", axis=0, tiled=True),
    )
    query_heads = split_heads(queries)
    key_heads = split_heads(keys_all)
    value_heads = split_heads(values_all)
    posk_heads = split_heads(pos_keys)
    posq_heads = split_heads(pos_queries)

    def head_scores(query_h, key_h, posk_h, posq_h):
        content = inner_last(query_h, key_h)
        table_a = inner_last(query_h, posk_h)
        key_padded = jnp.pad(key_h, ((SPAN, SPAN), (0, 0)))
        key_window = lax.dynamic_slice_in_dim(key_padded, first_row, window, 0)
        table_w = inner_last(key_window, posq_h)
        end_rows = jnp.stack([posq_h[0], posq_h[buckets - 1]])
        edge_terms = inner_last(end_rows, key_h)
        raw = content + pos_terms(table_a, table_w, edge_terms)
        masked = jnp.where(visible, raw * score_scale, -jnp.inf)
        return (masked, table_a, table_w, edge_terms, key_window, end_rows)

    def head_forward(operands):
        query_h, key_h, value_h, posk_h, posq_h = operands
        scores = head_scores(query_h, key_h, posk_h, posq_h)[0]
        highest = jnp.max(scores, axis=1, keepdims=True)
        expo = jnp.exp(scores - highest)
        totals = jnp.sum(expo, axis=1, keepdims=True)
        probs_low = (expo / totals).astype(jnp.bfloat16)
        return (product(probs_low, value_h), (highest + jnp.log(totals))[:, 0])

    contexts, log_totals = lax.map(
        head_forward, (query_heads, key_heads, value_heads, posk_heads, posq_heads)
    )
    context = join_heads(contexts).astype(jnp.bfloat16)
    hidden_f = hidden_in.astype(jnp.float32)
    residual1 = hidden_f + product(context, full_out) + full_ob.astype(jnp.float32)
    gain1 = full_g1.astype(jnp.float32)
    shift1 = full_b1.astype(jnp.float32)
    normed = normalize(residual1, gain1, shift1)
    normed_low = normed.astype(jnp.bfloat16)
    expanded = product(normed_low, full_up) + full_ub.astype(jnp.float32)
    activated = gelu_exact(expanded).astype(jnp.bfloat16)
    residual2 = normed + product(activated, full_down) + full_db.astype(jnp.float32)
    gain2 = full_g2.astype(jnp.float32)
    shift2 = full_b2.astype(jnp.float32)
    hidden_out = normalize(residual2, gain2, shift2).astype(jnp.bfloat16)
    regathered = (
        lax.all_gather(w_qkv, ("dp", "seq"), axis=0, tiled=True),
        lax.all_gather(q_bias, ("dp", "seq"), axis=0, tiled=True),
        lax.all_gather(v_bias, ("dp", "seq"), axis=0, tiled=True),
        lax.all_gather(rel_table, ("dp", "seq"), axis=0, tiled=True),
        lax.all_gather(w_posk, ("dp", "seq"), axis=0, tiled=True),
        lax.all_gather(w_posq, ("dp", "seq"), axis=0, tiled=True),
        lax.all_gather(posq_bias, ("dp", "seq"), axis=0, tiled=True),
        lax.all_gather(w_out, ("dp", "seq"), axis=0, tiled=True),
        lax.all_gather(out_bias, ("dp", "seq"), axis=0, tiled=True),
        lax.all_gather(norm1_gain, ("dp", "seq"), axis=0, tiled=True),
        lax.all_gather(norm1_bias, ("dp", "seq"), axis=0, tiled=True),
        lax.all_gather(w_up, ("dp", "seq"), axis=0, tiled=True),
        lax.all_gather(up_bias, ("dp", "seq"), axis=0, tiled=True),
        lax.all_gather(w_down, ("dp", "seq"), axis=0, tiled=True),
        lax.all_gather(down_bias, ("dp", "seq"), axis=0, tiled=True),
        lax.all_gather(norm2_gain, ("dp", "seq"), axis=0, tiled=True),
        lax.all_gather(norm2_bias, ("dp", "seq"), axis=0, tiled=True),
    )
    (
        back_qkv,
        back_qb,
        back_vb,
        back_table,
        back_posk,
        back_posq,
        back_pqb,
        back_out,
        back_ob,
        back_g1,
        back_b1,
        back_up,
        back_ub,
        back_down,
        back_db,
        back_g2,
        back_b2,
    ) = regathered
    _, pull_second = jax.vjp(normalize, residual2, gain2, shift2)
    d_res2, d_gain2, d_shift2 = pull_second(out_grad.astype(jnp.float32))
    d_reduced = d_res2.astype(jnp.bfloat16)
    d_wdown = inner_first(activated, d_reduced)
    d_down_bias = column_sums(d_reduced)
    d_activated = inner_last(d_reduced, back_down)
    _, pull_gelu = jax.vjp(gelu_exact, expanded)
    d_expanded = pull_gelu(d_activated)[0].astype(jnp.bfloat16)
    d_wup = inner_first(normed_low, d_expanded)
    d_up_bias = column_sums(d_expanded)
    d_normed = inner_last(d_expanded, back_up) + d_res2
    _, pull_first = jax.vjp(normalize, residual1, gain1, shift1)
    d_res1, d_gain1, d_shift1 = pull_first(d_normed)
    d_attended = d_res1.astype(jnp.bfloat16)
    d_wout = inner_first(context, d_attended)
    d_out_bias = column_sums(d_attended)
    d_context = inner_last(d_attended, back_out).astype(jnp.bfloat16)
    dctx_heads = split_heads(d_context)

    def head_backward(operands):
        query_h, key_h, value_h, posk_h, posq_h, log_total, dctx_h = operands
        scores, table_a, table_w, edge_terms, key_window, end_rows = head_scores(
            query_h, key_h, posk_h, posq_h
        )
        probs = jnp.exp(scores - log_total[:, None])
        probs_low = probs.astype(jnp.bfloat16)
        d_probs = inner_last(dctx_h, value_h)
        d_value = inner_first(probs_low, dctx_h)
        row_dot = jnp.sum(probs * d_probs, axis=1, keepdims=True)
        d_raw = (probs * (d_probs - row_dot) * score_scale).astype(jnp.bfloat16)
        _, pull_terms = jax.vjp(pos_terms, table_a, table_w, edge_terms)
        d_table_a, d_table_w, d_edges = pull_terms(d_raw.astype(jnp.float32))
        d_table_a = d_table_a.astype(jnp.bfloat16)
        d_table_w = d_table_w.astype(jnp.bfloat16)
        d_edges = d_edges.astype(jnp.bfloat16)
        d_query = product(d_raw, key_h) + product(d_table_a, posk_h)
        window_grad = product(d_table_w, posq_h)
        key_canvas = jnp.zeros((seq_length + buckets, HEAD_DIM), jnp.float32)
        placed_grad = lax.dynamic_update_slice(
            key_canvas, window_grad, (first_row, jnp.zeros((), jnp.int32))
        )
        d_key = (
            inner_first(d_raw, query_h)
            + placed_grad[SPAN : SPAN + seq_length]
            + inner_first(d_edges, end_rows)
        )
        d_posk = inner_first(d_table_a, query_h)
        end_grads = product(d_edges, key_h)
        d_posq = inner_first(d_table_w, key_window)
        d_posq = d_posq.at[0].add(end_grads[0]).at[buckets - 1].add(end_grads[1])
        return (d_query, d_key, d_value, d_posk, d_posq)

    d_q_heads, d_k_heads, d_v_heads, d_posk_heads, d_posq_heads = lax.map(
        head_backward,
        (query_heads, key_heads, value_heads, posk_heads, posq_heads, log_totals, dctx_heads),
    )
    d_queries = join_heads(d_q_heads).astype(jnp.bfloat16)
    d_keys_part, d_values_part = (
        lax.psum_scatter(
            join_heads(d_k_heads).astype(jnp.bfloat16), "seq", scatter_dimension=0, tiled=True
        ).astype(jnp.float32),
        lax.psum_scatter(
            join_heads(d_v_heads).astype(jnp.bfloat16), "seq", scatter_dimension=0, tiled=True
        ).astype(jnp.float32),
    )
    d_keys = d_keys_part.astype(jnp.bfloat16)
    d_values = d_values_part.astype(jnp.bfloat16)
    d_merged = jnp.concatenate([d_queries, d_keys, d_values], axis=1)
    d_wqkv = inner_first(hidden_in, d_merged)
    d_q_bias = column_sums(d_queries)
    d_v_bias = column_sums(d_values)
    in_grad = d_res1 + inner_last(d_merged, back_qkv)
    d_posk_rows, d_posq_rows = (
        lax.psum_scatter(join_heads(d_posk_heads), ("dp", "seq"), scatter_dimension=0, tiled=True),
        lax.psum_scatter(join_heads(d_posq_heads), ("dp", "seq"), scatter_dimension=0, tiled=True),
    )
    d_posk_low = d_posk_rows.astype(jnp.bfloat16)
    d_posq_low = d_posq_rows.astype(jnp.bfloat16)
    rel_table_grad = inner_last(d_posk_low, back_posk) + inner_last(d_posq_low, back_posq)
    d_wposk = inner_first(rel_table, d_posk_low)
    d_wposq = inner_first(rel_table, d_posq_low)
    d_posq_bias = column_sums(d_posq_low)
    summed = (
        lax.psum_scatter(d_wqkv, ("dp", "seq"), scatter_dimension=0, tiled=True),
        lax.psum_scatter(d_q_bias, ("dp", "seq"), scatter_dimension=0, tiled=True),
        lax.psum_scatter(d_v_bias, ("dp", "seq"), scatter_dimension=0, tiled=True),
        lax.psum_scatter(d_wposk, ("dp", "seq"), scatter_dimension=0, tiled=True),
        lax.psum_scatter(d_wposq, ("dp", "seq"), scatter_dimension=0, tiled=True),
        lax.psum_scatter(d_posq_bias, ("dp", "seq"), scatter_dimension=0, tiled=True),
        lax.psum_scatter(d_wout, ("dp", "seq"), scatter_dimension=0, tiled=True),
        lax.psum_scatter(d_out_bias, ("dp", "seq"), scatter_dimension=0, tiled=True),
        lax.psum_scatter(d_gain1, ("dp", "seq"), scatter_dimension=0, tiled=True),
        lax.psum_scatter(d_shift1, ("dp", "seq"), scatter_dimension=0, tiled=True),
        lax.psum_scatter(d_wup, ("dp", "seq"), scatter_dimension=0, tiled=True),
        lax.psum_scatter(d_up_bias, ("dp", "seq"), scatter_dimension=0, tiled=True),
        lax.psum_scatter(d_wdown, ("dp", "seq"), scatter_dimension=0, tiled=True),
        lax.psum_scatter(d_down_bias, ("dp", "seq"), scatter_dimension=0, tiled=True),
        lax.psum_scatter(d_gain2, ("dp", "seq"), scatter_dimension=0, tiled=True),
        lax.psum_scatter(d_shift2, ("dp", "seq"), scatter_dimension=0, tiled=True),
    )
    return (
        hidden_out,
        in_grad,
        summed[0],
        summed[1],
        summed[2],
        rel_table_grad,
        summed[3],
        summed[4],
        summed[5],
        summed[6],
        summed[7],
        summed[8],
        summed[9],
        summed[10],
        summed[11],
        summed[12],
        summed[13],
        summed[14],
        summed[15],
    )


def solution(mesh):
    placed = (
        P(("dp", "seq"), None),
        P("dp"),
        P(("dp", "seq"), None),
        P(("dp", "seq")),
        P(("dp", "seq")),
        P(("dp", "seq"), None),
        P(("dp", "seq"), None),
        P(("dp", "seq"), None),
        P(("dp", "seq")),
        P(("dp", "seq"), None),
        P(("dp", "seq")),
        P(("dp", "seq")),
        P(("dp", "seq")),
        P(("dp", "seq"), None),
        P(("dp", "seq")),
        P(("dp", "seq"), None),
        P(("dp", "seq")),
        P(("dp", "seq")),
        P(("dp", "seq")),
        P(("dp", "seq"), None),
    )
    return jax.shard_map(
        head_split if dict(mesh.shape) == {"dp": 16, "seq": 2} else row_split,
        mesh=mesh,
        in_specs=placed,
        out_specs=(
            P(("dp", "seq"), None),
            P(("dp", "seq"), None),
            P(("dp", "seq"), None),
            P(("dp", "seq")),
            P(("dp", "seq")),
            P(("dp", "seq"), None),
            P(("dp", "seq"), None),
            P(("dp", "seq"), None),
            P(("dp", "seq")),
            P(("dp", "seq"), None),
            P(("dp", "seq")),
            P(("dp", "seq")),
            P(("dp", "seq")),
            P(("dp", "seq"), None),
            P(("dp", "seq")),
            P(("dp", "seq"), None),
            P(("dp", "seq")),
            P(("dp", "seq")),
            P(("dp", "seq")),
        ),
        check_vma=False,
    )
```

```python
import math

import jax
import jax.numpy as jnp
from jax import lax
from jax.experimental import pallas as pl
from jax.experimental.pallas import tpu as pltpu
from jax.sharding import PartitionSpec as P

D = 768
HEADS = 12
HEAD_DIM = 64
SPAN = 256
TILE = 128
BLOCK = 256
BAND = 768
PAIR = 2 * HEAD_DIM


eps_norm = 1e-07


def normalize(value, gain, shift):
    average = jnp.mean(value, axis=-1, keepdims=True)
    centred = value - average
    variance = jnp.mean(centred * centred, axis=-1, keepdims=True)
    return centred * lax.rsqrt(variance + eps_norm) * gain + shift


def gelu_exact(value):
    return jax.nn.gelu(value, approximate=False)


def product(left, right):
    return jnp.dot(left, right, preferred_element_type=jnp.float32)


def inner_first(left, right):
    return lax.dot_general(
        left, right, (((0,), (0,)), ((), ())), preferred_element_type=jnp.float32
    )


def inner_last(left, right):
    return lax.dot_general(
        left, right, (((1,), (1,)), ((), ())), preferred_element_type=jnp.float32
    )


def split_heads(matrix):
    return matrix.reshape(matrix.shape[0], HEADS, HEAD_DIM).transpose(1, 0, 2)


def join_heads(stacked):
    return stacked.transpose(1, 0, 2).reshape(stacked.shape[1], D)


def column_sums(matrix):
    return jnp.sum(matrix.astype(jnp.float32), axis=0)


def nn(left, right):
    return lax.dot_general(
        left, right, (((1,), (0,)), ((), ())), preferred_element_type=jnp.float32
    )


def nt(left, right):
    return lax.dot_general(
        left, right, (((1,), (1,)), ((), ())), preferred_element_type=jnp.float32
    )


def unit_matrix(size, reverse=False):
    rows = lax.broadcasted_iota(jnp.int32, (size, size), 0)
    cols = lax.broadcasted_iota(jnp.int32, (size, size), 1)
    if reverse:
        cols = size - 1 - cols
    return jnp.where(rows == cols, 1.0, 0.0).astype(jnp.bfloat16)


def head_lanes(head):
    lanes = lax.broadcasted_iota(jnp.int32, (1, PAIR), 1)
    return lanes // HEAD_DIM == head


def head_rows(head):
    rows = lax.broadcasted_iota(jnp.int32, (HEAD_DIM, PAIR), 0)
    cols = lax.broadcasted_iota(jnp.int32, (HEAD_DIM, PAIR), 1)
    return jnp.where(cols == rows + head * HEAD_DIM, 1.0, 0.0).astype(jnp.bfloat16)


def key_tiles(block, length):
    return max(length // 2, (block + 1) * BLOCK) // TILE


def tile_seen(query_tile, key_tile, length):
    return key_tile < key_tiles(query_tile * TILE // BLOCK, length)


def skewed(window):
    return pltpu.roll(window, 0, 1, stride=1, stride_axis=0)


def forward_body(prefix_ref, q_ref, k_ref, v_ref, pk_ref, pq_ref, ctx_ref, p_ref, wb_ref, far_ref, s_ref):
    length = q_ref.shape[0]
    head = pl.program_id(1)
    mine = head_lanes(head)
    prefix = prefix_ref[0]
    eye = unit_matrix(TILE)
    eye_block = unit_matrix(BLOCK)
    zero = jnp.zeros((), jnp.bfloat16)
    scale = math.log2(math.e) / math.sqrt(3 * HEAD_DIM)
    for tile in range(length // TILE):
        rows = slice(tile * TILE, (tile + 1) * TILE)
        table = nt(jnp.where(mine, k_ref[rows, :], zero), pq_ref[...])
        wb_ref[rows, :] = skewed(table)
        wb_ref[rows, 0:TILE] = table[:, BAND - TILE :]
        far_ref[rows, :] = table[:, 0:TILE]
    v_cols = nt(jnp.where(lax.broadcasted_iota(jnp.int32, (PAIR, PAIR), 0) // HEAD_DIM == head, unit_matrix(PAIR), zero), v_ref[...]).astype(jnp.bfloat16)
    for block in range(length // BLOCK):
        cols = slice(block * BLOCK, (block + 1) * BLOCK)
        q_own = jnp.where(mine, q_ref[cols, :], zero)
        skews, highs, lows = [], [], []
        for sub in range(2):
            table = nt(q_own[sub * TILE : (sub + 1) * TILE], pk_ref[...])
            skews.append(skewed(table).astype(jnp.bfloat16))
            highs.append(table[:, 0:TILE].astype(jnp.bfloat16))
            lows.append(table[:, BAND - TILE :].astype(jnp.bfloat16))
        count = key_tiles(block, length)
        highest = None
        for tile in range(count):
            rows = slice(tile * TILE, (tile + 1) * TILE)
            parts_a, parts_b = [], []
            for sub in range(2):
                step = 2 * block + sub - tile
                if step >= 3:
                    parts_a.append(highs[sub])
                    parts_b.append(wb_ref[rows, 0:TILE])
                elif step <= -3:
                    parts_a.append(lows[sub])
                    parts_b.append(far_ref[rows, :])
                else:
                    at = 384 - TILE * step
                    parts_a.append(skews[sub][:, at : at + TILE])
                    at = 384 + TILE * step
                    parts_b.append(wb_ref[rows, at : at + TILE])
            right = jnp.concatenate([jnp.concatenate(parts_a, axis=0), q_own], axis=1)
            left = jnp.concatenate([eye, k_ref[rows, :]], axis=1)
            raw = nt(left, right) + jnp.concatenate(parts_b, axis=1)
            if (tile + 1) * TILE > block * BLOCK + 1:
                keys = tile * TILE + lax.broadcasted_iota(jnp.int32, (TILE, BLOCK), 0)
                queries = block * BLOCK + lax.broadcasted_iota(jnp.int32, (TILE, BLOCK), 1)
                raw = jnp.where((keys < prefix) | (keys <= queries), raw, -jnp.inf)
            s_ref[rows, :] = raw
            top = jnp.max(raw, axis=0, keepdims=True)
            highest = top if highest is None else jnp.maximum(highest, top)
        total = jnp.zeros((1, BLOCK), jnp.float32)
        for tile in range(count):
            rows = slice(tile * TILE, (tile + 1) * TILE)
            expo = jnp.exp2((s_ref[rows, :] - highest) * scale)
            s_ref[rows, :] = expo
            total = total + jnp.sum(expo, axis=0, keepdims=True)
        inverse = 1.0 / total
        for tile in range(count):
            rows = slice(tile * TILE, (tile + 1) * TILE)
            p_ref[rows, cols] = (s_ref[rows, :] * inverse).astype(jnp.bfloat16)
        seen = count * TILE
        ctx_cols = nn(v_cols[:, :seen], p_ref[0:seen, cols]).astype(jnp.bfloat16)
        ctx = nt(eye_block, ctx_cols).astype(jnp.bfloat16)

        @pl.when(head == 0)
        def _():
            ctx_ref[cols, :] = ctx

        @pl.when(head == 1)
        def _():
            ctx_ref[cols, :] = ctx_ref[cols, :] + ctx


def attention_forward(prefix, merged, pos_band, pair):
    length, width = merged.shape[0], merged.shape[1] // 3
    pairs = width // PAIR
    tall = [pl.BlockSpec((length, PAIR), lambda p, h, at=at: (0, at)) for at in (pair, pairs + pair, 2 * pairs + pair)]
    band = [pl.BlockSpec((BAND, PAIR), lambda p, h, at=at: (0, at)) for at in (pair, pairs + pair)]
    return pl.pallas_call(
        forward_body,
        grid=(1, 2),
        in_specs=[pl.BlockSpec(memory_space=pltpu.SMEM)] + tall + band,
        out_specs=[
            pl.BlockSpec((length, PAIR), lambda p, h: (0, 0)),
            pl.BlockSpec((None, length, length), lambda p, h: (h, 0, 0)),
        ],
        out_shape=[
            jax.ShapeDtypeStruct((length, PAIR), jnp.bfloat16),
            jax.ShapeDtypeStruct((2, length, length), jnp.bfloat16),
        ],
        scratch_shapes=[
            pltpu.VMEM((length, BAND), jnp.float32),
            pltpu.VMEM((length, TILE), jnp.float32),
            pltpu.VMEM((length, BLOCK), jnp.float32),
        ],
        compiler_params=pltpu.CompilerParams(dimension_semantics=("arbitrary", "arbitrary"), vmem_limit_bytes=40 << 20),
        cost_estimate=pl.CostEstimate(flops=12 * 10**9, transcendentals=2 * length * length, bytes_accessed=6 << 20),
        name="attention_forward",
    )(prefix, merged, merged, merged, pos_band, pos_band)


def backward_body(q_ref, k_ref, v_ref, dctx_ref, p_ref, pk_ref, pq_ref, dq_ref, dk_ref, dv_ref, dpk_ref, dpq_ref, dr_ref, dk_acc, dv_acc):
    length = q_ref.shape[0]
    head = pl.program_id(1)
    mine = head_lanes(head)
    flip = unit_matrix(TILE, reverse=True)
    pick = head_rows(head)
    bf = jnp.bfloat16
    zero = jnp.zeros((), bf)
    scale = 1.0 / math.sqrt(3 * HEAD_DIM)
    back = BAND - (TILE - 1)
    blank = jnp.zeros((TILE, TILE), bf)
    dk_acc[...] = jnp.zeros_like(dk_acc)
    dv_acc[...] = jnp.zeros_like(dv_acc)
    dpk_ref[...] = jnp.zeros_like(dpk_ref)
    dpq_ref[...] = jnp.zeros_like(dpq_ref)

    def put(ref, rows, value):
        @pl.when(head == 0)
        def _():
            ref[rows, :] = jnp.where(mine, value, 0.0).astype(bf)

        @pl.when(head == 1)
        def _():
            ref[rows, :] = jnp.where(mine, value.astype(bf), ref[rows, :])

    for block in range(length // BLOCK):
        cols = slice(block * BLOCK, (block + 1) * BLOCK)
        count = key_tiles(block, length)
        seen = count * TILE
        dctx = dctx_ref[cols, :]
        v_own = jnp.where(mine, v_ref[0:seen, :], zero)
        probs_low = p_ref[0:seen, cols]
        probs = probs_low.astype(jnp.float32)
        d_probs = nt(v_own, dctx)
        row_dot = jnp.sum(probs * d_probs, axis=0, keepdims=True)
        d_raw = (probs * ((d_probs - row_dot) * scale)).astype(bf)
        dr_ref[0:seen, cols] = d_raw
        dv_acc[0:seen, :] += nn(probs_low, dctx)
        dk_acc[0:seen, :] += nn(d_raw, q_ref[cols, :])
        for sub in range(2):
            tile = 2 * block + sub
            own = slice(tile * TILE, (tile + 1) * TILE)
            turned_f = nt(flip, dr_ref[0:seen, own])
            turned = turned_f.astype(bf)
            dq = nn(turned, k_ref[0:seen, :])

            def piece(key_tile):
                return turned[:, key_tile * TILE : (key_tile + 1) * TILE]

            band = [blank]
            for step in (2, 1, 0, -1, -2):
                key_tile = tile - step
                band.append(piece(key_tile) if 0 <= key_tile < count else blank)
            spread = pltpu.roll(jnp.concatenate(band, axis=1), back, 1, stride=1, stride_axis=0)
            near = [turned_f[:, t * TILE : (t + 1) * TILE] for t in range(count) if tile - t >= 3]
            far = [turned_f[:, t * TILE : (t + 1) * TILE] for t in range(count) if tile - t <= -3]
            spread = add_edges(spread, near, far)
            dq = dq + nn(spread, pk_ref[...])
            put(dq_ref, own, nn(flip, dq.astype(bf)))
            q_turned = nn(flip, q_ref[own, :]).astype(bf)
            q_cols = nt(pick, q_turned).astype(bf)
            dpk_ref[...] += nn(q_cols, spread)
    tiles = length // TILE
    for key_tile in range(tiles):
        rows = slice(key_tile * TILE, (key_tile + 1) * TILE)

        def held(query_tile):
            return dr_ref[rows, query_tile * TILE : (query_tile + 1) * TILE]

        seen_by = [t for t in range(tiles) if tile_seen(t, key_tile, length)]
        band = [blank]
        for step in (-2, -1, 0, 1, 2):
            query_tile = key_tile + step
            band.append(held(query_tile) if query_tile in seen_by else blank)
        later = [held(t).astype(jnp.float32) for t in seen_by if t - key_tile >= 3]
        earlier = [held(t).astype(jnp.float32) for t in seen_by if t - key_tile <= -3]
        spread = pltpu.roll(nn(flip, jnp.concatenate(band, axis=1)).astype(bf), back, 1, stride=1, stride_axis=0)
        flat = lambda parts: [nn(flip, sum(parts[1:], parts[0]).astype(bf))] if parts else []
        spread = add_edges(spread, flat(earlier), flat(later))
        d_key = nn(flip, nn(spread, pq_ref[...]).astype(bf))
        put(dk_ref, rows, dk_acc[rows, :] + d_key)
        k_turned = nn(flip, k_ref[rows, :]).astype(bf)
        k_cols = nt(pick, k_turned).astype(bf)
        dpq_ref[...] += nn(k_cols, spread)
        put(dv_ref, rows, dv_acc[rows, :])


def add_edges(spread, first, last):
    parts = [spread[:, 0:TILE], spread[:, TILE : BAND - TILE], spread[:, BAND - TILE :]]
    for place, tiles in ((0, first), (2, last)):
        if tiles:
            total = parts[place].astype(jnp.float32)
            for tile in tiles:
                total = total + tile
            parts[place] = total.astype(jnp.bfloat16)
    return jnp.concatenate(parts, axis=1)


def attention_backward(merged, dctx, probs, pos_band, pair):
    length, width = merged.shape[0], merged.shape[1] // 3
    pairs = width // PAIR
    tall = [pl.BlockSpec((length, PAIR), lambda p, h, at=at: (0, at)) for at in (pair, pairs + pair, 2 * pairs + pair, pair)]
    band = [pl.BlockSpec((BAND, PAIR), lambda p, h, at=at: (0, at)) for at in (pair, pairs + pair)]
    own = pl.BlockSpec((length, PAIR), lambda p, h: (0, 0))
    table = pl.BlockSpec((HEAD_DIM, BAND), lambda p, h: (h, 0))
    flat = jax.ShapeDtypeStruct((length, PAIR), jnp.bfloat16)
    wide = jax.ShapeDtypeStruct((PAIR, BAND), jnp.float32)
    return pl.pallas_call(
        backward_body,
        grid=(1, 2),
        in_specs=tall + [pl.BlockSpec((None, length, length), lambda p, h: (h, 0, 0))] + band,
        out_specs=[own, own, own, table, table],
        out_shape=[flat, flat, flat, wide, wide],
        scratch_shapes=[
            pltpu.VMEM((length, length), jnp.bfloat16),
            pltpu.VMEM((length, PAIR), jnp.float32),
            pltpu.VMEM((length, PAIR), jnp.float32),
        ],
        compiler_params=pltpu.CompilerParams(dimension_semantics=("arbitrary", "arbitrary"), vmem_limit_bytes=40 << 20),
        cost_estimate=pl.CostEstimate(flops=35 * 10**9, transcendentals=0, bytes_accessed=8 << 20),
        name="attention_backward",
    )(merged, merged, merged, dctx, probs, pos_band, pos_band)


CORES = [(0, 1), (1, 0)]


def swap(value):
    return lax.ppermute(value, "seq", CORES)


def ordered(core, own, other, axis=0):
    return jnp.concatenate(
        [jnp.where(core == 0, own, other), jnp.where(core == 0, other, own)], axis=axis
    )


def half_of(core, matrix, axis):
    size = matrix.shape[axis] // 2
    return lax.dynamic_slice_in_dim(matrix, core * size, size, axis)


def chip_bits():
    chip = lax.axis_index("dp")
    return chip // 4, (chip // 2) % 2, chip % 2


def exchange(value, mask):
    return lax.ppermute(value, "dp", [(i, i ^ mask) for i in range(16)])


def tied(*values):
    return lax.optimization_barrier(values)


class Gather:
    def __init__(self, value):
        self.below, self.above = [value], [value]
        self.state = value

    def hold(self, *others):
        self.state, *others = tied(self.state, *others)
        return others

    def line(self, step):
        up = [(i, i + 4) for i in range(12) if i // 4 >= step - 1]
        down = [(i + 4, i) for i in range(12) if i // 4 <= 3 - step]
        if step == 1:
            self.below, self.above = [self.state], [self.state]
        self.below.append(lax.ppermute(self.below[-1], "dp", up))
        self.above.append(lax.ppermute(self.above[-1], "dp", down))
        if step == 3:
            z = chip_bits()[0]
            blocks = []
            for block in range(4):
                options = [self.below[k - block] if k >= block else self.above[block - k] for k in range(4)]
                blocks.append(lax.select_n(z, *options))
            self.state = (jnp.stack([b[0] for b in blocks]), jnp.stack([b[1] for b in blocks]))

    def pair(self, step):
        _, y, x = chip_bits()
        first, second = self.state
        order = ((x, 1), (y, 2)) if step == 1 else ((y, 2), (x, 1))
        result = []
        for value, (bit, mask) in zip((first, second), order):
            other = exchange(value, mask)
            result.append(jnp.stack([jnp.where(bit == 0, value, other), jnp.where(bit == 0, other, value)]))
        self.state = tuple(result)

    def rows(self):
        first, second = self.state
        first = jnp.moveaxis(first, (0, 1, 2), (1, 2, 0))
        second = jnp.moveaxis(second, (0, 1, 2), (2, 1, 0))
        whole = jnp.stack([first, second], axis=3)
        return whole.reshape(-1, whole.shape[-1])


class Scatter:
    def __init__(self, value):
        grid = value.reshape((4, 2, 2) + value.shape[1:])
        self.state = (jnp.moveaxis(grid[:, :, :, 0], 2, 0), jnp.moveaxis(grid[:, :, :, 1], 1, 0))
        self.dtype = value.dtype

    def hold(self, *others):
        self.state, *others = tied(self.state, *others)
        return others

    def pair(self, step):
        _, y, x = chip_bits()
        order = ((x, 1), (y, 2)) if step == 1 else ((y, 2), (x, 1))
        result = []
        for value, (bit, mask) in zip(self.state, order):
            keep = jnp.where(bit == 0, value[0], value[1])
            give = jnp.where(bit == 0, value[1], value[0])
            total = (keep.astype(jnp.float32) + exchange(give, mask).astype(jnp.float32)).astype(self.dtype)
            result.append(jnp.moveaxis(total, 1, 0) if step == 1 else total)
        self.state = tuple(result) if step == 1 else (jnp.stack(result, axis=1), None, None)

    def line(self, step):
        z = chip_bits()[0]
        value, up, down = self.state
        offset = 4 - step

        def block(at):
            options = [value[min(max(k + at, 0), 3)] for k in range(4)]
            return lax.select_n(z, *options).astype(jnp.float32)

        to_above, to_below = block(offset), block(-offset)
        if up is not None:
            to_above = to_above + up.astype(jnp.float32)
            to_below = to_below + down.astype(jnp.float32)
        ups = [(i, i + 4) for i in range(12) if i // 4 + offset <= 3]
        downs = [(i + 4, i) for i in range(12) if i // 4 + 1 - offset >= 0]
        up = lax.ppermute(to_above.astype(self.dtype), "dp", ups)
        down = lax.ppermute(to_below.astype(self.dtype), "dp", downs)
        self.state = (value, up, down)
        if step == 3:
            self.total = block(0) + up.astype(jnp.float32) + down.astype(jnp.float32)


def norm_parts(value):
    average = jnp.mean(value, axis=-1, keepdims=True)
    centred = value - average
    variance = jnp.mean(centred * centred, axis=-1, keepdims=True)
    inverse = lax.rsqrt(variance + eps_norm)
    return centred * inverse, inverse


def norm_back(unit, inverse, gain, grad):
    scaled = grad * gain
    mean_grad = jnp.mean(scaled, axis=-1, keepdims=True)
    mean_along = jnp.mean(scaled * unit, axis=-1, keepdims=True)
    return inverse * (scaled - mean_grad - unit * mean_along)


def head_split(
    hidden_in, prefix, w_qkv, q_bias, v_bias, rel_table, w_posk, w_posq, posq_bias, w_out, out_bias,
    norm1_gain, norm1_bias, w_up, up_bias, w_down, down_bias, norm2_gain, norm2_bias, out_grad,
):
    bf = jnp.bfloat16
    f32 = jnp.float32
    core = lax.axis_index("seq")
    rows = w_qkv.shape[0]
    units = w_down.shape[0]
    table_rows = rel_table.shape[0]
    chips = 16
    half = D // 2
    ff_half = chips * units
    buckets = 2 * SPAN

    small = jnp.concatenate(
        [q_bias, v_bias, posq_bias, out_bias, norm1_gain, norm1_bias, down_bias, norm2_gain, norm2_bias, up_bias]
    )
    small = jnp.pad(small, (0, half - small.shape[0]))[None, :]
    last_rows = rows - table_rows - 1

    def columns(side):
        qkv = w_qkv.reshape(rows, 3, 2, half)[:, :, side].reshape(rows, 3 * half)
        corner = jnp.concatenate(
            [rel_table[:, side * half : (side + 1) * half], small, jnp.zeros((last_rows, half), bf)], axis=0
        )
        cut = slice(side * half, (side + 1) * half)
        up = w_up.reshape(rows, chips, 2, units)[:, :, side].reshape(rows, ff_half)
        down = w_down[:, cut].reshape(-1, rows, half)
        down = jnp.concatenate([down[i] for i in range(down.shape[0])], axis=1)
        return (
            jnp.concatenate([qkv, w_posk[:, cut], w_posq[:, cut], corner], axis=1),
            jnp.concatenate([w_out[:, cut], up], axis=1),
            down,
        )

    early0, late0, down0 = columns(0)
    early1, late1, down1 = columns(1)
    early_got = swap(jnp.where(core == 0, early1, early0))
    late_got = swap(jnp.where(core == 0, late1, late0))
    hidden_got = swap(hidden_in)

    def by_core(first, second, got):
        own = jnp.where(core == 0, first, second)
        return jnp.stack([jnp.where(core == 0, own, got), jnp.where(core == 0, got, own)])

    early_chain = Gather(by_core(early0, early1, early_got))
    late_chain = Gather(
        jnp.concatenate([by_core(late0, late1, late_got), jnp.stack([down0, down1])], axis=2)
    )
    for step in (1, 2, 3):
        early_chain.line(step)
    (early_chain.state,) = late_chain.hold(early_chain.state)
    early_chain.pair(1)
    late_chain.line(1)
    late_chain.line(2)
    early_chain.pair(2)
    late_chain.line(3)
    (early_chain.state,) = late_chain.hold(early_chain.state)
    late_chain.pair(1)
    hidden_all = ordered(core, hidden_in, hidden_got)
    early = early_chain.rows()
    w_qkv_own = early[:, : 3 * half]
    w_pos_own = early[:, 3 * half : 5 * half]
    corner = early[:, 5 * half :].reshape(2 * chips, rows, half)
    table_half = corner[:, :table_rows].reshape(buckets, half)
    table = ordered(core, table_half, swap(table_half), axis=1)
    vectors = corner[:, table_rows].astype(f32)
    lists = vectors[:, : 9 * rows].reshape(2 * chips, 9, rows).transpose(1, 0, 2).reshape(9, D)
    qb, vb, pqb, ob, gain1, shift1, db, gain2, shift2 = [lists[i] for i in range(9)]
    up_lists = vectors[:, 9 * rows : 9 * rows + units].reshape(chips, 2, units)
    ub = jnp.where(core == 0, up_lists[:, 0], up_lists[:, 1]).reshape(ff_half)

    band = lax.broadcasted_iota(jnp.int32, (BAND, buckets), 0)
    bucket = lax.broadcasted_iota(jnp.int32, (BAND, buckets), 1)
    chosen = (jnp.clip(SPAN + 384 - band, 0, buckets - 1) == bucket).astype(bf)
    pos_shift = jnp.concatenate([jnp.zeros((half,), f32), half_of(core, pqb, 0)])
    pos = (product(table, w_pos_own) + pos_shift).astype(bf)
    pos_band = product(chosen, pos).astype(bf)

    qkv_shift = jnp.concatenate([half_of(core, qb, 0), jnp.zeros((half,), f32), half_of(core, vb, 0)])
    merged = (product(hidden_all, w_qkv_own) + qkv_shift).astype(bf)
    context_parts, prob_parts = [], []
    for pair in range(half // PAIR):
        part, kept = attention_forward(prefix, merged, pos_band, pair)
        if pair == 0:
            part, merged = late_chain.hold(part, merged)
            late_chain.pair(2)
        context_parts.append(part)
        prob_parts.append(kept)
    context = jnp.concatenate(context_parts, axis=1)
    late = late_chain.rows()
    out_columns = late[:, :half]
    w_out_own = ordered(
        core, half_of(core, out_columns, 0), swap(half_of(1 - core, out_columns, 0)), axis=1
    )
    w_up_own = late[:, half : half + ff_half]
    w_down_own = (
        late[:, half + ff_half :].reshape(chips, 2, rows, -1, half).transpose(0, 3, 2, 1, 4).reshape(ff_half, D)
    )

    def summed_rows(left, multiply):
        given = swap(multiply(half_of(1 - core, left, 0)))
        return multiply(half_of(core, left, 0)) + given

    hidden_f = hidden_in.astype(f32)
    residual1 = hidden_f + summed_rows(context, lambda part: product(part, w_out_own)) + ob
    unit1, inverse1 = norm_parts(residual1)
    normed = unit1 * gain1 + shift1
    normed_low = normed.astype(bf)
    normed_all = ordered(core, normed_low, swap(normed_low))
    expanded = product(normed_all, w_up_own) + ub
    normal_cdf = 0.5 + 0.5 * lax.erf(expanded * math.sqrt(0.5))
    activated = (expanded * normal_cdf).astype(bf)
    slope = (
        normal_cdf + expanded * jnp.exp(-0.5 * expanded * expanded) * (1.0 / math.sqrt(2.0 * math.pi))
    ).astype(bf)
    residual2 = normed + summed_rows(activated, lambda part: product(part, w_down_own)) + db
    unit2, inverse2 = norm_parts(residual2)
    hidden_out = (unit2 * gain2 + shift2).astype(bf)

    grad = out_grad.astype(f32)
    d_res2 = norm_back(unit2, inverse2, gain2, grad)
    d_gain2 = jnp.sum(grad * unit2, axis=0)
    d_shift2 = jnp.sum(grad, axis=0)
    d_reduced = d_res2.astype(bf)
    d_down_bias = column_sums(d_reduced)
    reduced_all = ordered(core, d_reduced, swap(d_reduced))
    d_expanded = (inner_last(reduced_all, w_down_own) * slope.astype(f32)).astype(bf)
    d_normed = summed_rows(d_expanded, lambda part: inner_last(part, w_up_own)) + d_res2
    d_wdown = inner_first(activated, reduced_all).astype(bf)
    d_wup = inner_first(normed_all, d_expanded).astype(bf)
    d_up_bias = column_sums(d_expanded)
    d_res1 = norm_back(unit1, inverse1, gain1, d_normed)
    d_gain1 = jnp.sum(d_normed * unit1, axis=0)
    d_shift1 = jnp.sum(d_normed, axis=0)
    d_attended = d_res1.astype(bf)
    d_out_bias = column_sums(d_attended)
    attended_all = ordered(core, d_attended, swap(d_attended))
    d_context = inner_last(attended_all, w_out_own).astype(bf)
    d_wout_rows = inner_first(context, attended_all).astype(bf)
    d_wout = ordered(
        core, half_of(core, d_wout_rows, 1), swap(half_of(1 - core, d_wout_rows, 1)), axis=0
    )

    def rejoin(first, second):
        own = jnp.where(core == 0, first, second)
        got = swap(jnp.where(core == 0, second, first))
        return jnp.where(core == 0, own, got), jnp.where(core == 0, got, own)

    late_cols = jnp.concatenate([d_wout, d_wup], axis=1).reshape(chips, 2, rows, half + ff_half)
    down_cols = d_wdown.reshape(chips, -1, rows, 2, half).transpose(0, 3, 2, 1, 4).reshape(chips, 2, rows, ff_half)
    late_sums = Scatter(jnp.concatenate([late_cols, down_cols], axis=3))
    late_steps = [lambda: late_sums.pair(1), lambda: late_sums.pair(2), lambda: late_sums.line(1)]
    grads = []
    (d_context,) = late_sums.hold(d_context)
    for pair in range(half // PAIR):
        late_steps[pair]()
        found = attention_backward(merged, d_context, prob_parts[pair], pos_band, pair)
        *found, d_context = late_sums.hold(*found, d_context)
        grads.append(found)
    late_sums.line(2)
    d_merged = jnp.concatenate([g[i] for i in range(3) for g in grads], axis=1)
    d_q, d_v = d_merged[:, :half], d_merged[:, 2 * half :]
    in_grad = d_res1 + summed_rows(d_merged, lambda part: inner_last(part, w_qkv_own))
    d_wqkv = inner_first(hidden_all, d_merged).astype(bf)
    d_q_bias = column_sums(d_q)
    d_v_bias = column_sums(d_v)
    d_band = jnp.concatenate([g[i] for i in (3, 4) for g in grads], axis=0).astype(bf)
    d_pos = lax.dot_general(
        chosen, d_band, (((0,), (1,)), ((), ())), preferred_element_type=f32
    )
    d_posq_bias = jnp.sum(d_pos[:, half:], axis=0)
    d_pos_low = d_pos.astype(bf)
    d_wpos = inner_first(table, d_pos_low).astype(bf)
    d_table_all = inner_last(d_pos_low, w_pos_own).astype(bf)
    d_table = (
        half_of(core, d_table_all, 1).astype(f32)
        + swap(half_of(1 - core, d_table_all, 1)).astype(f32)
    ).astype(bf)

    def whole(part):
        blank = jnp.zeros_like(part)
        return ordered(core, part, blank)

    lists_grad = jnp.stack(
        [
            whole(d_q_bias), whole(d_v_bias), whole(d_posq_bias), d_out_bias, d_gain1, d_shift1,
            d_down_bias, d_gain2, d_shift2,
        ]
    ).reshape(9, chips, 2, rows).transpose(2, 1, 0, 3).reshape(2, chips, 9 * rows)
    vector_own = jnp.where(core == 0, lists_grad[0], lists_grad[1])
    vector_got = swap(jnp.where(core == 0, lists_grad[1], lists_grad[0]))
    vector = jnp.concatenate(
        [vector_own + vector_got, d_up_bias.reshape(chips, units), jnp.zeros((chips, half - 9 * rows - units), f32)],
        axis=1,
    ).astype(bf)
    vector = jnp.broadcast_to(vector[:, None, None, :], (chips, 2, 1, half))
    corner_grad = jnp.concatenate(
        [d_table.reshape(chips, 2, table_rows, half), vector, jnp.zeros((chips, 2, last_rows, half), bf)], axis=2
    ).reshape(chips * 2 * rows, half)
    late_sums.line(3)
    early_sums = Scatter(
        jnp.concatenate([d_wqkv, d_wpos, corner_grad], axis=1).reshape(chips, 2, rows, 6 * half)
    )
    early_sums.pair(1)
    early_sums.pair(2)
    for step in (1, 2, 3):
        early_sums.line(step)
    early_grads, late_grads = early_sums.total, late_sums.total
    down_own = late_grads[:, :, half + ff_half :].reshape(2, rows, -1, half).transpose(2, 1, 0, 3).reshape(units, D)
    g_wdown = down_own
    vector_sum = jnp.where(core == 0, early_grads[0], early_grads[1])[table_rows, 5 * half :]
    early_left, early_right = rejoin(early_grads[0], early_grads[1])
    late_left, late_right = rejoin(late_grads[0, :, : half + ff_half], late_grads[1, :, : half + ff_half])

    def side_by_side(left, right, at, count):
        pieces = []
        for index in range(count):
            cut = slice((at + index) * half, (at + index + 1) * half)
            pieces += [left[:, cut], right[:, cut]]
        return jnp.concatenate(pieces, axis=1)

    g_wqkv = side_by_side(early_left, early_right, 0, 3)
    g_wposk = side_by_side(early_left, early_right, 3, 1)
    g_wposq = side_by_side(early_left, early_right, 4, 1)
    g_table = side_by_side(early_left, early_right, 5, 1)[:table_rows]
    g_wout = side_by_side(late_left, late_right, 0, 1)
    g_wup = jnp.stack(
        [late_left[:, half:].reshape(rows, chips, units), late_right[:, half:].reshape(rows, chips, units)], axis=2
    ).reshape(rows, 2 * ff_half)
    g = [vector_sum[i * rows : (i + 1) * rows] for i in range(9)]
    g_up_bias = vector_sum[9 * rows : 9 * rows + units]
    return (
        hidden_out, in_grad, g_wqkv, g[0], g[1], g_table, g_wposk, g_wposq, g[2], g_wout, g[3], g[4], g[5],
        g_wup, g_up_bias, g_wdown, g[6], g[7], g[8],
    )


def row_split(
    hidden_in,
    prefix,
    w_qkv,
    q_bias,
    v_bias,
    rel_table,
    w_posk,
    w_posq,
    posq_bias,
    w_out,
    out_bias,
    norm1_gain,
    norm1_bias,
    w_up,
    up_bias,
    w_down,
    down_bias,
    norm2_gain,
    norm2_bias,
    out_grad,
):
    gathered = (
        lax.all_gather(w_qkv, ("dp", "seq"), axis=0, tiled=True),
        lax.all_gather(q_bias, ("dp", "seq"), axis=0, tiled=True),
        lax.all_gather(v_bias, ("dp", "seq"), axis=0, tiled=True),
        lax.all_gather(rel_table, ("dp", "seq"), axis=0, tiled=True),
        lax.all_gather(w_posk, ("dp", "seq"), axis=0, tiled=True),
        lax.all_gather(w_posq, ("dp", "seq"), axis=0, tiled=True),
        lax.all_gather(posq_bias, ("dp", "seq"), axis=0, tiled=True),
        lax.all_gather(w_out, ("dp", "seq"), axis=0, tiled=True),
        lax.all_gather(out_bias, ("dp", "seq"), axis=0, tiled=True),
        lax.all_gather(norm1_gain, ("dp", "seq"), axis=0, tiled=True),
        lax.all_gather(norm1_bias, ("dp", "seq"), axis=0, tiled=True),
        lax.all_gather(w_up, ("dp", "seq"), axis=0, tiled=True),
        lax.all_gather(up_bias, ("dp", "seq"), axis=0, tiled=True),
        lax.all_gather(w_down, ("dp", "seq"), axis=0, tiled=True),
        lax.all_gather(down_bias, ("dp", "seq"), axis=0, tiled=True),
        lax.all_gather(norm2_gain, ("dp", "seq"), axis=0, tiled=True),
        lax.all_gather(norm2_bias, ("dp", "seq"), axis=0, tiled=True),
    )
    (
        full_qkv,
        full_qb,
        full_vb,
        full_table,
        full_posk,
        full_posq,
        full_pqb,
        full_out,
        full_ob,
        full_g1,
        full_b1,
        full_up,
        full_ub,
        full_down,
        full_db,
        full_g2,
        full_b2,
    ) = gathered
    row_count = hidden_in.shape[0]
    groups = lax.axis_size("seq")
    seq_length = row_count * groups
    seq_rank = lax.axis_index("seq")
    prefix_len = prefix[0]
    score_scale = 1.0 / math.sqrt(3 * HEAD_DIM)
    buckets = 2 * SPAN
    window = row_count + buckets
    first_row = seq_rank * row_count
    query_pos = first_row + jnp.arange(row_count, dtype=jnp.int32)
    key_pos = jnp.arange(seq_length, dtype=jnp.int32)
    visible = (key_pos[None, :] < prefix_len) | (key_pos[None, :] <= query_pos[:, None])
    padded_cols = jnp.arange(seq_length + buckets, dtype=jnp.int32)
    below_window = padded_cols[None, :] < first_row

    def skew_table(table, row_total, offset, col_total):
        shifted = jnp.pad(
            jnp.flip(table, axis=1), ((0, 0), (row_count, row_count - 1)), mode="edge"
        )
        stride = shifted.shape[1] - 1
        flattened = shifted.reshape(-1)
        picked = lax.slice_in_dim(flattened, offset, offset + row_total * stride)
        return picked.reshape(row_total, stride)[:, :col_total]

    def pos_terms(table_a, table_w, edge_terms):
        band_terms = (
            skew_table(table_a, row_count, row_count - 1, window)
            + skew_table(table_w, window, window - 1, row_count).T
        )
        low_side = table_a[:, buckets - 1 : buckets] + jnp.pad(edge_terms[0], (SPAN, SPAN))[None, :]
        high_side = table_a[:, 0:1] + jnp.pad(edge_terms[1], (SPAN, SPAN))[None, :]
        backdrop = jnp.where(below_window, low_side, high_side)
        placed = lax.dynamic_update_slice(
            backdrop, band_terms, (jnp.zeros((), jnp.int32), first_row)
        )
        return placed[:, SPAN : SPAN + seq_length]

    pos_keys = product(full_table, full_posk).astype(jnp.bfloat16)
    pos_queries = (product(full_table, full_posq) + full_pqb.astype(jnp.float32)).astype(
        jnp.bfloat16
    )
    merged = product(hidden_in, full_qkv)
    queries = (merged[:, :D] + full_qb.astype(jnp.float32)).astype(jnp.bfloat16)
    keys_local = merged[:, D : 2 * D].astype(jnp.bfloat16)
    values_local = (merged[:, 2 * D :] + full_vb.astype(jnp.float32)).astype(jnp.bfloat16)
    keys_all, values_all = (
        lax.all_gather(keys_local, "seq", axis=0, tiled=True),
        lax.all_gather(values_local, "seq", axis=0, tiled=True),
    )
    query_heads = split_heads(queries)
    key_heads = split_heads(keys_all)
    value_heads = split_heads(values_all)
    posk_heads = split_heads(pos_keys)
    posq_heads = split_heads(pos_queries)

    def head_scores(query_h, key_h, posk_h, posq_h):
        content = inner_last(query_h, key_h)
        table_a = inner_last(query_h, posk_h)
        key_padded = jnp.pad(key_h, ((SPAN, SPAN), (0, 0)))
        key_window = lax.dynamic_slice_in_dim(key_padded, first_row, window, 0)
        table_w = inner_last(key_window, posq_h)
        end_rows = jnp.stack([posq_h[0], posq_h[buckets - 1]])
        edge_terms = inner_last(end_rows, key_h)
        raw = content + pos_terms(table_a, table_w, edge_terms)
        masked = jnp.where(visible, raw * score_scale, -jnp.inf)
        return (masked, table_a, table_w, edge_terms, key_window, end_rows)

    def head_forward(operands):
        query_h, key_h, value_h, posk_h, posq_h = operands
        scores = head_scores(query_h, key_h, posk_h, posq_h)[0]
        highest = jnp.max(scores, axis=1, keepdims=True)
        expo = jnp.exp(scores - highest)
        totals = jnp.sum(expo, axis=1, keepdims=True)
        probs_low = (expo / totals).astype(jnp.bfloat16)
        return (product(probs_low, value_h), (highest + jnp.log(totals))[:, 0])

    contexts, log_totals = lax.map(
        head_forward, (query_heads, key_heads, value_heads, posk_heads, posq_heads)
    )
    context = join_heads(contexts).astype(jnp.bfloat16)
    hidden_f = hidden_in.astype(jnp.float32)
    residual1 = hidden_f + product(context, full_out) + full_ob.astype(jnp.float32)
    gain1 = full_g1.astype(jnp.float32)
    shift1 = full_b1.astype(jnp.float32)
    normed = normalize(residual1, gain1, shift1)
    normed_low = normed.astype(jnp.bfloat16)
    expanded = product(normed_low, full_up) + full_ub.astype(jnp.float32)
    activated = gelu_exact(expanded).astype(jnp.bfloat16)
    residual2 = normed + product(activated, full_down) + full_db.astype(jnp.float32)
    gain2 = full_g2.astype(jnp.float32)
    shift2 = full_b2.astype(jnp.float32)
    hidden_out = normalize(residual2, gain2, shift2).astype(jnp.bfloat16)
    regathered = (
        lax.all_gather(w_qkv, ("dp", "seq"), axis=0, tiled=True),
        lax.all_gather(q_bias, ("dp", "seq"), axis=0, tiled=True),
        lax.all_gather(v_bias, ("dp", "seq"), axis=0, tiled=True),
        lax.all_gather(rel_table, ("dp", "seq"), axis=0, tiled=True),
        lax.all_gather(w_posk, ("dp", "seq"), axis=0, tiled=True),
        lax.all_gather(w_posq, ("dp", "seq"), axis=0, tiled=True),
        lax.all_gather(posq_bias, ("dp", "seq"), axis=0, tiled=True),
        lax.all_gather(w_out, ("dp", "seq"), axis=0, tiled=True),
        lax.all_gather(out_bias, ("dp", "seq"), axis=0, tiled=True),
        lax.all_gather(norm1_gain, ("dp", "seq"), axis=0, tiled=True),
        lax.all_gather(norm1_bias, ("dp", "seq"), axis=0, tiled=True),
        lax.all_gather(w_up, ("dp", "seq"), axis=0, tiled=True),
        lax.all_gather(up_bias, ("dp", "seq"), axis=0, tiled=True),
        lax.all_gather(w_down, ("dp", "seq"), axis=0, tiled=True),
        lax.all_gather(down_bias, ("dp", "seq"), axis=0, tiled=True),
        lax.all_gather(norm2_gain, ("dp", "seq"), axis=0, tiled=True),
        lax.all_gather(norm2_bias, ("dp", "seq"), axis=0, tiled=True),
    )
    (
        back_qkv,
        back_qb,
        back_vb,
        back_table,
        back_posk,
        back_posq,
        back_pqb,
        back_out,
        back_ob,
        back_g1,
        back_b1,
        back_up,
        back_ub,
        back_down,
        back_db,
        back_g2,
        back_b2,
    ) = regathered
    _, pull_second = jax.vjp(normalize, residual2, gain2, shift2)
    d_res2, d_gain2, d_shift2 = pull_second(out_grad.astype(jnp.float32))
    d_reduced = d_res2.astype(jnp.bfloat16)
    d_wdown = inner_first(activated, d_reduced)
    d_down_bias = column_sums(d_reduced)
    d_activated = inner_last(d_reduced, back_down)
    _, pull_gelu = jax.vjp(gelu_exact, expanded)
    d_expanded = pull_gelu(d_activated)[0].astype(jnp.bfloat16)
    d_wup = inner_first(normed_low, d_expanded)
    d_up_bias = column_sums(d_expanded)
    d_normed = inner_last(d_expanded, back_up) + d_res2
    _, pull_first = jax.vjp(normalize, residual1, gain1, shift1)
    d_res1, d_gain1, d_shift1 = pull_first(d_normed)
    d_attended = d_res1.astype(jnp.bfloat16)
    d_wout = inner_first(context, d_attended)
    d_out_bias = column_sums(d_attended)
    d_context = inner_last(d_attended, back_out).astype(jnp.bfloat16)
    dctx_heads = split_heads(d_context)

    def head_backward(operands):
        query_h, key_h, value_h, posk_h, posq_h, log_total, dctx_h = operands
        scores, table_a, table_w, edge_terms, key_window, end_rows = head_scores(
            query_h, key_h, posk_h, posq_h
        )
        probs = jnp.exp(scores - log_total[:, None])
        probs_low = probs.astype(jnp.bfloat16)
        d_probs = inner_last(dctx_h, value_h)
        d_value = inner_first(probs_low, dctx_h)
        row_dot = jnp.sum(probs * d_probs, axis=1, keepdims=True)
        d_raw = (probs * (d_probs - row_dot) * score_scale).astype(jnp.bfloat16)
        _, pull_terms = jax.vjp(pos_terms, table_a, table_w, edge_terms)
        d_table_a, d_table_w, d_edges = pull_terms(d_raw.astype(jnp.float32))
        d_table_a = d_table_a.astype(jnp.bfloat16)
        d_table_w = d_table_w.astype(jnp.bfloat16)
        d_edges = d_edges.astype(jnp.bfloat16)
        d_query = product(d_raw, key_h) + product(d_table_a, posk_h)
        window_grad = product(d_table_w, posq_h)
        key_canvas = jnp.zeros((seq_length + buckets, HEAD_DIM), jnp.float32)
        placed_grad = lax.dynamic_update_slice(
            key_canvas, window_grad, (first_row, jnp.zeros((), jnp.int32))
        )
        d_key = (
            inner_first(d_raw, query_h)
            + placed_grad[SPAN : SPAN + seq_length]
            + inner_first(d_edges, end_rows)
        )
        d_posk = inner_first(d_table_a, query_h)
        end_grads = product(d_edges, key_h)
        d_posq = inner_first(d_table_w, key_window)
        d_posq = d_posq.at[0].add(end_grads[0]).at[buckets - 1].add(end_grads[1])
        return (d_query, d_key, d_value, d_posk, d_posq)

    d_q_heads, d_k_heads, d_v_heads, d_posk_heads, d_posq_heads = lax.map(
        head_backward,
        (query_heads, key_heads, value_heads, posk_heads, posq_heads, log_totals, dctx_heads),
    )
    d_queries = join_heads(d_q_heads).astype(jnp.bfloat16)
    d_keys_part, d_values_part = (
        lax.psum_scatter(
            join_heads(d_k_heads).astype(jnp.bfloat16), "seq", scatter_dimension=0, tiled=True
        ).astype(jnp.float32),
        lax.psum_scatter(
            join_heads(d_v_heads).astype(jnp.bfloat16), "seq", scatter_dimension=0, tiled=True
        ).astype(jnp.float32),
    )
    d_keys = d_keys_part.astype(jnp.bfloat16)
    d_values = d_values_part.astype(jnp.bfloat16)
    d_merged = jnp.concatenate([d_queries, d_keys, d_values], axis=1)
    d_wqkv = inner_first(hidden_in, d_merged)
    d_q_bias = column_sums(d_queries)
    d_v_bias = column_sums(d_values)
    in_grad = d_res1 + inner_last(d_merged, back_qkv)
    d_posk_rows, d_posq_rows = (
        lax.psum_scatter(join_heads(d_posk_heads), ("dp", "seq"), scatter_dimension=0, tiled=True),
        lax.psum_scatter(join_heads(d_posq_heads), ("dp", "seq"), scatter_dimension=0, tiled=True),
    )
    d_posk_low = d_posk_rows.astype(jnp.bfloat16)
    d_posq_low = d_posq_rows.astype(jnp.bfloat16)
    rel_table_grad = inner_last(d_posk_low, back_posk) + inner_last(d_posq_low, back_posq)
    d_wposk = inner_first(rel_table, d_posk_low)
    d_wposq = inner_first(rel_table, d_posq_low)
    d_posq_bias = column_sums(d_posq_low)
    summed = (
        lax.psum_scatter(d_wqkv, ("dp", "seq"), scatter_dimension=0, tiled=True),
        lax.psum_scatter(d_q_bias, ("dp", "seq"), scatter_dimension=0, tiled=True),
        lax.psum_scatter(d_v_bias, ("dp", "seq"), scatter_dimension=0, tiled=True),
        lax.psum_scatter(d_wposk, ("dp", "seq"), scatter_dimension=0, tiled=True),
        lax.psum_scatter(d_wposq, ("dp", "seq"), scatter_dimension=0, tiled=True),
        lax.psum_scatter(d_posq_bias, ("dp", "seq"), scatter_dimension=0, tiled=True),
        lax.psum_scatter(d_wout, ("dp", "seq"), scatter_dimension=0, tiled=True),
        lax.psum_scatter(d_out_bias, ("dp", "seq"), scatter_dimension=0, tiled=True),
        lax.psum_scatter(d_gain1, ("dp", "seq"), scatter_dimension=0, tiled=True),
        lax.psum_scatter(d_shift1, ("dp", "seq"), scatter_dimension=0, tiled=True),
        lax.psum_scatter(d_wup, ("dp", "seq"), scatter_dimension=0, tiled=True),
        lax.psum_scatter(d_up_bias, ("dp", "seq"), scatter_dimension=0, tiled=True),
        lax.psum_scatter(d_wdown, ("dp", "seq"), scatter_dimension=0, tiled=True),
        lax.psum_scatter(d_down_bias, ("dp", "seq"), scatter_dimension=0, tiled=True),
        lax.psum_scatter(d_gain2, ("dp", "seq"), scatter_dimension=0, tiled=True),
        lax.psum_scatter(d_shift2, ("dp", "seq"), scatter_dimension=0, tiled=True),
    )
    return (
        hidden_out,
        in_grad,
        summed[0],
        summed[1],
        summed[2],
        rel_table_grad,
        summed[3],
        summed[4],
        summed[5],
        summed[6],
        summed[7],
        summed[8],
        summed[9],
        summed[10],
        summed[11],
        summed[12],
        summed[13],
        summed[14],
        summed[15],
    )


def solution(mesh):
    placed = (
        P(("dp", "seq"), None),
        P("dp"),
        P(("dp", "seq"), None),
        P(("dp", "seq")),
        P(("dp", "seq")),
        P(("dp", "seq"), None),
        P(("dp", "seq"), None),
        P(("dp", "seq"), None),
        P(("dp", "seq")),
        P(("dp", "seq"), None),
        P(("dp", "seq")),
        P(("dp", "seq")),
        P(("dp", "seq")),
        P(("dp", "seq"), None),
        P(("dp", "seq")),
        P(("dp", "seq"), None),
        P(("dp", "seq")),
        P(("dp", "seq")),
        P(("dp", "seq")),
        P(("dp", "seq"), None),
    )
    return jax.shard_map(
        head_split if dict(mesh.shape) == {"dp": 16, "seq": 2} else row_split,
        mesh=mesh,
        in_specs=placed,
        out_specs=(
            P(("dp", "seq"), None),
            P(("dp", "seq"), None),
            P(("dp", "seq"), None),
            P(("dp", "seq")),
            P(("dp", "seq")),
            P(("dp", "seq"), None),
            P(("dp", "seq"), None),
            P(("dp", "seq"), None),
            P(("dp", "seq")),
            P(("dp", "seq"), None),
            P(("dp", "seq")),
            P(("dp", "seq")),
            P(("dp", "seq")),
            P(("dp", "seq"), None),
            P(("dp", "seq")),
            P(("dp", "seq"), None),
            P(("dp", "seq")),
            P(("dp", "seq")),
            P(("dp", "seq")),
        ),
        check_vma=False,
    )
```

```python
import math

import jax
import jax.numpy as jnp
from jax import lax
from jax.experimental import pallas as pl
from jax.experimental.pallas import tpu as pltpu
from jax.sharding import PartitionSpec as P

D = 768
HEADS = 12
HEAD_DIM = 64
SPAN = 256
TILE = 128
BLOCK = 256
BAND = 768
PAIR = 2 * HEAD_DIM


eps_norm = 1e-07


def normalize(value, gain, shift):
    average = jnp.mean(value, axis=-1, keepdims=True)
    centred = value - average
    variance = jnp.mean(centred * centred, axis=-1, keepdims=True)
    return centred * lax.rsqrt(variance + eps_norm) * gain + shift


def gelu_exact(value):
    return jax.nn.gelu(value, approximate=False)


def product(left, right):
    return jnp.dot(left, right, preferred_element_type=jnp.float32)


def inner_first(left, right):
    return lax.dot_general(
        left, right, (((0,), (0,)), ((), ())), preferred_element_type=jnp.float32
    )


def inner_last(left, right):
    return lax.dot_general(
        left, right, (((1,), (1,)), ((), ())), preferred_element_type=jnp.float32
    )


def split_heads(matrix):
    return matrix.reshape(matrix.shape[0], HEADS, HEAD_DIM).transpose(1, 0, 2)


def join_heads(stacked):
    return stacked.transpose(1, 0, 2).reshape(stacked.shape[1], D)


def column_sums(matrix):
    return jnp.sum(matrix.astype(jnp.float32), axis=0)


def nn(left, right):
    return lax.dot_general(
        left, right, (((1,), (0,)), ((), ())), preferred_element_type=jnp.float32
    )


def nt(left, right):
    return lax.dot_general(
        left, right, (((1,), (1,)), ((), ())), preferred_element_type=jnp.float32
    )


def unit_matrix(size, reverse=False):
    rows = lax.broadcasted_iota(jnp.int32, (size, size), 0)
    cols = lax.broadcasted_iota(jnp.int32, (size, size), 1)
    if reverse:
        cols = size - 1 - cols
    return jnp.where(rows == cols, 1.0, 0.0).astype(jnp.bfloat16)


def turn_matrix():
    rows = lax.broadcasted_iota(jnp.int32, (BLOCK, BLOCK), 0)
    cols = lax.broadcasted_iota(jnp.int32, (BLOCK, BLOCK), 1)
    mirrored = rows // TILE * (2 * TILE) + TILE - 1 - rows
    return jnp.where(mirrored == cols, 1.0, 0.0).astype(jnp.bfloat16)


def head_lanes(head):
    lanes = lax.broadcasted_iota(jnp.int32, (1, PAIR), 1)
    return lanes // HEAD_DIM == head


def head_rows(head):
    rows = lax.broadcasted_iota(jnp.int32, (HEAD_DIM, PAIR), 0)
    cols = lax.broadcasted_iota(jnp.int32, (HEAD_DIM, PAIR), 1)
    return jnp.where(cols == rows + head * HEAD_DIM, 1.0, 0.0).astype(jnp.bfloat16)


def key_tiles(block, length):
    return max(length // 2, (block + 1) * BLOCK) // TILE


def tile_seen(query_tile, key_tile, length):
    return key_tile < key_tiles(query_tile * TILE // BLOCK, length)


def skewed(window):
    return pltpu.roll(window, 0, 1, stride=1, stride_axis=0)


def forward_body(prefix_ref, q_ref, k_ref, v_ref, pk_ref, pq_ref, ctx_ref, p_ref, wb_ref, far_ref, s_ref):
    length = q_ref.shape[0]
    head = pl.program_id(1)
    mine = head_lanes(head)
    prefix = prefix_ref[0]
    eye = unit_matrix(TILE)
    eye_block = unit_matrix(BLOCK)
    zero = jnp.zeros((), jnp.bfloat16)
    scale = math.log2(math.e) / math.sqrt(3 * HEAD_DIM)
    for tile in range(length // TILE):
        rows = slice(tile * TILE, (tile + 1) * TILE)
        table = nt(jnp.where(mine, k_ref[rows, :], zero), pq_ref[...])
        wb_ref[rows, :] = skewed(table)
        wb_ref[rows, 0:TILE] = table[:, BAND - TILE :]
        far_ref[rows, :] = table[:, 0:TILE]
    v_cols = nt(jnp.where(lax.broadcasted_iota(jnp.int32, (PAIR, PAIR), 0) // HEAD_DIM == head, unit_matrix(PAIR), zero), v_ref[...]).astype(jnp.bfloat16)
    for block in range(length // BLOCK):
        cols = slice(block * BLOCK, (block + 1) * BLOCK)
        q_own = jnp.where(mine, q_ref[cols, :], zero)
        skews, highs, lows = [], [], []
        for sub in range(2):
            table = nt(q_own[sub * TILE : (sub + 1) * TILE], pk_ref[...])
            skews.append(skewed(table).astype(jnp.bfloat16))
            highs.append(table[:, 0:TILE].astype(jnp.bfloat16))
            lows.append(table[:, BAND - TILE :].astype(jnp.bfloat16))
        count = key_tiles(block, length)
        highest = None
        for tile in range(count):
            rows = slice(tile * TILE, (tile + 1) * TILE)
            parts_a, parts_b = [], []
            for sub in range(2):
                step = 2 * block + sub - tile
                if step >= 3:
                    parts_a.append(highs[sub])
                    parts_b.append(wb_ref[rows, 0:TILE])
                elif step <= -3:
                    parts_a.append(lows[sub])
                    parts_b.append(far_ref[rows, :])
                else:
                    at = 384 - TILE * step
                    parts_a.append(skews[sub][:, at : at + TILE])
                    at = 384 + TILE * step
                    parts_b.append(wb_ref[rows, at : at + TILE])
            right = jnp.concatenate([jnp.concatenate(parts_a, axis=0), q_own], axis=1)
            left = jnp.concatenate([eye, k_ref[rows, :]], axis=1)
            raw = nt(left, right) + jnp.concatenate(parts_b, axis=1)
            if (tile + 1) * TILE > block * BLOCK + 1:
                keys = tile * TILE + lax.broadcasted_iota(jnp.int32, (TILE, BLOCK), 0)
                queries = block * BLOCK + lax.broadcasted_iota(jnp.int32, (TILE, BLOCK), 1)
                raw = jnp.where((keys < prefix) | (keys <= queries), raw, -jnp.inf)
            s_ref[rows, :] = raw
            top = jnp.max(raw, axis=0, keepdims=True)
            highest = top if highest is None else jnp.maximum(highest, top)
        total = jnp.zeros((1, BLOCK), jnp.float32)
        for tile in range(count):
            rows = slice(tile * TILE, (tile + 1) * TILE)
            expo = jnp.exp2((s_ref[rows, :] - highest) * scale)
            s_ref[rows, :] = expo
            total = total + jnp.sum(expo, axis=0, keepdims=True)
        inverse = 1.0 / total
        for tile in range(count):
            rows = slice(tile * TILE, (tile + 1) * TILE)
            p_ref[rows, cols] = (s_ref[rows, :] * inverse).astype(jnp.bfloat16)
        seen = count * TILE
        ctx_cols = nn(v_cols[:, :seen], p_ref[0:seen, cols]).astype(jnp.bfloat16)
        ctx = nt(eye_block, ctx_cols).astype(jnp.bfloat16)

        @pl.when(head == 0)
        def _():
            ctx_ref[cols, :] = ctx

        @pl.when(head == 1)
        def _():
            ctx_ref[cols, :] = ctx_ref[cols, :] + ctx


def attention_forward(prefix, merged, pos_band, pair):
    length, width = merged.shape[0], merged.shape[1] // 3
    pairs = width // PAIR
    tall = [pl.BlockSpec((length, PAIR), lambda p, h, at=at: (0, at)) for at in (pair, pairs + pair, 2 * pairs + pair)]
    band = [pl.BlockSpec((BAND, PAIR), lambda p, h, at=at: (0, at)) for at in (pair, pairs + pair)]
    return pl.pallas_call(
        forward_body,
        grid=(1, 2),
        in_specs=[pl.BlockSpec(memory_space=pltpu.SMEM)] + tall + band,
        out_specs=[
            pl.BlockSpec((length, PAIR), lambda p, h: (0, 0)),
            pl.BlockSpec((None, length, length), lambda p, h: (h, 0, 0)),
        ],
        out_shape=[
            jax.ShapeDtypeStruct((length, PAIR), jnp.bfloat16),
            jax.ShapeDtypeStruct((2, length, length), jnp.bfloat16),
        ],
        scratch_shapes=[
            pltpu.VMEM((length, BAND), jnp.float32),
            pltpu.VMEM((length, TILE), jnp.float32),
            pltpu.VMEM((length, BLOCK), jnp.float32),
        ],
        compiler_params=pltpu.CompilerParams(dimension_semantics=("arbitrary", "arbitrary"), vmem_limit_bytes=40 << 20),
        cost_estimate=pl.CostEstimate(flops=12 * 10**9, transcendentals=2 * length * length, bytes_accessed=6 << 20),
        name="attention_forward",
    )(prefix, merged, merged, merged, pos_band, pos_band)


def backward_body(q_ref, k_ref, v_ref, dctx_ref, p_ref, pk_ref, pq_ref, dq_ref, dk_ref, dv_ref, dpk_ref, dpq_ref, dr_ref, dk_acc, dv_acc):
    length = q_ref.shape[0]
    head = pl.program_id(1)
    mine = head_lanes(head)
    flip = turn_matrix()
    pick = head_rows(head)
    bf = jnp.bfloat16
    zero = jnp.zeros((), bf)
    scale = 1.0 / math.sqrt(3 * HEAD_DIM)
    back = BAND - (TILE - 1)
    blank = jnp.zeros((TILE, TILE), bf)
    dk_acc[...] = jnp.zeros_like(dk_acc)
    dv_acc[...] = jnp.zeros_like(dv_acc)
    dpk = jnp.zeros((HEAD_DIM, BAND), jnp.float32)
    dpq = jnp.zeros((HEAD_DIM, BAND), jnp.float32)
    tiles = length // TILE

    def put(ref, rows, value):
        @pl.when(head == 0)
        def _():
            ref[rows, :] = jnp.where(mine, value, 0.0).astype(bf)

        @pl.when(head == 1)
        def _():
            ref[rows, :] = jnp.where(mine, value.astype(bf), ref[rows, :])

    def unskew(parts):
        return pltpu.roll(jnp.concatenate(parts, axis=1), back, 1, stride=1, stride_axis=0)

    for block in range(length // BLOCK):
        cols = slice(block * BLOCK, (block + 1) * BLOCK)
        count = key_tiles(block, length)
        seen = count * TILE
        dctx = dctx_ref[cols, :]
        v_own = jnp.where(mine, v_ref[0:seen, :], zero)
        probs_low = p_ref[0:seen, cols]
        probs = probs_low.astype(jnp.float32)
        d_probs = nt(v_own, dctx)
        row_dot = jnp.sum(probs * d_probs, axis=0, keepdims=True)
        dr_ref[0:seen, cols] = (probs * ((d_probs - row_dot) * scale)).astype(bf)
        d_raw = dr_ref[0:seen, cols]
        dv_acc[0:seen, :] += nn(probs_low, dctx)
        dk_acc[0:seen, :] += nn(d_raw, q_ref[cols, :])
        turned = nt(flip, d_raw).astype(bf)
        spreads = []
        for sub in range(2):
            tile = 2 * block + sub
            own = turned[sub * TILE : (sub + 1) * TILE]

            def piece(key_tile):
                return own[:, key_tile * TILE : (key_tile + 1) * TILE]

            near = [t for t in range(count) if tile - t >= 3]
            far = [t for t in range(count) if tile - t <= -3]
            band = [blank]
            for step in (2, 1, 0, -1, -2):
                key_tile = tile - step
                band.append(piece(key_tile) if 0 <= key_tile < count else blank)
            spreads.append(
                add_edges(unskew(band), [piece(t).astype(jnp.float32) for t in near], [piece(t).astype(jnp.float32) for t in far])
            )
        spread = jnp.concatenate(spreads, axis=0)
        dq = nn(turned, k_ref[0:seen, :]) + nn(spread, pk_ref[...])
        put(dq_ref, cols, nn(flip, dq.astype(bf)))
        q_cols = nt(pick, nn(flip, q_ref[cols, :]).astype(bf)).astype(bf)
        dpk = dpk + nn(q_cols, spread)
    dpk_ref[...] = dpk
    for block in range(length // BLOCK):
        rows = slice(block * BLOCK, (block + 1) * BLOCK)
        groups, edges = [], []
        for sub in range(2):
            key_tile = 2 * block + sub
            own = slice(key_tile * TILE, (key_tile + 1) * TILE)
            seen_by = [t for t in range(tiles) if tile_seen(t, key_tile, length)]

            def held(query_tile):
                return dr_ref[own, query_tile * TILE : (query_tile + 1) * TILE]

            band = [blank]
            for step in (-2, -1, 0, 1, 2):
                query_tile = key_tile + step
                band.append(held(query_tile) if query_tile in seen_by else blank)
            ends = []
            for chosen in ([t for t in seen_by if t - key_tile <= -3], [t for t in seen_by if t - key_tile >= 3]):
                total = blank
                if chosen:
                    total = sum((held(t).astype(jnp.float32) for t in chosen[1:]), held(chosen[0]).astype(jnp.float32)).astype(bf)
                ends.append(total)
            groups.append(jnp.concatenate(band[1:] + ends, axis=1))
        turned = nn(flip, jnp.concatenate(groups, axis=0))
        width = BAND - TILE
        spreads = []
        for sub in range(2):
            own = turned[sub * TILE : (sub + 1) * TILE]
            spreads.append(
                add_edges(unskew([blank, own[:, :width].astype(bf)]), [own[:, width : width + TILE]], [own[:, width + TILE :]])
            )
        spread = jnp.concatenate(spreads, axis=0)
        d_key = nn(flip, nn(spread, pq_ref[...]).astype(bf))
        put(dk_ref, rows, dk_acc[rows, :] + d_key)
        k_cols = nt(pick, nn(flip, k_ref[rows, :]).astype(bf)).astype(bf)
        dpq = dpq + nn(k_cols, spread)
        put(dv_ref, rows, dv_acc[rows, :])
    dpq_ref[...] = dpq


def add_edges(spread, first, last):
    parts = [spread[:, 0:TILE], spread[:, TILE : BAND - TILE], spread[:, BAND - TILE :]]
    for place, tiles in ((0, first), (2, last)):
        if tiles:
            total = parts[place].astype(jnp.float32)
            for tile in tiles:
                total = total + tile
            parts[place] = total.astype(jnp.bfloat16)
    return jnp.concatenate(parts, axis=1)


def attention_backward(merged, dctx, probs, pos_band, pair):
    length, width = merged.shape[0], merged.shape[1] // 3
    pairs = width // PAIR
    tall = [pl.BlockSpec((length, PAIR), lambda p, h, at=at: (0, at)) for at in (pair, pairs + pair, 2 * pairs + pair, pair)]
    band = [pl.BlockSpec((BAND, PAIR), lambda p, h, at=at: (0, at)) for at in (pair, pairs + pair)]
    own = pl.BlockSpec((length, PAIR), lambda p, h: (0, 0))
    table = pl.BlockSpec((HEAD_DIM, BAND), lambda p, h: (h, 0))
    flat = jax.ShapeDtypeStruct((length, PAIR), jnp.bfloat16)
    wide = jax.ShapeDtypeStruct((PAIR, BAND), jnp.float32)
    return pl.pallas_call(
        backward_body,
        grid=(1, 2),
        in_specs=tall + [pl.BlockSpec((None, length, length), lambda p, h: (h, 0, 0))] + band,
        out_specs=[own, own, own, table, table],
        out_shape=[flat, flat, flat, wide, wide],
        scratch_shapes=[
            pltpu.VMEM((length, length), jnp.bfloat16),
            pltpu.VMEM((length, PAIR), jnp.float32),
            pltpu.VMEM((length, PAIR), jnp.float32),
        ],
        compiler_params=pltpu.CompilerParams(dimension_semantics=("arbitrary", "arbitrary"), vmem_limit_bytes=40 << 20),
        cost_estimate=pl.CostEstimate(flops=35 * 10**9, transcendentals=0, bytes_accessed=8 << 20),
        name="attention_backward",
    )(merged, merged, merged, dctx, probs, pos_band, pos_band)


CORES = [(0, 1), (1, 0)]


def swap(value):
    return lax.ppermute(value, "seq", CORES)


def ordered(core, own, other, axis=0):
    return jnp.concatenate(
        [jnp.where(core == 0, own, other), jnp.where(core == 0, other, own)], axis=axis
    )


def half_of(core, matrix, axis):
    size = matrix.shape[axis] // 2
    return lax.dynamic_slice_in_dim(matrix, core * size, size, axis)


def chip_bits():
    chip = lax.axis_index("dp")
    return chip // 4, (chip // 2) % 2, chip % 2


def exchange(value, mask):
    return lax.ppermute(value, "dp", [(i, i ^ mask) for i in range(16)])


def tie_all(chain, others):
    chain.state, others = lax.optimization_barrier((chain.state, others))
    return others


class Gather:
    def __init__(self, *values):
        self.state = values

    def line(self, step):
        up = [(i, i + 4) for i in range(12) if i // 4 >= step - 1]
        down = [(i + 4, i) for i in range(12) if i // 4 <= 3 - step]
        if step == 1:
            self.state = [([value], [value]) for value in self.state]
        self.state = [
            (below + [lax.ppermute(below[-1], "dp", up)], above + [lax.ppermute(above[-1], "dp", down)])
            for below, above in self.state
        ]
        if step == 3:
            z = chip_bits()[0]
            lines = []
            for below, above in self.state:
                blocks = []
                for block in range(4):
                    options = [below[k - block] if k >= block else above[block - k] for k in range(4)]
                    blocks.append(lax.select_n(z, *options))
                lines.append(tuple(jnp.stack([b[side] for b in blocks]) for side in range(2)))
            self.state = lines

    def pair(self, step):
        _, y, x = chip_bits()
        order = ((x, 1), (y, 2)) if step == 1 else ((y, 2), (x, 1))
        lines = []
        for halves in self.state:
            result = []
            for value, (bit, mask) in zip(halves, order):
                other = exchange(value, mask)
                result.append(jnp.stack([jnp.where(bit == 0, value, other), jnp.where(bit == 0, other, value)]))
            lines.append(tuple(result))
        self.state = lines

    def rows(self, index, low, high):
        first, second = [half[..., low:high] for half in self.state[index]]
        first = jnp.moveaxis(first, (0, 1, 2), (1, 2, 0))
        second = jnp.moveaxis(second, (0, 1, 2), (2, 1, 0))
        whole = jnp.stack([first, second], axis=3)
        return whole.reshape(-1, whole.shape[-1])


class Scatter:
    def __init__(self, *values):
        self.state = []
        for value in values:
            grid = value.reshape((4, 2, 2) + value.shape[1:])
            self.state.append((jnp.moveaxis(grid[:, :, :, 0], 2, 0), jnp.moveaxis(grid[:, :, :, 1], 1, 0)))

    def pair(self, step):
        _, y, x = chip_bits()
        order = ((x, 1), (y, 2)) if step == 1 else ((y, 2), (x, 1))
        sums = []
        for halves in self.state:
            result = []
            for value, (bit, mask) in zip(halves, order):
                keep = jnp.where(bit == 0, value[0], value[1])
                give = jnp.where(bit == 0, value[1], value[0])
                total = (keep.astype(jnp.float32) + exchange(give, mask).astype(jnp.float32)).astype(value.dtype)
                result.append(jnp.moveaxis(total, 1, 0) if step == 1 else total)
            sums.append(tuple(result) if step == 1 else (jnp.stack(result, axis=1), None, None))
        self.state = sums

    def line(self, step):
        z = chip_bits()[0]
        offset = 4 - step
        ups = [(i, i + 4) for i in range(12) if i // 4 + offset <= 3]
        downs = [(i + 4, i) for i in range(12) if i // 4 + 1 - offset >= 0]
        sums, self.totals = [], []
        for value, up, down in self.state:

            def block(at):
                options = [value[min(max(k + at, 0), 3)] for k in range(4)]
                return lax.select_n(z, *options).astype(jnp.float32)

            to_above, to_below = block(offset), block(-offset)
            if up is not None:
                to_above = to_above + up.astype(jnp.float32)
                to_below = to_below + down.astype(jnp.float32)
            up = lax.ppermute(to_above.astype(value.dtype), "dp", ups)
            down = lax.ppermute(to_below.astype(value.dtype), "dp", downs)
            sums.append((value, up, down))
            if step == 3:
                self.totals.append(block(0) + up.astype(jnp.float32) + down.astype(jnp.float32))
        self.state = sums


def norm_parts(value):
    average = jnp.mean(value, axis=-1, keepdims=True)
    centred = value - average
    variance = jnp.mean(centred * centred, axis=-1, keepdims=True)
    inverse = lax.rsqrt(variance + eps_norm)
    return centred * inverse, inverse


def norm_back(unit, inverse, gain, grad):
    scaled = grad * gain
    mean_grad = jnp.mean(scaled, axis=-1, keepdims=True)
    mean_along = jnp.mean(scaled * unit, axis=-1, keepdims=True)
    return inverse * (scaled - mean_grad - unit * mean_along)


def head_split(
    hidden_in, prefix, w_qkv, q_bias, v_bias, rel_table, w_posk, w_posq, posq_bias, w_out, out_bias,
    norm1_gain, norm1_bias, w_up, up_bias, w_down, down_bias, norm2_gain, norm2_bias, out_grad,
):
    bf = jnp.bfloat16
    f32 = jnp.float32
    core = lax.axis_index("seq")
    rows = w_qkv.shape[0]
    units = w_down.shape[0]
    table_rows = rel_table.shape[0]
    chips = 16
    half = D // 2
    ff_half = chips * units
    buckets = 2 * SPAN

    last_rows = rows - table_rows

    def columns(side):
        qkv = w_qkv.reshape(rows, 3, 2, half)[:, :, side].reshape(rows, 3 * half)
        corner = jnp.pad(rel_table[:, side * half : (side + 1) * half], ((0, last_rows), (0, 0)))
        cut = slice(side * half, (side + 1) * half)
        up = w_up.reshape(rows, chips, 2, units)[:, :, side].reshape(rows, ff_half)
        return (
            jnp.concatenate([qkv, w_posk[:, cut], w_posq[:, cut], corner], axis=1),
            jnp.concatenate([w_out[:, cut], up], axis=1),
        )

    early0, late0 = columns(0)
    early1, late1 = columns(1)
    early_got = swap(jnp.where(core == 0, early1, early0))
    late_got = swap(jnp.where(core == 0, late1, late0))
    hidden_got = swap(hidden_in)

    def by_core(first, second, got):
        own = jnp.where(core == 0, first, second)
        return jnp.stack([jnp.where(core == 0, own, got), jnp.where(core == 0, got, own)])

    early_chain = Gather(by_core(early0, early1, early_got))
    late_chain = Gather(by_core(late0, late1, late_got), w_down.reshape(2, units // 2, D))
    vectors = (q_bias, v_bias, posq_bias, out_bias, norm1_gain, norm1_bias, down_bias, norm2_gain)
    left = jnp.stack(vectors)
    right = jnp.concatenate(
        [jnp.pad(norm2_bias, (0, units - rows))[None], up_bias[None], jnp.zeros((6, units), bf)], axis=0
    )
    small = jnp.concatenate([jnp.pad(left, ((0, 0), (0, 128 - rows))), jnp.pad(right, ((0, 0), (0, 128 - units)))], axis=1)
    small = lax.all_gather(small, ("dp", "seq"), axis=0, tiled=True).reshape(2 * chips, 8, 256)
    for step in (1, 2, 3):
        early_chain.line(step)
    late_chain.state = tie_all(early_chain, late_chain.state)
    early_chain.pair(1)
    late_chain.line(1)
    late_chain.line(2)
    early_chain.pair(2)
    late_chain.line(3)
    late_chain.state = tie_all(early_chain, late_chain.state)
    late_chain.pair(1)
    hidden_all = ordered(core, hidden_in, hidden_got)
    w_qkv_own = early_chain.rows(0, 0, 3 * half)
    w_pos_own = early_chain.rows(0, 3 * half, 5 * half)
    table_half = early_chain.rows(0, 5 * half, 6 * half).reshape(2 * chips, rows, half)[:, :table_rows].reshape(buckets, half)
    table = ordered(core, table_half, swap(table_half), axis=1)

    owner = (lax.broadcasted_iota(jnp.int32, (2 * chips, D), 1) // rows == lax.broadcasted_iota(jnp.int32, (2 * chips, D), 0)).astype(bf)
    inside = lax.broadcasted_iota(jnp.int32, (rows, D), 1) % rows == lax.broadcasted_iota(jnp.int32, (rows, D), 0)
    unit_owner = (
        2 * (lax.broadcasted_iota(jnp.int32, (2 * chips, ff_half), 1) // units) + core
        == lax.broadcasted_iota(jnp.int32, (2 * chips, ff_half), 0)
    ).astype(bf)
    unit_inside = lax.broadcasted_iota(jnp.int32, (units, ff_half), 1) % units == lax.broadcasted_iota(jnp.int32, (units, ff_half), 0)
    spots = jnp.concatenate([small[:, :, :rows], small[:, :, 128 : 128 + rows]], axis=1)
    wide = lax.dot_general(spots, owner, (((0,), (0,)), ((), ())), preferred_element_type=f32)
    lists = jnp.sum(jnp.where(inside, wide, 0.0), axis=1)
    qb, vb, pqb, ob, gain1, shift1, db, gain2, shift2 = [lists[i] for i in range(9)]
    wide = inner_first(small[:, 1, 128 : 128 + units], unit_owner)
    ub = jnp.sum(jnp.where(unit_inside, wide, 0.0), axis=0)

    band = lax.broadcasted_iota(jnp.int32, (BAND, buckets), 0)
    bucket = lax.broadcasted_iota(jnp.int32, (BAND, buckets), 1)
    chosen = (jnp.clip(SPAN + 384 - band, 0, buckets - 1) == bucket).astype(bf)
    pos_shift = jnp.concatenate([jnp.zeros((half,), f32), half_of(core, pqb, 0)])
    pos = (product(table, w_pos_own) + pos_shift).astype(bf)
    pos_band = product(chosen, pos).astype(bf)

    qkv_shift = jnp.concatenate([half_of(core, qb, 0), jnp.zeros((half,), f32), half_of(core, vb, 0)])
    merged = (product(hidden_all, w_qkv_own) + qkv_shift).astype(bf)
    context_parts, prob_parts = [], []
    for pair in range(half // PAIR):
        part, kept = attention_forward(prefix, merged, pos_band, pair)
        if pair == 0:
            part, merged = tie_all(late_chain, (part, merged))
            late_chain.pair(2)
        context_parts.append(part)
        prob_parts.append(kept)
    context = jnp.concatenate(context_parts, axis=1)
    out_columns = late_chain.rows(0, 0, half)
    w_out_own = ordered(
        core, half_of(core, out_columns, 0), swap(half_of(1 - core, out_columns, 0)), axis=1
    )
    w_up_own = late_chain.rows(0, half, half + ff_half)
    w_down_own = late_chain.rows(1, 0, D)

    def summed_rows(left, multiply):
        given = swap(multiply(half_of(1 - core, left, 0)))
        return multiply(half_of(core, left, 0)) + given

    hidden_f = hidden_in.astype(f32)
    residual1 = hidden_f + summed_rows(context, lambda part: product(part, w_out_own)) + ob
    unit1, inverse1 = norm_parts(residual1)
    normed = unit1 * gain1 + shift1
    normed_low = normed.astype(bf)
    normed_all = ordered(core, normed_low, swap(normed_low))
    expanded = product(normed_all, w_up_own) + ub
    normal_cdf = 0.5 + 0.5 * lax.erf(expanded * math.sqrt(0.5))
    activated = (expanded * normal_cdf).astype(bf)
    slope = (
        normal_cdf + expanded * jnp.exp(-0.5 * expanded * expanded) * (1.0 / math.sqrt(2.0 * math.pi))
    ).astype(bf)
    residual2 = normed + summed_rows(activated, lambda part: product(part, w_down_own)) + db
    unit2, inverse2 = norm_parts(residual2)
    hidden_out = (unit2 * gain2 + shift2).astype(bf)

    grad = out_grad.astype(f32)
    d_res2 = norm_back(unit2, inverse2, gain2, grad)
    d_gain2 = jnp.sum(grad * unit2, axis=0, keepdims=True)
    d_shift2 = jnp.sum(grad, axis=0, keepdims=True)
    d_reduced = d_res2.astype(bf)
    d_down_bias = column_sums(d_reduced)[None]
    reduced_all = ordered(core, d_reduced, swap(d_reduced))
    d_expanded = (inner_last(reduced_all, w_down_own) * slope.astype(f32)).astype(bf)
    d_normed = summed_rows(d_expanded, lambda part: inner_last(part, w_up_own)) + d_res2
    d_wdown = inner_first(activated, reduced_all).astype(bf)
    d_wup = inner_first(normed_all, d_expanded).astype(bf)
    d_up_bias = column_sums(d_expanded)
    d_res1 = norm_back(unit1, inverse1, gain1, d_normed)
    d_gain1 = jnp.sum(d_normed * unit1, axis=0, keepdims=True)
    d_shift1 = jnp.sum(d_normed, axis=0, keepdims=True)
    d_attended = d_res1.astype(bf)
    d_out_bias = column_sums(d_attended)[None]
    attended_all = ordered(core, d_attended, swap(d_attended))
    d_context = inner_last(attended_all, w_out_own).astype(bf)
    d_wout_rows = inner_first(context, attended_all).astype(bf)
    d_wout = ordered(
        core, half_of(core, d_wout_rows, 1), swap(half_of(1 - core, d_wout_rows, 1)), axis=0
    )

    def rejoin(first, second):
        own = jnp.where(core == 0, first, second)
        got = swap(jnp.where(core == 0, second, first))
        return jnp.where(core == 0, own, got), jnp.where(core == 0, got, own)

    late_cols = jnp.concatenate([d_wout, d_wup], axis=1).reshape(chips, 2, rows, half + ff_half)
    late_sums = Scatter(late_cols, d_wdown.reshape(chips, 2, units // 2, D))
    late_steps = [lambda: late_sums.pair(1), lambda: late_sums.pair(2), lambda: late_sums.line(1)]
    grads = []
    d_context = tie_all(late_sums, d_context)
    for pair in range(half // PAIR):
        late_steps[pair]()
        found = attention_backward(merged, d_context, prob_parts[pair], pos_band, pair)
        found, d_context = tie_all(late_sums, (found, d_context))
        grads.append(found)
    late_sums.line(2)
    d_merged = jnp.concatenate([g[i] for i in range(3) for g in grads], axis=1)
    d_q, d_v = d_merged[:, :half], d_merged[:, 2 * half :]
    in_grad = d_res1 + summed_rows(d_merged, lambda part: inner_last(part, w_qkv_own))
    d_wqkv = inner_first(hidden_all, d_merged).astype(bf)
    d_q_bias = column_sums(d_q)[None]
    d_v_bias = column_sums(d_v)[None]
    d_band = jnp.concatenate([g[i] for i in (3, 4) for g in grads], axis=0).astype(bf)
    d_pos = lax.dot_general(
        chosen, d_band, (((0,), (1,)), ((), ())), preferred_element_type=f32
    )
    d_posq_bias = jnp.sum(d_pos[:, half:], axis=0, keepdims=True)
    d_pos_low = d_pos.astype(bf)
    d_wpos = inner_first(table, d_pos_low).astype(bf)
    d_table_all = inner_last(d_pos_low, w_pos_own).astype(bf)
    d_table = (
        half_of(core, d_table_all, 1).astype(f32)
        + swap(half_of(1 - core, d_table_all, 1)).astype(f32)
    ).astype(bf)

    def whole(part):
        blank = jnp.zeros_like(part)
        return ordered(core, part, blank, axis=1)

    lists_grad = jnp.concatenate(
        [whole(jnp.concatenate([d_q_bias, d_v_bias, d_posq_bias], axis=0)), d_out_bias, d_gain1, d_shift1, d_down_bias, d_gain2, d_shift2],
        axis=0,
    ).astype(bf)
    lists_grad = jnp.pad(lists_grad, ((0, 7), (0, 0)))
    pieces = jnp.where(inside, lists_grad[:, None, :], jnp.zeros((), bf)).reshape(16 * rows, D)
    unit_at = lax.broadcasted_iota(jnp.int32, (half, ff_half), 1) % units + 256 == lax.broadcasted_iota(jnp.int32, (half, ff_half), 0)
    unit_pieces = jnp.where(unit_at, d_up_bias.astype(bf), jnp.zeros((), bf))
    vector = (inner_last(owner, pieces) + inner_last(unit_owner, unit_pieces)).astype(bf)
    corner_grad = jnp.concatenate(
        [
            d_table.reshape(2 * chips, table_rows, half),
            jnp.pad(vector[:, None, :], ((0, 0), (0, last_rows - 1), (0, 0))),
        ],
        axis=1,
    ).reshape(chips * 2 * rows, half)
    early_sums = Scatter(
        jnp.concatenate([d_wqkv, d_wpos, corner_grad], axis=1).reshape(chips, 2, rows, 6 * half)
    )
    early_sums.pair(1)
    late_sums.line(3)
    late_grads, down_grads = late_sums.totals
    late_left, late_right = rejoin(late_grads[0], late_grads[1])
    early_sums.pair(2)
    g_wdown = down_grads.reshape(units, D)
    g_wout = jnp.concatenate([late_left[:, :half], late_right[:, :half]], axis=1)
    g_wup = jnp.stack(
        [late_left[:, half:].reshape(rows, chips, units), late_right[:, half:].reshape(rows, chips, units)], axis=2
    ).reshape(rows, 2 * ff_half)
    g_wdown, g_wout, g_wup, in_grad = tie_all(early_sums, (g_wdown, g_wout, g_wup, in_grad))
    for step in (1, 2, 3):
        early_sums.line(step)
    early_grads = early_sums.totals[0]
    early_left, early_right = rejoin(early_grads[0], early_grads[1])
    vector_sum = early_left[table_rows, 5 * half :] + early_right[table_rows, 5 * half :]

    def side_by_side(left, right, at, count):
        pieces = []
        for index in range(count):
            cut = slice((at + index) * half, (at + index + 1) * half)
            pieces += [left[:, cut], right[:, cut]]
        return jnp.concatenate(pieces, axis=1)

    g_wqkv = side_by_side(early_left, early_right, 0, 3)
    g_wposk = side_by_side(early_left, early_right, 3, 1)
    g_wposq = side_by_side(early_left, early_right, 4, 1)
    g_table = side_by_side(early_left, early_right, 5, 1)[:table_rows]
    g = [vector_sum[i * rows : (i + 1) * rows] for i in range(9)]
    g_up_bias = vector_sum[256 : 256 + units]
    return (
        hidden_out, in_grad, g_wqkv, g[0], g[1], g_table, g_wposk, g_wposq, g[2], g_wout, g[3], g[4], g[5],
        g_wup, g_up_bias, g_wdown, g[6], g[7], g[8],
    )


def row_split(
    hidden_in,
    prefix,
    w_qkv,
    q_bias,
    v_bias,
    rel_table,
    w_posk,
    w_posq,
    posq_bias,
    w_out,
    out_bias,
    norm1_gain,
    norm1_bias,
    w_up,
    up_bias,
    w_down,
    down_bias,
    norm2_gain,
    norm2_bias,
    out_grad,
):
    gathered = (
        lax.all_gather(w_qkv, ("dp", "seq"), axis=0, tiled=True),
        lax.all_gather(q_bias, ("dp", "seq"), axis=0, tiled=True),
        lax.all_gather(v_bias, ("dp", "seq"), axis=0, tiled=True),
        lax.all_gather(rel_table, ("dp", "seq"), axis=0, tiled=True),
        lax.all_gather(w_posk, ("dp", "seq"), axis=0, tiled=True),
        lax.all_gather(w_posq, ("dp", "seq"), axis=0, tiled=True),
        lax.all_gather(posq_bias, ("dp", "seq"), axis=0, tiled=True),
        lax.all_gather(w_out, ("dp", "seq"), axis=0, tiled=True),
        lax.all_gather(out_bias, ("dp", "seq"), axis=0, tiled=True),
        lax.all_gather(norm1_gain, ("dp", "seq"), axis=0, tiled=True),
        lax.all_gather(norm1_bias, ("dp", "seq"), axis=0, tiled=True),
        lax.all_gather(w_up, ("dp", "seq"), axis=0, tiled=True),
        lax.all_gather(up_bias, ("dp", "seq"), axis=0, tiled=True),
        lax.all_gather(w_down, ("dp", "seq"), axis=0, tiled=True),
        lax.all_gather(down_bias, ("dp", "seq"), axis=0, tiled=True),
        lax.all_gather(norm2_gain, ("dp", "seq"), axis=0, tiled=True),
        lax.all_gather(norm2_bias, ("dp", "seq"), axis=0, tiled=True),
    )
    (
        full_qkv,
        full_qb,
        full_vb,
        full_table,
        full_posk,
        full_posq,
        full_pqb,
        full_out,
        full_ob,
        full_g1,
        full_b1,
        full_up,
        full_ub,
        full_down,
        full_db,
        full_g2,
        full_b2,
    ) = gathered
    row_count = hidden_in.shape[0]
    groups = lax.axis_size("seq")
    seq_length = row_count * groups
    seq_rank = lax.axis_index("seq")
    prefix_len = prefix[0]
    score_scale = 1.0 / math.sqrt(3 * HEAD_DIM)
    buckets = 2 * SPAN
    window = row_count + buckets
    first_row = seq_rank * row_count
    query_pos = first_row + jnp.arange(row_count, dtype=jnp.int32)
    key_pos = jnp.arange(seq_length, dtype=jnp.int32)
    visible = (key_pos[None, :] < prefix_len) | (key_pos[None, :] <= query_pos[:, None])
    padded_cols = jnp.arange(seq_length + buckets, dtype=jnp.int32)
    below_window = padded_cols[None, :] < first_row

    def skew_table(table, row_total, offset, col_total):
        shifted = jnp.pad(
            jnp.flip(table, axis=1), ((0, 0), (row_count, row_count - 1)), mode="edge"
        )
        stride = shifted.shape[1] - 1
        flattened = shifted.reshape(-1)
        picked = lax.slice_in_dim(flattened, offset, offset + row_total * stride)
        return picked.reshape(row_total, stride)[:, :col_total]

    def pos_terms(table_a, table_w, edge_terms):
        band_terms = (
            skew_table(table_a, row_count, row_count - 1, window)
            + skew_table(table_w, window, window - 1, row_count).T
        )
        low_side = table_a[:, buckets - 1 : buckets] + jnp.pad(edge_terms[0], (SPAN, SPAN))[None, :]
        high_side = table_a[:, 0:1] + jnp.pad(edge_terms[1], (SPAN, SPAN))[None, :]
        backdrop = jnp.where(below_window, low_side, high_side)
        placed = lax.dynamic_update_slice(
            backdrop, band_terms, (jnp.zeros((), jnp.int32), first_row)
        )
        return placed[:, SPAN : SPAN + seq_length]

    pos_keys = product(full_table, full_posk).astype(jnp.bfloat16)
    pos_queries = (product(full_table, full_posq) + full_pqb.astype(jnp.float32)).astype(
        jnp.bfloat16
    )
    merged = product(hidden_in, full_qkv)
    queries = (merged[:, :D] + full_qb.astype(jnp.float32)).astype(jnp.bfloat16)
    keys_local = merged[:, D : 2 * D].astype(jnp.bfloat16)
    values_local = (merged[:, 2 * D :] + full_vb.astype(jnp.float32)).astype(jnp.bfloat16)
    keys_all, values_all = (
        lax.all_gather(keys_local, "seq", axis=0, tiled=True),
        lax.all_gather(values_local, "seq", axis=0, tiled=True),
    )
    query_heads = split_heads(queries)
    key_heads = split_heads(keys_all)
    value_heads = split_heads(values_all)
    posk_heads = split_heads(pos_keys)
    posq_heads = split_heads(pos_queries)

    def head_scores(query_h, key_h, posk_h, posq_h):
        content = inner_last(query_h, key_h)
        table_a = inner_last(query_h, posk_h)
        key_padded = jnp.pad(key_h, ((SPAN, SPAN), (0, 0)))
        key_window = lax.dynamic_slice_in_dim(key_padded, first_row, window, 0)
        table_w = inner_last(key_window, posq_h)
        end_rows = jnp.stack([posq_h[0], posq_h[buckets - 1]])
        edge_terms = inner_last(end_rows, key_h)
        raw = content + pos_terms(table_a, table_w, edge_terms)
        masked = jnp.where(visible, raw * score_scale, -jnp.inf)
        return (masked, table_a, table_w, edge_terms, key_window, end_rows)

    def head_forward(operands):
        query_h, key_h, value_h, posk_h, posq_h = operands
        scores = head_scores(query_h, key_h, posk_h, posq_h)[0]
        highest = jnp.max(scores, axis=1, keepdims=True)
        expo = jnp.exp(scores - highest)
        totals = jnp.sum(expo, axis=1, keepdims=True)
        probs_low = (expo / totals).astype(jnp.bfloat16)
        return (product(probs_low, value_h), (highest + jnp.log(totals))[:, 0])

    contexts, log_totals = lax.map(
        head_forward, (query_heads, key_heads, value_heads, posk_heads, posq_heads)
    )
    context = join_heads(contexts).astype(jnp.bfloat16)
    hidden_f = hidden_in.astype(jnp.float32)
    residual1 = hidden_f + product(context, full_out) + full_ob.astype(jnp.float32)
    gain1 = full_g1.astype(jnp.float32)
    shift1 = full_b1.astype(jnp.float32)
    normed = normalize(residual1, gain1, shift1)
    normed_low = normed.astype(jnp.bfloat16)
    expanded = product(normed_low, full_up) + full_ub.astype(jnp.float32)
    activated = gelu_exact(expanded).astype(jnp.bfloat16)
    residual2 = normed + product(activated, full_down) + full_db.astype(jnp.float32)
    gain2 = full_g2.astype(jnp.float32)
    shift2 = full_b2.astype(jnp.float32)
    hidden_out = normalize(residual2, gain2, shift2).astype(jnp.bfloat16)
    regathered = (
        lax.all_gather(w_qkv, ("dp", "seq"), axis=0, tiled=True),
        lax.all_gather(q_bias, ("dp", "seq"), axis=0, tiled=True),
        lax.all_gather(v_bias, ("dp", "seq"), axis=0, tiled=True),
        lax.all_gather(rel_table, ("dp", "seq"), axis=0, tiled=True),
        lax.all_gather(w_posk, ("dp", "seq"), axis=0, tiled=True),
        lax.all_gather(w_posq, ("dp", "seq"), axis=0, tiled=True),
        lax.all_gather(posq_bias, ("dp", "seq"), axis=0, tiled=True),
        lax.all_gather(w_out, ("dp", "seq"), axis=0, tiled=True),
        lax.all_gather(out_bias, ("dp", "seq"), axis=0, tiled=True),
        lax.all_gather(norm1_gain, ("dp", "seq"), axis=0, tiled=True),
        lax.all_gather(norm1_bias, ("dp", "seq"), axis=0, tiled=True),
        lax.all_gather(w_up, ("dp", "seq"), axis=0, tiled=True),
        lax.all_gather(up_bias, ("dp", "seq"), axis=0, tiled=True),
        lax.all_gather(w_down, ("dp", "seq"), axis=0, tiled=True),
        lax.all_gather(down_bias, ("dp", "seq"), axis=0, tiled=True),
        lax.all_gather(norm2_gain, ("dp", "seq"), axis=0, tiled=True),
        lax.all_gather(norm2_bias, ("dp", "seq"), axis=0, tiled=True),
    )
    (
        back_qkv,
        back_qb,
        back_vb,
        back_table,
        back_posk,
        back_posq,
        back_pqb,
        back_out,
        back_ob,
        back_g1,
        back_b1,
        back_up,
        back_ub,
        back_down,
        back_db,
        back_g2,
        back_b2,
    ) = regathered
    _, pull_second = jax.vjp(normalize, residual2, gain2, shift2)
    d_res2, d_gain2, d_shift2 = pull_second(out_grad.astype(jnp.float32))
    d_reduced = d_res2.astype(jnp.bfloat16)
    d_wdown = inner_first(activated, d_reduced)
    d_down_bias = column_sums(d_reduced)
    d_activated = inner_last(d_reduced, back_down)
    _, pull_gelu = jax.vjp(gelu_exact, expanded)
    d_expanded = pull_gelu(d_activated)[0].astype(jnp.bfloat16)
    d_wup = inner_first(normed_low, d_expanded)
    d_up_bias = column_sums(d_expanded)
    d_normed = inner_last(d_expanded, back_up) + d_res2
    _, pull_first = jax.vjp(normalize, residual1, gain1, shift1)
    d_res1, d_gain1, d_shift1 = pull_first(d_normed)
    d_attended = d_res1.astype(jnp.bfloat16)
    d_wout = inner_first(context, d_attended)
    d_out_bias = column_sums(d_attended)
    d_context = inner_last(d_attended, back_out).astype(jnp.bfloat16)
    dctx_heads = split_heads(d_context)

    def head_backward(operands):
        query_h, key_h, value_h, posk_h, posq_h, log_total, dctx_h = operands
        scores, table_a, table_w, edge_terms, key_window, end_rows = head_scores(
            query_h, key_h, posk_h, posq_h
        )
        probs = jnp.exp(scores - log_total[:, None])
        probs_low = probs.astype(jnp.bfloat16)
        d_probs = inner_last(dctx_h, value_h)
        d_value = inner_first(probs_low, dctx_h)
        row_dot = jnp.sum(probs * d_probs, axis=1, keepdims=True)
        d_raw = (probs * (d_probs - row_dot) * score_scale).astype(jnp.bfloat16)
        _, pull_terms = jax.vjp(pos_terms, table_a, table_w, edge_terms)
        d_table_a, d_table_w, d_edges = pull_terms(d_raw.astype(jnp.float32))
        d_table_a = d_table_a.astype(jnp.bfloat16)
        d_table_w = d_table_w.astype(jnp.bfloat16)
        d_edges = d_edges.astype(jnp.bfloat16)
        d_query = product(d_raw, key_h) + product(d_table_a, posk_h)
        window_grad = product(d_table_w, posq_h)
        key_canvas = jnp.zeros((seq_length + buckets, HEAD_DIM), jnp.float32)
        placed_grad = lax.dynamic_update_slice(
            key_canvas, window_grad, (first_row, jnp.zeros((), jnp.int32))
        )
        d_key = (
            inner_first(d_raw, query_h)
            + placed_grad[SPAN : SPAN + seq_length]
            + inner_first(d_edges, end_rows)
        )
        d_posk = inner_first(d_table_a, query_h)
        end_grads = product(d_edges, key_h)
        d_posq = inner_first(d_table_w, key_window)
        d_posq = d_posq.at[0].add(end_grads[0]).at[buckets - 1].add(end_grads[1])
        return (d_query, d_key, d_value, d_posk, d_posq)

    d_q_heads, d_k_heads, d_v_heads, d_posk_heads, d_posq_heads = lax.map(
        head_backward,
        (query_heads, key_heads, value_heads, posk_heads, posq_heads, log_totals, dctx_heads),
    )
    d_queries = join_heads(d_q_heads).astype(jnp.bfloat16)
    d_keys_part, d_values_part = (
        lax.psum_scatter(
            join_heads(d_k_heads).astype(jnp.bfloat16), "seq", scatter_dimension=0, tiled=True
        ).astype(jnp.float32),
        lax.psum_scatter(
            join_heads(d_v_heads).astype(jnp.bfloat16), "seq", scatter_dimension=0, tiled=True
        ).astype(jnp.float32),
    )
    d_keys = d_keys_part.astype(jnp.bfloat16)
    d_values = d_values_part.astype(jnp.bfloat16)
    d_merged = jnp.concatenate([d_queries, d_keys, d_values], axis=1)
    d_wqkv = inner_first(hidden_in, d_merged)
    d_q_bias = column_sums(d_queries)
    d_v_bias = column_sums(d_values)
    in_grad = d_res1 + inner_last(d_merged, back_qkv)
    d_posk_rows, d_posq_rows = (
        lax.psum_scatter(join_heads(d_posk_heads), ("dp", "seq"), scatter_dimension=0, tiled=True),
        lax.psum_scatter(join_heads(d_posq_heads), ("dp", "seq"), scatter_dimension=0, tiled=True),
    )
    d_posk_low = d_posk_rows.astype(jnp.bfloat16)
    d_posq_low = d_posq_rows.astype(jnp.bfloat16)
    rel_table_grad = inner_last(d_posk_low, back_posk) + inner_last(d_posq_low, back_posq)
    d_wposk = inner_first(rel_table, d_posk_low)
    d_wposq = inner_first(rel_table, d_posq_low)
    d_posq_bias = column_sums(d_posq_low)
    summed = (
        lax.psum_scatter(d_wqkv, ("dp", "seq"), scatter_dimension=0, tiled=True),
        lax.psum_scatter(d_q_bias, ("dp", "seq"), scatter_dimension=0, tiled=True),
        lax.psum_scatter(d_v_bias, ("dp", "seq"), scatter_dimension=0, tiled=True),
        lax.psum_scatter(d_wposk, ("dp", "seq"), scatter_dimension=0, tiled=True),
        lax.psum_scatter(d_wposq, ("dp", "seq"), scatter_dimension=0, tiled=True),
        lax.psum_scatter(d_posq_bias, ("dp", "seq"), scatter_dimension=0, tiled=True),
        lax.psum_scatter(d_wout, ("dp", "seq"), scatter_dimension=0, tiled=True),
        lax.psum_scatter(d_out_bias, ("dp", "seq"), scatter_dimension=0, tiled=True),
        lax.psum_scatter(d_gain1, ("dp", "seq"), scatter_dimension=0, tiled=True),
        lax.psum_scatter(d_shift1, ("dp", "seq"), scatter_dimension=0, tiled=True),
        lax.psum_scatter(d_wup, ("dp", "seq"), scatter_dimension=0, tiled=True),
        lax.psum_scatter(d_up_bias, ("dp", "seq"), scatter_dimension=0, tiled=True),
        lax.psum_scatter(d_wdown, ("dp", "seq"), scatter_dimension=0, tiled=True),
        lax.psum_scatter(d_down_bias, ("dp", "seq"), scatter_dimension=0, tiled=True),
        lax.psum_scatter(d_gain2, ("dp", "seq"), scatter_dimension=0, tiled=True),
        lax.psum_scatter(d_shift2, ("dp", "seq"), scatter_dimension=0, tiled=True),
    )
    return (
        hidden_out,
        in_grad,
        summed[0],
        summed[1],
        summed[2],
        rel_table_grad,
        summed[3],
        summed[4],
        summed[5],
        summed[6],
        summed[7],
        summed[8],
        summed[9],
        summed[10],
        summed[11],
        summed[12],
        summed[13],
        summed[14],
        summed[15],
    )


def solution(mesh):
    placed = (
        P(("dp", "seq"), None),
        P("dp"),
        P(("dp", "seq"), None),
        P(("dp", "seq")),
        P(("dp", "seq")),
        P(("dp", "seq"), None),
        P(("dp", "seq"), None),
        P(("dp", "seq"), None),
        P(("dp", "seq")),
        P(("dp", "seq"), None),
        P(("dp", "seq")),
        P(("dp", "seq")),
        P(("dp", "seq")),
        P(("dp", "seq"), None),
        P(("dp", "seq")),
        P(("dp", "seq"), None),
        P(("dp", "seq")),
        P(("dp", "seq")),
        P(("dp", "seq")),
        P(("dp", "seq"), None),
    )
    return jax.shard_map(
        head_split if dict(mesh.shape) == {"dp": 16, "seq": 2} else row_split,
        mesh=mesh,
        in_specs=placed,
        out_specs=(
            P(("dp", "seq"), None),
            P(("dp", "seq"), None),
            P(("dp", "seq"), None),
            P(("dp", "seq")),
            P(("dp", "seq")),
            P(("dp", "seq"), None),
            P(("dp", "seq"), None),
            P(("dp", "seq"), None),
            P(("dp", "seq")),
            P(("dp", "seq"), None),
            P(("dp", "seq")),
            P(("dp", "seq")),
            P(("dp", "seq")),
            P(("dp", "seq"), None),
            P(("dp", "seq")),
            P(("dp", "seq"), None),
            P(("dp", "seq")),
            P(("dp", "seq")),
            P(("dp", "seq")),
        ),
        check_vma=False,
    )
```

```python
import functools
import math

import jax
import jax.numpy as jnp
from jax import lax
from jax.experimental import pallas as pl
from jax.experimental.pallas import tpu as pltpu
from jax.sharding import PartitionSpec as P

D = 768
HEADS = 12
HEAD_DIM = 64
SPAN = 256
TILE = 128
BLOCK = 256
BAND = 768
PAIR = 2 * HEAD_DIM


eps_norm = 1e-07


def normalize(value, gain, shift):
    average = jnp.mean(value, axis=-1, keepdims=True)
    centred = value - average
    variance = jnp.mean(centred * centred, axis=-1, keepdims=True)
    return centred * lax.rsqrt(variance + eps_norm) * gain + shift


def gelu_exact(value):
    return jax.nn.gelu(value, approximate=False)


def product(left, right):
    return jnp.dot(left, right, preferred_element_type=jnp.float32)


def inner_first(left, right):
    return lax.dot_general(
        left, right, (((0,), (0,)), ((), ())), preferred_element_type=jnp.float32
    )


def inner_last(left, right):
    return lax.dot_general(
        left, right, (((1,), (1,)), ((), ())), preferred_element_type=jnp.float32
    )


def split_heads(matrix):
    return matrix.reshape(matrix.shape[0], HEADS, HEAD_DIM).transpose(1, 0, 2)


def join_heads(stacked):
    return stacked.transpose(1, 0, 2).reshape(stacked.shape[1], D)


def column_sums(matrix):
    return jnp.sum(matrix.astype(jnp.float32), axis=0)


def nn(left, right):
    return lax.dot_general(
        left, right, (((1,), (0,)), ((), ())), preferred_element_type=jnp.float32
    )


def nt(left, right):
    return lax.dot_general(
        left, right, (((1,), (1,)), ((), ())), preferred_element_type=jnp.float32
    )


def unit_matrix(size, reverse=False):
    rows = lax.broadcasted_iota(jnp.int32, (size, size), 0)
    cols = lax.broadcasted_iota(jnp.int32, (size, size), 1)
    if reverse:
        cols = size - 1 - cols
    return jnp.where(rows == cols, 1.0, 0.0).astype(jnp.bfloat16)


def turn_matrix():
    rows = lax.broadcasted_iota(jnp.int32, (BLOCK, BLOCK), 0)
    cols = lax.broadcasted_iota(jnp.int32, (BLOCK, BLOCK), 1)
    mirrored = rows // TILE * (2 * TILE) + TILE - 1 - rows
    return jnp.where(mirrored == cols, 1.0, 0.0).astype(jnp.bfloat16)


def head_lanes(head):
    lanes = lax.broadcasted_iota(jnp.int32, (1, PAIR), 1)
    return lanes // HEAD_DIM == head


def head_rows(head):
    rows = lax.broadcasted_iota(jnp.int32, (HEAD_DIM, PAIR), 0)
    cols = lax.broadcasted_iota(jnp.int32, (HEAD_DIM, PAIR), 1)
    return jnp.where(cols == rows + head * HEAD_DIM, 1.0, 0.0).astype(jnp.bfloat16)


def key_tiles(block, length):
    return max(length // 2, (block + 1) * BLOCK) // TILE


def tile_seen(query_tile, key_tile, length):
    return key_tile < key_tiles(query_tile * TILE // BLOCK, length)


def skewed(window):
    return pltpu.roll(window, 0, 1, stride=1, stride_axis=0)


def forward_body(prefix_ref, q_ref, k_ref, v_ref, pk_ref, pq_ref, ctx_ref, p_ref, wb_ref, far_ref, s_ref):
    length = q_ref.shape[0]
    head = pl.program_id(1)
    mine = head_lanes(head)
    prefix = prefix_ref[0]
    eye = unit_matrix(TILE)
    eye_block = unit_matrix(BLOCK)
    zero = jnp.zeros((), jnp.bfloat16)
    scale = math.log2(math.e) / math.sqrt(3 * HEAD_DIM)
    for tile in range(length // TILE):
        rows = slice(tile * TILE, (tile + 1) * TILE)
        table = nt(jnp.where(mine, k_ref[rows, :], zero), pq_ref[...])
        wb_ref[rows, :] = skewed(table)
        wb_ref[rows, 0:TILE] = table[:, BAND - TILE :]
        far_ref[rows, :] = table[:, 0:TILE]
    v_cols = nt(jnp.where(lax.broadcasted_iota(jnp.int32, (PAIR, PAIR), 0) // HEAD_DIM == head, unit_matrix(PAIR), zero), v_ref[...]).astype(jnp.bfloat16)
    for block in range(length // BLOCK):
        cols = slice(block * BLOCK, (block + 1) * BLOCK)
        q_own = jnp.where(mine, q_ref[cols, :], zero)
        skews, highs, lows = [], [], []
        for sub in range(2):
            table = nt(q_own[sub * TILE : (sub + 1) * TILE], pk_ref[...])
            skews.append(skewed(table).astype(jnp.bfloat16))
            highs.append(table[:, 0:TILE].astype(jnp.bfloat16))
            lows.append(table[:, BAND - TILE :].astype(jnp.bfloat16))
        count = key_tiles(block, length)
        highest = None
        for tile in range(count):
            rows = slice(tile * TILE, (tile + 1) * TILE)
            parts_a, parts_b = [], []
            for sub in range(2):
                step = 2 * block + sub - tile
                if step >= 3:
                    parts_a.append(highs[sub])
                    parts_b.append(wb_ref[rows, 0:TILE])
                elif step <= -3:
                    parts_a.append(lows[sub])
                    parts_b.append(far_ref[rows, :])
                else:
                    at = 384 - TILE * step
                    parts_a.append(skews[sub][:, at : at + TILE])
                    at = 384 + TILE * step
                    parts_b.append(wb_ref[rows, at : at + TILE])
            right = jnp.concatenate([jnp.concatenate(parts_a, axis=0), q_own], axis=1)
            left = jnp.concatenate([eye, k_ref[rows, :]], axis=1)
            raw = nt(left, right) + jnp.concatenate(parts_b, axis=1)
            if (tile + 1) * TILE > block * BLOCK + 1:
                keys = tile * TILE + lax.broadcasted_iota(jnp.int32, (TILE, BLOCK), 0)
                queries = block * BLOCK + lax.broadcasted_iota(jnp.int32, (TILE, BLOCK), 1)
                raw = jnp.where((keys < prefix) | (keys <= queries), raw, -jnp.inf)
            s_ref[rows, :] = raw
            top = jnp.max(raw, axis=0, keepdims=True)
            highest = top if highest is None else jnp.maximum(highest, top)
        total = jnp.zeros((1, BLOCK), jnp.float32)
        for tile in range(count):
            rows = slice(tile * TILE, (tile + 1) * TILE)
            expo = jnp.exp2((s_ref[rows, :] - highest) * scale)
            s_ref[rows, :] = expo
            total = total + jnp.sum(expo, axis=0, keepdims=True)
        inverse = 1.0 / total
        for tile in range(count):
            rows = slice(tile * TILE, (tile + 1) * TILE)
            p_ref[rows, cols] = (s_ref[rows, :] * inverse).astype(jnp.bfloat16)
        seen = count * TILE
        ctx_cols = nn(v_cols[:, :seen], p_ref[0:seen, cols]).astype(jnp.bfloat16)
        ctx = nt(eye_block, ctx_cols).astype(jnp.bfloat16)

        @pl.when(head == 0)
        def _():
            ctx_ref[cols, :] = ctx

        @pl.when(head == 1)
        def _():
            ctx_ref[cols, :] = ctx_ref[cols, :] + ctx


def attention_forward(prefix, merged, pos_band, pair):
    length, width = merged.shape[0], merged.shape[1] // 3
    pairs = width // PAIR
    tall = [pl.BlockSpec((length, PAIR), lambda p, h, at=at: (0, at)) for at in (pair, pairs + pair, 2 * pairs + pair)]
    band = [pl.BlockSpec((BAND, PAIR), lambda p, h, at=at: (0, at)) for at in (pair, pairs + pair)]
    return pl.pallas_call(
        forward_body,
        grid=(1, 2),
        in_specs=[pl.BlockSpec(memory_space=pltpu.SMEM)] + tall + band,
        out_specs=[
            pl.BlockSpec((length, PAIR), lambda p, h: (0, 0)),
            pl.BlockSpec((None, length, length), lambda p, h: (h, 0, 0)),
        ],
        out_shape=[
            jax.ShapeDtypeStruct((length, PAIR), jnp.bfloat16),
            jax.ShapeDtypeStruct((2, length, length), jnp.bfloat16),
        ],
        scratch_shapes=[
            pltpu.VMEM((length, BAND), jnp.float32),
            pltpu.VMEM((length, TILE), jnp.float32),
            pltpu.VMEM((length, BLOCK), jnp.float32),
        ],
        compiler_params=pltpu.CompilerParams(dimension_semantics=("arbitrary", "arbitrary"), vmem_limit_bytes=40 << 20),
        cost_estimate=pl.CostEstimate(flops=12 * 10**9, transcendentals=2 * length * length, bytes_accessed=6 << 20),
        name="attention_forward",
    )(prefix, merged, merged, merged, pos_band, pos_band)


def backward_body(first, q_ref, k_ref, v_ref, dctx_ref, p_ref, pk_ref, pq_ref, *refs):
    dq_ref, dk_ref, dv_ref, dpk_ref, dpq_ref, dr_ref, dk_acc, dv_acc = refs[-8:]
    outs = (dq_ref, dk_ref, dv_ref)
    earlier = refs[: len(refs) - 8] or outs
    length = q_ref.shape[0]
    head = pl.program_id(1) + first
    mine = head_lanes(head)
    flip = turn_matrix()
    pick = head_rows(head)
    bf = jnp.bfloat16
    zero = jnp.zeros((), bf)
    scale = 1.0 / math.sqrt(3 * HEAD_DIM)
    back = BAND - (TILE - 1)
    blank = jnp.zeros((TILE, TILE), bf)
    dk_acc[...] = jnp.zeros_like(dk_acc)
    dv_acc[...] = jnp.zeros_like(dv_acc)
    dpk = jnp.zeros((HEAD_DIM, BAND), jnp.float32)
    dpq = jnp.zeros((HEAD_DIM, BAND), jnp.float32)
    tiles = length // TILE

    def put(index, rows, value):
        ref = outs[index]

        @pl.when(head == 0)
        def _():
            ref[rows, :] = jnp.where(mine, value, 0.0).astype(bf)

        @pl.when(head == 1)
        def _():
            ref[rows, :] = jnp.where(mine, value.astype(bf), earlier[index][rows, :])

    def unskew(parts):
        return pltpu.roll(jnp.concatenate(parts, axis=1), back, 1, stride=1, stride_axis=0)

    for block in range(length // BLOCK):
        cols = slice(block * BLOCK, (block + 1) * BLOCK)
        count = key_tiles(block, length)
        seen = count * TILE
        dctx = dctx_ref[cols, :]
        v_own = jnp.where(mine, v_ref[0:seen, :], zero)
        probs_low = p_ref[0:seen, cols]
        probs = probs_low.astype(jnp.float32)
        d_probs = nt(v_own, dctx)
        row_dot = jnp.sum(probs * d_probs, axis=0, keepdims=True)
        dr_ref[0:seen, cols] = (probs * ((d_probs - row_dot) * scale)).astype(bf)
        d_raw = dr_ref[0:seen, cols]
        dv_acc[0:seen, :] += nn(probs_low, dctx)
        dk_acc[0:seen, :] += nn(d_raw, q_ref[cols, :])
        turned = nt(flip, d_raw).astype(bf)
        spreads = []
        for sub in range(2):
            tile = 2 * block + sub
            own = turned[sub * TILE : (sub + 1) * TILE]

            def piece(key_tile):
                return own[:, key_tile * TILE : (key_tile + 1) * TILE]

            near = [t for t in range(count) if tile - t >= 3]
            far = [t for t in range(count) if tile - t <= -3]
            band = [blank]
            for step in (2, 1, 0, -1, -2):
                key_tile = tile - step
                band.append(piece(key_tile) if 0 <= key_tile < count else blank)
            spreads.append(
                add_edges(unskew(band), [piece(t).astype(jnp.float32) for t in near], [piece(t).astype(jnp.float32) for t in far])
            )
        spread = jnp.concatenate(spreads, axis=0)
        dq = nn(turned, k_ref[0:seen, :]) + nn(spread, pk_ref[...])
        put(0, cols, nn(flip, dq.astype(bf)))
        q_cols = nt(pick, nn(flip, q_ref[cols, :]).astype(bf)).astype(bf)
        dpk = dpk + nn(q_cols, spread)
    dpk_ref[...] = dpk
    for block in range(length // BLOCK):
        rows = slice(block * BLOCK, (block + 1) * BLOCK)
        groups, edges = [], []
        for sub in range(2):
            key_tile = 2 * block + sub
            own = slice(key_tile * TILE, (key_tile + 1) * TILE)
            seen_by = [t for t in range(tiles) if tile_seen(t, key_tile, length)]

            def held(query_tile):
                return dr_ref[own, query_tile * TILE : (query_tile + 1) * TILE]

            band = [blank]
            for step in (-2, -1, 0, 1, 2):
                query_tile = key_tile + step
                band.append(held(query_tile) if query_tile in seen_by else blank)
            ends = []
            for chosen in ([t for t in seen_by if t - key_tile <= -3], [t for t in seen_by if t - key_tile >= 3]):
                total = blank
                if chosen:
                    total = sum((held(t).astype(jnp.float32) for t in chosen[1:]), held(chosen[0]).astype(jnp.float32)).astype(bf)
                ends.append(total)
            groups.append(jnp.concatenate(band[1:] + ends, axis=1))
        turned = nn(flip, jnp.concatenate(groups, axis=0))
        width = BAND - TILE
        spreads = []
        for sub in range(2):
            own = turned[sub * TILE : (sub + 1) * TILE]
            spreads.append(
                add_edges(unskew([blank, own[:, :width].astype(bf)]), [own[:, width : width + TILE]], [own[:, width + TILE :]])
            )
        spread = jnp.concatenate(spreads, axis=0)
        d_key = nn(flip, nn(spread, pq_ref[...]).astype(bf))
        put(1, rows, dk_acc[rows, :] + d_key)
        k_cols = nt(pick, nn(flip, k_ref[rows, :]).astype(bf)).astype(bf)
        dpq = dpq + nn(k_cols, spread)
        put(2, rows, dv_acc[rows, :])
    dpq_ref[...] = dpq


def add_edges(spread, first, last):
    parts = [spread[:, 0:TILE], spread[:, TILE : BAND - TILE], spread[:, BAND - TILE :]]
    for place, tiles in ((0, first), (2, last)):
        if tiles:
            total = parts[place].astype(jnp.float32)
            for tile in tiles:
                total = total + tile
            parts[place] = total.astype(jnp.bfloat16)
    return jnp.concatenate(parts, axis=1)


def attention_backward(merged, dctx, probs, pos_band, pair, heads=(0, 1), found=()):
    length, width = merged.shape[0], merged.shape[1] // 3
    pairs = width // PAIR
    count, first = len(heads), heads[0]
    tall = [pl.BlockSpec((length, PAIR), lambda p, h, at=at: (0, at)) for at in (pair, pairs + pair, 2 * pairs + pair, pair)]
    band = [pl.BlockSpec((BAND, PAIR), lambda p, h, at=at: (0, at)) for at in (pair, pairs + pair)]
    own = pl.BlockSpec((length, PAIR), lambda p, h: (0, 0))
    table = pl.BlockSpec((HEAD_DIM, BAND), lambda p, h: (h, 0))
    flat = jax.ShapeDtypeStruct((length, PAIR), jnp.bfloat16)
    wide = jax.ShapeDtypeStruct((count * HEAD_DIM, BAND), jnp.float32)
    return pl.pallas_call(
        functools.partial(backward_body, first),
        grid=(1, count),
        in_specs=tall + [pl.BlockSpec((None, length, length), lambda p, h: (h + first, 0, 0))] + band + [own] * len(found),
        out_specs=[own, own, own, table, table],
        out_shape=[flat, flat, flat, wide, wide],
        scratch_shapes=[
            pltpu.VMEM((length, length), jnp.bfloat16),
            pltpu.VMEM((length, PAIR), jnp.float32),
            pltpu.VMEM((length, PAIR), jnp.float32),
        ],
        compiler_params=pltpu.CompilerParams(dimension_semantics=("arbitrary", "arbitrary"), vmem_limit_bytes=40 << 20),
        cost_estimate=pl.CostEstimate(flops=13 * count * 10**9, transcendentals=0, bytes_accessed=4 * count << 20),
        name="attention_backward",
    )(merged, merged, merged, dctx, probs, pos_band, pos_band, *found)


CORES = [(0, 1), (1, 0)]


def swap(value):
    return lax.ppermute(value, "seq", CORES)


def ordered(core, own, other, axis=0):
    return jnp.concatenate(
        [jnp.where(core == 0, own, other), jnp.where(core == 0, other, own)], axis=axis
    )


def half_of(core, matrix, axis):
    size = matrix.shape[axis] // 2
    return lax.dynamic_slice_in_dim(matrix, core * size, size, axis)


def chip_bits():
    chip = lax.axis_index("dp")
    return chip // 4, (chip // 2) % 2, chip % 2


def exchange(value, mask):
    return lax.ppermute(value, "dp", [(i, i ^ mask) for i in range(16)])


def tie_all(chain, others):
    chain.state, others = lax.optimization_barrier((chain.state, others))
    return others


class Gather:
    def __init__(self, *values):
        self.state = values

    def line(self, step):
        up = [(i, i + 4) for i in range(12) if i // 4 >= step - 1]
        down = [(i + 4, i) for i in range(12) if i // 4 <= 3 - step]
        if step == 1:
            self.state = [([value], [value]) for value in self.state]
        self.state = [
            (below + [lax.ppermute(below[-1], "dp", up)], above + [lax.ppermute(above[-1], "dp", down)])
            for below, above in self.state
        ]
        if step == 3:
            z = chip_bits()[0]
            lines = []
            for below, above in self.state:
                blocks = []
                for block in range(4):
                    options = [below[k - block] if k >= block else above[block - k] for k in range(4)]
                    blocks.append(lax.select_n(z, *options))
                lines.append(tuple(jnp.stack([b[side] for b in blocks]) for side in range(2)))
            self.state = lines

    def pair(self, step):
        _, y, x = chip_bits()
        order = ((x, 1), (y, 2)) if step == 1 else ((y, 2), (x, 1))
        lines = []
        for halves in self.state:
            result = []
            for value, (bit, mask) in zip(halves, order):
                other = exchange(value, mask)
                result.append(jnp.stack([jnp.where(bit == 0, value, other), jnp.where(bit == 0, other, value)]))
            lines.append(tuple(result))
        self.state = lines

    def rows(self, index, low, high):
        first, second = [half[..., low:high] for half in self.state[index]]
        first = jnp.moveaxis(first, (0, 1, 2), (1, 2, 0))
        second = jnp.moveaxis(second, (0, 1, 2), (2, 1, 0))
        whole = jnp.stack([first, second], axis=3)
        return whole.reshape(-1, whole.shape[-1])


class Scatter:
    def __init__(self, *values):
        self.state = []
        for value in values:
            grid = value.reshape((4, 2, 2) + value.shape[1:])
            self.state.append((jnp.moveaxis(grid[:, :, :, 0], 2, 0), jnp.moveaxis(grid[:, :, :, 1], 1, 0)))

    def pair(self, step):
        _, y, x = chip_bits()
        order = ((x, 1), (y, 2)) if step == 1 else ((y, 2), (x, 1))
        sums = []
        for halves in self.state:
            result = []
            for value, (bit, mask) in zip(halves, order):
                keep = jnp.where(bit == 0, value[0], value[1])
                give = jnp.where(bit == 0, value[1], value[0])
                total = (keep.astype(jnp.float32) + exchange(give, mask).astype(jnp.float32)).astype(value.dtype)
                result.append(jnp.moveaxis(total, 1, 0) if step == 1 else total)
            sums.append(tuple(result) if step == 1 else (jnp.stack(result, axis=1), None, None))
        self.state = sums

    def line(self, step):
        z = chip_bits()[0]
        offset = 4 - step
        ups = [(i, i + 4) for i in range(12) if i // 4 + offset <= 3]
        downs = [(i + 4, i) for i in range(12) if i // 4 + 1 - offset >= 0]
        sums, self.totals = [], []
        for value, up, down in self.state:

            def block(at):
                options = [value[min(max(k + at, 0), 3)] for k in range(4)]
                return lax.select_n(z, *options).astype(jnp.float32)

            to_above, to_below = block(offset), block(-offset)
            if up is not None:
                to_above = to_above + up.astype(jnp.float32)
                to_below = to_below + down.astype(jnp.float32)
            up = lax.ppermute(to_above.astype(value.dtype), "dp", ups)
            down = lax.ppermute(to_below.astype(value.dtype), "dp", downs)
            sums.append((value, up, down))
            if step == 3:
                self.totals.append(block(0) + up.astype(jnp.float32) + down.astype(jnp.float32))
        self.state = sums


def norm_parts(value):
    average = jnp.mean(value, axis=-1, keepdims=True)
    centred = value - average
    variance = jnp.mean(centred * centred, axis=-1, keepdims=True)
    inverse = lax.rsqrt(variance + eps_norm)
    return centred * inverse, inverse


def norm_back(unit, inverse, gain, grad):
    scaled = grad * gain
    mean_grad = jnp.mean(scaled, axis=-1, keepdims=True)
    mean_along = jnp.mean(scaled * unit, axis=-1, keepdims=True)
    return inverse * (scaled - mean_grad - unit * mean_along)


def head_split(
    hidden_in, prefix, w_qkv, q_bias, v_bias, rel_table, w_posk, w_posq, posq_bias, w_out, out_bias,
    norm1_gain, norm1_bias, w_up, up_bias, w_down, down_bias, norm2_gain, norm2_bias, out_grad,
):
    bf = jnp.bfloat16
    f32 = jnp.float32
    core = lax.axis_index("seq")
    rows = w_qkv.shape[0]
    units = w_down.shape[0]
    table_rows = rel_table.shape[0]
    chips = 16
    half = D // 2
    ff_half = chips * units
    buckets = 2 * SPAN

    last_rows = rows - table_rows
    vectors = (q_bias, v_bias, posq_bias, out_bias, norm1_gain, norm1_bias, down_bias, norm2_gain)
    left = jnp.stack(vectors)
    right = jnp.concatenate(
        [jnp.pad(norm2_bias, (0, units - rows))[None], up_bias[None], jnp.zeros((last_rows - 2, units), bf)], axis=0
    )
    small = jnp.concatenate([jnp.pad(left, ((0, 0), (0, 128 - rows))), jnp.pad(right, ((0, 0), (0, half - 128 - units)))], axis=1)

    def columns(side):
        qkv = w_qkv.reshape(rows, 3, 2, half)[:, :, side].reshape(rows, 3 * half)
        corner = jnp.concatenate([rel_table[:, side * half : (side + 1) * half], small], axis=0)
        cut = slice(side * half, (side + 1) * half)
        up = w_up.reshape(rows, chips, 2, units)[:, :, side].reshape(rows, ff_half)
        return (
            jnp.concatenate([qkv, w_posk[:, cut], w_posq[:, cut], corner], axis=1),
            jnp.concatenate([w_out[:, cut], up], axis=1),
        )

    early0, late0 = columns(0)
    early1, late1 = columns(1)
    early_got = swap(jnp.where(core == 0, early1, early0))
    late_got = swap(jnp.where(core == 0, late1, late0))
    hidden_got = swap(hidden_in)

    def by_core(first, second, got):
        own = jnp.where(core == 0, first, second)
        return jnp.stack([jnp.where(core == 0, own, got), jnp.where(core == 0, got, own)])

    early_chain = Gather(by_core(early0, early1, early_got))
    downs = jnp.concatenate([w_down.reshape(2, 2, rows, D)[:, 0], w_down.reshape(2, 2, rows, D)[:, 1]], axis=-1)
    late_chain = Gather(jnp.concatenate([by_core(late0, late1, late_got), downs], axis=-1))
    for step in (1, 2, 3):
        early_chain.line(step)
    late_chain.state = tie_all(early_chain, late_chain.state)
    early_chain.pair(1)
    late_chain.line(1)
    late_chain.state = tie_all(early_chain, late_chain.state)
    early_chain.pair(2)
    late_chain.line(2)
    late_chain.line(3)
    hidden_all = ordered(core, hidden_in, hidden_got)
    w_qkv_own = early_chain.rows(0, 0, 3 * half)
    w_pos_own = early_chain.rows(0, 3 * half, 5 * half)
    corner = early_chain.rows(0, 5 * half, 6 * half).reshape(2 * chips, rows, half)
    table_half = corner[:, :table_rows].reshape(buckets, half)
    small = corner[:, table_rows:]
    table = ordered(core, table_half, swap(table_half), axis=1)

    owner = (lax.broadcasted_iota(jnp.int32, (2 * chips, D), 1) // rows == lax.broadcasted_iota(jnp.int32, (2 * chips, D), 0)).astype(bf)
    inside = lax.broadcasted_iota(jnp.int32, (rows, D), 1) % rows == lax.broadcasted_iota(jnp.int32, (rows, D), 0)
    unit_owner = (
        2 * (lax.broadcasted_iota(jnp.int32, (2 * chips, ff_half), 1) // units) + core
        == lax.broadcasted_iota(jnp.int32, (2 * chips, ff_half), 0)
    ).astype(bf)
    unit_inside = lax.broadcasted_iota(jnp.int32, (units, ff_half), 1) % units == lax.broadcasted_iota(jnp.int32, (units, ff_half), 0)
    spots = jnp.concatenate([small[:, :, :rows], small[:, :, 128 : 128 + rows]], axis=1)
    wide = lax.dot_general(spots, owner, (((0,), (0,)), ((), ())), preferred_element_type=f32)
    lists = jnp.sum(jnp.where(inside, wide, 0.0), axis=1)
    qb, vb, pqb, ob, gain1, shift1, db, gain2, shift2 = [lists[i] for i in range(9)]
    wide = inner_first(small[:, 1, 128 : 128 + units], unit_owner)
    ub = jnp.sum(jnp.where(unit_inside, wide, 0.0), axis=0)

    band = lax.broadcasted_iota(jnp.int32, (BAND, buckets), 0)
    bucket = lax.broadcasted_iota(jnp.int32, (BAND, buckets), 1)
    chosen = (jnp.clip(SPAN + 384 - band, 0, buckets - 1) == bucket).astype(bf)
    pos_shift = jnp.concatenate([jnp.zeros((half,), f32), half_of(core, pqb, 0)])
    pos = (product(table, w_pos_own) + pos_shift).astype(bf)
    pos_band = product(chosen, pos).astype(bf)

    qkv_shift = jnp.concatenate([half_of(core, qb, 0), jnp.zeros((half,), f32), half_of(core, vb, 0)])
    merged = (product(hidden_all, w_qkv_own) + qkv_shift).astype(bf)
    merged, pos_band = tie_all(late_chain, (merged, pos_band))
    late_chain.pair(1)
    context_parts, prob_parts = [], []
    for pair in range(half // PAIR):
        part, kept = attention_forward(prefix, merged, pos_band, pair)
        if pair == 0:
            part, merged = tie_all(late_chain, (part, merged))
            late_chain.pair(2)
        context_parts.append(part)
        prob_parts.append(kept)
    context = jnp.concatenate(context_parts, axis=1)
    out_columns = late_chain.rows(0, 0, half)
    w_out_own = ordered(
        core, half_of(core, out_columns, 0), swap(half_of(1 - core, out_columns, 0)), axis=1
    )
    w_up_own = late_chain.rows(0, half, half + ff_half)
    down_at = half + ff_half
    down_parts = [late_chain.rows(0, at, at + D).reshape(2 * chips, rows, D) for at in (down_at, down_at + D)]
    w_down_own = jnp.stack(down_parts, axis=1).reshape(ff_half, D)

    def summed_rows(left, multiply):
        given = swap(multiply(half_of(1 - core, left, 0)))
        return multiply(half_of(core, left, 0)) + given

    hidden_f = hidden_in.astype(f32)
    residual1 = hidden_f + summed_rows(context, lambda part: product(part, w_out_own)) + ob
    unit1, inverse1 = norm_parts(residual1)
    normed = unit1 * gain1 + shift1
    normed_low = normed.astype(bf)
    normed_all = ordered(core, normed_low, swap(normed_low))
    expanded = product(normed_all, w_up_own) + ub
    normal_cdf = 0.5 + 0.5 * lax.erf(expanded * math.sqrt(0.5))
    activated = (expanded * normal_cdf).astype(bf)
    slope = (
        normal_cdf + expanded * jnp.exp(-0.5 * expanded * expanded) * (1.0 / math.sqrt(2.0 * math.pi))
    ).astype(bf)
    residual2 = normed + summed_rows(activated, lambda part: product(part, w_down_own)) + db
    unit2, inverse2 = norm_parts(residual2)
    hidden_out = (unit2 * gain2 + shift2).astype(bf)

    grad = out_grad.astype(f32)
    d_res2 = norm_back(unit2, inverse2, gain2, grad)
    d_gain2 = jnp.sum(grad * unit2, axis=0, keepdims=True)
    d_shift2 = jnp.sum(grad, axis=0, keepdims=True)
    d_reduced = d_res2.astype(bf)
    d_down_bias = column_sums(d_reduced)[None]
    reduced_all = ordered(core, d_reduced, swap(d_reduced))
    d_expanded = (inner_last(reduced_all, w_down_own) * slope.astype(f32)).astype(bf)
    d_normed = summed_rows(d_expanded, lambda part: inner_last(part, w_up_own)) + d_res2
    d_wdown = inner_first(activated, reduced_all).astype(bf)
    d_wup = inner_first(normed_all, d_expanded).astype(bf)
    d_up_bias = column_sums(d_expanded)
    d_res1 = norm_back(unit1, inverse1, gain1, d_normed)
    d_gain1 = jnp.sum(d_normed * unit1, axis=0, keepdims=True)
    d_shift1 = jnp.sum(d_normed, axis=0, keepdims=True)
    d_attended = d_res1.astype(bf)
    d_out_bias = column_sums(d_attended)[None]
    attended_all = ordered(core, d_attended, swap(d_attended))
    d_context = inner_last(attended_all, w_out_own).astype(bf)
    d_wout_rows = inner_first(context, attended_all).astype(bf)
    d_wout = ordered(
        core, half_of(core, d_wout_rows, 1), swap(half_of(1 - core, d_wout_rows, 1)), axis=0
    )

    def rejoin(first, second):
        own = jnp.where(core == 0, first, second)
        got = swap(jnp.where(core == 0, second, first))
        return jnp.where(core == 0, own, got), jnp.where(core == 0, got, own)

    late_cols = jnp.concatenate([d_wout, d_wup], axis=1).reshape(chips, 2, rows, half + ff_half)
    down_cols = d_wdown.reshape(chips, 2, 2, rows, D)
    late_sums = Scatter(jnp.concatenate([late_cols, down_cols[:, :, 0], down_cols[:, :, 1]], axis=-1))
    grads = []
    d_context = tie_all(late_sums, d_context)
    late_sums.pair(1)
    found = attention_backward(merged, d_context, prob_parts[0], pos_band, 0)
    found, d_context = tie_all(late_sums, (found, d_context))
    grads.append(found)
    late_sums.pair(2)
    found = attention_backward(merged, d_context, prob_parts[1], pos_band, 1)
    found, d_context = tie_all(late_sums, (found, d_context))
    grads.append(found)
    late_sums.line(1)
    found = attention_backward(merged, d_context, prob_parts[2], pos_band, 2, (0,))
    found, d_context = tie_all(late_sums, (found, d_context))
    late_sums.line(2)
    later = attention_backward(merged, d_context, prob_parts[2], pos_band, 2, (1,), found[:3])
    found, later = tie_all(late_sums, (found, later))
    grads.append([*later[:3], *[jnp.concatenate(pair, axis=0) for pair in zip(found[3:], later[3:])]])
    late_sums.line(3)
    d_merged = jnp.concatenate([g[i] for i in range(3) for g in grads], axis=1)
    d_q, d_v = d_merged[:, :half], d_merged[:, 2 * half :]
    in_grad = d_res1 + summed_rows(d_merged, lambda part: inner_last(part, w_qkv_own))
    d_wqkv = inner_first(hidden_all, d_merged).astype(bf)
    d_q_bias = column_sums(d_q)[None]
    d_v_bias = column_sums(d_v)[None]
    d_band = jnp.concatenate([g[i] for i in (3, 4) for g in grads], axis=0).astype(bf)
    d_pos = lax.dot_general(
        chosen, d_band, (((0,), (1,)), ((), ())), preferred_element_type=f32
    )
    d_posq_bias = jnp.sum(d_pos[:, half:], axis=0, keepdims=True)
    d_pos_low = d_pos.astype(bf)
    d_wpos = inner_first(table, d_pos_low).astype(bf)
    d_table_all = inner_last(d_pos_low, w_pos_own).astype(bf)
    d_table = (
        half_of(core, d_table_all, 1).astype(f32)
        + swap(half_of(1 - core, d_table_all, 1)).astype(f32)
    ).astype(bf)

    def whole(part):
        blank = jnp.zeros_like(part)
        return ordered(core, part, blank, axis=1)

    lists_grad = jnp.concatenate(
        [whole(jnp.concatenate([d_q_bias, d_v_bias, d_posq_bias], axis=0)), d_out_bias, d_gain1, d_shift1, d_down_bias, d_gain2, d_shift2],
        axis=0,
    ).astype(bf)
    lists_grad = jnp.pad(lists_grad, ((0, 7), (0, 0)))
    pieces = jnp.where(inside, lists_grad[:, None, :], jnp.zeros((), bf)).reshape(16 * rows, D)
    unit_at = lax.broadcasted_iota(jnp.int32, (half, ff_half), 1) % units + 256 == lax.broadcasted_iota(jnp.int32, (half, ff_half), 0)
    unit_pieces = jnp.where(unit_at, d_up_bias.astype(bf), jnp.zeros((), bf))
    vector = (inner_last(owner, pieces) + inner_last(unit_owner, unit_pieces)).astype(bf)
    corner_grad = jnp.concatenate(
        [
            d_table.reshape(2 * chips, table_rows, half),
            jnp.pad(vector[:, None, :], ((0, 0), (0, last_rows - 1), (0, 0))),
        ],
        axis=1,
    ).reshape(chips * 2 * rows, half)
    early_sums = Scatter(
        jnp.concatenate([d_wqkv, d_wpos, corner_grad], axis=1).reshape(chips, 2, rows, 6 * half)
    )
    early_sums.pair(1)
    late_grads = late_sums.totals[0]
    down_grads = late_grads[:, :, half + ff_half :]
    late_grads = late_grads[:, :, : half + ff_half]
    late_left, late_right = rejoin(late_grads[0], late_grads[1])
    early_sums.pair(2)
    g_wdown = jnp.stack([down_grads[:, :, :D], down_grads[:, :, D:]], axis=1).reshape(units, D)
    g_wout = jnp.concatenate([late_left[:, :half], late_right[:, :half]], axis=1)
    g_wup = jnp.stack(
        [late_left[:, half:].reshape(rows, chips, units), late_right[:, half:].reshape(rows, chips, units)], axis=2
    ).reshape(rows, 2 * ff_half)
    g_wdown, g_wout, g_wup, in_grad = tie_all(early_sums, (g_wdown, g_wout, g_wup, in_grad))
    for step in (1, 2, 3):
        early_sums.line(step)
    early_grads = early_sums.totals[0]
    early_left, early_right = rejoin(early_grads[0], early_grads[1])
    vector_sum = early_left[table_rows, 5 * half :] + early_right[table_rows, 5 * half :]

    def side_by_side(left, right, at, count):
        pieces = []
        for index in range(count):
            cut = slice((at + index) * half, (at + index + 1) * half)
            pieces += [left[:, cut], right[:, cut]]
        return jnp.concatenate(pieces, axis=1)

    g_wqkv = side_by_side(early_left, early_right, 0, 3)
    g_wposk = side_by_side(early_left, early_right, 3, 1)
    g_wposq = side_by_side(early_left, early_right, 4, 1)
    g_table = side_by_side(early_left, early_right, 5, 1)[:table_rows]
    g = [vector_sum[i * rows : (i + 1) * rows] for i in range(9)]
    g_up_bias = vector_sum[256 : 256 + units]
    return (
        hidden_out, in_grad, g_wqkv, g[0], g[1], g_table, g_wposk, g_wposq, g[2], g_wout, g[3], g[4], g[5],
        g_wup, g_up_bias, g_wdown, g[6], g[7], g[8],
    )


def row_split(
    hidden_in,
    prefix,
    w_qkv,
    q_bias,
    v_bias,
    rel_table,
    w_posk,
    w_posq,
    posq_bias,
    w_out,
    out_bias,
    norm1_gain,
    norm1_bias,
    w_up,
    up_bias,
    w_down,
    down_bias,
    norm2_gain,
    norm2_bias,
    out_grad,
):
    gathered = (
        lax.all_gather(w_qkv, ("dp", "seq"), axis=0, tiled=True),
        lax.all_gather(q_bias, ("dp", "seq"), axis=0, tiled=True),
        lax.all_gather(v_bias, ("dp", "seq"), axis=0, tiled=True),
        lax.all_gather(rel_table, ("dp", "seq"), axis=0, tiled=True),
        lax.all_gather(w_posk, ("dp", "seq"), axis=0, tiled=True),
        lax.all_gather(w_posq, ("dp", "seq"), axis=0, tiled=True),
        lax.all_gather(posq_bias, ("dp", "seq"), axis=0, tiled=True),
        lax.all_gather(w_out, ("dp", "seq"), axis=0, tiled=True),
        lax.all_gather(out_bias, ("dp", "seq"), axis=0, tiled=True),
        lax.all_gather(norm1_gain, ("dp", "seq"), axis=0, tiled=True),
        lax.all_gather(norm1_bias, ("dp", "seq"), axis=0, tiled=True),
        lax.all_gather(w_up, ("dp", "seq"), axis=0, tiled=True),
        lax.all_gather(up_bias, ("dp", "seq"), axis=0, tiled=True),
        lax.all_gather(w_down, ("dp", "seq"), axis=0, tiled=True),
        lax.all_gather(down_bias, ("dp", "seq"), axis=0, tiled=True),
        lax.all_gather(norm2_gain, ("dp", "seq"), axis=0, tiled=True),
        lax.all_gather(norm2_bias, ("dp", "seq"), axis=0, tiled=True),
    )
    (
        full_qkv,
        full_qb,
        full_vb,
        full_table,
        full_posk,
        full_posq,
        full_pqb,
        full_out,
        full_ob,
        full_g1,
        full_b1,
        full_up,
        full_ub,
        full_down,
        full_db,
        full_g2,
        full_b2,
    ) = gathered
    row_count = hidden_in.shape[0]
    groups = lax.axis_size("seq")
    seq_length = row_count * groups
    seq_rank = lax.axis_index("seq")
    prefix_len = prefix[0]
    score_scale = 1.0 / math.sqrt(3 * HEAD_DIM)
    buckets = 2 * SPAN
    window = row_count + buckets
    first_row = seq_rank * row_count
    query_pos = first_row + jnp.arange(row_count, dtype=jnp.int32)
    key_pos = jnp.arange(seq_length, dtype=jnp.int32)
    visible = (key_pos[None, :] < prefix_len) | (key_pos[None, :] <= query_pos[:, None])
    padded_cols = jnp.arange(seq_length + buckets, dtype=jnp.int32)
    below_window = padded_cols[None, :] < first_row

    def skew_table(table, row_total, offset, col_total):
        shifted = jnp.pad(
            jnp.flip(table, axis=1), ((0, 0), (row_count, row_count - 1)), mode="edge"
        )
        stride = shifted.shape[1] - 1
        flattened = shifted.reshape(-1)
        picked = lax.slice_in_dim(flattened, offset, offset + row_total * stride)
        return picked.reshape(row_total, stride)[:, :col_total]

    def pos_terms(table_a, table_w, edge_terms):
        band_terms = (
            skew_table(table_a, row_count, row_count - 1, window)
            + skew_table(table_w, window, window - 1, row_count).T
        )
        low_side = table_a[:, buckets - 1 : buckets] + jnp.pad(edge_terms[0], (SPAN, SPAN))[None, :]
        high_side = table_a[:, 0:1] + jnp.pad(edge_terms[1], (SPAN, SPAN))[None, :]
        backdrop = jnp.where(below_window, low_side, high_side)
        placed = lax.dynamic_update_slice(
            backdrop, band_terms, (jnp.zeros((), jnp.int32), first_row)
        )
        return placed[:, SPAN : SPAN + seq_length]

    pos_keys = product(full_table, full_posk).astype(jnp.bfloat16)
    pos_queries = (product(full_table, full_posq) + full_pqb.astype(jnp.float32)).astype(
        jnp.bfloat16
    )
    merged = product(hidden_in, full_qkv)
    queries = (merged[:, :D] + full_qb.astype(jnp.float32)).astype(jnp.bfloat16)
    keys_local = merged[:, D : 2 * D].astype(jnp.bfloat16)
    values_local = (merged[:, 2 * D :] + full_vb.astype(jnp.float32)).astype(jnp.bfloat16)
    keys_all, values_all = (
        lax.all_gather(keys_local, "seq", axis=0, tiled=True),
        lax.all_gather(values_local, "seq", axis=0, tiled=True),
    )
    query_heads = split_heads(queries)
    key_heads = split_heads(keys_all)
    value_heads = split_heads(values_all)
    posk_heads = split_heads(pos_keys)
    posq_heads = split_heads(pos_queries)

    def head_scores(query_h, key_h, posk_h, posq_h):
        content = inner_last(query_h, key_h)
        table_a = inner_last(query_h, posk_h)
        key_padded = jnp.pad(key_h, ((SPAN, SPAN), (0, 0)))
        key_window = lax.dynamic_slice_in_dim(key_padded, first_row, window, 0)
        table_w = inner_last(key_window, posq_h)
        end_rows = jnp.stack([posq_h[0], posq_h[buckets - 1]])
        edge_terms = inner_last(end_rows, key_h)
        raw = content + pos_terms(table_a, table_w, edge_terms)
        masked = jnp.where(visible, raw * score_scale, -jnp.inf)
        return (masked, table_a, table_w, edge_terms, key_window, end_rows)

    def head_forward(operands):
        query_h, key_h, value_h, posk_h, posq_h = operands
        scores = head_scores(query_h, key_h, posk_h, posq_h)[0]
        highest = jnp.max(scores, axis=1, keepdims=True)
        expo = jnp.exp(scores - highest)
        totals = jnp.sum(expo, axis=1, keepdims=True)
        probs_low = (expo / totals).astype(jnp.bfloat16)
        return (product(probs_low, value_h), (highest + jnp.log(totals))[:, 0])

    contexts, log_totals = lax.map(
        head_forward, (query_heads, key_heads, value_heads, posk_heads, posq_heads)
    )
    context = join_heads(contexts).astype(jnp.bfloat16)
    hidden_f = hidden_in.astype(jnp.float32)
    residual1 = hidden_f + product(context, full_out) + full_ob.astype(jnp.float32)
    gain1 = full_g1.astype(jnp.float32)
    shift1 = full_b1.astype(jnp.float32)
    normed = normalize(residual1, gain1, shift1)
    normed_low = normed.astype(jnp.bfloat16)
    expanded = product(normed_low, full_up) + full_ub.astype(jnp.float32)
    activated = gelu_exact(expanded).astype(jnp.bfloat16)
    residual2 = normed + product(activated, full_down) + full_db.astype(jnp.float32)
    gain2 = full_g2.astype(jnp.float32)
    shift2 = full_b2.astype(jnp.float32)
    hidden_out = normalize(residual2, gain2, shift2).astype(jnp.bfloat16)
    regathered = (
        lax.all_gather(w_qkv, ("dp", "seq"), axis=0, tiled=True),
        lax.all_gather(q_bias, ("dp", "seq"), axis=0, tiled=True),
        lax.all_gather(v_bias, ("dp", "seq"), axis=0, tiled=True),
        lax.all_gather(rel_table, ("dp", "seq"), axis=0, tiled=True),
        lax.all_gather(w_posk, ("dp", "seq"), axis=0, tiled=True),
        lax.all_gather(w_posq, ("dp", "seq"), axis=0, tiled=True),
        lax.all_gather(posq_bias, ("dp", "seq"), axis=0, tiled=True),
        lax.all_gather(w_out, ("dp", "seq"), axis=0, tiled=True),
        lax.all_gather(out_bias, ("dp", "seq"), axis=0, tiled=True),
        lax.all_gather(norm1_gain, ("dp", "seq"), axis=0, tiled=True),
        lax.all_gather(norm1_bias, ("dp", "seq"), axis=0, tiled=True),
        lax.all_gather(w_up, ("dp", "seq"), axis=0, tiled=True),
        lax.all_gather(up_bias, ("dp", "seq"), axis=0, tiled=True),
        lax.all_gather(w_down, ("dp", "seq"), axis=0, tiled=True),
        lax.all_gather(down_bias, ("dp", "seq"), axis=0, tiled=True),
        lax.all_gather(norm2_gain, ("dp", "seq"), axis=0, tiled=True),
        lax.all_gather(norm2_bias, ("dp", "seq"), axis=0, tiled=True),
    )
    (
        back_qkv,
        back_qb,
        back_vb,
        back_table,
        back_posk,
        back_posq,
        back_pqb,
        back_out,
        back_ob,
        back_g1,
        back_b1,
        back_up,
        back_ub,
        back_down,
        back_db,
        back_g2,
        back_b2,
    ) = regathered
    _, pull_second = jax.vjp(normalize, residual2, gain2, shift2)
    d_res2, d_gain2, d_shift2 = pull_second(out_grad.astype(jnp.float32))
    d_reduced = d_res2.astype(jnp.bfloat16)
    d_wdown = inner_first(activated, d_reduced)
    d_down_bias = column_sums(d_reduced)
    d_activated = inner_last(d_reduced, back_down)
    _, pull_gelu = jax.vjp(gelu_exact, expanded)
    d_expanded = pull_gelu(d_activated)[0].astype(jnp.bfloat16)
    d_wup = inner_first(normed_low, d_expanded)
    d_up_bias = column_sums(d_expanded)
    d_normed = inner_last(d_expanded, back_up) + d_res2
    _, pull_first = jax.vjp(normalize, residual1, gain1, shift1)
    d_res1, d_gain1, d_shift1 = pull_first(d_normed)
    d_attended = d_res1.astype(jnp.bfloat16)
    d_wout = inner_first(context, d_attended)
    d_out_bias = column_sums(d_attended)
    d_context = inner_last(d_attended, back_out).astype(jnp.bfloat16)
    dctx_heads = split_heads(d_context)

    def head_backward(operands):
        query_h, key_h, value_h, posk_h, posq_h, log_total, dctx_h = operands
        scores, table_a, table_w, edge_terms, key_window, end_rows = head_scores(
            query_h, key_h, posk_h, posq_h
        )
        probs = jnp.exp(scores - log_total[:, None])
        probs_low = probs.astype(jnp.bfloat16)
        d_probs = inner_last(dctx_h, value_h)
        d_value = inner_first(probs_low, dctx_h)
        row_dot = jnp.sum(probs * d_probs, axis=1, keepdims=True)
        d_raw = (probs * (d_probs - row_dot) * score_scale).astype(jnp.bfloat16)
        _, pull_terms = jax.vjp(pos_terms, table_a, table_w, edge_terms)
        d_table_a, d_table_w, d_edges = pull_terms(d_raw.astype(jnp.float32))
        d_table_a = d_table_a.astype(jnp.bfloat16)
        d_table_w = d_table_w.astype(jnp.bfloat16)
        d_edges = d_edges.astype(jnp.bfloat16)
        d_query = product(d_raw, key_h) + product(d_table_a, posk_h)
        window_grad = product(d_table_w, posq_h)
        key_canvas = jnp.zeros((seq_length + buckets, HEAD_DIM), jnp.float32)
        placed_grad = lax.dynamic_update_slice(
            key_canvas, window_grad, (first_row, jnp.zeros((), jnp.int32))
        )
        d_key = (
            inner_first(d_raw, query_h)
            + placed_grad[SPAN : SPAN + seq_length]
            + inner_first(d_edges, end_rows)
        )
        d_posk = inner_first(d_table_a, query_h)
        end_grads = product(d_edges, key_h)
        d_posq = inner_first(d_table_w, key_window)
        d_posq = d_posq.at[0].add(end_grads[0]).at[buckets - 1].add(end_grads[1])
        return (d_query, d_key, d_value, d_posk, d_posq)

    d_q_heads, d_k_heads, d_v_heads, d_posk_heads, d_posq_heads = lax.map(
        head_backward,
        (query_heads, key_heads, value_heads, posk_heads, posq_heads, log_totals, dctx_heads),
    )
    d_queries = join_heads(d_q_heads).astype(jnp.bfloat16)
    d_keys_part, d_values_part = (
        lax.psum_scatter(
            join_heads(d_k_heads).astype(jnp.bfloat16), "seq", scatter_dimension=0, tiled=True
        ).astype(jnp.float32),
        lax.psum_scatter(
            join_heads(d_v_heads).astype(jnp.bfloat16), "seq", scatter_dimension=0, tiled=True
        ).astype(jnp.float32),
    )
    d_keys = d_keys_part.astype(jnp.bfloat16)
    d_values = d_values_part.astype(jnp.bfloat16)
    d_merged = jnp.concatenate([d_queries, d_keys, d_values], axis=1)
    d_wqkv = inner_first(hidden_in, d_merged)
    d_q_bias = column_sums(d_queries)
    d_v_bias = column_sums(d_values)
    in_grad = d_res1 + inner_last(d_merged, back_qkv)
    d_posk_rows, d_posq_rows = (
        lax.psum_scatter(join_heads(d_posk_heads), ("dp", "seq"), scatter_dimension=0, tiled=True),
        lax.psum_scatter(join_heads(d_posq_heads), ("dp", "seq"), scatter_dimension=0, tiled=True),
    )
    d_posk_low = d_posk_rows.astype(jnp.bfloat16)
    d_posq_low = d_posq_rows.astype(jnp.bfloat16)
    rel_table_grad = inner_last(d_posk_low, back_posk) + inner_last(d_posq_low, back_posq)
    d_wposk = inner_first(rel_table, d_posk_low)
    d_wposq = inner_first(rel_table, d_posq_low)
    d_posq_bias = column_sums(d_posq_low)
    summed = (
        lax.psum_scatter(d_wqkv, ("dp", "seq"), scatter_dimension=0, tiled=True),
        lax.psum_scatter(d_q_bias, ("dp", "seq"), scatter_dimension=0, tiled=True),
        lax.psum_scatter(d_v_bias, ("dp", "seq"), scatter_dimension=0, tiled=True),
        lax.psum_scatter(d_wposk, ("dp", "seq"), scatter_dimension=0, tiled=True),
        lax.psum_scatter(d_wposq, ("dp", "seq"), scatter_dimension=0, tiled=True),
        lax.psum_scatter(d_posq_bias, ("dp", "seq"), scatter_dimension=0, tiled=True),
        lax.psum_scatter(d_wout, ("dp", "seq"), scatter_dimension=0, tiled=True),
        lax.psum_scatter(d_out_bias, ("dp", "seq"), scatter_dimension=0, tiled=True),
        lax.psum_scatter(d_gain1, ("dp", "seq"), scatter_dimension=0, tiled=True),
        lax.psum_scatter(d_shift1, ("dp", "seq"), scatter_dimension=0, tiled=True),
        lax.psum_scatter(d_wup, ("dp", "seq"), scatter_dimension=0, tiled=True),
        lax.psum_scatter(d_up_bias, ("dp", "seq"), scatter_dimension=0, tiled=True),
        lax.psum_scatter(d_wdown, ("dp", "seq"), scatter_dimension=0, tiled=True),
        lax.psum_scatter(d_down_bias, ("dp", "seq"), scatter_dimension=0, tiled=True),
        lax.psum_scatter(d_gain2, ("dp", "seq"), scatter_dimension=0, tiled=True),
        lax.psum_scatter(d_shift2, ("dp", "seq"), scatter_dimension=0, tiled=True),
    )
    return (
        hidden_out,
        in_grad,
        summed[0],
        summed[1],
        summed[2],
        rel_table_grad,
        summed[3],
        summed[4],
        summed[5],
        summed[6],
        summed[7],
        summed[8],
        summed[9],
        summed[10],
        summed[11],
        summed[12],
        summed[13],
        summed[14],
        summed[15],
    )


def solution(mesh):
    placed = (
        P(("dp", "seq"), None),
        P("dp"),
        P(("dp", "seq"), None),
        P(("dp", "seq")),
        P(("dp", "seq")),
        P(("dp", "seq"), None),
        P(("dp", "seq"), None),
        P(("dp", "seq"), None),
        P(("dp", "seq")),
        P(("dp", "seq"), None),
        P(("dp", "seq")),
        P(("dp", "seq")),
        P(("dp", "seq")),
        P(("dp", "seq"), None),
        P(("dp", "seq")),
        P(("dp", "seq"), None),
        P(("dp", "seq")),
        P(("dp", "seq")),
        P(("dp", "seq")),
        P(("dp", "seq"), None),
    )
    return jax.shard_map(
        head_split if dict(mesh.shape) == {"dp": 16, "seq": 2} else row_split,
        mesh=mesh,
        in_specs=placed,
        out_specs=(
            P(("dp", "seq"), None),
            P(("dp", "seq"), None),
            P(("dp", "seq"), None),
            P(("dp", "seq")),
            P(("dp", "seq")),
            P(("dp", "seq"), None),
            P(("dp", "seq"), None),
            P(("dp", "seq"), None),
            P(("dp", "seq")),
            P(("dp", "seq"), None),
            P(("dp", "seq")),
            P(("dp", "seq")),
            P(("dp", "seq")),
            P(("dp", "seq"), None),
            P(("dp", "seq")),
            P(("dp", "seq"), None),
            P(("dp", "seq")),
            P(("dp", "seq")),
            P(("dp", "seq")),
        ),
        check_vma=False,
    )
```

```python
import functools
import math

import jax
import jax.numpy as jnp
from jax import lax
from jax.experimental import pallas as pl
from jax.experimental.pallas import tpu as pltpu
from jax.sharding import PartitionSpec as P

D = 768
HEADS = 12
HEAD_DIM = 64
SPAN = 256
TILE = 128
BLOCK = 256
BAND = 768
PAIR = 2 * HEAD_DIM


eps_norm = 1e-07


def normalize(value, gain, shift):
    average = jnp.mean(value, axis=-1, keepdims=True)
    centred = value - average
    variance = jnp.mean(centred * centred, axis=-1, keepdims=True)
    return centred * lax.rsqrt(variance + eps_norm) * gain + shift


def gelu_exact(value):
    return jax.nn.gelu(value, approximate=False)


def product(left, right):
    return jnp.dot(left, right, preferred_element_type=jnp.float32)


def inner_first(left, right):
    return lax.dot_general(
        left, right, (((0,), (0,)), ((), ())), preferred_element_type=jnp.float32
    )


def inner_last(left, right):
    return lax.dot_general(
        left, right, (((1,), (1,)), ((), ())), preferred_element_type=jnp.float32
    )


def split_heads(matrix):
    return matrix.reshape(matrix.shape[0], HEADS, HEAD_DIM).transpose(1, 0, 2)


def join_heads(stacked):
    return stacked.transpose(1, 0, 2).reshape(stacked.shape[1], D)


def column_sums(matrix):
    return jnp.sum(matrix.astype(jnp.float32), axis=0)


def nn(left, right):
    return lax.dot_general(
        left, right, (((1,), (0,)), ((), ())), preferred_element_type=jnp.float32
    )


def nt(left, right):
    return lax.dot_general(
        left, right, (((1,), (1,)), ((), ())), preferred_element_type=jnp.float32
    )


def unit_matrix(size, reverse=False):
    rows = lax.broadcasted_iota(jnp.int32, (size, size), 0)
    cols = lax.broadcasted_iota(jnp.int32, (size, size), 1)
    if reverse:
        cols = size - 1 - cols
    return jnp.where(rows == cols, 1.0, 0.0).astype(jnp.bfloat16)


def turn_matrix():
    rows = lax.broadcasted_iota(jnp.int32, (BLOCK, BLOCK), 0)
    cols = lax.broadcasted_iota(jnp.int32, (BLOCK, BLOCK), 1)
    mirrored = rows // TILE * (2 * TILE) + TILE - 1 - rows
    return jnp.where(mirrored == cols, 1.0, 0.0).astype(jnp.bfloat16)


def head_lanes(head):
    lanes = lax.broadcasted_iota(jnp.int32, (1, PAIR), 1)
    return lanes // HEAD_DIM == head


def head_rows(head):
    rows = lax.broadcasted_iota(jnp.int32, (HEAD_DIM, PAIR), 0)
    cols = lax.broadcasted_iota(jnp.int32, (HEAD_DIM, PAIR), 1)
    return jnp.where(cols == rows + head * HEAD_DIM, 1.0, 0.0).astype(jnp.bfloat16)


def key_tiles(block, length):
    return max(length // 2, (block + 1) * BLOCK) // TILE


def tile_seen(query_tile, key_tile, length):
    return key_tile < key_tiles(query_tile * TILE // BLOCK, length)


def skewed(window):
    return pltpu.roll(window, 0, 1, stride=1, stride_axis=0)


def forward_body(head, prefix_ref, q_ref, k_ref, v_ref, pk_ref, pq_ref, *refs):
    ctx_ref, p_ref, wb_ref, far_ref, s_ref = refs[-5:]
    length = q_ref.shape[0]
    mine = head_lanes(head)
    prefix = prefix_ref[0]
    eye = unit_matrix(TILE)
    eye_block = unit_matrix(BLOCK)
    zero = jnp.zeros((), jnp.bfloat16)
    scale = math.log2(math.e) / math.sqrt(3 * HEAD_DIM)
    for tile in range(length // TILE):
        rows = slice(tile * TILE, (tile + 1) * TILE)
        table = nt(jnp.where(mine, k_ref[rows, :], zero), pq_ref[...])
        wb_ref[rows, :] = skewed(table)
        wb_ref[rows, 0:TILE] = table[:, BAND - TILE :]
        far_ref[rows, :] = table[:, 0:TILE]
    v_cols = nt(jnp.where(lax.broadcasted_iota(jnp.int32, (PAIR, PAIR), 0) // HEAD_DIM == head, unit_matrix(PAIR), zero), v_ref[...]).astype(jnp.bfloat16)
    for block in range(length // BLOCK):
        cols = slice(block * BLOCK, (block + 1) * BLOCK)
        q_own = jnp.where(mine, q_ref[cols, :], zero)
        skews, highs, lows = [], [], []
        for sub in range(2):
            table = nt(q_own[sub * TILE : (sub + 1) * TILE], pk_ref[...])
            skews.append(skewed(table).astype(jnp.bfloat16))
            highs.append(table[:, 0:TILE].astype(jnp.bfloat16))
            lows.append(table[:, BAND - TILE :].astype(jnp.bfloat16))
        count = key_tiles(block, length)
        highest = None
        for tile in range(count):
            rows = slice(tile * TILE, (tile + 1) * TILE)
            parts_a, parts_b = [], []
            for sub in range(2):
                step = 2 * block + sub - tile
                if step >= 3:
                    parts_a.append(highs[sub])
                    parts_b.append(wb_ref[rows, 0:TILE])
                elif step <= -3:
                    parts_a.append(lows[sub])
                    parts_b.append(far_ref[rows, :])
                else:
                    at = 384 - TILE * step
                    parts_a.append(skews[sub][:, at : at + TILE])
                    at = 384 + TILE * step
                    parts_b.append(wb_ref[rows, at : at + TILE])
            right = jnp.concatenate([jnp.concatenate(parts_a, axis=0), q_own], axis=1)
            left = jnp.concatenate([eye, k_ref[rows, :]], axis=1)
            raw = nt(left, right) + jnp.concatenate(parts_b, axis=1)
            if (tile + 1) * TILE > block * BLOCK + 1:
                keys = tile * TILE + lax.broadcasted_iota(jnp.int32, (TILE, BLOCK), 0)
                queries = block * BLOCK + lax.broadcasted_iota(jnp.int32, (TILE, BLOCK), 1)
                raw = jnp.where((keys < prefix) | (keys <= queries), raw, -jnp.inf)
            s_ref[rows, :] = raw
            top = jnp.max(raw, axis=0, keepdims=True)
            highest = top if highest is None else jnp.maximum(highest, top)
        total = jnp.zeros((1, BLOCK), jnp.float32)
        for tile in range(count):
            rows = slice(tile * TILE, (tile + 1) * TILE)
            expo = jnp.exp2((s_ref[rows, :] - highest) * scale)
            s_ref[rows, :] = expo
            total = total + jnp.sum(expo, axis=0, keepdims=True)
        inverse = 1.0 / total
        for tile in range(count):
            rows = slice(tile * TILE, (tile + 1) * TILE)
            p_ref[rows, cols] = (s_ref[rows, :] * inverse).astype(jnp.bfloat16)
        seen = count * TILE
        ctx_cols = nn(v_cols[:, :seen], p_ref[0:seen, cols]).astype(jnp.bfloat16)
        ctx = nt(eye_block, ctx_cols).astype(jnp.bfloat16)

        ctx_ref[cols, :] = ctx if head == 0 else refs[0][cols, :] + ctx


def attention_forward(prefix, merged, pos_band, pair, head, found=()):
    length, width = merged.shape[0], merged.shape[1] // 3
    pairs = width // PAIR
    tall = [pl.BlockSpec((length, PAIR), lambda p, at=at: (0, at)) for at in (pair, pairs + pair, 2 * pairs + pair)]
    band = [pl.BlockSpec((BAND, PAIR), lambda p, at=at: (0, at)) for at in (pair, pairs + pair)]
    own = pl.BlockSpec((length, PAIR), lambda p: (0, 0))
    return pl.pallas_call(
        functools.partial(forward_body, head),
        grid=(1,),
        in_specs=[pl.BlockSpec(memory_space=pltpu.SMEM)] + tall + band + [own] * len(found),
        out_specs=[own, pl.BlockSpec((length, length), lambda p: (0, 0))],
        out_shape=[
            jax.ShapeDtypeStruct((length, PAIR), jnp.bfloat16),
            jax.ShapeDtypeStruct((length, length), jnp.bfloat16),
        ],
        scratch_shapes=[
            pltpu.VMEM((length, BAND), jnp.float32),
            pltpu.VMEM((length, TILE), jnp.float32),
            pltpu.VMEM((length, BLOCK), jnp.float32),
        ],
        compiler_params=pltpu.CompilerParams(dimension_semantics=("arbitrary",), vmem_limit_bytes=24 << 20),
        cost_estimate=pl.CostEstimate(flops=10**9, transcendentals=length * length, bytes_accessed=3 << 20),
        name="attention_forward",
    )(prefix, merged, merged, merged, pos_band, pos_band, *found)


def backward_body(head, q_ref, k_ref, v_ref, dctx_ref, p_ref, pk_ref, pq_ref, *refs):
    dq_ref, dk_ref, dv_ref, dpk_ref, dpq_ref, dr_ref, dk_acc, dv_acc = refs[-8:]
    outs = (dq_ref, dk_ref, dv_ref)
    length = q_ref.shape[0]
    mine = head_lanes(head)
    flip = turn_matrix()
    pick = head_rows(head)
    bf = jnp.bfloat16
    zero = jnp.zeros((), bf)
    scale = 1.0 / math.sqrt(3 * HEAD_DIM)
    back = BAND - (TILE - 1)
    blank = jnp.zeros((TILE, TILE), bf)
    dk_acc[...] = jnp.zeros_like(dk_acc)
    dv_acc[...] = jnp.zeros_like(dv_acc)
    dpk = jnp.zeros((HEAD_DIM, BAND), jnp.float32)
    dpq = jnp.zeros((HEAD_DIM, BAND), jnp.float32)
    tiles = length // TILE

    def put(index, rows, value):
        earlier = jnp.zeros((), bf) if head == 0 else refs[index][rows, :]
        outs[index][rows, :] = jnp.where(mine, value.astype(bf), earlier)

    def unskew(parts):
        return pltpu.roll(jnp.concatenate(parts, axis=1), back, 1, stride=1, stride_axis=0)

    for block in range(length // BLOCK):
        cols = slice(block * BLOCK, (block + 1) * BLOCK)
        count = key_tiles(block, length)
        seen = count * TILE
        dctx = dctx_ref[cols, :]
        v_own = jnp.where(mine, v_ref[0:seen, :], zero)
        probs_low = p_ref[0:seen, cols]
        probs = probs_low.astype(jnp.float32)
        d_probs = nt(v_own, dctx)
        row_dot = jnp.sum(probs * d_probs, axis=0, keepdims=True)
        dr_ref[0:seen, cols] = (probs * ((d_probs - row_dot) * scale)).astype(bf)
        d_raw = dr_ref[0:seen, cols]
        dv_acc[0:seen, :] += nn(probs_low, dctx)
        dk_acc[0:seen, :] += nn(d_raw, q_ref[cols, :])
        turned = nt(flip, d_raw).astype(bf)
        spreads = []
        for sub in range(2):
            tile = 2 * block + sub
            own = turned[sub * TILE : (sub + 1) * TILE]

            def piece(key_tile):
                return own[:, key_tile * TILE : (key_tile + 1) * TILE]

            near = [t for t in range(count) if tile - t >= 3]
            far = [t for t in range(count) if tile - t <= -3]
            band = [blank]
            for step in (2, 1, 0, -1, -2):
                key_tile = tile - step
                band.append(piece(key_tile) if 0 <= key_tile < count else blank)
            spreads.append(
                add_edges(unskew(band), [piece(t).astype(jnp.float32) for t in near], [piece(t).astype(jnp.float32) for t in far])
            )
        spread = jnp.concatenate(spreads, axis=0)
        dq = nn(turned, k_ref[0:seen, :]) + nn(spread, pk_ref[...])
        put(0, cols, nn(flip, dq.astype(bf)))
        q_cols = nt(pick, nn(flip, q_ref[cols, :]).astype(bf)).astype(bf)
        dpk = dpk + nn(q_cols, spread)
    dpk_ref[...] = dpk
    for block in range(length // BLOCK):
        rows = slice(block * BLOCK, (block + 1) * BLOCK)
        groups, edges = [], []
        for sub in range(2):
            key_tile = 2 * block + sub
            own = slice(key_tile * TILE, (key_tile + 1) * TILE)
            seen_by = [t for t in range(tiles) if tile_seen(t, key_tile, length)]

            def held(query_tile):
                return dr_ref[own, query_tile * TILE : (query_tile + 1) * TILE]

            band = [blank]
            for step in (-2, -1, 0, 1, 2):
                query_tile = key_tile + step
                band.append(held(query_tile) if query_tile in seen_by else blank)
            ends = []
            for chosen in ([t for t in seen_by if t - key_tile <= -3], [t for t in seen_by if t - key_tile >= 3]):
                total = blank
                if chosen:
                    total = sum((held(t).astype(jnp.float32) for t in chosen[1:]), held(chosen[0]).astype(jnp.float32)).astype(bf)
                ends.append(total)
            groups.append(jnp.concatenate(band[1:] + ends, axis=1))
        turned = nn(flip, jnp.concatenate(groups, axis=0))
        width = BAND - TILE
        spreads = []
        for sub in range(2):
            own = turned[sub * TILE : (sub + 1) * TILE]
            spreads.append(
                add_edges(unskew([blank, own[:, :width].astype(bf)]), [own[:, width : width + TILE]], [own[:, width + TILE :]])
            )
        spread = jnp.concatenate(spreads, axis=0)
        d_key = nn(flip, nn(spread, pq_ref[...]).astype(bf))
        put(1, rows, dk_acc[rows, :] + d_key)
        k_cols = nt(pick, nn(flip, k_ref[rows, :]).astype(bf)).astype(bf)
        dpq = dpq + nn(k_cols, spread)
        put(2, rows, dv_acc[rows, :])
    dpq_ref[...] = dpq


def add_edges(spread, first, last):
    parts = [spread[:, 0:TILE], spread[:, TILE : BAND - TILE], spread[:, BAND - TILE :]]
    for place, tiles in ((0, first), (2, last)):
        if tiles:
            total = parts[place].astype(jnp.float32)
            for tile in tiles:
                total = total + tile
            parts[place] = total.astype(jnp.bfloat16)
    return jnp.concatenate(parts, axis=1)


def attention_backward(merged, dctx, probs, pos_band, pair, head, found=()):
    length, width = merged.shape[0], merged.shape[1] // 3
    pairs = width // PAIR
    tall = [pl.BlockSpec((length, PAIR), lambda p, at=at: (0, at)) for at in (pair, pairs + pair, 2 * pairs + pair, pair)]
    band = [pl.BlockSpec((BAND, PAIR), lambda p, at=at: (0, at)) for at in (pair, pairs + pair)]
    own = pl.BlockSpec((length, PAIR), lambda p: (0, 0))
    table = pl.BlockSpec((HEAD_DIM, BAND), lambda p: (0, 0))
    flat = jax.ShapeDtypeStruct((length, PAIR), jnp.bfloat16)
    wide = jax.ShapeDtypeStruct((HEAD_DIM, BAND), jnp.float32)
    return pl.pallas_call(
        functools.partial(backward_body, head),
        grid=(1,),
        in_specs=tall + [pl.BlockSpec((length, length), lambda p: (0, 0))] + band + [own] * len(found),
        out_specs=[own, own, own, table, table],
        out_shape=[flat, flat, flat, wide, wide],
        scratch_shapes=[
            pltpu.VMEM((length, length), jnp.bfloat16),
            pltpu.VMEM((length, PAIR), jnp.float32),
            pltpu.VMEM((length, PAIR), jnp.float32),
        ],
        compiler_params=pltpu.CompilerParams(dimension_semantics=("arbitrary",), vmem_limit_bytes=24 << 20),
        cost_estimate=pl.CostEstimate(flops=2 * 10**9, transcendentals=0, bytes_accessed=4 << 20),
        name="attention_backward",
    )(merged, merged, merged, dctx, probs, pos_band, pos_band, *found)


CORES = [(0, 1), (1, 0)]


def swap(value):
    return lax.ppermute(value, "seq", CORES)


def ordered(core, own, other, axis=0):
    return jnp.concatenate(
        [jnp.where(core == 0, own, other), jnp.where(core == 0, other, own)], axis=axis
    )


def half_of(core, matrix, axis):
    size = matrix.shape[axis] // 2
    return lax.dynamic_slice_in_dim(matrix, core * size, size, axis)


def chip_bits():
    chip = lax.axis_index("dp")
    return chip // 4, (chip // 2) % 2, chip % 2


def exchange(value, mask):
    return lax.ppermute(value, "dp", [(i, i ^ mask) for i in range(16)])


def tie(chains, others=()):
    states, others = lax.optimization_barrier(([chain.state for chain in chains], others))
    for chain, state in zip(chains, states):
        chain.state = state
    return others


class Gather:
    def __init__(self, *values):
        self.state = values

    def line(self, step):
        up = [(i, i + 4) for i in range(12) if i // 4 >= step - 1]
        down = [(i + 4, i) for i in range(12) if i // 4 <= 3 - step]
        if step == 1:
            self.state = [([value], [value]) for value in self.state]
        self.state = [
            (below + [lax.ppermute(below[-1], "dp", up)], above + [lax.ppermute(above[-1], "dp", down)])
            for below, above in self.state
        ]
        if step == 3:
            z = chip_bits()[0]
            lines = []
            for below, above in self.state:
                blocks = []
                for block in range(4):
                    options = [below[k - block] if k >= block else above[block - k] for k in range(4)]
                    blocks.append(lax.select_n(z, *options))
                lines.append(tuple(jnp.stack([b[side] for b in blocks]) for side in range(2)))
            self.state = lines

    def double(self, step):
        z = chip_bits()[0]
        bit = z % 2 if step == 1 else z // 2
        result = []
        for value in self.state:
            other = exchange(value, 4 * step)
            result.append(jnp.stack([jnp.where(bit == 0, value, other), jnp.where(bit == 0, other, value)]))
        self.state = result
        if step == 2:
            self.state = [
                tuple(value[:, :, side].reshape((4,) + value.shape[3:]) for side in range(2)) for value in result
            ]

    def pair(self, step):
        _, y, x = chip_bits()
        order = ((x, 1), (y, 2)) if step == 1 else ((y, 2), (x, 1))
        lines = []
        for halves in self.state:
            result = []
            for value, (bit, mask) in zip(halves, order):
                other = exchange(value, mask)
                result.append(jnp.stack([jnp.where(bit == 0, value, other), jnp.where(bit == 0, other, value)]))
            lines.append(tuple(result))
        self.state = lines

    def rows(self, index, low, high):
        first, second = [half[..., low:high] for half in self.state[index]]
        first = jnp.moveaxis(first, (0, 1, 2), (1, 2, 0))
        second = jnp.moveaxis(second, (0, 1, 2), (2, 1, 0))
        whole = jnp.stack([first, second], axis=3)
        return whole.reshape(-1, whole.shape[-1])


class Scatter:
    def __init__(self, *values):
        self.state = []
        for value in values:
            grid = value.reshape((4, 2, 2) + value.shape[1:])
            self.state.append((jnp.moveaxis(grid[:, :, :, 0], 2, 0), jnp.moveaxis(grid[:, :, :, 1], 1, 0)))

    def pair(self, step):
        _, y, x = chip_bits()
        order = ((x, 1), (y, 2)) if step == 1 else ((y, 2), (x, 1))
        sums = []
        for halves in self.state:
            result = []
            for value, (bit, mask) in zip(halves, order):
                keep = jnp.where(bit == 0, value[0], value[1])
                give = jnp.where(bit == 0, value[1], value[0])
                total = (keep.astype(jnp.float32) + exchange(give, mask).astype(jnp.float32)).astype(value.dtype)
                result.append(jnp.moveaxis(total, 1, 0) if step == 1 else total)
            sums.append(tuple(result) if step == 1 else (jnp.stack(result, axis=1), None, None))
        self.state = sums

    def line(self, step):
        z = chip_bits()[0]
        offset = 4 - step
        ups = [(i, i + 4) for i in range(12) if i // 4 + offset <= 3]
        downs = [(i + 4, i) for i in range(12) if i // 4 + 1 - offset >= 0]
        sums, self.totals = [], []
        for value, up, down in self.state:

            def block(at):
                options = [value[min(max(k + at, 0), 3)] for k in range(4)]
                return lax.select_n(z, *options).astype(jnp.float32)

            to_above, to_below = block(offset), block(-offset)
            if up is not None:
                to_above = to_above + up.astype(jnp.float32)
                to_below = to_below + down.astype(jnp.float32)
            up = lax.ppermute(to_above.astype(value.dtype), "dp", ups)
            down = lax.ppermute(to_below.astype(value.dtype), "dp", downs)
            sums.append((value, up, down))
            if step == 3:
                self.totals.append(block(0) + up.astype(jnp.float32) + down.astype(jnp.float32))
        self.state = sums


def norm_parts(value):
    average = jnp.mean(value, axis=-1, keepdims=True)
    centred = value - average
    variance = jnp.mean(centred * centred, axis=-1, keepdims=True)
    inverse = lax.rsqrt(variance + eps_norm)
    return centred * inverse, inverse


def norm_back(unit, inverse, gain, grad):
    scaled = grad * gain
    mean_grad = jnp.mean(scaled, axis=-1, keepdims=True)
    mean_along = jnp.mean(scaled * unit, axis=-1, keepdims=True)
    return inverse * (scaled - mean_grad - unit * mean_along)


def head_split(
    hidden_in, prefix, w_qkv, q_bias, v_bias, rel_table, w_posk, w_posq, posq_bias, w_out, out_bias,
    norm1_gain, norm1_bias, w_up, up_bias, w_down, down_bias, norm2_gain, norm2_bias, out_grad,
):
    bf = jnp.bfloat16
    f32 = jnp.float32
    core = lax.axis_index("seq")
    rows = w_qkv.shape[0]
    units = w_down.shape[0]
    table_rows = rel_table.shape[0]
    chips = 16
    half = D // 2
    ff_half = chips * units
    buckets = 2 * SPAN

    last_rows = rows - table_rows
    vectors = (q_bias, v_bias, posq_bias, out_bias, norm1_gain, norm1_bias, down_bias, norm2_gain)
    left = jnp.stack(vectors)
    right = jnp.concatenate(
        [jnp.pad(norm2_bias, (0, units - rows))[None], up_bias[None], jnp.zeros((last_rows - 2, units), bf)], axis=0
    )
    small = jnp.concatenate([jnp.pad(left, ((0, 0), (0, 128 - rows))), jnp.pad(right, ((0, 0), (0, half - 128 - units)))], axis=1)

    def columns(side):
        qkv = w_qkv.reshape(rows, 3, 2, half)[:, :, side].reshape(rows, 3 * half)
        corner = jnp.concatenate([rel_table[:, side * half : (side + 1) * half], small], axis=0)
        cut = slice(side * half, (side + 1) * half)
        up = w_up.reshape(rows, chips, 2, units)[:, :, side].reshape(rows, ff_half)
        return (
            jnp.concatenate([qkv, w_posk[:, cut], w_posq[:, cut], corner], axis=1),
            jnp.concatenate([w_out[:, cut], up], axis=1),
        )

    early0, late0 = columns(0)
    early1, late1 = columns(1)
    early_got = swap(jnp.where(core == 0, early1, early0))
    late_got = swap(jnp.where(core == 0, late1, late0))
    hidden_got = swap(hidden_in)

    def by_core(first, second, got):
        own = jnp.where(core == 0, first, second)
        return jnp.stack([jnp.where(core == 0, own, got), jnp.where(core == 0, got, own)])

    early_chain = Gather(by_core(early0, early1, early_got))
    downs = jnp.concatenate([w_down.reshape(2, 2, rows, D)[:, 0], w_down.reshape(2, 2, rows, D)[:, 1]], axis=-1)
    late_chain = Gather(jnp.concatenate([by_core(late0, late1, late_got), downs], axis=-1))
    for step in (1, 2, 3):
        early_chain.line(step)
    tie((early_chain, late_chain))
    early_chain.pair(1)
    late_chain.double(1)
    tie((early_chain, late_chain))
    early_chain.pair(2)
    late_chain.double(2)
    hidden_all = ordered(core, hidden_in, hidden_got)
    w_qkv_own = early_chain.rows(0, 0, 3 * half)
    w_pos_own = early_chain.rows(0, 3 * half, 5 * half)
    corner = early_chain.rows(0, 5 * half, 6 * half).reshape(2 * chips, rows, half)
    table_half = corner[:, :table_rows].reshape(buckets, half)
    small = corner[:, table_rows:]
    table = ordered(core, table_half, swap(table_half), axis=1)

    owner = (lax.broadcasted_iota(jnp.int32, (2 * chips, D), 1) // rows == lax.broadcasted_iota(jnp.int32, (2 * chips, D), 0)).astype(bf)
    inside = lax.broadcasted_iota(jnp.int32, (rows, D), 1) % rows == lax.broadcasted_iota(jnp.int32, (rows, D), 0)
    unit_owner = (
        2 * (lax.broadcasted_iota(jnp.int32, (2 * chips, ff_half), 1) // units) + core
        == lax.broadcasted_iota(jnp.int32, (2 * chips, ff_half), 0)
    ).astype(bf)
    unit_inside = lax.broadcasted_iota(jnp.int32, (units, ff_half), 1) % units == lax.broadcasted_iota(jnp.int32, (units, ff_half), 0)
    spots = jnp.concatenate([small[:, :, :rows], small[:, :, 128 : 128 + rows]], axis=1)
    wide = lax.dot_general(spots, owner, (((0,), (0,)), ((), ())), preferred_element_type=f32)
    lists = jnp.sum(jnp.where(inside, wide, 0.0), axis=1)
    qb, vb, pqb, ob, gain1, shift1, db, gain2, shift2 = [lists[i] for i in range(9)]
    wide = inner_first(small[:, 1, 128 : 128 + units], unit_owner)
    ub = jnp.sum(jnp.where(unit_inside, wide, 0.0), axis=0)

    band = lax.broadcasted_iota(jnp.int32, (BAND, buckets), 0)
    bucket = lax.broadcasted_iota(jnp.int32, (BAND, buckets), 1)
    chosen = (jnp.clip(SPAN + 384 - band, 0, buckets - 1) == bucket).astype(bf)
    pos_shift = jnp.concatenate([jnp.zeros((half,), f32), half_of(core, pqb, 0)])
    pos = (product(table, w_pos_own) + pos_shift).astype(bf)
    pos_band = product(chosen, pos).astype(bf)

    qkv_shift = jnp.concatenate([half_of(core, qb, 0), jnp.zeros((half,), f32), half_of(core, vb, 0)])
    merged = (product(hidden_all, w_qkv_own) + qkv_shift).astype(bf)
    merged, pos_band = tie((late_chain,), (merged, pos_band))
    late_chain.pair(1)
    context_parts, prob_parts = [], []
    for pair in range(half // PAIR):
        part, kept = attention_forward(prefix, merged, pos_band, pair, 0)
        prob_parts.append(kept)
        part, kept = attention_forward(prefix, merged, pos_band, pair, 1, (part,))
        prob_parts.append(kept)
        if pair == 0:
            part, merged = tie((late_chain,), (part, merged))
            late_chain.pair(2)
        context_parts.append(part)
    context = jnp.concatenate(context_parts, axis=1)
    out_columns = late_chain.rows(0, 0, half)
    w_out_own = ordered(
        core, half_of(core, out_columns, 0), swap(half_of(1 - core, out_columns, 0)), axis=1
    )
    w_up_own = late_chain.rows(0, half, half + ff_half)
    down_at = half + ff_half
    down_parts = [late_chain.rows(0, at, at + D).reshape(2 * chips, rows, D) for at in (down_at, down_at + D)]
    w_down_own = jnp.stack(down_parts, axis=1).reshape(ff_half, D)

    def summed_rows(left, multiply):
        given = swap(multiply(half_of(1 - core, left, 0)).astype(bf))
        return multiply(half_of(core, left, 0)) + given.astype(f32)

    hidden_f = hidden_in.astype(f32)
    residual1 = hidden_f + summed_rows(context, lambda part: product(part, w_out_own)) + ob
    unit1, inverse1 = norm_parts(residual1)
    normed = unit1 * gain1 + shift1
    normed_low = normed.astype(bf)
    normed_all = ordered(core, normed_low, swap(normed_low))
    expanded = product(normed_all, w_up_own) + ub
    normal_cdf = 0.5 + 0.5 * lax.erf(expanded * math.sqrt(0.5))
    activated = (expanded * normal_cdf).astype(bf)
    slope = (
        normal_cdf + expanded * jnp.exp(-0.5 * expanded * expanded) * (1.0 / math.sqrt(2.0 * math.pi))
    ).astype(bf)
    residual2 = normed + summed_rows(activated, lambda part: product(part, w_down_own)) + db
    unit2, inverse2 = norm_parts(residual2)
    hidden_out = (unit2 * gain2 + shift2).astype(bf)

    grad = out_grad.astype(f32)
    d_res2 = norm_back(unit2, inverse2, gain2, grad)
    d_gain2 = jnp.sum(grad * unit2, axis=0, keepdims=True)
    d_shift2 = jnp.sum(grad, axis=0, keepdims=True)
    d_reduced = d_res2.astype(bf)
    d_down_bias = column_sums(d_reduced)[None]
    reduced_all = ordered(core, d_reduced, swap(d_reduced))
    d_expanded = (inner_last(reduced_all, w_down_own) * slope.astype(f32)).astype(bf)
    d_normed = summed_rows(d_expanded, lambda part: inner_last(part, w_up_own)) + d_res2
    d_wdown = inner_first(activated, reduced_all).astype(bf)
    d_wup = inner_first(normed_all, d_expanded).astype(bf)
    d_up_bias = column_sums(d_expanded)
    d_res1 = norm_back(unit1, inverse1, gain1, d_normed)
    d_gain1 = jnp.sum(d_normed * unit1, axis=0, keepdims=True)
    d_shift1 = jnp.sum(d_normed, axis=0, keepdims=True)
    d_attended = d_res1.astype(bf)
    d_out_bias = column_sums(d_attended)[None]
    attended_all = ordered(core, d_attended, swap(d_attended))
    d_context = inner_last(attended_all, w_out_own).astype(bf)
    d_wout_rows = inner_first(context, attended_all).astype(bf)
    d_wout = ordered(
        core, half_of(core, d_wout_rows, 1), swap(half_of(1 - core, d_wout_rows, 1)), axis=0
    )

    def rejoin(first, second):
        own = jnp.where(core == 0, first, second)
        got = swap(jnp.where(core == 0, second, first))
        return jnp.where(core == 0, own, got), jnp.where(core == 0, got, own)

    late_cols = jnp.concatenate([d_wout, d_wup], axis=1).reshape(chips, 2, rows, half + ff_half)
    down_cols = d_wdown.reshape(chips, 2, 2, rows, D)
    late_sums = Scatter(jnp.concatenate([late_cols, down_cols[:, :, 0], down_cols[:, :, 1]], axis=-1))
    grads = []
    late_steps = {0: lambda: late_sums.pair(1), 3: lambda: late_sums.pair(2), 5: lambda: late_sums.line(1)}
    found = ()
    for index in range(half // HEAD_DIM):
        if index in late_steps:
            found, d_context = tie((late_sums,), (found, d_context))
            late_steps[index]()
        if index % 2 == 0:
            found = ()
        found = attention_backward(merged, d_context, prob_parts[index], pos_band, index // 2, index % 2, tuple(found[:3]))
        grads.append(found)
    grads[-1] = tie((late_sums,), found)
    late_sums.line(2)
    d_merged = jnp.concatenate([g[i] for i in range(3) for g in grads[1::2]], axis=1)
    d_q, d_v = d_merged[:, :half], d_merged[:, 2 * half :]
    d_wqkv = inner_first(hidden_all, d_merged).astype(bf)
    d_q_bias = column_sums(d_q)[None]
    d_v_bias = column_sums(d_v)[None]
    d_band = jnp.concatenate([g[i] for i in (3, 4) for g in grads], axis=0).astype(bf)
    d_pos = lax.dot_general(
        chosen, d_band, (((0,), (1,)), ((), ())), preferred_element_type=f32
    )
    d_posq_bias = jnp.sum(d_pos[:, half:], axis=0, keepdims=True)
    d_pos_low = d_pos.astype(bf)
    d_wpos = inner_first(table, d_pos_low).astype(bf)
    d_table_all = inner_last(d_pos_low, w_pos_own).astype(bf)
    d_table = (
        half_of(core, d_table_all, 1).astype(f32)
        + swap(half_of(1 - core, d_table_all, 1)).astype(f32)
    ).astype(bf)

    def whole(part):
        blank = jnp.zeros_like(part)
        return ordered(core, part, blank, axis=1)

    lists_grad = jnp.concatenate(
        [whole(jnp.concatenate([d_q_bias, d_v_bias, d_posq_bias], axis=0)), d_out_bias, d_gain1, d_shift1, d_down_bias, d_gain2, d_shift2],
        axis=0,
    ).astype(bf)
    lists_grad = jnp.pad(lists_grad, ((0, 7), (0, 0)))
    pieces = jnp.where(inside, lists_grad[:, None, :], jnp.zeros((), bf)).reshape(16 * rows, D)
    unit_at = lax.broadcasted_iota(jnp.int32, (half, ff_half), 1) % units + 256 == lax.broadcasted_iota(jnp.int32, (half, ff_half), 0)
    unit_pieces = jnp.where(unit_at, d_up_bias.astype(bf), jnp.zeros((), bf))
    vector = (inner_last(owner, pieces) + inner_last(unit_owner, unit_pieces)).astype(bf)
    corner_grad = jnp.concatenate(
        [
            d_table.reshape(2 * chips, table_rows, half),
            jnp.pad(vector[:, None, :], ((0, 0), (0, last_rows - 1), (0, 0))),
        ],
        axis=1,
    ).reshape(chips * 2 * rows, half)
    early_sums = Scatter(
        jnp.concatenate([d_wqkv, d_wpos, corner_grad], axis=1).reshape(chips, 2, rows, 6 * half)
    )
    d_merged = tie((early_sums,), d_merged)
    early_sums.pair(1)
    in_grad = d_res1 + summed_rows(d_merged, lambda part: inner_last(part, w_qkv_own))
    in_grad = tie((late_sums,), in_grad)
    late_sums.line(3)
    late_grads = late_sums.totals[0]
    down_grads = late_grads[:, :, half + ff_half :]
    late_grads = late_grads[:, :, : half + ff_half]
    late_left, late_right = rejoin(late_grads[0], late_grads[1])
    place = lax.broadcasted_iota(jnp.int32, (D, D), 0)
    place = (place % half) // units * (2 * units) + place // half * units + place % units
    unit_order = (place == lax.broadcasted_iota(jnp.int32, (D, D), 1)).astype(bf)
    early_sums.pair(2)
    g_wdown = jnp.stack([down_grads[:, :, :D], down_grads[:, :, D:]], axis=1).reshape(units, D)
    g_wout = jnp.concatenate([late_left[:, :half], late_right[:, :half]], axis=1)
    joined = []
    for group in range(ff_half // half):
        cut = slice(half + group * half, half + (group + 1) * half)
        joined.append(jnp.concatenate([late_left[:, cut], late_right[:, cut]], axis=1))
    joined = product(jnp.concatenate(joined, axis=0).astype(bf), unit_order)
    g_wup = jnp.concatenate([joined[g * rows : (g + 1) * rows] for g in range(ff_half // half)], axis=1)
    g_wdown, g_wout, g_wup, in_grad = tie((early_sums,), (g_wdown, g_wout, g_wup, in_grad))
    for step in (1, 2, 3):
        early_sums.line(step)
    early_grads = early_sums.totals[0]
    early_left, early_right = rejoin(early_grads[0], early_grads[1])
    vector_sum = early_left[table_rows, 5 * half :] + early_right[table_rows, 5 * half :]

    def side_by_side(left, right, at, count):
        pieces = []
        for index in range(count):
            cut = slice((at + index) * half, (at + index + 1) * half)
            pieces += [left[:, cut], right[:, cut]]
        return jnp.concatenate(pieces, axis=1)

    g_wqkv = side_by_side(early_left, early_right, 0, 3)
    g_wposk = side_by_side(early_left, early_right, 3, 1)
    g_wposq = side_by_side(early_left, early_right, 4, 1)
    g_table = side_by_side(early_left, early_right, 5, 1)[:table_rows]
    g = [vector_sum[i * rows : (i + 1) * rows] for i in range(9)]
    g_up_bias = vector_sum[256 : 256 + units]
    return (
        hidden_out, in_grad, g_wqkv, g[0], g[1], g_table, g_wposk, g_wposq, g[2], g_wout, g[3], g[4], g[5],
        g_wup, g_up_bias, g_wdown, g[6], g[7], g[8],
    )


def row_split(
    hidden_in,
    prefix,
    w_qkv,
    q_bias,
    v_bias,
    rel_table,
    w_posk,
    w_posq,
    posq_bias,
    w_out,
    out_bias,
    norm1_gain,
    norm1_bias,
    w_up,
    up_bias,
    w_down,
    down_bias,
    norm2_gain,
    norm2_bias,
    out_grad,
):
    gathered = (
        lax.all_gather(w_qkv, ("dp", "seq"), axis=0, tiled=True),
        lax.all_gather(q_bias, ("dp", "seq"), axis=0, tiled=True),
        lax.all_gather(v_bias, ("dp", "seq"), axis=0, tiled=True),
        lax.all_gather(rel_table, ("dp", "seq"), axis=0, tiled=True),
        lax.all_gather(w_posk, ("dp", "seq"), axis=0, tiled=True),
        lax.all_gather(w_posq, ("dp", "seq"), axis=0, tiled=True),
        lax.all_gather(posq_bias, ("dp", "seq"), axis=0, tiled=True),
        lax.all_gather(w_out, ("dp", "seq"), axis=0, tiled=True),
        lax.all_gather(out_bias, ("dp", "seq"), axis=0, tiled=True),
        lax.all_gather(norm1_gain, ("dp", "seq"), axis=0, tiled=True),
        lax.all_gather(norm1_bias, ("dp", "seq"), axis=0, tiled=True),
        lax.all_gather(w_up, ("dp", "seq"), axis=0, tiled=True),
        lax.all_gather(up_bias, ("dp", "seq"), axis=0, tiled=True),
        lax.all_gather(w_down, ("dp", "seq"), axis=0, tiled=True),
        lax.all_gather(down_bias, ("dp", "seq"), axis=0, tiled=True),
        lax.all_gather(norm2_gain, ("dp", "seq"), axis=0, tiled=True),
        lax.all_gather(norm2_bias, ("dp", "seq"), axis=0, tiled=True),
    )
    (
        full_qkv,
        full_qb,
        full_vb,
        full_table,
        full_posk,
        full_posq,
        full_pqb,
        full_out,
        full_ob,
        full_g1,
        full_b1,
        full_up,
        full_ub,
        full_down,
        full_db,
        full_g2,
        full_b2,
    ) = gathered
    row_count = hidden_in.shape[0]
    groups = lax.axis_size("seq")
    seq_length = row_count * groups
    seq_rank = lax.axis_index("seq")
    prefix_len = prefix[0]
    score_scale = 1.0 / math.sqrt(3 * HEAD_DIM)
    buckets = 2 * SPAN
    window = row_count + buckets
    first_row = seq_rank * row_count
    query_pos = first_row + jnp.arange(row_count, dtype=jnp.int32)
    key_pos = jnp.arange(seq_length, dtype=jnp.int32)
    visible = (key_pos[None, :] < prefix_len) | (key_pos[None, :] <= query_pos[:, None])
    padded_cols = jnp.arange(seq_length + buckets, dtype=jnp.int32)
    below_window = padded_cols[None, :] < first_row

    def skew_table(table, row_total, offset, col_total):
        shifted = jnp.pad(
            jnp.flip(table, axis=1), ((0, 0), (row_count, row_count - 1)), mode="edge"
        )
        stride = shifted.shape[1] - 1
        flattened = shifted.reshape(-1)
        picked = lax.slice_in_dim(flattened, offset, offset + row_total * stride)
        return picked.reshape(row_total, stride)[:, :col_total]

    def pos_terms(table_a, table_w, edge_terms):
        band_terms = (
            skew_table(table_a, row_count, row_count - 1, window)
            + skew_table(table_w, window, window - 1, row_count).T
        )
        low_side = table_a[:, buckets - 1 : buckets] + jnp.pad(edge_terms[0], (SPAN, SPAN))[None, :]
        high_side = table_a[:, 0:1] + jnp.pad(edge_terms[1], (SPAN, SPAN))[None, :]
        backdrop = jnp.where(below_window, low_side, high_side)
        placed = lax.dynamic_update_slice(
            backdrop, band_terms, (jnp.zeros((), jnp.int32), first_row)
        )
        return placed[:, SPAN : SPAN + seq_length]

    pos_keys = product(full_table, full_posk).astype(jnp.bfloat16)
    pos_queries = (product(full_table, full_posq) + full_pqb.astype(jnp.float32)).astype(
        jnp.bfloat16
    )
    merged = product(hidden_in, full_qkv)
    queries = (merged[:, :D] + full_qb.astype(jnp.float32)).astype(jnp.bfloat16)
    keys_local = merged[:, D : 2 * D].astype(jnp.bfloat16)
    values_local = (merged[:, 2 * D :] + full_vb.astype(jnp.float32)).astype(jnp.bfloat16)
    keys_all, values_all = (
        lax.all_gather(keys_local, "seq", axis=0, tiled=True),
        lax.all_gather(values_local, "seq", axis=0, tiled=True),
    )
    query_heads = split_heads(queries)
    key_heads = split_heads(keys_all)
    value_heads = split_heads(values_all)
    posk_heads = split_heads(pos_keys)
    posq_heads = split_heads(pos_queries)

    def head_scores(query_h, key_h, posk_h, posq_h):
        content = inner_last(query_h, key_h)
        table_a = inner_last(query_h, posk_h)
        key_padded = jnp.pad(key_h, ((SPAN, SPAN), (0, 0)))
        key_window = lax.dynamic_slice_in_dim(key_padded, first_row, window, 0)
        table_w = inner_last(key_window, posq_h)
        end_rows = jnp.stack([posq_h[0], posq_h[buckets - 1]])
        edge_terms = inner_last(end_rows, key_h)
        raw = content + pos_terms(table_a, table_w, edge_terms)
        masked = jnp.where(visible, raw * score_scale, -jnp.inf)
        return (masked, table_a, table_w, edge_terms, key_window, end_rows)

    def head_forward(operands):
        query_h, key_h, value_h, posk_h, posq_h = operands
        scores = head_scores(query_h, key_h, posk_h, posq_h)[0]
        highest = jnp.max(scores, axis=1, keepdims=True)
        expo = jnp.exp(scores - highest)
        totals = jnp.sum(expo, axis=1, keepdims=True)
        probs_low = (expo / totals).astype(jnp.bfloat16)
        return (product(probs_low, value_h), (highest + jnp.log(totals))[:, 0])

    contexts, log_totals = lax.map(
        head_forward, (query_heads, key_heads, value_heads, posk_heads, posq_heads)
    )
    context = join_heads(contexts).astype(jnp.bfloat16)
    hidden_f = hidden_in.astype(jnp.float32)
    residual1 = hidden_f + product(context, full_out) + full_ob.astype(jnp.float32)
    gain1 = full_g1.astype(jnp.float32)
    shift1 = full_b1.astype(jnp.float32)
    normed = normalize(residual1, gain1, shift1)
    normed_low = normed.astype(jnp.bfloat16)
    expanded = product(normed_low, full_up) + full_ub.astype(jnp.float32)
    activated = gelu_exact(expanded).astype(jnp.bfloat16)
    residual2 = normed + product(activated, full_down) + full_db.astype(jnp.float32)
    gain2 = full_g2.astype(jnp.float32)
    shift2 = full_b2.astype(jnp.float32)
    hidden_out = normalize(residual2, gain2, shift2).astype(jnp.bfloat16)
    regathered = (
        lax.all_gather(w_qkv, ("dp", "seq"), axis=0, tiled=True),
        lax.all_gather(q_bias, ("dp", "seq"), axis=0, tiled=True),
        lax.all_gather(v_bias, ("dp", "seq"), axis=0, tiled=True),
        lax.all_gather(rel_table, ("dp", "seq"), axis=0, tiled=True),
        lax.all_gather(w_posk, ("dp", "seq"), axis=0, tiled=True),
        lax.all_gather(w_posq, ("dp", "seq"), axis=0, tiled=True),
        lax.all_gather(posq_bias, ("dp", "seq"), axis=0, tiled=True),
        lax.all_gather(w_out, ("dp", "seq"), axis=0, tiled=True),
        lax.all_gather(out_bias, ("dp", "seq"), axis=0, tiled=True),
        lax.all_gather(norm1_gain, ("dp", "seq"), axis=0, tiled=True),
        lax.all_gather(norm1_bias, ("dp", "seq"), axis=0, tiled=True),
        lax.all_gather(w_up, ("dp", "seq"), axis=0, tiled=True),
        lax.all_gather(up_bias, ("dp", "seq"), axis=0, tiled=True),
        lax.all_gather(w_down, ("dp", "seq"), axis=0, tiled=True),
        lax.all_gather(down_bias, ("dp", "seq"), axis=0, tiled=True),
        lax.all_gather(norm2_gain, ("dp", "seq"), axis=0, tiled=True),
        lax.all_gather(norm2_bias, ("dp", "seq"), axis=0, tiled=True),
    )
    (
        back_qkv,
        back_qb,
        back_vb,
        back_table,
        back_posk,
        back_posq,
        back_pqb,
        back_out,
        back_ob,
        back_g1,
        back_b1,
        back_up,
        back_ub,
        back_down,
        back_db,
        back_g2,
        back_b2,
    ) = regathered
    _, pull_second = jax.vjp(normalize, residual2, gain2, shift2)
    d_res2, d_gain2, d_shift2 = pull_second(out_grad.astype(jnp.float32))
    d_reduced = d_res2.astype(jnp.bfloat16)
    d_wdown = inner_first(activated, d_reduced)
    d_down_bias = column_sums(d_reduced)
    d_activated = inner_last(d_reduced, back_down)
    _, pull_gelu = jax.vjp(gelu_exact, expanded)
    d_expanded = pull_gelu(d_activated)[0].astype(jnp.bfloat16)
    d_wup = inner_first(normed_low, d_expanded)
    d_up_bias = column_sums(d_expanded)
    d_normed = inner_last(d_expanded, back_up) + d_res2
    _, pull_first = jax.vjp(normalize, residual1, gain1, shift1)
    d_res1, d_gain1, d_shift1 = pull_first(d_normed)
    d_attended = d_res1.astype(jnp.bfloat16)
    d_wout = inner_first(context, d_attended)
    d_out_bias = column_sums(d_attended)
    d_context = inner_last(d_attended, back_out).astype(jnp.bfloat16)
    dctx_heads = split_heads(d_context)

    def head_backward(operands):
        query_h, key_h, value_h, posk_h, posq_h, log_total, dctx_h = operands
        scores, table_a, table_w, edge_terms, key_window, end_rows = head_scores(
            query_h, key_h, posk_h, posq_h
        )
        probs = jnp.exp(scores - log_total[:, None])
        probs_low = probs.astype(jnp.bfloat16)
        d_probs = inner_last(dctx_h, value_h)
        d_value = inner_first(probs_low, dctx_h)
        row_dot = jnp.sum(probs * d_probs, axis=1, keepdims=True)
        d_raw = (probs * (d_probs - row_dot) * score_scale).astype(jnp.bfloat16)
        _, pull_terms = jax.vjp(pos_terms, table_a, table_w, edge_terms)
        d_table_a, d_table_w, d_edges = pull_terms(d_raw.astype(jnp.float32))
        d_table_a = d_table_a.astype(jnp.bfloat16)
        d_table_w = d_table_w.astype(jnp.bfloat16)
        d_edges = d_edges.astype(jnp.bfloat16)
        d_query = product(d_raw, key_h) + product(d_table_a, posk_h)
        window_grad = product(d_table_w, posq_h)
        key_canvas = jnp.zeros((seq_length + buckets, HEAD_DIM), jnp.float32)
        placed_grad = lax.dynamic_update_slice(
            key_canvas, window_grad, (first_row, jnp.zeros((), jnp.int32))
        )
        d_key = (
            inner_first(d_raw, query_h)
            + placed_grad[SPAN : SPAN + seq_length]
            + inner_first(d_edges, end_rows)
        )
        d_posk = inner_first(d_table_a, query_h)
        end_grads = product(d_edges, key_h)
        d_posq = inner_first(d_table_w, key_window)
        d_posq = d_posq.at[0].add(end_grads[0]).at[buckets - 1].add(end_grads[1])
        return (d_query, d_key, d_value, d_posk, d_posq)

    d_q_heads, d_k_heads, d_v_heads, d_posk_heads, d_posq_heads = lax.map(
        head_backward,
        (query_heads, key_heads, value_heads, posk_heads, posq_heads, log_totals, dctx_heads),
    )
    d_queries = join_heads(d_q_heads).astype(jnp.bfloat16)
    d_keys_part, d_values_part = (
        lax.psum_scatter(
            join_heads(d_k_heads).astype(jnp.bfloat16), "seq", scatter_dimension=0, tiled=True
        ).astype(jnp.float32),
        lax.psum_scatter(
            join_heads(d_v_heads).astype(jnp.bfloat16), "seq", scatter_dimension=0, tiled=True
        ).astype(jnp.float32),
    )
    d_keys = d_keys_part.astype(jnp.bfloat16)
    d_values = d_values_part.astype(jnp.bfloat16)
    d_merged = jnp.concatenate([d_queries, d_keys, d_values], axis=1)
    d_wqkv = inner_first(hidden_in, d_merged)
    d_q_bias = column_sums(d_queries)
    d_v_bias = column_sums(d_values)
    in_grad = d_res1 + inner_last(d_merged, back_qkv)
    d_posk_rows, d_posq_rows = (
        lax.psum_scatter(join_heads(d_posk_heads), ("dp", "seq"), scatter_dimension=0, tiled=True),
        lax.psum_scatter(join_heads(d_posq_heads), ("dp", "seq"), scatter_dimension=0, tiled=True),
    )
    d_posk_low = d_posk_rows.astype(jnp.bfloat16)
    d_posq_low = d_posq_rows.astype(jnp.bfloat16)
    rel_table_grad = inner_last(d_posk_low, back_posk) + inner_last(d_posq_low, back_posq)
    d_wposk = inner_first(rel_table, d_posk_low)
    d_wposq = inner_first(rel_table, d_posq_low)
    d_posq_bias = column_sums(d_posq_low)
    summed = (
        lax.psum_scatter(d_wqkv, ("dp", "seq"), scatter_dimension=0, tiled=True),
        lax.psum_scatter(d_q_bias, ("dp", "seq"), scatter_dimension=0, tiled=True),
        lax.psum_scatter(d_v_bias, ("dp", "seq"), scatter_dimension=0, tiled=True),
        lax.psum_scatter(d_wposk, ("dp", "seq"), scatter_dimension=0, tiled=True),
        lax.psum_scatter(d_wposq, ("dp", "seq"), scatter_dimension=0, tiled=True),
        lax.psum_scatter(d_posq_bias, ("dp", "seq"), scatter_dimension=0, tiled=True),
        lax.psum_scatter(d_wout, ("dp", "seq"), scatter_dimension=0, tiled=True),
        lax.psum_scatter(d_out_bias, ("dp", "seq"), scatter_dimension=0, tiled=True),
        lax.psum_scatter(d_gain1, ("dp", "seq"), scatter_dimension=0, tiled=True),
        lax.psum_scatter(d_shift1, ("dp", "seq"), scatter_dimension=0, tiled=True),
        lax.psum_scatter(d_wup, ("dp", "seq"), scatter_dimension=0, tiled=True),
        lax.psum_scatter(d_up_bias, ("dp", "seq"), scatter_dimension=0, tiled=True),
        lax.psum_scatter(d_wdown, ("dp", "seq"), scatter_dimension=0, tiled=True),
        lax.psum_scatter(d_down_bias, ("dp", "seq"), scatter_dimension=0, tiled=True),
        lax.psum_scatter(d_gain2, ("dp", "seq"), scatter_dimension=0, tiled=True),
        lax.psum_scatter(d_shift2, ("dp", "seq"), scatter_dimension=0, tiled=True),
    )
    return (
        hidden_out,
        in_grad,
        summed[0],
        summed[1],
        summed[2],
        rel_table_grad,
        summed[3],
        summed[4],
        summed[5],
        summed[6],
        summed[7],
        summed[8],
        summed[9],
        summed[10],
        summed[11],
        summed[12],
        summed[13],
        summed[14],
        summed[15],
    )


def solution(mesh):
    placed = (
        P(("dp", "seq"), None),
        P("dp"),
        P(("dp", "seq"), None),
        P(("dp", "seq")),
        P(("dp", "seq")),
        P(("dp", "seq"), None),
        P(("dp", "seq"), None),
        P(("dp", "seq"), None),
        P(("dp", "seq")),
        P(("dp", "seq"), None),
        P(("dp", "seq")),
        P(("dp", "seq")),
        P(("dp", "seq")),
        P(("dp", "seq"), None),
        P(("dp", "seq")),
        P(("dp", "seq"), None),
        P(("dp", "seq")),
        P(("dp", "seq")),
        P(("dp", "seq")),
        P(("dp", "seq"), None),
    )
    return jax.shard_map(
        head_split if dict(mesh.shape) == {"dp": 16, "seq": 2} else row_split,
        mesh=mesh,
        in_specs=placed,
        out_specs=(
            P(("dp", "seq"), None),
            P(("dp", "seq"), None),
            P(("dp", "seq"), None),
            P(("dp", "seq")),
            P(("dp", "seq")),
            P(("dp", "seq"), None),
            P(("dp", "seq"), None),
            P(("dp", "seq"), None),
            P(("dp", "seq")),
            P(("dp", "seq"), None),
            P(("dp", "seq")),
            P(("dp", "seq")),
            P(("dp", "seq")),
            P(("dp", "seq"), None),
            P(("dp", "seq")),
            P(("dp", "seq"), None),
            P(("dp", "seq")),
            P(("dp", "seq")),
            P(("dp", "seq")),
        ),
        check_vma=False,
    )
```

```python
import functools
import math

import jax
import jax.numpy as jnp
from jax import lax
from jax.experimental import pallas as pl
from jax.experimental.pallas import tpu as pltpu
from jax.sharding import PartitionSpec as P

D = 768
HEADS = 12
HEAD_DIM = 64
SPAN = 256
TILE = 128
BLOCK = 256
BAND = 768
PAIR = 2 * HEAD_DIM


eps_norm = 1e-07


def normalize(value, gain, shift):
    average = jnp.mean(value, axis=-1, keepdims=True)
    centred = value - average
    variance = jnp.mean(centred * centred, axis=-1, keepdims=True)
    return centred * lax.rsqrt(variance + eps_norm) * gain + shift


def gelu_exact(value):
    return jax.nn.gelu(value, approximate=False)


def product(left, right):
    return jnp.dot(left, right, preferred_element_type=jnp.float32)


def inner_first(left, right):
    return lax.dot_general(
        left, right, (((0,), (0,)), ((), ())), preferred_element_type=jnp.float32
    )


def inner_last(left, right):
    return lax.dot_general(
        left, right, (((1,), (1,)), ((), ())), preferred_element_type=jnp.float32
    )


def split_heads(matrix):
    return matrix.reshape(matrix.shape[0], HEADS, HEAD_DIM).transpose(1, 0, 2)


def join_heads(stacked):
    return stacked.transpose(1, 0, 2).reshape(stacked.shape[1], D)


def column_sums(matrix):
    return jnp.sum(matrix.astype(jnp.float32), axis=0)


def nn(left, right):
    return lax.dot_general(
        left, right, (((1,), (0,)), ((), ())), preferred_element_type=jnp.float32
    )


def nt(left, right):
    return lax.dot_general(
        left, right, (((1,), (1,)), ((), ())), preferred_element_type=jnp.float32
    )


def unit_matrix(size, reverse=False):
    rows = lax.broadcasted_iota(jnp.int32, (size, size), 0)
    cols = lax.broadcasted_iota(jnp.int32, (size, size), 1)
    if reverse:
        cols = size - 1 - cols
    return jnp.where(rows == cols, 1.0, 0.0).astype(jnp.bfloat16)


def turn_matrix():
    rows = lax.broadcasted_iota(jnp.int32, (BLOCK, BLOCK), 0)
    cols = lax.broadcasted_iota(jnp.int32, (BLOCK, BLOCK), 1)
    mirrored = rows // TILE * (2 * TILE) + TILE - 1 - rows
    return jnp.where(mirrored == cols, 1.0, 0.0).astype(jnp.bfloat16)


def head_lanes(head):
    lanes = lax.broadcasted_iota(jnp.int32, (1, PAIR), 1)
    return lanes // HEAD_DIM == head


def head_rows(head):
    rows = lax.broadcasted_iota(jnp.int32, (HEAD_DIM, PAIR), 0)
    cols = lax.broadcasted_iota(jnp.int32, (HEAD_DIM, PAIR), 1)
    return jnp.where(cols == rows + head * HEAD_DIM, 1.0, 0.0).astype(jnp.bfloat16)


def key_tiles(block, length):
    return max(length // 2, (block + 1) * BLOCK) // TILE


def tile_seen(query_tile, key_tile, length):
    return key_tile < key_tiles(query_tile * TILE // BLOCK, length)


def skewed(window):
    return pltpu.roll(window, 0, 1, stride=1, stride_axis=0)


def forward_body(head, prefix_ref, q_ref, k_ref, v_ref, pk_ref, pq_ref, *refs):
    ctx_ref, p_ref, wb_ref, far_ref, s_ref = refs[-5:]
    length = q_ref.shape[0]
    mine = head_lanes(head)
    prefix = prefix_ref[0]
    eye = unit_matrix(TILE)
    eye_block = unit_matrix(BLOCK)
    zero = jnp.zeros((), jnp.bfloat16)
    scale = math.log2(math.e) / math.sqrt(3 * HEAD_DIM)
    for tile in range(length // TILE):
        rows = slice(tile * TILE, (tile + 1) * TILE)
        table = nt(jnp.where(mine, k_ref[rows, :], zero), pq_ref[...])
        wb_ref[rows, :] = skewed(table)
        wb_ref[rows, 0:TILE] = table[:, BAND - TILE :]
        far_ref[rows, :] = table[:, 0:TILE]
    v_cols = nt(jnp.where(lax.broadcasted_iota(jnp.int32, (PAIR, PAIR), 0) // HEAD_DIM == head, unit_matrix(PAIR), zero), v_ref[...]).astype(jnp.bfloat16)
    for block in range(length // BLOCK):
        cols = slice(block * BLOCK, (block + 1) * BLOCK)
        q_own = jnp.where(mine, q_ref[cols, :], zero)
        skews, highs, lows = [], [], []
        for sub in range(2):
            table = nt(q_own[sub * TILE : (sub + 1) * TILE], pk_ref[...])
            skews.append(skewed(table).astype(jnp.bfloat16))
            highs.append(table[:, 0:TILE].astype(jnp.bfloat16))
            lows.append(table[:, BAND - TILE :].astype(jnp.bfloat16))
        count = key_tiles(block, length)
        highest = None
        for tile in range(count):
            rows = slice(tile * TILE, (tile + 1) * TILE)
            parts_a, parts_b = [], []
            for sub in range(2):
                step = 2 * block + sub - tile
                if step >= 3:
                    parts_a.append(highs[sub])
                    parts_b.append(wb_ref[rows, 0:TILE])
                elif step <= -3:
                    parts_a.append(lows[sub])
                    parts_b.append(far_ref[rows, :])
                else:
                    at = 384 - TILE * step
                    parts_a.append(skews[sub][:, at : at + TILE])
                    at = 384 + TILE * step
                    parts_b.append(wb_ref[rows, at : at + TILE])
            right = jnp.concatenate([jnp.concatenate(parts_a, axis=0), q_own], axis=1)
            left = jnp.concatenate([eye, k_ref[rows, :]], axis=1)
            raw = nt(left, right) + jnp.concatenate(parts_b, axis=1)
            if (tile + 1) * TILE > block * BLOCK + 1:
                keys = tile * TILE + lax.broadcasted_iota(jnp.int32, (TILE, BLOCK), 0)
                queries = block * BLOCK + lax.broadcasted_iota(jnp.int32, (TILE, BLOCK), 1)
                raw = jnp.where((keys < prefix) | (keys <= queries), raw, -jnp.inf)
            s_ref[rows, :] = raw
            top = jnp.max(raw, axis=0, keepdims=True)
            highest = top if highest is None else jnp.maximum(highest, top)
        total = jnp.zeros((1, BLOCK), jnp.float32)
        for tile in range(count):
            rows = slice(tile * TILE, (tile + 1) * TILE)
            expo = jnp.exp2((s_ref[rows, :] - highest) * scale)
            s_ref[rows, :] = expo
            total = total + jnp.sum(expo, axis=0, keepdims=True)
        inverse = 1.0 / total
        for tile in range(count):
            rows = slice(tile * TILE, (tile + 1) * TILE)
            p_ref[rows, cols] = (s_ref[rows, :] * inverse).astype(jnp.bfloat16)
        seen = count * TILE
        ctx_cols = nn(v_cols[:, :seen], p_ref[0:seen, cols]).astype(jnp.bfloat16)
        ctx = nt(eye_block, ctx_cols).astype(jnp.bfloat16)

        ctx_ref[cols, :] = ctx if head == 0 else refs[0][cols, :] + ctx


def attention_forward(prefix, merged, pos_band, pair, head, found=()):
    length, width = merged.shape[0], merged.shape[1] // 3
    pairs = width // PAIR
    tall = [pl.BlockSpec((length, PAIR), lambda p, at=at: (0, at)) for at in (pair, pairs + pair, 2 * pairs + pair)]
    band = [pl.BlockSpec((BAND, PAIR), lambda p, at=at: (0, at)) for at in (pair, pairs + pair)]
    own = pl.BlockSpec((length, PAIR), lambda p: (0, 0))
    return pl.pallas_call(
        functools.partial(forward_body, head),
        grid=(1,),
        in_specs=[pl.BlockSpec(memory_space=pltpu.SMEM)] + tall + band + [own] * len(found),
        out_specs=[own, pl.BlockSpec((length, length), lambda p: (0, 0))],
        out_shape=[
            jax.ShapeDtypeStruct((length, PAIR), jnp.bfloat16),
            jax.ShapeDtypeStruct((length, length), jnp.bfloat16),
        ],
        scratch_shapes=[
            pltpu.VMEM((length, BAND), jnp.float32),
            pltpu.VMEM((length, TILE), jnp.float32),
            pltpu.VMEM((length, BLOCK), jnp.float32),
        ],
        compiler_params=pltpu.CompilerParams(dimension_semantics=("arbitrary",), vmem_limit_bytes=24 << 20),
        cost_estimate=pl.CostEstimate(flops=2 * 10**9, transcendentals=length * length, bytes_accessed=3 << 20),
        name="attention_forward",
    )(prefix, merged, merged, merged, pos_band, pos_band, *found)


def backward_body(head, q_ref, k_ref, v_ref, dctx_ref, p_ref, pk_ref, pq_ref, *refs):
    dq_ref, dk_ref, dv_ref, dpk_ref, dpq_ref, dr_ref, dk_acc, dv_acc = refs[-8:]
    outs = (dq_ref, dk_ref, dv_ref)
    length = q_ref.shape[0]
    mine = head_lanes(head)
    flip = turn_matrix()
    pick = head_rows(head)
    bf = jnp.bfloat16
    zero = jnp.zeros((), bf)
    scale = 1.0 / math.sqrt(3 * HEAD_DIM)
    back = BAND - (TILE - 1)
    blank = jnp.zeros((TILE, TILE), bf)
    dk_acc[...] = jnp.zeros_like(dk_acc)
    dv_acc[...] = jnp.zeros_like(dv_acc)
    dpk = jnp.zeros((HEAD_DIM, BAND), jnp.float32)
    dpq = jnp.zeros((HEAD_DIM, BAND), jnp.float32)
    tiles = length // TILE

    def put(index, rows, value):
        earlier = jnp.zeros((), bf) if head == 0 else refs[index][rows, :]
        outs[index][rows, :] = jnp.where(mine, value.astype(bf), earlier)

    def unskew(parts):
        return pltpu.roll(jnp.concatenate(parts, axis=1), back, 1, stride=1, stride_axis=0)

    for block in range(length // BLOCK):
        cols = slice(block * BLOCK, (block + 1) * BLOCK)
        count = key_tiles(block, length)
        seen = count * TILE
        dctx = dctx_ref[cols, :]
        v_own = jnp.where(mine, v_ref[0:seen, :], zero)
        probs_low = p_ref[0:seen, cols]
        probs = probs_low.astype(jnp.float32)
        d_probs = nt(v_own, dctx)
        row_dot = jnp.sum(probs * d_probs, axis=0, keepdims=True)
        dr_ref[0:seen, cols] = (probs * ((d_probs - row_dot) * scale)).astype(bf)
        d_raw = dr_ref[0:seen, cols]
        dv_acc[0:seen, :] += nn(probs_low, dctx)
        dk_acc[0:seen, :] += nn(d_raw, q_ref[cols, :])
        turned = nt(flip, d_raw).astype(bf)
        spreads = []
        for sub in range(2):
            tile = 2 * block + sub
            own = turned[sub * TILE : (sub + 1) * TILE]

            def piece(key_tile):
                return own[:, key_tile * TILE : (key_tile + 1) * TILE]

            near = [t for t in range(count) if tile - t >= 3]
            far = [t for t in range(count) if tile - t <= -3]
            band = [blank]
            for step in (2, 1, 0, -1, -2):
                key_tile = tile - step
                band.append(piece(key_tile) if 0 <= key_tile < count else blank)
            spreads.append(
                add_edges(unskew(band), [piece(t).astype(jnp.float32) for t in near], [piece(t).astype(jnp.float32) for t in far])
            )
        spread = jnp.concatenate(spreads, axis=0)
        dq = nn(turned, k_ref[0:seen, :]) + nn(spread, pk_ref[...])
        put(0, cols, nn(flip, dq.astype(bf)))
        q_cols = nt(pick, nn(flip, q_ref[cols, :]).astype(bf)).astype(bf)
        dpk = dpk + nn(q_cols, spread)
    dpk_ref[...] = dpk
    for block in range(length // BLOCK):
        rows = slice(block * BLOCK, (block + 1) * BLOCK)
        groups, edges = [], []
        for sub in range(2):
            key_tile = 2 * block + sub
            own = slice(key_tile * TILE, (key_tile + 1) * TILE)
            seen_by = [t for t in range(tiles) if tile_seen(t, key_tile, length)]

            def held(query_tile):
                return dr_ref[own, query_tile * TILE : (query_tile + 1) * TILE]

            band = [blank]
            for step in (-2, -1, 0, 1, 2):
                query_tile = key_tile + step
                band.append(held(query_tile) if query_tile in seen_by else blank)
            ends = []
            for chosen in ([t for t in seen_by if t - key_tile <= -3], [t for t in seen_by if t - key_tile >= 3]):
                total = blank
                if chosen:
                    total = sum((held(t).astype(jnp.float32) for t in chosen[1:]), held(chosen[0]).astype(jnp.float32)).astype(bf)
                ends.append(total)
            groups.append(jnp.concatenate(band[1:] + ends, axis=1))
        turned = nn(flip, jnp.concatenate(groups, axis=0))
        width = BAND - TILE
        spreads = []
        for sub in range(2):
            own = turned[sub * TILE : (sub + 1) * TILE]
            spreads.append(
                add_edges(unskew([blank, own[:, :width].astype(bf)]), [own[:, width : width + TILE]], [own[:, width + TILE :]])
            )
        spread = jnp.concatenate(spreads, axis=0)
        d_key = nn(flip, nn(spread, pq_ref[...]).astype(bf))
        put(1, rows, dk_acc[rows, :] + d_key)
        k_cols = nt(pick, nn(flip, k_ref[rows, :]).astype(bf)).astype(bf)
        dpq = dpq + nn(k_cols, spread)
        put(2, rows, dv_acc[rows, :])
    dpq_ref[...] = dpq


def add_edges(spread, first, last):
    parts = [spread[:, 0:TILE], spread[:, TILE : BAND - TILE], spread[:, BAND - TILE :]]
    for place, tiles in ((0, first), (2, last)):
        if tiles:
            total = parts[place].astype(jnp.float32)
            for tile in tiles:
                total = total + tile
            parts[place] = total.astype(jnp.bfloat16)
    return jnp.concatenate(parts, axis=1)


def attention_backward(merged, dctx, probs, pos_band, pair, head, found=()):
    length, width = merged.shape[0], merged.shape[1] // 3
    pairs = width // PAIR
    tall = [pl.BlockSpec((length, PAIR), lambda p, at=at: (0, at)) for at in (pair, pairs + pair, 2 * pairs + pair, pair)]
    band = [pl.BlockSpec((BAND, PAIR), lambda p, at=at: (0, at)) for at in (pair, pairs + pair)]
    own = pl.BlockSpec((length, PAIR), lambda p: (0, 0))
    table = pl.BlockSpec((HEAD_DIM, BAND), lambda p: (0, 0))
    flat = jax.ShapeDtypeStruct((length, PAIR), jnp.bfloat16)
    wide = jax.ShapeDtypeStruct((HEAD_DIM, BAND), jnp.float32)
    return pl.pallas_call(
        functools.partial(backward_body, head),
        grid=(1,),
        in_specs=tall + [pl.BlockSpec((length, length), lambda p: (0, 0))] + band + [own] * len(found),
        out_specs=[own, own, own, table, table],
        out_shape=[flat, flat, flat, wide, wide],
        scratch_shapes=[
            pltpu.VMEM((length, length), jnp.bfloat16),
            pltpu.VMEM((length, PAIR), jnp.float32),
            pltpu.VMEM((length, PAIR), jnp.float32),
        ],
        compiler_params=pltpu.CompilerParams(dimension_semantics=("arbitrary",), vmem_limit_bytes=24 << 20),
        cost_estimate=pl.CostEstimate(flops=4 * 10**9, transcendentals=0, bytes_accessed=4 << 20),
        name="attention_backward",
    )(merged, merged, merged, dctx, probs, pos_band, pos_band, *found)


CORES = [(0, 1), (1, 0)]


def swap(value):
    return lax.ppermute(value, "seq", CORES)


def ordered(core, own, other, axis=0):
    return jnp.concatenate(
        [jnp.where(core == 0, own, other), jnp.where(core == 0, other, own)], axis=axis
    )


def half_of(core, matrix, axis):
    size = matrix.shape[axis] // 2
    return lax.dynamic_slice_in_dim(matrix, core * size, size, axis)


def chip_bits():
    chip = lax.axis_index("dp")
    return chip // 4, (chip // 2) % 2, chip % 2


def exchange(value, mask):
    return lax.ppermute(value, "dp", [(i, i ^ mask) for i in range(16)])


def tie(chains, others=()):
    states, others = lax.optimization_barrier(([chain.state for chain in chains], others))
    for chain, state in zip(chains, states):
        chain.state = state
    return others


class Gather:
    def __init__(self, *values):
        self.state = values

    def line(self, step):
        up = [(i, i + 4) for i in range(12) if i // 4 >= step - 1]
        down = [(i + 4, i) for i in range(12) if i // 4 <= 3 - step]
        if step == 1:
            self.state = [([value], [value]) for value in self.state]
        self.state = [
            (below + [lax.ppermute(below[-1], "dp", up)], above + [lax.ppermute(above[-1], "dp", down)])
            for below, above in self.state
        ]
        if step == 3:
            z = chip_bits()[0]
            lines = []
            for below, above in self.state:
                blocks = []
                for block in range(4):
                    options = [below[k - block] if k >= block else above[block - k] for k in range(4)]
                    blocks.append(lax.select_n(z, *options))
                lines.append(tuple(jnp.stack([b[side] for b in blocks]) for side in range(2)))
            self.state = lines

    def double(self, step):
        self.state = [(value, exchange(value, 4 * step)) for value in self.state]

    def finish_double(self, step):
        z = chip_bits()[0]
        bit = z % 2 if step == 1 else z // 2
        result = [
            jnp.stack([jnp.where(bit == 0, value, other), jnp.where(bit == 0, other, value)])
            for value, other in self.state
        ]
        if step == 2:
            result = [tuple(value[:, :, side].reshape((4,) + value.shape[3:]) for side in range(2)) for value in result]
        self.state = result

    def pair(self, step):
        masks = (1, 2) if step == 1 else (2, 1)
        self.state = [
            tuple((value, exchange(value, mask)) for value, mask in zip(halves, masks)) for halves in self.state
        ]

    def finish_pair(self, step):
        _, y, x = chip_bits()
        bits = (x, y) if step == 1 else (y, x)
        self.state = [
            tuple(
                jnp.stack([jnp.where(bit == 0, value, other), jnp.where(bit == 0, other, value)])
                for (value, other), bit in zip(halves, bits)
            )
            for halves in self.state
        ]

    def rows(self, index, low, high):
        first, second = [half[..., low:high] for half in self.state[index]]
        first = jnp.moveaxis(first, (0, 1, 2), (1, 2, 0))
        second = jnp.moveaxis(second, (0, 1, 2), (2, 1, 0))
        whole = jnp.stack([first, second], axis=3)
        return whole.reshape(-1, whole.shape[-1])


class Scatter:
    def __init__(self, *values):
        self.state = []
        for value in values:
            grid = value.reshape((4, 2, 2) + value.shape[1:])
            self.state.append((jnp.moveaxis(grid[:, :, :, 0], 2, 0), jnp.moveaxis(grid[:, :, :, 1], 1, 0)))

    def pair(self, step):
        _, y, x = chip_bits()
        order = ((x, 1), (y, 2)) if step == 1 else ((y, 2), (x, 1))
        sums = []
        for halves in self.state:
            result = []
            for value, (bit, mask) in zip(halves, order):
                keep = jnp.where(bit == 0, value[0], value[1])
                give = jnp.where(bit == 0, value[1], value[0])
                total = (keep.astype(jnp.float32) + exchange(give, mask).astype(jnp.float32)).astype(value.dtype)
                result.append(jnp.moveaxis(total, 1, 0) if step == 1 else total)
            sums.append(tuple(result) if step == 1 else (jnp.stack(result, axis=1), None, None))
        self.state = sums

    def line(self, step):
        z = chip_bits()[0]
        offset = 4 - step
        ups = [(i, i + 4) for i in range(12) if i // 4 + offset <= 3]
        downs = [(i + 4, i) for i in range(12) if i // 4 + 1 - offset >= 0]
        sums, self.totals = [], []
        for value, up, down in self.state:

            def block(at):
                options = [value[min(max(k + at, 0), 3)] for k in range(4)]
                return lax.select_n(z, *options).astype(jnp.float32)

            to_above, to_below = block(offset), block(-offset)
            if up is not None:
                to_above = to_above + up.astype(jnp.float32)
                to_below = to_below + down.astype(jnp.float32)
            up = lax.ppermute(to_above.astype(value.dtype), "dp", ups)
            down = lax.ppermute(to_below.astype(value.dtype), "dp", downs)
            sums.append((value, up, down))
            if step == 3:
                self.totals.append(block(0) + up.astype(jnp.float32) + down.astype(jnp.float32))
        self.state = sums


def norm_parts(value):
    average = jnp.mean(value, axis=-1, keepdims=True)
    centred = value - average
    variance = jnp.mean(centred * centred, axis=-1, keepdims=True)
    inverse = lax.rsqrt(variance + eps_norm)
    return centred * inverse, inverse


def norm_back(unit, inverse, gain, grad):
    scaled = grad * gain
    mean_grad = jnp.mean(scaled, axis=-1, keepdims=True)
    mean_along = jnp.mean(scaled * unit, axis=-1, keepdims=True)
    return inverse * (scaled - mean_grad - unit * mean_along)


def head_split(
    hidden_in, prefix, w_qkv, q_bias, v_bias, rel_table, w_posk, w_posq, posq_bias, w_out, out_bias,
    norm1_gain, norm1_bias, w_up, up_bias, w_down, down_bias, norm2_gain, norm2_bias, out_grad,
):
    bf = jnp.bfloat16
    f32 = jnp.float32
    core = lax.axis_index("seq")
    rows = w_qkv.shape[0]
    units = w_down.shape[0]
    table_rows = rel_table.shape[0]
    chips = 16
    half = D // 2
    ff_half = chips * units
    buckets = 2 * SPAN

    last_rows = rows - table_rows
    vectors = (q_bias, v_bias, posq_bias, out_bias, norm1_gain, norm1_bias, down_bias, norm2_gain)
    left = jnp.stack(vectors)
    right = jnp.concatenate(
        [jnp.pad(norm2_bias, (0, units - rows))[None], up_bias[None], jnp.zeros((last_rows - 2, units), bf)], axis=0
    )
    small = jnp.concatenate([jnp.pad(left, ((0, 0), (0, 128 - rows))), jnp.pad(right, ((0, 0), (0, half - 128 - units)))], axis=1)

    def columns(side):
        qkv = w_qkv.reshape(rows, 3, 2, half)[:, :, side].reshape(rows, 3 * half)
        corner = jnp.concatenate([rel_table[:, side * half : (side + 1) * half], small], axis=0)
        cut = slice(side * half, (side + 1) * half)
        up = w_up.reshape(rows, chips, 2, units)[:, :, side].reshape(rows, ff_half)
        return (
            jnp.concatenate([qkv, w_posk[:, cut], w_posq[:, cut], corner], axis=1),
            jnp.concatenate([w_out[:, cut], up], axis=1),
        )

    early0, late0 = columns(0)
    early1, late1 = columns(1)
    early_got = swap(jnp.where(core == 0, early1, early0))
    late_got = swap(jnp.where(core == 0, late1, late0))
    hidden_got = swap(hidden_in)

    def by_core(first, second, got):
        own = jnp.where(core == 0, first, second)
        return jnp.stack([jnp.where(core == 0, own, got), jnp.where(core == 0, got, own)])

    early_chain = Gather(by_core(early0, early1, early_got))
    downs = jnp.concatenate([w_down.reshape(2, 2, rows, D)[:, 0], w_down.reshape(2, 2, rows, D)[:, 1]], axis=-1)
    late_chain = Gather(jnp.concatenate([by_core(late0, late1, late_got), downs], axis=-1))
    for step in (1, 2, 3):
        early_chain.line(step)
    tie((early_chain, late_chain))
    early_chain.pair(1)
    late_chain.double(1)
    tie((early_chain, late_chain))
    early_chain.finish_pair(1)
    late_chain.finish_double(1)
    early_chain.pair(2)
    late_chain.double(2)
    early_chain.finish_pair(2)
    hidden_all = ordered(core, hidden_in, hidden_got)
    w_qkv_own = early_chain.rows(0, 0, 3 * half)
    w_pos_own = early_chain.rows(0, 3 * half, 5 * half)
    corner = early_chain.rows(0, 5 * half, 6 * half).reshape(2 * chips, rows, half)
    table_half = corner[:, :table_rows].reshape(buckets, half)
    small = corner[:, table_rows:]
    table = ordered(core, table_half, swap(table_half), axis=1)

    owner = (lax.broadcasted_iota(jnp.int32, (2 * chips, D), 1) // rows == lax.broadcasted_iota(jnp.int32, (2 * chips, D), 0)).astype(bf)
    inside = lax.broadcasted_iota(jnp.int32, (rows, D), 1) % rows == lax.broadcasted_iota(jnp.int32, (rows, D), 0)
    unit_owner = (
        2 * (lax.broadcasted_iota(jnp.int32, (2 * chips, ff_half), 1) // units) + core
        == lax.broadcasted_iota(jnp.int32, (2 * chips, ff_half), 0)
    ).astype(bf)
    unit_inside = lax.broadcasted_iota(jnp.int32, (units, ff_half), 1) % units == lax.broadcasted_iota(jnp.int32, (units, ff_half), 0)
    spots = jnp.concatenate([small[:, :, :rows], small[:, :, 128 : 128 + rows]], axis=1)
    wide = lax.dot_general(spots, owner, (((0,), (0,)), ((), ())), preferred_element_type=f32)
    lists = jnp.sum(jnp.where(inside, wide, 0.0), axis=1)
    qb, vb, pqb, ob, gain1, shift1, db, gain2, shift2 = [lists[i] for i in range(9)]
    wide = inner_first(small[:, 1, 128 : 128 + units], unit_owner)
    ub = jnp.sum(jnp.where(unit_inside, wide, 0.0), axis=0)

    band = lax.broadcasted_iota(jnp.int32, (BAND, buckets), 0)
    bucket = lax.broadcasted_iota(jnp.int32, (BAND, buckets), 1)
    chosen = (jnp.clip(SPAN + 384 - band, 0, buckets - 1) == bucket).astype(bf)
    pos_shift = jnp.concatenate([jnp.zeros((half,), f32), half_of(core, pqb, 0)])
    pos = (product(table, w_pos_own) + pos_shift).astype(bf)
    pos_band = product(chosen, pos).astype(bf)

    qkv_shift = jnp.concatenate([half_of(core, qb, 0), jnp.zeros((half,), f32), half_of(core, vb, 0)])
    merged = (product(hidden_all, w_qkv_own) + qkv_shift).astype(bf)
    merged, pos_band = tie((late_chain,), (merged, pos_band))
    late_chain.finish_double(2)
    late_chain.pair(1)
    context_parts, prob_parts = [], []
    for pair in range(half // PAIR):
        part, kept = attention_forward(prefix, merged, pos_band, pair, 0)
        prob_parts.append(kept)
        part, kept = attention_forward(prefix, merged, pos_band, pair, 1, (part,))
        prob_parts.append(kept)
        if pair == 0:
            part, merged = tie((late_chain,), (part, merged))
            late_chain.finish_pair(1)
            late_chain.pair(2)
        context_parts.append(part)
    context_parts = tie((late_chain,), context_parts)
    late_chain.finish_pair(2)
    context = jnp.concatenate(context_parts, axis=1)
    out_columns = late_chain.rows(0, 0, half)
    w_out_own = ordered(
        core, half_of(core, out_columns, 0), swap(half_of(1 - core, out_columns, 0)), axis=1
    )
    w_up_own = late_chain.rows(0, half, half + ff_half)
    down_at = half + ff_half
    down_parts = [late_chain.rows(0, at, at + D).reshape(2 * chips, rows, D) for at in (down_at, down_at + D)]
    w_down_own = jnp.stack(down_parts, axis=1).reshape(ff_half, D)

    def summed_rows(left, multiply):
        given = swap(multiply(half_of(1 - core, left, 0)).astype(bf))
        return multiply(half_of(core, left, 0)) + given.astype(f32)

    hidden_f = hidden_in.astype(f32)
    residual1 = hidden_f + summed_rows(context, lambda part: product(part, w_out_own)) + ob
    unit1, inverse1 = norm_parts(residual1)
    normed = unit1 * gain1 + shift1
    normed_low = normed.astype(bf)
    normed_all = ordered(core, normed_low, swap(normed_low))
    expanded = product(normed_all, w_up_own) + ub
    normal_cdf = 0.5 + 0.5 * lax.erf(expanded * math.sqrt(0.5))
    activated = (expanded * normal_cdf).astype(bf)
    slope = (
        normal_cdf + expanded * jnp.exp(-0.5 * expanded * expanded) * (1.0 / math.sqrt(2.0 * math.pi))
    ).astype(bf)
    residual2 = normed + summed_rows(activated, lambda part: product(part, w_down_own)) + db
    unit2, inverse2 = norm_parts(residual2)
    hidden_out = (unit2 * gain2 + shift2).astype(bf)

    grad = out_grad.astype(f32)
    d_res2 = norm_back(unit2, inverse2, gain2, grad)
    d_gain2 = jnp.sum(grad * unit2, axis=0, keepdims=True)
    d_shift2 = jnp.sum(grad, axis=0, keepdims=True)
    d_reduced = d_res2.astype(bf)
    d_down_bias = column_sums(d_reduced)[None]
    reduced_all = ordered(core, d_reduced, swap(d_reduced))
    d_expanded = (inner_last(reduced_all, w_down_own) * slope.astype(f32)).astype(bf)
    d_normed = summed_rows(d_expanded, lambda part: inner_last(part, w_up_own)) + d_res2
    d_wdown = inner_first(activated, reduced_all).astype(bf)
    d_wup = inner_first(normed_all, d_expanded).astype(bf)
    d_up_bias = column_sums(d_expanded)
    d_res1 = norm_back(unit1, inverse1, gain1, d_normed)
    d_gain1 = jnp.sum(d_normed * unit1, axis=0, keepdims=True)
    d_shift1 = jnp.sum(d_normed, axis=0, keepdims=True)
    d_attended = d_res1.astype(bf)
    d_out_bias = column_sums(d_attended)[None]
    attended_all = ordered(core, d_attended, swap(d_attended))
    d_context = inner_last(attended_all, w_out_own).astype(bf)
    d_wout_rows = inner_first(context, attended_all).astype(bf)
    d_wout = ordered(
        core, half_of(core, d_wout_rows, 1), swap(half_of(1 - core, d_wout_rows, 1)), axis=0
    )

    def rejoin(first, second):
        own = jnp.where(core == 0, first, second)
        got = swap(jnp.where(core == 0, second, first))
        return jnp.where(core == 0, own, got), jnp.where(core == 0, got, own)

    late_cols = jnp.concatenate([d_wout, d_wup], axis=1).reshape(chips, 2, rows, half + ff_half)
    down_cols = d_wdown.reshape(chips, 2, 2, rows, D)
    late_sums = Scatter(jnp.concatenate([late_cols, down_cols[:, :, 0], down_cols[:, :, 1]], axis=-1))
    grads = []
    late_steps = {0: lambda: late_sums.pair(1), 3: lambda: late_sums.pair(2), 5: lambda: late_sums.line(1)}
    found = ()
    for index in range(half // HEAD_DIM):
        if index in late_steps:
            found, d_context = tie((late_sums,), (found, d_context))
            late_steps[index]()
        if index % 2 == 0:
            found = ()
        found = attention_backward(merged, d_context, prob_parts[index], pos_band, index // 2, index % 2, tuple(found[:3]))
        grads.append(found)
    grads[-1] = tie((late_sums,), found)
    late_sums.line(2)
    d_merged = jnp.concatenate([g[i] for i in range(3) for g in grads[1::2]], axis=1)
    d_q, d_v = d_merged[:, :half], d_merged[:, 2 * half :]
    d_wqkv = inner_first(hidden_all, d_merged).astype(bf)
    d_q_bias = column_sums(d_q)[None]
    d_v_bias = column_sums(d_v)[None]
    d_band = jnp.concatenate([g[i] for i in (3, 4) for g in grads], axis=0).astype(bf)
    d_pos = lax.dot_general(
        chosen, d_band, (((0,), (1,)), ((), ())), preferred_element_type=f32
    )
    d_posq_bias = jnp.sum(d_pos[:, half:], axis=0, keepdims=True)
    d_pos_low = d_pos.astype(bf)
    d_wpos = inner_first(table, d_pos_low).astype(bf)
    d_table_all = inner_last(d_pos_low, w_pos_own).astype(bf)
    d_table = (
        half_of(core, d_table_all, 1).astype(f32)
        + swap(half_of(1 - core, d_table_all, 1)).astype(f32)
    ).astype(bf)

    def whole(part):
        blank = jnp.zeros_like(part)
        return ordered(core, part, blank, axis=1)

    lists_grad = jnp.concatenate(
        [whole(jnp.concatenate([d_q_bias, d_v_bias, d_posq_bias], axis=0)), d_out_bias, d_gain1, d_shift1, d_down_bias, d_gain2, d_shift2],
        axis=0,
    ).astype(bf)
    lists_grad = jnp.pad(lists_grad, ((0, 7), (0, 0)))
    pieces = jnp.where(inside, lists_grad[:, None, :], jnp.zeros((), bf)).reshape(16 * rows, D)
    unit_at = lax.broadcasted_iota(jnp.int32, (half, ff_half), 1) % units + 256 == lax.broadcasted_iota(jnp.int32, (half, ff_half), 0)
    unit_pieces = jnp.where(unit_at, d_up_bias.astype(bf), jnp.zeros((), bf))
    vector = (inner_last(owner, pieces) + inner_last(unit_owner, unit_pieces)).astype(bf)
    corner_grad = jnp.concatenate(
        [
            d_table.reshape(2 * chips, table_rows, half),
            jnp.pad(vector[:, None, :], ((0, 0), (0, last_rows - 1), (0, 0))),
        ],
        axis=1,
    ).reshape(chips * 2 * rows, half)
    early_sums = Scatter(
        jnp.concatenate([d_wqkv, d_wpos, corner_grad], axis=1).reshape(chips, 2, rows, 6 * half)
    )
    d_merged = tie((early_sums,), d_merged)
    early_sums.pair(1)
    in_grad = d_res1 + summed_rows(d_merged, lambda part: inner_last(part, w_qkv_own))
    in_grad = tie((late_sums,), in_grad)
    late_sums.line(3)
    late_grads = late_sums.totals[0]
    down_grads = late_grads[:, :, half + ff_half :]
    late_grads = late_grads[:, :, : half + ff_half]
    late_left, late_right = rejoin(late_grads[0], late_grads[1])
    place = lax.broadcasted_iota(jnp.int32, (D, D), 0)
    place = (place % half) // units * (2 * units) + place // half * units + place % units
    unit_order = (place == lax.broadcasted_iota(jnp.int32, (D, D), 1)).astype(bf)
    early_sums.pair(2)
    g_wdown = jnp.stack([down_grads[:, :, :D], down_grads[:, :, D:]], axis=1).reshape(units, D)
    g_wout = jnp.concatenate([late_left[:, :half], late_right[:, :half]], axis=1)
    joined = []
    for group in range(ff_half // half):
        cut = slice(half + group * half, half + (group + 1) * half)
        joined.append(jnp.concatenate([late_left[:, cut], late_right[:, cut]], axis=1))
    joined = product(jnp.concatenate(joined, axis=0).astype(bf), unit_order)
    g_wup = jnp.concatenate([joined[g * rows : (g + 1) * rows] for g in range(ff_half // half)], axis=1)
    g_wdown, g_wout, g_wup, in_grad = tie((early_sums,), (g_wdown, g_wout, g_wup, in_grad))
    for step in (1, 2, 3):
        early_sums.line(step)
    early_grads = early_sums.totals[0]
    early_left, early_right = rejoin(early_grads[0], early_grads[1])
    vector_sum = early_left[table_rows, 5 * half :] + early_right[table_rows, 5 * half :]

    def side_by_side(left, right, at, count):
        pieces = []
        for index in range(count):
            cut = slice((at + index) * half, (at + index + 1) * half)
            pieces += [left[:, cut], right[:, cut]]
        return jnp.concatenate(pieces, axis=1)

    g_wqkv = side_by_side(early_left, early_right, 0, 3)
    g_wposk = side_by_side(early_left, early_right, 3, 1)
    g_wposq = side_by_side(early_left, early_right, 4, 1)
    g_table = side_by_side(early_left, early_right, 5, 1)[:table_rows]
    g = [vector_sum[i * rows : (i + 1) * rows] for i in range(9)]
    g_up_bias = vector_sum[256 : 256 + units]
    return (
        hidden_out, in_grad, g_wqkv, g[0], g[1], g_table, g_wposk, g_wposq, g[2], g_wout, g[3], g[4], g[5],
        g_wup, g_up_bias, g_wdown, g[6], g[7], g[8],
    )


def row_split(
    hidden_in,
    prefix,
    w_qkv,
    q_bias,
    v_bias,
    rel_table,
    w_posk,
    w_posq,
    posq_bias,
    w_out,
    out_bias,
    norm1_gain,
    norm1_bias,
    w_up,
    up_bias,
    w_down,
    down_bias,
    norm2_gain,
    norm2_bias,
    out_grad,
):
    gathered = (
        lax.all_gather(w_qkv, ("dp", "seq"), axis=0, tiled=True),
        lax.all_gather(q_bias, ("dp", "seq"), axis=0, tiled=True),
        lax.all_gather(v_bias, ("dp", "seq"), axis=0, tiled=True),
        lax.all_gather(rel_table, ("dp", "seq"), axis=0, tiled=True),
        lax.all_gather(w_posk, ("dp", "seq"), axis=0, tiled=True),
        lax.all_gather(w_posq, ("dp", "seq"), axis=0, tiled=True),
        lax.all_gather(posq_bias, ("dp", "seq"), axis=0, tiled=True),
        lax.all_gather(w_out, ("dp", "seq"), axis=0, tiled=True),
        lax.all_gather(out_bias, ("dp", "seq"), axis=0, tiled=True),
        lax.all_gather(norm1_gain, ("dp", "seq"), axis=0, tiled=True),
        lax.all_gather(norm1_bias, ("dp", "seq"), axis=0, tiled=True),
        lax.all_gather(w_up, ("dp", "seq"), axis=0, tiled=True),
        lax.all_gather(up_bias, ("dp", "seq"), axis=0, tiled=True),
        lax.all_gather(w_down, ("dp", "seq"), axis=0, tiled=True),
        lax.all_gather(down_bias, ("dp", "seq"), axis=0, tiled=True),
        lax.all_gather(norm2_gain, ("dp", "seq"), axis=0, tiled=True),
        lax.all_gather(norm2_bias, ("dp", "seq"), axis=0, tiled=True),
    )
    (
        full_qkv,
        full_qb,
        full_vb,
        full_table,
        full_posk,
        full_posq,
        full_pqb,
        full_out,
        full_ob,
        full_g1,
        full_b1,
        full_up,
        full_ub,
        full_down,
        full_db,
        full_g2,
        full_b2,
    ) = gathered
    row_count = hidden_in.shape[0]
    groups = lax.axis_size("seq")
    seq_length = row_count * groups
    seq_rank = lax.axis_index("seq")
    prefix_len = prefix[0]
    score_scale = 1.0 / math.sqrt(3 * HEAD_DIM)
    buckets = 2 * SPAN
    window = row_count + buckets
    first_row = seq_rank * row_count
    query_pos = first_row + jnp.arange(row_count, dtype=jnp.int32)
    key_pos = jnp.arange(seq_length, dtype=jnp.int32)
    visible = (key_pos[None, :] < prefix_len) | (key_pos[None, :] <= query_pos[:, None])
    padded_cols = jnp.arange(seq_length + buckets, dtype=jnp.int32)
    below_window = padded_cols[None, :] < first_row

    def skew_table(table, row_total, offset, col_total):
        shifted = jnp.pad(
            jnp.flip(table, axis=1), ((0, 0), (row_count, row_count - 1)), mode="edge"
        )
        stride = shifted.shape[1] - 1
        flattened = shifted.reshape(-1)
        picked = lax.slice_in_dim(flattened, offset, offset + row_total * stride)
        return picked.reshape(row_total, stride)[:, :col_total]

    def pos_terms(table_a, table_w, edge_terms):
        band_terms = (
            skew_table(table_a, row_count, row_count - 1, window)
            + skew_table(table_w, window, window - 1, row_count).T
        )
        low_side = table_a[:, buckets - 1 : buckets] + jnp.pad(edge_terms[0], (SPAN, SPAN))[None, :]
        high_side = table_a[:, 0:1] + jnp.pad(edge_terms[1], (SPAN, SPAN))[None, :]
        backdrop = jnp.where(below_window, low_side, high_side)
        placed = lax.dynamic_update_slice(
            backdrop, band_terms, (jnp.zeros((), jnp.int32), first_row)
        )
        return placed[:, SPAN : SPAN + seq_length]

    pos_keys = product(full_table, full_posk).astype(jnp.bfloat16)
    pos_queries = (product(full_table, full_posq) + full_pqb.astype(jnp.float32)).astype(
        jnp.bfloat16
    )
    merged = product(hidden_in, full_qkv)
    queries = (merged[:, :D] + full_qb.astype(jnp.float32)).astype(jnp.bfloat16)
    keys_local = merged[:, D : 2 * D].astype(jnp.bfloat16)
    values_local = (merged[:, 2 * D :] + full_vb.astype(jnp.float32)).astype(jnp.bfloat16)
    keys_all, values_all = (
        lax.all_gather(keys_local, "seq", axis=0, tiled=True),
        lax.all_gather(values_local, "seq", axis=0, tiled=True),
    )
    query_heads = split_heads(queries)
    key_heads = split_heads(keys_all)
    value_heads = split_heads(values_all)
    posk_heads = split_heads(pos_keys)
    posq_heads = split_heads(pos_queries)

    def head_scores(query_h, key_h, posk_h, posq_h):
        content = inner_last(query_h, key_h)
        table_a = inner_last(query_h, posk_h)
        key_padded = jnp.pad(key_h, ((SPAN, SPAN), (0, 0)))
        key_window = lax.dynamic_slice_in_dim(key_padded, first_row, window, 0)
        table_w = inner_last(key_window, posq_h)
        end_rows = jnp.stack([posq_h[0], posq_h[buckets - 1]])
        edge_terms = inner_last(end_rows, key_h)
        raw = content + pos_terms(table_a, table_w, edge_terms)
        masked = jnp.where(visible, raw * score_scale, -jnp.inf)
        return (masked, table_a, table_w, edge_terms, key_window, end_rows)

    def head_forward(operands):
        query_h, key_h, value_h, posk_h, posq_h = operands
        scores = head_scores(query_h, key_h, posk_h, posq_h)[0]
        highest = jnp.max(scores, axis=1, keepdims=True)
        expo = jnp.exp(scores - highest)
        totals = jnp.sum(expo, axis=1, keepdims=True)
        probs_low = (expo / totals).astype(jnp.bfloat16)
        return (product(probs_low, value_h), (highest + jnp.log(totals))[:, 0])

    contexts, log_totals = lax.map(
        head_forward, (query_heads, key_heads, value_heads, posk_heads, posq_heads)
    )
    context = join_heads(contexts).astype(jnp.bfloat16)
    hidden_f = hidden_in.astype(jnp.float32)
    residual1 = hidden_f + product(context, full_out) + full_ob.astype(jnp.float32)
    gain1 = full_g1.astype(jnp.float32)
    shift1 = full_b1.astype(jnp.float32)
    normed = normalize(residual1, gain1, shift1)
    normed_low = normed.astype(jnp.bfloat16)
    expanded = product(normed_low, full_up) + full_ub.astype(jnp.float32)
    activated = gelu_exact(expanded).astype(jnp.bfloat16)
    residual2 = normed + product(activated, full_down) + full_db.astype(jnp.float32)
    gain2 = full_g2.astype(jnp.float32)
    shift2 = full_b2.astype(jnp.float32)
    hidden_out = normalize(residual2, gain2, shift2).astype(jnp.bfloat16)
    regathered = (
        lax.all_gather(w_qkv, ("dp", "seq"), axis=0, tiled=True),
        lax.all_gather(q_bias, ("dp", "seq"), axis=0, tiled=True),
        lax.all_gather(v_bias, ("dp", "seq"), axis=0, tiled=True),
        lax.all_gather(rel_table, ("dp", "seq"), axis=0, tiled=True),
        lax.all_gather(w_posk, ("dp", "seq"), axis=0, tiled=True),
        lax.all_gather(w_posq, ("dp", "seq"), axis=0, tiled=True),
        lax.all_gather(posq_bias, ("dp", "seq"), axis=0, tiled=True),
        lax.all_gather(w_out, ("dp", "seq"), axis=0, tiled=True),
        lax.all_gather(out_bias, ("dp", "seq"), axis=0, tiled=True),
        lax.all_gather(norm1_gain, ("dp", "seq"), axis=0, tiled=True),
        lax.all_gather(norm1_bias, ("dp", "seq"), axis=0, tiled=True),
        lax.all_gather(w_up, ("dp", "seq"), axis=0, tiled=True),
        lax.all_gather(up_bias, ("dp", "seq"), axis=0, tiled=True),
        lax.all_gather(w_down, ("dp", "seq"), axis=0, tiled=True),
        lax.all_gather(down_bias, ("dp", "seq"), axis=0, tiled=True),
        lax.all_gather(norm2_gain, ("dp", "seq"), axis=0, tiled=True),
        lax.all_gather(norm2_bias, ("dp", "seq"), axis=0, tiled=True),
    )
    (
        back_qkv,
        back_qb,
        back_vb,
        back_table,
        back_posk,
        back_posq,
        back_pqb,
        back_out,
        back_ob,
        back_g1,
        back_b1,
        back_up,
        back_ub,
        back_down,
        back_db,
        back_g2,
        back_b2,
    ) = regathered
    _, pull_second = jax.vjp(normalize, residual2, gain2, shift2)
    d_res2, d_gain2, d_shift2 = pull_second(out_grad.astype(jnp.float32))
    d_reduced = d_res2.astype(jnp.bfloat16)
    d_wdown = inner_first(activated, d_reduced)
    d_down_bias = column_sums(d_reduced)
    d_activated = inner_last(d_reduced, back_down)
    _, pull_gelu = jax.vjp(gelu_exact, expanded)
    d_expanded = pull_gelu(d_activated)[0].astype(jnp.bfloat16)
    d_wup = inner_first(normed_low, d_expanded)
    d_up_bias = column_sums(d_expanded)
    d_normed = inner_last(d_expanded, back_up) + d_res2
    _, pull_first = jax.vjp(normalize, residual1, gain1, shift1)
    d_res1, d_gain1, d_shift1 = pull_first(d_normed)
    d_attended = d_res1.astype(jnp.bfloat16)
    d_wout = inner_first(context, d_attended)
    d_out_bias = column_sums(d_attended)
    d_context = inner_last(d_attended, back_out).astype(jnp.bfloat16)
    dctx_heads = split_heads(d_context)

    def head_backward(operands):
        query_h, key_h, value_h, posk_h, posq_h, log_total, dctx_h = operands
        scores, table_a, table_w, edge_terms, key_window, end_rows = head_scores(
            query_h, key_h, posk_h, posq_h
        )
        probs = jnp.exp(scores - log_total[:, None])
        probs_low = probs.astype(jnp.bfloat16)
        d_probs = inner_last(dctx_h, value_h)
        d_value = inner_first(probs_low, dctx_h)
        row_dot = jnp.sum(probs * d_probs, axis=1, keepdims=True)
        d_raw = (probs * (d_probs - row_dot) * score_scale).astype(jnp.bfloat16)
        _, pull_terms = jax.vjp(pos_terms, table_a, table_w, edge_terms)
        d_table_a, d_table_w, d_edges = pull_terms(d_raw.astype(jnp.float32))
        d_table_a = d_table_a.astype(jnp.bfloat16)
        d_table_w = d_table_w.astype(jnp.bfloat16)
        d_edges = d_edges.astype(jnp.bfloat16)
        d_query = product(d_raw, key_h) + product(d_table_a, posk_h)
        window_grad = product(d_table_w, posq_h)
        key_canvas = jnp.zeros((seq_length + buckets, HEAD_DIM), jnp.float32)
        placed_grad = lax.dynamic_update_slice(
            key_canvas, window_grad, (first_row, jnp.zeros((), jnp.int32))
        )
        d_key = (
            inner_first(d_raw, query_h)
            + placed_grad[SPAN : SPAN + seq_length]
            + inner_first(d_edges, end_rows)
        )
        d_posk = inner_first(d_table_a, query_h)
        end_grads = product(d_edges, key_h)
        d_posq = inner_first(d_table_w, key_window)
        d_posq = d_posq.at[0].add(end_grads[0]).at[buckets - 1].add(end_grads[1])
        return (d_query, d_key, d_value, d_posk, d_posq)

    d_q_heads, d_k_heads, d_v_heads, d_posk_heads, d_posq_heads = lax.map(
        head_backward,
        (query_heads, key_heads, value_heads, posk_heads, posq_heads, log_totals, dctx_heads),
    )
    d_queries = join_heads(d_q_heads).astype(jnp.bfloat16)
    d_keys_part, d_values_part = (
        lax.psum_scatter(
            join_heads(d_k_heads).astype(jnp.bfloat16), "seq", scatter_dimension=0, tiled=True
        ).astype(jnp.float32),
        lax.psum_scatter(
            join_heads(d_v_heads).astype(jnp.bfloat16), "seq", scatter_dimension=0, tiled=True
        ).astype(jnp.float32),
    )
    d_keys = d_keys_part.astype(jnp.bfloat16)
    d_values = d_values_part.astype(jnp.bfloat16)
    d_merged = jnp.concatenate([d_queries, d_keys, d_values], axis=1)
    d_wqkv = inner_first(hidden_in, d_merged)
    d_q_bias = column_sums(d_queries)
    d_v_bias = column_sums(d_values)
    in_grad = d_res1 + inner_last(d_merged, back_qkv)
    d_posk_rows, d_posq_rows = (
        lax.psum_scatter(join_heads(d_posk_heads), ("dp", "seq"), scatter_dimension=0, tiled=True),
        lax.psum_scatter(join_heads(d_posq_heads), ("dp", "seq"), scatter_dimension=0, tiled=True),
    )
    d_posk_low = d_posk_rows.astype(jnp.bfloat16)
    d_posq_low = d_posq_rows.astype(jnp.bfloat16)
    rel_table_grad = inner_last(d_posk_low, back_posk) + inner_last(d_posq_low, back_posq)
    d_wposk = inner_first(rel_table, d_posk_low)
    d_wposq = inner_first(rel_table, d_posq_low)
    d_posq_bias = column_sums(d_posq_low)
    summed = (
        lax.psum_scatter(d_wqkv, ("dp", "seq"), scatter_dimension=0, tiled=True),
        lax.psum_scatter(d_q_bias, ("dp", "seq"), scatter_dimension=0, tiled=True),
        lax.psum_scatter(d_v_bias, ("dp", "seq"), scatter_dimension=0, tiled=True),
        lax.psum_scatter(d_wposk, ("dp", "seq"), scatter_dimension=0, tiled=True),
        lax.psum_scatter(d_wposq, ("dp", "seq"), scatter_dimension=0, tiled=True),
        lax.psum_scatter(d_posq_bias, ("dp", "seq"), scatter_dimension=0, tiled=True),
        lax.psum_scatter(d_wout, ("dp", "seq"), scatter_dimension=0, tiled=True),
        lax.psum_scatter(d_out_bias, ("dp", "seq"), scatter_dimension=0, tiled=True),
        lax.psum_scatter(d_gain1, ("dp", "seq"), scatter_dimension=0, tiled=True),
        lax.psum_scatter(d_shift1, ("dp", "seq"), scatter_dimension=0, tiled=True),
        lax.psum_scatter(d_wup, ("dp", "seq"), scatter_dimension=0, tiled=True),
        lax.psum_scatter(d_up_bias, ("dp", "seq"), scatter_dimension=0, tiled=True),
        lax.psum_scatter(d_wdown, ("dp", "seq"), scatter_dimension=0, tiled=True),
        lax.psum_scatter(d_down_bias, ("dp", "seq"), scatter_dimension=0, tiled=True),
        lax.psum_scatter(d_gain2, ("dp", "seq"), scatter_dimension=0, tiled=True),
        lax.psum_scatter(d_shift2, ("dp", "seq"), scatter_dimension=0, tiled=True),
    )
    return (
        hidden_out,
        in_grad,
        summed[0],
        summed[1],
        summed[2],
        rel_table_grad,
        summed[3],
        summed[4],
        summed[5],
        summed[6],
        summed[7],
        summed[8],
        summed[9],
        summed[10],
        summed[11],
        summed[12],
        summed[13],
        summed[14],
        summed[15],
    )


def solution(mesh):
    placed = (
        P(("dp", "seq"), None),
        P("dp"),
        P(("dp", "seq"), None),
        P(("dp", "seq")),
        P(("dp", "seq")),
        P(("dp", "seq"), None),
        P(("dp", "seq"), None),
        P(("dp", "seq"), None),
        P(("dp", "seq")),
        P(("dp", "seq"), None),
        P(("dp", "seq")),
        P(("dp", "seq")),
        P(("dp", "seq")),
        P(("dp", "seq"), None),
        P(("dp", "seq")),
        P(("dp", "seq"), None),
        P(("dp", "seq")),
        P(("dp", "seq")),
        P(("dp", "seq")),
        P(("dp", "seq"), None),
    )
    return jax.shard_map(
        head_split if dict(mesh.shape) == {"dp": 16, "seq": 2} else row_split,
        mesh=mesh,
        in_specs=placed,
        out_specs=(
            P(("dp", "seq"), None),
            P(("dp", "seq"), None),
            P(("dp", "seq"), None),
            P(("dp", "seq")),
            P(("dp", "seq")),
            P(("dp", "seq"), None),
            P(("dp", "seq"), None),
            P(("dp", "seq"), None),
            P(("dp", "seq")),
            P(("dp", "seq"), None),
            P(("dp", "seq")),
            P(("dp", "seq")),
            P(("dp", "seq")),
            P(("dp", "seq"), None),
            P(("dp", "seq")),
            P(("dp", "seq"), None),
            P(("dp", "seq")),
            P(("dp", "seq")),
            P(("dp", "seq")),
        ),
        check_vma=False,
    )
```

```python
import functools
import math

import jax
import jax.numpy as jnp
from jax import lax
from jax.experimental import pallas as pl
from jax.experimental.pallas import tpu as pltpu
from jax.sharding import PartitionSpec as P

D = 768
HEADS = 12
HEAD_DIM = 64
SPAN = 256
TILE = 128
BLOCK = 256
BAND = 768
PAIR = 2 * HEAD_DIM


eps_norm = 1e-07


def normalize(value, gain, shift):
    average = jnp.mean(value, axis=-1, keepdims=True)
    centred = value - average
    variance = jnp.mean(centred * centred, axis=-1, keepdims=True)
    return centred * lax.rsqrt(variance + eps_norm) * gain + shift


def gelu_exact(value):
    return jax.nn.gelu(value, approximate=False)


def product(left, right):
    return jnp.dot(left, right, preferred_element_type=jnp.float32)


def inner_first(left, right):
    return lax.dot_general(
        left, right, (((0,), (0,)), ((), ())), preferred_element_type=jnp.float32
    )


def inner_last(left, right):
    return lax.dot_general(
        left, right, (((1,), (1,)), ((), ())), preferred_element_type=jnp.float32
    )


def split_heads(matrix):
    return matrix.reshape(matrix.shape[0], HEADS, HEAD_DIM).transpose(1, 0, 2)


def join_heads(stacked):
    return stacked.transpose(1, 0, 2).reshape(stacked.shape[1], D)


def column_sums(matrix):
    return jnp.sum(matrix.astype(jnp.float32), axis=0)


def nn(left, right):
    return lax.dot_general(
        left, right, (((1,), (0,)), ((), ())), preferred_element_type=jnp.float32
    )


def nt(left, right):
    return lax.dot_general(
        left, right, (((1,), (1,)), ((), ())), preferred_element_type=jnp.float32
    )


def unit_matrix(size, reverse=False):
    rows = lax.broadcasted_iota(jnp.int32, (size, size), 0)
    cols = lax.broadcasted_iota(jnp.int32, (size, size), 1)
    if reverse:
        cols = size - 1 - cols
    return jnp.where(rows == cols, 1.0, 0.0).astype(jnp.bfloat16)


def turn_matrix():
    rows = lax.broadcasted_iota(jnp.int32, (BLOCK, BLOCK), 0)
    cols = lax.broadcasted_iota(jnp.int32, (BLOCK, BLOCK), 1)
    mirrored = rows // TILE * (2 * TILE) + TILE - 1 - rows
    return jnp.where(mirrored == cols, 1.0, 0.0).astype(jnp.bfloat16)


def head_lanes(head):
    lanes = lax.broadcasted_iota(jnp.int32, (1, PAIR), 1)
    return lanes // HEAD_DIM == head


def head_rows(head):
    rows = lax.broadcasted_iota(jnp.int32, (HEAD_DIM, PAIR), 0)
    cols = lax.broadcasted_iota(jnp.int32, (HEAD_DIM, PAIR), 1)
    return jnp.where(cols == rows + head * HEAD_DIM, 1.0, 0.0).astype(jnp.bfloat16)


def key_tiles(block, length):
    return max(length // 2, (block + 1) * BLOCK) // TILE


def tile_seen(query_tile, key_tile, length):
    return key_tile < key_tiles(query_tile * TILE // BLOCK, length)


def skewed(window):
    return pltpu.roll(window, 0, 1, stride=1, stride_axis=0)


def forward_body(head, prefix_ref, q_ref, k_ref, v_ref, pk_ref, pq_ref, *refs):
    ctx_ref, p_ref, wb_ref, far_ref, s_ref = refs[-5:]
    length = q_ref.shape[0]
    mine = head_lanes(head)
    prefix = prefix_ref[0]
    eye = unit_matrix(TILE)
    eye_block = unit_matrix(BLOCK)
    zero = jnp.zeros((), jnp.bfloat16)
    scale = math.log2(math.e) / math.sqrt(3 * HEAD_DIM)
    for tile in range(length // TILE):
        rows = slice(tile * TILE, (tile + 1) * TILE)
        table = nt(jnp.where(mine, k_ref[rows, :], zero), pq_ref[...])
        wb_ref[rows, :] = skewed(table)
        wb_ref[rows, 0:TILE] = table[:, BAND - TILE :]
        far_ref[rows, :] = table[:, 0:TILE]
    v_cols = nt(jnp.where(lax.broadcasted_iota(jnp.int32, (PAIR, PAIR), 0) // HEAD_DIM == head, unit_matrix(PAIR), zero), v_ref[...]).astype(jnp.bfloat16)
    for block in range(length // BLOCK):
        cols = slice(block * BLOCK, (block + 1) * BLOCK)
        q_own = jnp.where(mine, q_ref[cols, :], zero)
        skews, highs, lows = [], [], []
        for sub in range(2):
            table = nt(q_own[sub * TILE : (sub + 1) * TILE], pk_ref[...])
            skews.append(skewed(table).astype(jnp.bfloat16))
            highs.append(table[:, 0:TILE].astype(jnp.bfloat16))
            lows.append(table[:, BAND - TILE :].astype(jnp.bfloat16))
        count = key_tiles(block, length)
        highest = None
        for tile in range(count):
            rows = slice(tile * TILE, (tile + 1) * TILE)
            parts_a, parts_b = [], []
            for sub in range(2):
                step = 2 * block + sub - tile
                if step >= 3:
                    parts_a.append(highs[sub])
                    parts_b.append(wb_ref[rows, 0:TILE])
                elif step <= -3:
                    parts_a.append(lows[sub])
                    parts_b.append(far_ref[rows, :])
                else:
                    at = 384 - TILE * step
                    parts_a.append(skews[sub][:, at : at + TILE])
                    at = 384 + TILE * step
                    parts_b.append(wb_ref[rows, at : at + TILE])
            right = jnp.concatenate([jnp.concatenate(parts_a, axis=0), q_own], axis=1)
            left = jnp.concatenate([eye, k_ref[rows, :]], axis=1)
            raw = nt(left, right) + jnp.concatenate(parts_b, axis=1)
            if (tile + 1) * TILE > block * BLOCK + 1:
                keys = tile * TILE + lax.broadcasted_iota(jnp.int32, (TILE, BLOCK), 0)
                queries = block * BLOCK + lax.broadcasted_iota(jnp.int32, (TILE, BLOCK), 1)
                raw = jnp.where((keys < prefix) | (keys <= queries), raw, -jnp.inf)
            s_ref[rows, :] = raw
            top = jnp.max(raw, axis=0, keepdims=True)
            highest = top if highest is None else jnp.maximum(highest, top)
        total = jnp.zeros((1, BLOCK), jnp.float32)
        for tile in range(count):
            rows = slice(tile * TILE, (tile + 1) * TILE)
            expo = jnp.exp2((s_ref[rows, :] - highest) * scale)
            s_ref[rows, :] = expo
            total = total + jnp.sum(expo, axis=0, keepdims=True)
        inverse = 1.0 / total
        for tile in range(count):
            rows = slice(tile * TILE, (tile + 1) * TILE)
            p_ref[rows, cols] = (s_ref[rows, :] * inverse).astype(jnp.bfloat16)
        seen = count * TILE
        ctx_cols = nn(v_cols[:, :seen], p_ref[0:seen, cols]).astype(jnp.bfloat16)
        ctx = nt(eye_block, ctx_cols).astype(jnp.bfloat16)

        ctx_ref[cols, :] = ctx if head == 0 else refs[0][cols, :] + ctx


def attention_forward(prefix, merged, pos_band, pair, head, found=()):
    length, width = merged.shape[0], merged.shape[1] // 3
    pairs = width // PAIR
    tall = [pl.BlockSpec((length, PAIR), lambda p, at=at: (0, at)) for at in (pair, pairs + pair, 2 * pairs + pair)]
    band = [pl.BlockSpec((BAND, PAIR), lambda p, at=at: (0, at)) for at in (pair, pairs + pair)]
    own = pl.BlockSpec((length, PAIR), lambda p: (0, 0))
    return pl.pallas_call(
        functools.partial(forward_body, head),
        grid=(1,),
        in_specs=[pl.BlockSpec(memory_space=pltpu.SMEM)] + tall + band + [own] * len(found),
        out_specs=[own, pl.BlockSpec((length, length), lambda p: (0, 0))],
        out_shape=[
            jax.ShapeDtypeStruct((length, PAIR), jnp.bfloat16),
            jax.ShapeDtypeStruct((length, length), jnp.bfloat16),
        ],
        scratch_shapes=[
            pltpu.VMEM((length, BAND), jnp.float32),
            pltpu.VMEM((length, TILE), jnp.float32),
            pltpu.VMEM((length, BLOCK), jnp.float32),
        ],
        compiler_params=pltpu.CompilerParams(dimension_semantics=("arbitrary",), vmem_limit_bytes=24 << 20),
        cost_estimate=pl.CostEstimate(flops=3 * 10**8, transcendentals=0, bytes_accessed=3 << 20),
        name="attention_forward",
    )(prefix, merged, merged, merged, pos_band, pos_band, *found)


def backward_body(head, q_ref, k_ref, v_ref, dctx_ref, p_ref, pk_ref, pq_ref, *refs):
    dq_ref, dk_ref, dv_ref, dpk_ref, dpq_ref, dr_ref, dk_acc, dv_acc = refs[-8:]
    outs = (dq_ref, dk_ref, dv_ref)
    length = q_ref.shape[0]
    mine = head_lanes(head)
    flip = turn_matrix()
    pick = head_rows(head)
    bf = jnp.bfloat16
    zero = jnp.zeros((), bf)
    scale = 1.0 / math.sqrt(3 * HEAD_DIM)
    back = BAND - (TILE - 1)
    blank = jnp.zeros((TILE, TILE), bf)
    dk_acc[...] = jnp.zeros_like(dk_acc)
    dv_acc[...] = jnp.zeros_like(dv_acc)
    dpk = jnp.zeros((HEAD_DIM, BAND), jnp.float32)
    dpq = jnp.zeros((HEAD_DIM, BAND), jnp.float32)
    tiles = length // TILE

    def put(index, rows, value):
        earlier = jnp.zeros((), bf) if head == 0 else refs[index][rows, :]
        outs[index][rows, :] = jnp.where(mine, value.astype(bf), earlier)

    def unskew(parts):
        return pltpu.roll(jnp.concatenate(parts, axis=1), back, 1, stride=1, stride_axis=0)

    for block in range(length // BLOCK):
        cols = slice(block * BLOCK, (block + 1) * BLOCK)
        count = key_tiles(block, length)
        seen = count * TILE
        dctx = dctx_ref[cols, :]
        v_own = jnp.where(mine, v_ref[0:seen, :], zero)
        probs_low = p_ref[0:seen, cols]
        probs = probs_low.astype(jnp.float32)
        d_probs = nt(v_own, dctx)
        row_dot = jnp.sum(probs * d_probs, axis=0, keepdims=True)
        dr_ref[0:seen, cols] = (probs * ((d_probs - row_dot) * scale)).astype(bf)
        d_raw = dr_ref[0:seen, cols]
        dv_acc[0:seen, :] += nn(probs_low, dctx)
        dk_acc[0:seen, :] += nn(d_raw, q_ref[cols, :])
        turned = nt(flip, d_raw).astype(bf)
        spreads = []
        for sub in range(2):
            tile = 2 * block + sub
            own = turned[sub * TILE : (sub + 1) * TILE]

            def piece(key_tile):
                return own[:, key_tile * TILE : (key_tile + 1) * TILE]

            near = [t for t in range(count) if tile - t >= 3]
            far = [t for t in range(count) if tile - t <= -3]
            band = [blank]
            for step in (2, 1, 0, -1, -2):
                key_tile = tile - step
                band.append(piece(key_tile) if 0 <= key_tile < count else blank)
            spreads.append(
                add_edges(unskew(band), [piece(t).astype(jnp.float32) for t in near], [piece(t).astype(jnp.float32) for t in far])
            )
        spread = jnp.concatenate(spreads, axis=0)
        dq = nn(turned, k_ref[0:seen, :]) + nn(spread, pk_ref[...])
        put(0, cols, nn(flip, dq.astype(bf)))
        q_cols = nt(pick, nn(flip, q_ref[cols, :]).astype(bf)).astype(bf)
        dpk = dpk + nn(q_cols, spread)
    dpk_ref[...] = dpk
    for block in range(length // BLOCK):
        rows = slice(block * BLOCK, (block + 1) * BLOCK)
        groups, edges = [], []
        for sub in range(2):
            key_tile = 2 * block + sub
            own = slice(key_tile * TILE, (key_tile + 1) * TILE)
            seen_by = [t for t in range(tiles) if tile_seen(t, key_tile, length)]

            def held(query_tile):
                return dr_ref[own, query_tile * TILE : (query_tile + 1) * TILE]

            band = [blank]
            for step in (-2, -1, 0, 1, 2):
                query_tile = key_tile + step
                band.append(held(query_tile) if query_tile in seen_by else blank)
            ends = []
            for chosen in ([t for t in seen_by if t - key_tile <= -3], [t for t in seen_by if t - key_tile >= 3]):
                total = blank
                if chosen:
                    total = sum((held(t).astype(jnp.float32) for t in chosen[1:]), held(chosen[0]).astype(jnp.float32)).astype(bf)
                ends.append(total)
            groups.append(jnp.concatenate(band[1:] + ends, axis=1))
        turned = nn(flip, jnp.concatenate(groups, axis=0))
        width = BAND - TILE
        spreads = []
        for sub in range(2):
            own = turned[sub * TILE : (sub + 1) * TILE]
            spreads.append(
                add_edges(unskew([blank, own[:, :width].astype(bf)]), [own[:, width : width + TILE]], [own[:, width + TILE :]])
            )
        spread = jnp.concatenate(spreads, axis=0)
        d_key = nn(flip, nn(spread, pq_ref[...]).astype(bf))
        put(1, rows, dk_acc[rows, :] + d_key)
        k_cols = nt(pick, nn(flip, k_ref[rows, :]).astype(bf)).astype(bf)
        dpq = dpq + nn(k_cols, spread)
        put(2, rows, dv_acc[rows, :])
    dpq_ref[...] = dpq


def add_edges(spread, first, last):
    parts = [spread[:, 0:TILE], spread[:, TILE : BAND - TILE], spread[:, BAND - TILE :]]
    for place, tiles in ((0, first), (2, last)):
        if tiles:
            total = parts[place].astype(jnp.float32)
            for tile in tiles:
                total = total + tile
            parts[place] = total.astype(jnp.bfloat16)
    return jnp.concatenate(parts, axis=1)


def attention_backward(merged, dctx, probs, pos_band, pair, head, found=()):
    length, width = merged.shape[0], merged.shape[1] // 3
    pairs = width // PAIR
    tall = [pl.BlockSpec((length, PAIR), lambda p, at=at: (0, at)) for at in (pair, pairs + pair, 2 * pairs + pair, pair)]
    band = [pl.BlockSpec((BAND, PAIR), lambda p, at=at: (0, at)) for at in (pair, pairs + pair)]
    own = pl.BlockSpec((length, PAIR), lambda p: (0, 0))
    table = pl.BlockSpec((HEAD_DIM, BAND), lambda p: (0, 0))
    flat = jax.ShapeDtypeStruct((length, PAIR), jnp.bfloat16)
    wide = jax.ShapeDtypeStruct((HEAD_DIM, BAND), jnp.float32)
    return pl.pallas_call(
        functools.partial(backward_body, head),
        grid=(1,),
        in_specs=tall + [pl.BlockSpec((length, length), lambda p: (0, 0))] + band + [own] * len(found),
        out_specs=[own, own, own, table, table],
        out_shape=[flat, flat, flat, wide, wide],
        scratch_shapes=[
            pltpu.VMEM((length, length), jnp.bfloat16),
            pltpu.VMEM((length, PAIR), jnp.float32),
            pltpu.VMEM((length, PAIR), jnp.float32),
        ],
        compiler_params=pltpu.CompilerParams(dimension_semantics=("arbitrary",), vmem_limit_bytes=24 << 20),
        cost_estimate=pl.CostEstimate(flops=10**9, transcendentals=0, bytes_accessed=4 << 20),
        name="attention_backward",
    )(merged, merged, merged, dctx, probs, pos_band, pos_band, *found)


CORES = [(0, 1), (1, 0)]


def swap(value):
    return lax.ppermute(value, "seq", CORES)


def ordered(core, own, other, axis=0):
    return jnp.concatenate(
        [jnp.where(core == 0, own, other), jnp.where(core == 0, other, own)], axis=axis
    )


def half_of(core, matrix, axis):
    size = matrix.shape[axis] // 2
    return lax.dynamic_slice_in_dim(matrix, core * size, size, axis)


def chip_bits():
    chip = lax.axis_index("dp")
    return chip // 4, (chip // 2) % 2, chip % 2


def exchange(value, mask):
    return lax.ppermute(value, "dp", [(i, i ^ mask) for i in range(16)])


def tie(chains, others=()):
    states, others = lax.optimization_barrier(([chain.state for chain in chains], others))
    for chain, state in zip(chains, states):
        chain.state = state
    return others


class Gather:
    def __init__(self, *values):
        self.state = values

    def line(self, step):
        up = [(i, i + 4) for i in range(12) if i // 4 >= step - 1]
        down = [(i + 4, i) for i in range(12) if i // 4 <= 3 - step]
        if step == 1:
            self.state = [([value], [value]) for value in self.state]
        self.state = [
            (below + [lax.ppermute(below[-1], "dp", up)], above + [lax.ppermute(above[-1], "dp", down)])
            for below, above in self.state
        ]
        if step == 3:
            z = chip_bits()[0]
            lines = []
            for below, above in self.state:
                blocks = []
                for block in range(4):
                    options = [below[k - block] if k >= block else above[block - k] for k in range(4)]
                    blocks.append(lax.select_n(z, *options))
                lines.append(tuple(jnp.stack([b[side] for b in blocks]) for side in range(2)))
            self.state = lines

    def double(self, step):
        self.state = [(value, exchange(value, 4 * step)) for value in self.state]

    def finish_double(self, step):
        z = chip_bits()[0]
        bit = z % 2 if step == 1 else z // 2
        result = [
            jnp.stack([jnp.where(bit == 0, value, other), jnp.where(bit == 0, other, value)])
            for value, other in self.state
        ]
        if step == 2:
            result = [tuple(value[:, :, side].reshape((4,) + value.shape[3:]) for side in range(2)) for value in result]
        self.state = result

    def pair(self, step):
        masks = (1, 2) if step == 1 else (2, 1)
        self.state = [
            tuple((value, exchange(value, mask)) for value, mask in zip(halves, masks)) for halves in self.state
        ]

    def finish_pair(self, step):
        _, y, x = chip_bits()
        bits = (x, y) if step == 1 else (y, x)
        self.state = [
            tuple(
                jnp.stack([jnp.where(bit == 0, value, other), jnp.where(bit == 0, other, value)])
                for (value, other), bit in zip(halves, bits)
            )
            for halves in self.state
        ]

    def rows(self, index, low, high):
        first, second = [half[..., low:high] for half in self.state[index]]
        first = jnp.moveaxis(first, (0, 1, 2), (1, 2, 0))
        second = jnp.moveaxis(second, (0, 1, 2), (2, 1, 0))
        whole = jnp.stack([first, second], axis=3)
        return whole.reshape(-1, whole.shape[-1])


class Scatter:
    def __init__(self, *values):
        self.state = []
        for value in values:
            grid = value.reshape((4, 2, 2) + value.shape[1:])
            self.state.append((jnp.moveaxis(grid[:, :, :, 0], 2, 0), jnp.moveaxis(grid[:, :, :, 1], 1, 0)))

    def pair(self, step):
        _, y, x = chip_bits()
        order = ((x, 1), (y, 2)) if step == 1 else ((y, 2), (x, 1))
        sums = []
        for halves in self.state:
            result = []
            for value, (bit, mask) in zip(halves, order):
                keep = jnp.where(bit == 0, value[0], value[1])
                give = jnp.where(bit == 0, value[1], value[0])
                total = (keep.astype(jnp.float32) + exchange(give, mask).astype(jnp.float32)).astype(value.dtype)
                result.append(jnp.moveaxis(total, 1, 0) if step == 1 else total)
            sums.append(tuple(result) if step == 1 else (jnp.stack(result, axis=1), None, None))
        self.state = sums

    def line(self, step):
        z = chip_bits()[0]
        offset = 4 - step
        ups = [(i, i + 4) for i in range(12) if i // 4 + offset <= 3]
        downs = [(i + 4, i) for i in range(12) if i // 4 + 1 - offset >= 0]
        sums, self.totals = [], []
        for value, up, down in self.state:

            def block(at):
                options = [value[min(max(k + at, 0), 3)] for k in range(4)]
                return lax.select_n(z, *options).astype(jnp.float32)

            to_above, to_below = block(offset), block(-offset)
            if up is not None:
                to_above = to_above + up.astype(jnp.float32)
                to_below = to_below + down.astype(jnp.float32)
            up = lax.ppermute(to_above.astype(value.dtype), "dp", ups)
            down = lax.ppermute(to_below.astype(value.dtype), "dp", downs)
            sums.append((value, up, down))
            if step == 3:
                self.totals.append(block(0) + up.astype(jnp.float32) + down.astype(jnp.float32))
        self.state = sums


def norm_parts(value):
    average = jnp.mean(value, axis=-1, keepdims=True)
    centred = value - average
    variance = jnp.mean(centred * centred, axis=-1, keepdims=True)
    inverse = lax.rsqrt(variance + eps_norm)
    return centred * inverse, inverse


def norm_back(unit, inverse, gain, grad):
    scaled = grad * gain
    mean_grad = jnp.mean(scaled, axis=-1, keepdims=True)
    mean_along = jnp.mean(scaled * unit, axis=-1, keepdims=True)
    return inverse * (scaled - mean_grad - unit * mean_along)


def head_split(
    hidden_in, prefix, w_qkv, q_bias, v_bias, rel_table, w_posk, w_posq, posq_bias, w_out, out_bias,
    norm1_gain, norm1_bias, w_up, up_bias, w_down, down_bias, norm2_gain, norm2_bias, out_grad,
):
    bf = jnp.bfloat16
    f32 = jnp.float32
    core = lax.axis_index("seq")
    rows = w_qkv.shape[0]
    units = w_down.shape[0]
    table_rows = rel_table.shape[0]
    chips = 16
    half = D // 2
    ff_half = chips * units
    buckets = 2 * SPAN

    last_rows = rows - table_rows
    vectors = (q_bias, v_bias, posq_bias, out_bias, norm1_gain, norm1_bias, down_bias, norm2_gain)
    left = jnp.stack(vectors)
    right = jnp.concatenate(
        [jnp.pad(norm2_bias, (0, units - rows))[None], up_bias[None], jnp.zeros((last_rows - 2, units), bf)], axis=0
    )
    small = jnp.concatenate([jnp.pad(left, ((0, 0), (0, 128 - rows))), jnp.pad(right, ((0, 0), (0, half - 128 - units)))], axis=1)

    def columns(side):
        qkv = w_qkv.reshape(rows, 3, 2, half)[:, :, side].reshape(rows, 3 * half)
        corner = jnp.concatenate([rel_table[:, side * half : (side + 1) * half], small], axis=0)
        cut = slice(side * half, (side + 1) * half)
        up = w_up.reshape(rows, chips, 2, units)[:, :, side].reshape(rows, ff_half)
        return (
            jnp.concatenate([qkv, w_posk[:, cut], w_posq[:, cut], corner], axis=1),
            jnp.concatenate([w_out[:, cut], up], axis=1),
        )

    early0, late0 = columns(0)
    early1, late1 = columns(1)
    early_got = swap(jnp.where(core == 0, early1, early0))
    late_got = swap(jnp.where(core == 0, late1, late0))
    hidden_got = swap(hidden_in)

    def by_core(first, second, got):
        own = jnp.where(core == 0, first, second)
        return jnp.stack([jnp.where(core == 0, own, got), jnp.where(core == 0, got, own)])

    early_chain = Gather(by_core(early0, early1, early_got))
    downs = jnp.concatenate([w_down.reshape(2, 2, rows, D)[:, 0], w_down.reshape(2, 2, rows, D)[:, 1]], axis=-1)
    late_chain = Gather(jnp.concatenate([by_core(late0, late1, late_got), downs], axis=-1))
    for step in (1, 2, 3):
        early_chain.line(step)
    tie((early_chain, late_chain))
    early_chain.pair(1)
    late_chain.double(1)
    tie((early_chain, late_chain))
    early_chain.finish_pair(1)
    late_chain.finish_double(1)
    early_chain.pair(2)
    late_chain.double(2)
    early_chain.finish_pair(2)
    hidden_all = ordered(core, hidden_in, hidden_got)
    w_qkv_own = early_chain.rows(0, 0, 3 * half)
    w_pos_own = early_chain.rows(0, 3 * half, 5 * half)
    corner = early_chain.rows(0, 5 * half, 6 * half).reshape(2 * chips, rows, half)
    table_half = corner[:, :table_rows].reshape(buckets, half)
    small = corner[:, table_rows:]
    table = ordered(core, table_half, swap(table_half), axis=1)

    owner = (lax.broadcasted_iota(jnp.int32, (2 * chips, D), 1) // rows == lax.broadcasted_iota(jnp.int32, (2 * chips, D), 0)).astype(bf)
    inside = lax.broadcasted_iota(jnp.int32, (rows, D), 1) % rows == lax.broadcasted_iota(jnp.int32, (rows, D), 0)
    unit_owner = (
        2 * (lax.broadcasted_iota(jnp.int32, (2 * chips, ff_half), 1) // units) + core
        == lax.broadcasted_iota(jnp.int32, (2 * chips, ff_half), 0)
    ).astype(bf)
    unit_inside = lax.broadcasted_iota(jnp.int32, (units, ff_half), 1) % units == lax.broadcasted_iota(jnp.int32, (units, ff_half), 0)
    spots = jnp.concatenate([small[:, :, :rows], small[:, :, 128 : 128 + rows]], axis=1)
    wide = lax.dot_general(spots, owner, (((0,), (0,)), ((), ())), preferred_element_type=f32)
    lists = jnp.sum(jnp.where(inside, wide, 0.0), axis=1)
    qb, vb, pqb, ob, gain1, shift1, db, gain2, shift2 = [lists[i] for i in range(9)]
    wide = inner_first(small[:, 1, 128 : 128 + units], unit_owner)
    ub = jnp.sum(jnp.where(unit_inside, wide, 0.0), axis=0)

    band = lax.broadcasted_iota(jnp.int32, (BAND, buckets), 0)
    bucket = lax.broadcasted_iota(jnp.int32, (BAND, buckets), 1)
    chosen = (jnp.clip(SPAN + 384 - band, 0, buckets - 1) == bucket).astype(bf)
    pos_shift = jnp.concatenate([jnp.zeros((half,), f32), half_of(core, pqb, 0)])
    pos = (product(table, w_pos_own) + pos_shift).astype(bf)
    pos_band = product(chosen, pos).astype(bf)

    qkv_shift = jnp.concatenate([half_of(core, qb, 0), jnp.zeros((half,), f32), half_of(core, vb, 0)])
    merged = (product(hidden_all, w_qkv_own) + qkv_shift).astype(bf)
    merged, pos_band = tie((late_chain,), (merged, pos_band))
    late_chain.finish_double(2)
    late_chain.pair(1)
    context_parts, prob_parts = [], []
    for pair in range(half // PAIR):
        part, kept = attention_forward(prefix, merged, pos_band, pair, 0)
        prob_parts.append(kept)
        part, kept = attention_forward(prefix, merged, pos_band, pair, 1, (part,))
        prob_parts.append(kept)
        if pair == 0:
            part, merged = tie((late_chain,), (part, merged))
            late_chain.finish_pair(1)
            late_chain.pair(2)
        context_parts.append(part)
    context_parts = tie((late_chain,), context_parts)
    late_chain.finish_pair(2)
    context = jnp.concatenate(context_parts, axis=1)
    out_columns = late_chain.rows(0, 0, half)
    w_out_own = ordered(
        core, half_of(core, out_columns, 0), swap(half_of(1 - core, out_columns, 0)), axis=1
    )
    w_up_own = late_chain.rows(0, half, half + ff_half)
    down_at = half + ff_half
    down_parts = [late_chain.rows(0, at, at + D).reshape(2 * chips, rows, D) for at in (down_at, down_at + D)]
    w_down_own = jnp.stack(down_parts, axis=1).reshape(ff_half, D)

    def summed_rows(left, multiply):
        given = swap(multiply(half_of(1 - core, left, 0)).astype(bf))
        return multiply(half_of(core, left, 0)) + given.astype(f32)

    hidden_f = hidden_in.astype(f32)
    residual1 = hidden_f + summed_rows(context, lambda part: product(part, w_out_own)) + ob
    unit1, inverse1 = norm_parts(residual1)
    normed = unit1 * gain1 + shift1
    normed_low = normed.astype(bf)
    normed_all = ordered(core, normed_low, swap(normed_low))
    expanded = product(normed_all, w_up_own) + ub
    normal_cdf = 0.5 + 0.5 * lax.erf(expanded * math.sqrt(0.5))
    activated = (expanded * normal_cdf).astype(bf)
    slope = (
        normal_cdf + expanded * jnp.exp(-0.5 * expanded * expanded) * (1.0 / math.sqrt(2.0 * math.pi))
    ).astype(bf)
    activated, slope = lax.optimization_barrier((activated, slope))
    residual2 = normed + summed_rows(activated, lambda part: product(part, w_down_own)) + db
    unit2, inverse2 = norm_parts(residual2)
    hidden_out = (unit2 * gain2 + shift2).astype(bf)

    grad = out_grad.astype(f32)
    d_res2 = norm_back(unit2, inverse2, gain2, grad)
    d_gain2 = jnp.sum(grad * unit2, axis=0, keepdims=True)
    d_shift2 = jnp.sum(grad, axis=0, keepdims=True)
    d_reduced = d_res2.astype(bf)
    d_down_bias = column_sums(d_reduced)[None]
    reduced_all = ordered(core, d_reduced, swap(d_reduced))
    d_expanded = (inner_last(reduced_all, w_down_own) * slope.astype(f32)).astype(bf)
    d_normed = summed_rows(d_expanded, lambda part: inner_last(part, w_up_own)) + d_res2
    d_wdown = inner_first(activated, reduced_all).astype(bf)
    d_wup = inner_first(normed_all, d_expanded).astype(bf)
    d_up_bias = column_sums(d_expanded)
    d_res1 = norm_back(unit1, inverse1, gain1, d_normed)
    d_gain1 = jnp.sum(d_normed * unit1, axis=0, keepdims=True)
    d_shift1 = jnp.sum(d_normed, axis=0, keepdims=True)
    d_attended = d_res1.astype(bf)
    d_out_bias = column_sums(d_attended)[None]
    attended_all = ordered(core, d_attended, swap(d_attended))
    d_context = inner_last(attended_all, w_out_own).astype(bf)
    d_wout_rows = inner_first(context, attended_all).astype(bf)
    d_wout = ordered(
        core, half_of(core, d_wout_rows, 1), swap(half_of(1 - core, d_wout_rows, 1)), axis=0
    )

    def rejoin(first, second):
        own = jnp.where(core == 0, first, second)
        got = swap(jnp.where(core == 0, second, first))
        return jnp.where(core == 0, own, got), jnp.where(core == 0, got, own)

    late_cols = jnp.concatenate([d_wout, d_wup], axis=1).reshape(chips, 2, rows, half + ff_half)
    down_cols = d_wdown.reshape(chips, 2, 2, rows, D)
    late_sums = Scatter(jnp.concatenate([late_cols, down_cols[:, :, 0], down_cols[:, :, 1]], axis=-1))
    grads = []
    late_steps = {0: lambda: late_sums.pair(1), 3: lambda: late_sums.pair(2), 5: lambda: late_sums.line(1)}
    found = ()
    for index in range(half // HEAD_DIM):
        if index in late_steps:
            found, d_context = tie((late_sums,), (found, d_context))
            late_steps[index]()
        if index % 2 == 0:
            found = ()
        found = attention_backward(merged, d_context, prob_parts[index], pos_band, index // 2, index % 2, tuple(found[:3]))
        grads.append(found)
    grads[-1] = tie((late_sums,), found)
    d_merged = jnp.concatenate([g[i] for i in range(3) for g in grads[1::2]], axis=1)
    d_q, d_v = d_merged[:, :half], d_merged[:, 2 * half :]
    d_wqkv = inner_first(hidden_all, d_merged).astype(bf)
    d_q_bias = column_sums(d_q)[None]
    d_v_bias = column_sums(d_v)[None]
    d_band = jnp.concatenate([g[i] for i in (3, 4) for g in grads], axis=0).astype(bf)
    d_pos = lax.dot_general(
        chosen, d_band, (((0,), (1,)), ((), ())), preferred_element_type=f32
    )
    d_posq_bias = jnp.sum(d_pos[:, half:], axis=0, keepdims=True)
    d_pos_low = d_pos.astype(bf)
    d_wpos = inner_first(table, d_pos_low).astype(bf)
    d_table_all = inner_last(d_pos_low, w_pos_own).astype(bf)
    d_table = (
        half_of(core, d_table_all, 1).astype(f32)
        + swap(half_of(1 - core, d_table_all, 1)).astype(f32)
    ).astype(bf)

    def whole(part):
        blank = jnp.zeros_like(part)
        return ordered(core, part, blank, axis=1)

    lists_grad = jnp.concatenate(
        [whole(jnp.concatenate([d_q_bias, d_v_bias, d_posq_bias], axis=0)), d_out_bias, d_gain1, d_shift1, d_down_bias, d_gain2, d_shift2],
        axis=0,
    ).astype(bf)
    lists_grad = jnp.pad(lists_grad, ((0, 7), (0, 0)))
    pieces = jnp.where(inside, lists_grad[:, None, :], jnp.zeros((), bf)).reshape(16 * rows, D)
    unit_at = lax.broadcasted_iota(jnp.int32, (half, ff_half), 1) % units + 256 == lax.broadcasted_iota(jnp.int32, (half, ff_half), 0)
    unit_pieces = jnp.where(unit_at, d_up_bias.astype(bf), jnp.zeros((), bf))
    vector = (inner_last(owner, pieces) + inner_last(unit_owner, unit_pieces)).astype(bf)
    corner_grad = jnp.concatenate(
        [
            d_table.reshape(2 * chips, table_rows, half),
            jnp.pad(vector[:, None, :], ((0, 0), (0, last_rows - 1), (0, 0))),
        ],
        axis=1,
    ).reshape(chips * 2 * rows, half)
    early_sums = Scatter(
        jnp.concatenate([d_wqkv, d_wpos, corner_grad], axis=1).reshape(chips, 2, rows, 6 * half)
    )
    d_merged = tie((early_sums,), d_merged)
    early_sums.pair(1)
    in_grad = d_res1 + summed_rows(d_merged, lambda part: inner_last(part, w_qkv_own))
    in_grad = tie((late_sums,), in_grad)
    late_sums.line(2)
    late_sums.line(3)
    late_grads = late_sums.totals[0]
    down_grads = late_grads[:, :, half + ff_half :]
    late_grads = late_grads[:, :, : half + ff_half]
    late_left, late_right = rejoin(late_grads[0], late_grads[1])
    place = lax.broadcasted_iota(jnp.int32, (D, D), 0)
    place = (place % half) // units * (2 * units) + place // half * units + place % units
    unit_order = (place == lax.broadcasted_iota(jnp.int32, (D, D), 1)).astype(bf)
    early_sums.pair(2)
    g_wdown = jnp.stack([down_grads[:, :, :D], down_grads[:, :, D:]], axis=1).reshape(units, D)
    g_wout = jnp.concatenate([late_left[:, :half], late_right[:, :half]], axis=1)
    joined = []
    for group in range(ff_half // half):
        cut = slice(half + group * half, half + (group + 1) * half)
        joined.append(jnp.concatenate([late_left[:, cut], late_right[:, cut]], axis=1))
    joined = product(jnp.concatenate(joined, axis=0).astype(bf), unit_order)
    g_wup = jnp.concatenate([joined[g * rows : (g + 1) * rows] for g in range(ff_half // half)], axis=1)
    for step in (1, 2, 3):
        early_sums.line(step)
    early_grads = early_sums.totals[0]
    early_left, early_right = rejoin(early_grads[0], early_grads[1])
    vector_sum = early_left[table_rows, 5 * half :] + early_right[table_rows, 5 * half :]

    def side_by_side(left, right, at, count):
        pieces = []
        for index in range(count):
            cut = slice((at + index) * half, (at + index + 1) * half)
            pieces += [left[:, cut], right[:, cut]]
        return jnp.concatenate(pieces, axis=1)

    g_wqkv = side_by_side(early_left, early_right, 0, 3)
    g_wposk = side_by_side(early_left, early_right, 3, 1)
    g_wposq = side_by_side(early_left, early_right, 4, 1)
    g_table = side_by_side(early_left, early_right, 5, 1)[:table_rows]
    g = [vector_sum[i * rows : (i + 1) * rows] for i in range(9)]
    g_up_bias = vector_sum[256 : 256 + units]
    return (
        hidden_out, in_grad, g_wqkv, g[0], g[1], g_table, g_wposk, g_wposq, g[2], g_wout, g[3], g[4], g[5],
        g_wup, g_up_bias, g_wdown, g[6], g[7], g[8],
    )


def row_split(
    hidden_in,
    prefix,
    w_qkv,
    q_bias,
    v_bias,
    rel_table,
    w_posk,
    w_posq,
    posq_bias,
    w_out,
    out_bias,
    norm1_gain,
    norm1_bias,
    w_up,
    up_bias,
    w_down,
    down_bias,
    norm2_gain,
    norm2_bias,
    out_grad,
):
    gathered = (
        lax.all_gather(w_qkv, ("dp", "seq"), axis=0, tiled=True),
        lax.all_gather(q_bias, ("dp", "seq"), axis=0, tiled=True),
        lax.all_gather(v_bias, ("dp", "seq"), axis=0, tiled=True),
        lax.all_gather(rel_table, ("dp", "seq"), axis=0, tiled=True),
        lax.all_gather(w_posk, ("dp", "seq"), axis=0, tiled=True),
        lax.all_gather(w_posq, ("dp", "seq"), axis=0, tiled=True),
        lax.all_gather(posq_bias, ("dp", "seq"), axis=0, tiled=True),
        lax.all_gather(w_out, ("dp", "seq"), axis=0, tiled=True),
        lax.all_gather(out_bias, ("dp", "seq"), axis=0, tiled=True),
        lax.all_gather(norm1_gain, ("dp", "seq"), axis=0, tiled=True),
        lax.all_gather(norm1_bias, ("dp", "seq"), axis=0, tiled=True),
        lax.all_gather(w_up, ("dp", "seq"), axis=0, tiled=True),
        lax.all_gather(up_bias, ("dp", "seq"), axis=0, tiled=True),
        lax.all_gather(w_down, ("dp", "seq"), axis=0, tiled=True),
        lax.all_gather(down_bias, ("dp", "seq"), axis=0, tiled=True),
        lax.all_gather(norm2_gain, ("dp", "seq"), axis=0, tiled=True),
        lax.all_gather(norm2_bias, ("dp", "seq"), axis=0, tiled=True),
    )
    (
        full_qkv,
        full_qb,
        full_vb,
        full_table,
        full_posk,
        full_posq,
        full_pqb,
        full_out,
        full_ob,
        full_g1,
        full_b1,
        full_up,
        full_ub,
        full_down,
        full_db,
        full_g2,
        full_b2,
    ) = gathered
    row_count = hidden_in.shape[0]
    groups = lax.axis_size("seq")
    seq_length = row_count * groups
    seq_rank = lax.axis_index("seq")
    prefix_len = prefix[0]
    score_scale = 1.0 / math.sqrt(3 * HEAD_DIM)
    buckets = 2 * SPAN
    window = row_count + buckets
    first_row = seq_rank * row_count
    query_pos = first_row + jnp.arange(row_count, dtype=jnp.int32)
    key_pos = jnp.arange(seq_length, dtype=jnp.int32)
    visible = (key_pos[None, :] < prefix_len) | (key_pos[None, :] <= query_pos[:, None])
    padded_cols = jnp.arange(seq_length + buckets, dtype=jnp.int32)
    below_window = padded_cols[None, :] < first_row

    def skew_table(table, row_total, offset, col_total):
        shifted = jnp.pad(
            jnp.flip(table, axis=1), ((0, 0), (row_count, row_count - 1)), mode="edge"
        )
        stride = shifted.shape[1] - 1
        flattened = shifted.reshape(-1)
        picked = lax.slice_in_dim(flattened, offset, offset + row_total * stride)
        return picked.reshape(row_total, stride)[:, :col_total]

    def pos_terms(table_a, table_w, edge_terms):
        band_terms = (
            skew_table(table_a, row_count, row_count - 1, window)
            + skew_table(table_w, window, window - 1, row_count).T
        )
        low_side = table_a[:, buckets - 1 : buckets] + jnp.pad(edge_terms[0], (SPAN, SPAN))[None, :]
        high_side = table_a[:, 0:1] + jnp.pad(edge_terms[1], (SPAN, SPAN))[None, :]
        backdrop = jnp.where(below_window, low_side, high_side)
        placed = lax.dynamic_update_slice(
            backdrop, band_terms, (jnp.zeros((), jnp.int32), first_row)
        )
        return placed[:, SPAN : SPAN + seq_length]

    pos_keys = product(full_table, full_posk).astype(jnp.bfloat16)
    pos_queries = (product(full_table, full_posq) + full_pqb.astype(jnp.float32)).astype(
        jnp.bfloat16
    )
    merged = product(hidden_in, full_qkv)
    queries = (merged[:, :D] + full_qb.astype(jnp.float32)).astype(jnp.bfloat16)
    keys_local = merged[:, D : 2 * D].astype(jnp.bfloat16)
    values_local = (merged[:, 2 * D :] + full_vb.astype(jnp.float32)).astype(jnp.bfloat16)
    keys_all, values_all = (
        lax.all_gather(keys_local, "seq", axis=0, tiled=True),
        lax.all_gather(values_local, "seq", axis=0, tiled=True),
    )
    query_heads = split_heads(queries)
    key_heads = split_heads(keys_all)
    value_heads = split_heads(values_all)
    posk_heads = split_heads(pos_keys)
    posq_heads = split_heads(pos_queries)

    def head_scores(query_h, key_h, posk_h, posq_h):
        content = inner_last(query_h, key_h)
        table_a = inner_last(query_h, posk_h)
        key_padded = jnp.pad(key_h, ((SPAN, SPAN), (0, 0)))
        key_window = lax.dynamic_slice_in_dim(key_padded, first_row, window, 0)
        table_w = inner_last(key_window, posq_h)
        end_rows = jnp.stack([posq_h[0], posq_h[buckets - 1]])
        edge_terms = inner_last(end_rows, key_h)
        raw = content + pos_terms(table_a, table_w, edge_terms)
        masked = jnp.where(visible, raw * score_scale, -jnp.inf)
        return (masked, table_a, table_w, edge_terms, key_window, end_rows)

    def head_forward(operands):
        query_h, key_h, value_h, posk_h, posq_h = operands
        scores = head_scores(query_h, key_h, posk_h, posq_h)[0]
        highest = jnp.max(scores, axis=1, keepdims=True)
        expo = jnp.exp(scores - highest)
        totals = jnp.sum(expo, axis=1, keepdims=True)
        probs_low = (expo / totals).astype(jnp.bfloat16)
        return (product(probs_low, value_h), (highest + jnp.log(totals))[:, 0])

    contexts, log_totals = lax.map(
        head_forward, (query_heads, key_heads, value_heads, posk_heads, posq_heads)
    )
    context = join_heads(contexts).astype(jnp.bfloat16)
    hidden_f = hidden_in.astype(jnp.float32)
    residual1 = hidden_f + product(context, full_out) + full_ob.astype(jnp.float32)
    gain1 = full_g1.astype(jnp.float32)
    shift1 = full_b1.astype(jnp.float32)
    normed = normalize(residual1, gain1, shift1)
    normed_low = normed.astype(jnp.bfloat16)
    expanded = product(normed_low, full_up) + full_ub.astype(jnp.float32)
    activated = gelu_exact(expanded).astype(jnp.bfloat16)
    residual2 = normed + product(activated, full_down) + full_db.astype(jnp.float32)
    gain2 = full_g2.astype(jnp.float32)
    shift2 = full_b2.astype(jnp.float32)
    hidden_out = normalize(residual2, gain2, shift2).astype(jnp.bfloat16)
    regathered = (
        lax.all_gather(w_qkv, ("dp", "seq"), axis=0, tiled=True),
        lax.all_gather(q_bias, ("dp", "seq"), axis=0, tiled=True),
        lax.all_gather(v_bias, ("dp", "seq"), axis=0, tiled=True),
        lax.all_gather(rel_table, ("dp", "seq"), axis=0, tiled=True),
        lax.all_gather(w_posk, ("dp", "seq"), axis=0, tiled=True),
        lax.all_gather(w_posq, ("dp", "seq"), axis=0, tiled=True),
        lax.all_gather(posq_bias, ("dp", "seq"), axis=0, tiled=True),
        lax.all_gather(w_out, ("dp", "seq"), axis=0, tiled=True),
        lax.all_gather(out_bias, ("dp", "seq"), axis=0, tiled=True),
        lax.all_gather(norm1_gain, ("dp", "seq"), axis=0, tiled=True),
        lax.all_gather(norm1_bias, ("dp", "seq"), axis=0, tiled=True),
        lax.all_gather(w_up, ("dp", "seq"), axis=0, tiled=True),
        lax.all_gather(up_bias, ("dp", "seq"), axis=0, tiled=True),
        lax.all_gather(w_down, ("dp", "seq"), axis=0, tiled=True),
        lax.all_gather(down_bias, ("dp", "seq"), axis=0, tiled=True),
        lax.all_gather(norm2_gain, ("dp", "seq"), axis=0, tiled=True),
        lax.all_gather(norm2_bias, ("dp", "seq"), axis=0, tiled=True),
    )
    (
        back_qkv,
        back_qb,
        back_vb,
        back_table,
        back_posk,
        back_posq,
        back_pqb,
        back_out,
        back_ob,
        back_g1,
        back_b1,
        back_up,
        back_ub,
        back_down,
        back_db,
        back_g2,
        back_b2,
    ) = regathered
    _, pull_second = jax.vjp(normalize, residual2, gain2, shift2)
    d_res2, d_gain2, d_shift2 = pull_second(out_grad.astype(jnp.float32))
    d_reduced = d_res2.astype(jnp.bfloat16)
    d_wdown = inner_first(activated, d_reduced)
    d_down_bias = column_sums(d_reduced)
    d_activated = inner_last(d_reduced, back_down)
    _, pull_gelu = jax.vjp(gelu_exact, expanded)
    d_expanded = pull_gelu(d_activated)[0].astype(jnp.bfloat16)
    d_wup = inner_first(normed_low, d_expanded)
    d_up_bias = column_sums(d_expanded)
    d_normed = inner_last(d_expanded, back_up) + d_res2
    _, pull_first = jax.vjp(normalize, residual1, gain1, shift1)
    d_res1, d_gain1, d_shift1 = pull_first(d_normed)
    d_attended = d_res1.astype(jnp.bfloat16)
    d_wout = inner_first(context, d_attended)
    d_out_bias = column_sums(d_attended)
    d_context = inner_last(d_attended, back_out).astype(jnp.bfloat16)
    dctx_heads = split_heads(d_context)

    def head_backward(operands):
        query_h, key_h, value_h, posk_h, posq_h, log_total, dctx_h = operands
        scores, table_a, table_w, edge_terms, key_window, end_rows = head_scores(
            query_h, key_h, posk_h, posq_h
        )
        probs = jnp.exp(scores - log_total[:, None])
        probs_low = probs.astype(jnp.bfloat16)
        d_probs = inner_last(dctx_h, value_h)
        d_value = inner_first(probs_low, dctx_h)
        row_dot = jnp.sum(probs * d_probs, axis=1, keepdims=True)
        d_raw = (probs * (d_probs - row_dot) * score_scale).astype(jnp.bfloat16)
        _, pull_terms = jax.vjp(pos_terms, table_a, table_w, edge_terms)
        d_table_a, d_table_w, d_edges = pull_terms(d_raw.astype(jnp.float32))
        d_table_a = d_table_a.astype(jnp.bfloat16)
        d_table_w = d_table_w.astype(jnp.bfloat16)
        d_edges = d_edges.astype(jnp.bfloat16)
        d_query = product(d_raw, key_h) + product(d_table_a, posk_h)
        window_grad = product(d_table_w, posq_h)
        key_canvas = jnp.zeros((seq_length + buckets, HEAD_DIM), jnp.float32)
        placed_grad = lax.dynamic_update_slice(
            key_canvas, window_grad, (first_row, jnp.zeros((), jnp.int32))
        )
        d_key = (
            inner_first(d_raw, query_h)
            + placed_grad[SPAN : SPAN + seq_length]
            + inner_first(d_edges, end_rows)
        )
        d_posk = inner_first(d_table_a, query_h)
        end_grads = product(d_edges, key_h)
        d_posq = inner_first(d_table_w, key_window)
        d_posq = d_posq.at[0].add(end_grads[0]).at[buckets - 1].add(end_grads[1])
        return (d_query, d_key, d_value, d_posk, d_posq)

    d_q_heads, d_k_heads, d_v_heads, d_posk_heads, d_posq_heads = lax.map(
        head_backward,
        (query_heads, key_heads, value_heads, posk_heads, posq_heads, log_totals, dctx_heads),
    )
    d_queries = join_heads(d_q_heads).astype(jnp.bfloat16)
    d_keys_part, d_values_part = (
        lax.psum_scatter(
            join_heads(d_k_heads).astype(jnp.bfloat16), "seq", scatter_dimension=0, tiled=True
        ).astype(jnp.float32),
        lax.psum_scatter(
            join_heads(d_v_heads).astype(jnp.bfloat16), "seq", scatter_dimension=0, tiled=True
        ).astype(jnp.float32),
    )
    d_keys = d_keys_part.astype(jnp.bfloat16)
    d_values = d_values_part.astype(jnp.bfloat16)
    d_merged = jnp.concatenate([d_queries, d_keys, d_values], axis=1)
    d_wqkv = inner_first(hidden_in, d_merged)
    d_q_bias = column_sums(d_queries)
    d_v_bias = column_sums(d_values)
    in_grad = d_res1 + inner_last(d_merged, back_qkv)
    d_posk_rows, d_posq_rows = (
        lax.psum_scatter(join_heads(d_posk_heads), ("dp", "seq"), scatter_dimension=0, tiled=True),
        lax.psum_scatter(join_heads(d_posq_heads), ("dp", "seq"), scatter_dimension=0, tiled=True),
    )
    d_posk_low = d_posk_rows.astype(jnp.bfloat16)
    d_posq_low = d_posq_rows.astype(jnp.bfloat16)
    rel_table_grad = inner_last(d_posk_low, back_posk) + inner_last(d_posq_low, back_posq)
    d_wposk = inner_first(rel_table, d_posk_low)
    d_wposq = inner_first(rel_table, d_posq_low)
    d_posq_bias = column_sums(d_posq_low)
    summed = (
        lax.psum_scatter(d_wqkv, ("dp", "seq"), scatter_dimension=0, tiled=True),
        lax.psum_scatter(d_q_bias, ("dp", "seq"), scatter_dimension=0, tiled=True),
        lax.psum_scatter(d_v_bias, ("dp", "seq"), scatter_dimension=0, tiled=True),
        lax.psum_scatter(d_wposk, ("dp", "seq"), scatter_dimension=0, tiled=True),
        lax.psum_scatter(d_wposq, ("dp", "seq"), scatter_dimension=0, tiled=True),
        lax.psum_scatter(d_posq_bias, ("dp", "seq"), scatter_dimension=0, tiled=True),
        lax.psum_scatter(d_wout, ("dp", "seq"), scatter_dimension=0, tiled=True),
        lax.psum_scatter(d_out_bias, ("dp", "seq"), scatter_dimension=0, tiled=True),
        lax.psum_scatter(d_gain1, ("dp", "seq"), scatter_dimension=0, tiled=True),
        lax.psum_scatter(d_shift1, ("dp", "seq"), scatter_dimension=0, tiled=True),
        lax.psum_scatter(d_wup, ("dp", "seq"), scatter_dimension=0, tiled=True),
        lax.psum_scatter(d_up_bias, ("dp", "seq"), scatter_dimension=0, tiled=True),
        lax.psum_scatter(d_wdown, ("dp", "seq"), scatter_dimension=0, tiled=True),
        lax.psum_scatter(d_down_bias, ("dp", "seq"), scatter_dimension=0, tiled=True),
        lax.psum_scatter(d_gain2, ("dp", "seq"), scatter_dimension=0, tiled=True),
        lax.psum_scatter(d_shift2, ("dp", "seq"), scatter_dimension=0, tiled=True),
    )
    return (
        hidden_out,
        in_grad,
        summed[0],
        summed[1],
        summed[2],
        rel_table_grad,
        summed[3],
        summed[4],
        summed[5],
        summed[6],
        summed[7],
        summed[8],
        summed[9],
        summed[10],
        summed[11],
        summed[12],
        summed[13],
        summed[14],
        summed[15],
    )


def solution(mesh):
    placed = (
        P(("dp", "seq"), None),
        P("dp"),
        P(("dp", "seq"), None),
        P(("dp", "seq")),
        P(("dp", "seq")),
        P(("dp", "seq"), None),
        P(("dp", "seq"), None),
        P(("dp", "seq"), None),
        P(("dp", "seq")),
        P(("dp", "seq"), None),
        P(("dp", "seq")),
        P(("dp", "seq")),
        P(("dp", "seq")),
        P(("dp", "seq"), None),
        P(("dp", "seq")),
        P(("dp", "seq"), None),
        P(("dp", "seq")),
        P(("dp", "seq")),
        P(("dp", "seq")),
        P(("dp", "seq"), None),
    )
    return jax.shard_map(
        head_split if dict(mesh.shape) == {"dp": 16, "seq": 2} else row_split,
        mesh=mesh,
        in_specs=placed,
        out_specs=(
            P(("dp", "seq"), None),
            P(("dp", "seq"), None),
            P(("dp", "seq"), None),
            P(("dp", "seq")),
            P(("dp", "seq")),
            P(("dp", "seq"), None),
            P(("dp", "seq"), None),
            P(("dp", "seq"), None),
            P(("dp", "seq")),
            P(("dp", "seq"), None),
            P(("dp", "seq")),
            P(("dp", "seq")),
            P(("dp", "seq")),
            P(("dp", "seq"), None),
            P(("dp", "seq")),
            P(("dp", "seq"), None),
            P(("dp", "seq")),
            P(("dp", "seq")),
            P(("dp", "seq")),
        ),
        check_vma=False,
    )
```

```python
import functools
import math

import jax
import jax.numpy as jnp
from jax import lax
from jax.experimental import pallas as pl
from jax.experimental.pallas import tpu as pltpu
from jax.sharding import PartitionSpec as P

D = 768
HEADS = 12
HEAD_DIM = 64
SPAN = 256
TILE = 128
BLOCK = 256
BAND = 768
PAIR = 2 * HEAD_DIM


eps_norm = 1e-07


def normalize(value, gain, shift):
    average = jnp.mean(value, axis=-1, keepdims=True)
    centred = value - average
    variance = jnp.mean(centred * centred, axis=-1, keepdims=True)
    return centred * lax.rsqrt(variance + eps_norm) * gain + shift


def gelu_exact(value):
    return jax.nn.gelu(value, approximate=False)


def product(left, right):
    return jnp.dot(left, right, preferred_element_type=jnp.float32)


def inner_first(left, right):
    return lax.dot_general(
        left, right, (((0,), (0,)), ((), ())), preferred_element_type=jnp.float32
    )


def inner_last(left, right):
    return lax.dot_general(
        left, right, (((1,), (1,)), ((), ())), preferred_element_type=jnp.float32
    )


def split_heads(matrix):
    return matrix.reshape(matrix.shape[0], HEADS, HEAD_DIM).transpose(1, 0, 2)


def join_heads(stacked):
    return stacked.transpose(1, 0, 2).reshape(stacked.shape[1], D)


def column_sums(matrix):
    return jnp.sum(matrix.astype(jnp.float32), axis=0)


def nn(left, right):
    return lax.dot_general(
        left, right, (((1,), (0,)), ((), ())), preferred_element_type=jnp.float32
    )


def nt(left, right):
    return lax.dot_general(
        left, right, (((1,), (1,)), ((), ())), preferred_element_type=jnp.float32
    )


def unit_matrix(size, reverse=False):
    rows = lax.broadcasted_iota(jnp.int32, (size, size), 0)
    cols = lax.broadcasted_iota(jnp.int32, (size, size), 1)
    if reverse:
        cols = size - 1 - cols
    return jnp.where(rows == cols, 1.0, 0.0).astype(jnp.bfloat16)


def turn_matrix():
    rows = lax.broadcasted_iota(jnp.int32, (BLOCK, BLOCK), 0)
    cols = lax.broadcasted_iota(jnp.int32, (BLOCK, BLOCK), 1)
    mirrored = rows // TILE * (2 * TILE) + TILE - 1 - rows
    return jnp.where(mirrored == cols, 1.0, 0.0).astype(jnp.bfloat16)


def head_lanes(head):
    lanes = lax.broadcasted_iota(jnp.int32, (1, PAIR), 1)
    return lanes // HEAD_DIM == head


def head_rows(head):
    rows = lax.broadcasted_iota(jnp.int32, (HEAD_DIM, PAIR), 0)
    cols = lax.broadcasted_iota(jnp.int32, (HEAD_DIM, PAIR), 1)
    return jnp.where(cols == rows + head * HEAD_DIM, 1.0, 0.0).astype(jnp.bfloat16)


def key_tiles(block, length):
    return max(length // 2, (block + 1) * BLOCK) // TILE


def tile_seen(query_tile, key_tile, length):
    return key_tile < key_tiles(query_tile * TILE // BLOCK, length)


def skewed(window):
    return pltpu.roll(window, 0, 1, stride=1, stride_axis=0)


def forward_body(head, prefix_ref, q_ref, k_ref, v_ref, pk_ref, pq_ref, *refs):
    ctx_ref, p_ref, wb_ref, far_ref, s_ref = refs[-5:]
    length = q_ref.shape[0]
    mine = head_lanes(head)
    prefix = prefix_ref[0]
    eye = unit_matrix(TILE)
    eye_block = unit_matrix(BLOCK)
    zero = jnp.zeros((), jnp.bfloat16)
    scale = math.log2(math.e) / math.sqrt(3 * HEAD_DIM)
    for tile in range(length // TILE):
        rows = slice(tile * TILE, (tile + 1) * TILE)
        table = nt(jnp.where(mine, k_ref[rows, :], zero), pq_ref[...])
        wb_ref[rows, :] = skewed(table)
        wb_ref[rows, 0:TILE] = table[:, BAND - TILE :]
        far_ref[rows, :] = table[:, 0:TILE]
    v_cols = nt(jnp.where(lax.broadcasted_iota(jnp.int32, (PAIR, PAIR), 0) // HEAD_DIM == head, unit_matrix(PAIR), zero), v_ref[...]).astype(jnp.bfloat16)
    for block in range(length // BLOCK):
        cols = slice(block * BLOCK, (block + 1) * BLOCK)
        q_own = jnp.where(mine, q_ref[cols, :], zero)
        skews, highs, lows = [], [], []
        for sub in range(2):
            table = nt(q_own[sub * TILE : (sub + 1) * TILE], pk_ref[...])
            skews.append(skewed(table).astype(jnp.bfloat16))
            highs.append(table[:, 0:TILE].astype(jnp.bfloat16))
            lows.append(table[:, BAND - TILE :].astype(jnp.bfloat16))
        count = key_tiles(block, length)
        highest = None
        for tile in range(count):
            rows = slice(tile * TILE, (tile + 1) * TILE)
            parts_a, parts_b = [], []
            for sub in range(2):
                step = 2 * block + sub - tile
                if step >= 3:
                    parts_a.append(highs[sub])
                    parts_b.append(wb_ref[rows, 0:TILE])
                elif step <= -3:
                    parts_a.append(lows[sub])
                    parts_b.append(far_ref[rows, :])
                else:
                    at = 384 - TILE * step
                    parts_a.append(skews[sub][:, at : at + TILE])
                    at = 384 + TILE * step
                    parts_b.append(wb_ref[rows, at : at + TILE])
            right = jnp.concatenate([jnp.concatenate(parts_a, axis=0), q_own], axis=1)
            left = jnp.concatenate([eye, k_ref[rows, :]], axis=1)
            raw = nt(left, right) + jnp.concatenate(parts_b, axis=1)
            if (tile + 1) * TILE > block * BLOCK + 1:
                keys = tile * TILE + lax.broadcasted_iota(jnp.int32, (TILE, BLOCK), 0)
                queries = block * BLOCK + lax.broadcasted_iota(jnp.int32, (TILE, BLOCK), 1)
                raw = jnp.where((keys < prefix) | (keys <= queries), raw, -jnp.inf)
            s_ref[rows, :] = raw
            top = jnp.max(raw, axis=0, keepdims=True)
            highest = top if highest is None else jnp.maximum(highest, top)
        total = jnp.zeros((1, BLOCK), jnp.float32)
        for tile in range(count):
            rows = slice(tile * TILE, (tile + 1) * TILE)
            expo = jnp.exp2((s_ref[rows, :] - highest) * scale)
            s_ref[rows, :] = expo
            total = total + jnp.sum(expo, axis=0, keepdims=True)
        inverse = 1.0 / total
        for tile in range(count):
            rows = slice(tile * TILE, (tile + 1) * TILE)
            p_ref[rows, cols] = (s_ref[rows, :] * inverse).astype(jnp.bfloat16)
        seen = count * TILE
        ctx_cols = nn(v_cols[:, :seen], p_ref[0:seen, cols]).astype(jnp.bfloat16)
        ctx = nt(eye_block, ctx_cols).astype(jnp.bfloat16)

        ctx_ref[cols, :] = ctx if head == 0 else refs[0][cols, :] + ctx


def attention_forward(prefix, merged, pos_band, pair, head, found=()):
    length, width = merged.shape[0], merged.shape[1] // 3
    pairs = width // PAIR
    tall = [pl.BlockSpec((length, PAIR), lambda p, at=at: (0, at)) for at in (pair, pairs + pair, 2 * pairs + pair)]
    band = [pl.BlockSpec((BAND, PAIR), lambda p, at=at: (0, at)) for at in (pair, pairs + pair)]
    own = pl.BlockSpec((length, PAIR), lambda p: (0, 0))
    return pl.pallas_call(
        functools.partial(forward_body, head),
        grid=(1,),
        in_specs=[pl.BlockSpec(memory_space=pltpu.SMEM)] + tall + band + [own] * len(found),
        out_specs=[own, pl.BlockSpec((length, length), lambda p: (0, 0))],
        out_shape=[
            jax.ShapeDtypeStruct((length, PAIR), jnp.bfloat16),
            jax.ShapeDtypeStruct((length, length), jnp.bfloat16),
        ],
        scratch_shapes=[
            pltpu.VMEM((length, BAND), jnp.float32),
            pltpu.VMEM((length, TILE), jnp.float32),
            pltpu.VMEM((length, BLOCK), jnp.float32),
        ],
        compiler_params=pltpu.CompilerParams(dimension_semantics=("arbitrary",), vmem_limit_bytes=24 << 20),
        cost_estimate=pl.CostEstimate(flops=3 * 10**8, transcendentals=0, bytes_accessed=3 << 20),
        name="attention_forward",
    )(prefix, merged, merged, merged, pos_band, pos_band, *found)


def backward_body(head, q_ref, k_ref, v_ref, dctx_ref, p_ref, pk_ref, pq_ref, *refs):
    dq_ref, dk_ref, dv_ref, dpk_ref, dpq_ref, dr_ref, dk_acc, dv_acc = refs[-8:]
    outs = (dq_ref, dk_ref, dv_ref)
    length = q_ref.shape[0]
    mine = head_lanes(head)
    flip = turn_matrix()
    pick = head_rows(head)
    bf = jnp.bfloat16
    zero = jnp.zeros((), bf)
    scale = 1.0 / math.sqrt(3 * HEAD_DIM)
    back = BAND - (TILE - 1)
    blank = jnp.zeros((TILE, TILE), bf)
    dk_acc[...] = jnp.zeros_like(dk_acc)
    dv_acc[...] = jnp.zeros_like(dv_acc)
    dpk = jnp.zeros((HEAD_DIM, BAND), jnp.float32)
    dpq = jnp.zeros((HEAD_DIM, BAND), jnp.float32)
    tiles = length // TILE

    def put(index, rows, value):
        earlier = jnp.zeros((), bf) if head == 0 else refs[index][rows, :]
        outs[index][rows, :] = jnp.where(mine, value.astype(bf), earlier)

    def unskew(parts):
        return pltpu.roll(jnp.concatenate(parts, axis=1), back, 1, stride=1, stride_axis=0)

    for block in range(length // BLOCK):
        cols = slice(block * BLOCK, (block + 1) * BLOCK)
        count = key_tiles(block, length)
        seen = count * TILE
        dctx = dctx_ref[cols, :]
        v_own = jnp.where(mine, v_ref[0:seen, :], zero)
        probs_low = p_ref[0:seen, cols]
        probs = probs_low.astype(jnp.float32)
        d_probs = nt(v_own, dctx)
        row_dot = jnp.sum(probs * d_probs, axis=0, keepdims=True)
        dr_ref[0:seen, cols] = (probs * ((d_probs - row_dot) * scale)).astype(bf)
        d_raw = dr_ref[0:seen, cols]
        dv_acc[0:seen, :] += nn(probs_low, dctx)
        dk_acc[0:seen, :] += nn(d_raw, q_ref[cols, :])
        turned = nt(flip, d_raw).astype(bf)
        spreads = []
        for sub in range(2):
            tile = 2 * block + sub
            own = turned[sub * TILE : (sub + 1) * TILE]

            def piece(key_tile):
                return own[:, key_tile * TILE : (key_tile + 1) * TILE]

            near = [t for t in range(count) if tile - t >= 3]
            far = [t for t in range(count) if tile - t <= -3]
            band = [blank]
            for step in (2, 1, 0, -1, -2):
                key_tile = tile - step
                band.append(piece(key_tile) if 0 <= key_tile < count else blank)
            spreads.append(
                add_edges(unskew(band), [piece(t).astype(jnp.float32) for t in near], [piece(t).astype(jnp.float32) for t in far])
            )
        spread = jnp.concatenate(spreads, axis=0)
        dq = nn(turned, k_ref[0:seen, :]) + nn(spread, pk_ref[...])
        put(0, cols, nn(flip, dq.astype(bf)))
        q_cols = nt(pick, nn(flip, q_ref[cols, :]).astype(bf)).astype(bf)
        dpk = dpk + nn(q_cols, spread)
    dpk_ref[...] = dpk
    for block in range(length // BLOCK):
        rows = slice(block * BLOCK, (block + 1) * BLOCK)
        groups, edges = [], []
        for sub in range(2):
            key_tile = 2 * block + sub
            own = slice(key_tile * TILE, (key_tile + 1) * TILE)
            seen_by = [t for t in range(tiles) if tile_seen(t, key_tile, length)]

            def held(query_tile):
                return dr_ref[own, query_tile * TILE : (query_tile + 1) * TILE]

            band = [blank]
            for step in (-2, -1, 0, 1, 2):
                query_tile = key_tile + step
                band.append(held(query_tile) if query_tile in seen_by else blank)
            ends = []
            for chosen in ([t for t in seen_by if t - key_tile <= -3], [t for t in seen_by if t - key_tile >= 3]):
                total = blank
                if chosen:
                    total = sum((held(t).astype(jnp.float32) for t in chosen[1:]), held(chosen[0]).astype(jnp.float32)).astype(bf)
                ends.append(total)
            groups.append(jnp.concatenate(band[1:] + ends, axis=1))
        turned = nn(flip, jnp.concatenate(groups, axis=0))
        width = BAND - TILE
        spreads = []
        for sub in range(2):
            own = turned[sub * TILE : (sub + 1) * TILE]
            spreads.append(
                add_edges(unskew([blank, own[:, :width].astype(bf)]), [own[:, width : width + TILE]], [own[:, width + TILE :]])
            )
        spread = jnp.concatenate(spreads, axis=0)
        d_key = nn(flip, nn(spread, pq_ref[...]).astype(bf))
        put(1, rows, dk_acc[rows, :] + d_key)
        k_cols = nt(pick, nn(flip, k_ref[rows, :]).astype(bf)).astype(bf)
        dpq = dpq + nn(k_cols, spread)
        put(2, rows, dv_acc[rows, :])
    dpq_ref[...] = dpq


def add_edges(spread, first, last):
    parts = [spread[:, 0:TILE], spread[:, TILE : BAND - TILE], spread[:, BAND - TILE :]]
    for place, tiles in ((0, first), (2, last)):
        if tiles:
            total = parts[place].astype(jnp.float32)
            for tile in tiles:
                total = total + tile
            parts[place] = total.astype(jnp.bfloat16)
    return jnp.concatenate(parts, axis=1)


def attention_backward(merged, dctx, probs, pos_band, pair, head, found=()):
    length, width = merged.shape[0], merged.shape[1] // 3
    pairs = width // PAIR
    tall = [pl.BlockSpec((length, PAIR), lambda p, at=at: (0, at)) for at in (pair, pairs + pair, 2 * pairs + pair, pair)]
    band = [pl.BlockSpec((BAND, PAIR), lambda p, at=at: (0, at)) for at in (pair, pairs + pair)]
    own = pl.BlockSpec((length, PAIR), lambda p: (0, 0))
    table = pl.BlockSpec((HEAD_DIM, BAND), lambda p: (0, 0))
    flat = jax.ShapeDtypeStruct((length, PAIR), jnp.bfloat16)
    wide = jax.ShapeDtypeStruct((HEAD_DIM, BAND), jnp.float32)
    return pl.pallas_call(
        functools.partial(backward_body, head),
        grid=(1,),
        in_specs=tall + [pl.BlockSpec((length, length), lambda p: (0, 0))] + band + [own] * len(found),
        out_specs=[own, own, own, table, table],
        out_shape=[flat, flat, flat, wide, wide],
        scratch_shapes=[
            pltpu.VMEM((length, length), jnp.bfloat16),
            pltpu.VMEM((length, PAIR), jnp.float32),
            pltpu.VMEM((length, PAIR), jnp.float32),
        ],
        compiler_params=pltpu.CompilerParams(dimension_semantics=("arbitrary",), vmem_limit_bytes=24 << 20),
        cost_estimate=pl.CostEstimate(flops=10**9, transcendentals=0, bytes_accessed=4 << 20),
        name="attention_backward",
    )(merged, merged, merged, dctx, probs, pos_band, pos_band, *found)


CORES = [(0, 1), (1, 0)]


def swap(value):
    return lax.ppermute(value, "seq", CORES)


def ordered(core, own, other, axis=0):
    return jnp.concatenate(
        [jnp.where(core == 0, own, other), jnp.where(core == 0, other, own)], axis=axis
    )


def half_of(core, matrix, axis):
    size = matrix.shape[axis] // 2
    return lax.dynamic_slice_in_dim(matrix, core * size, size, axis)


def chip_bits():
    chip = lax.axis_index("dp")
    return chip // 4, (chip // 2) % 2, chip % 2


def exchange(value, mask):
    return lax.ppermute(value, "dp", [(i, i ^ mask) for i in range(16)])


def tie(chains, others=()):
    states, others = lax.optimization_barrier(([chain.state for chain in chains], others))
    for chain, state in zip(chains, states):
        chain.state = state
    return others


class Gather:
    def __init__(self, *values):
        self.state = values

    def line(self, step):
        up = [(i, i + 4) for i in range(12) if i // 4 >= step - 1]
        down = [(i + 4, i) for i in range(12) if i // 4 <= 3 - step]
        if step == 1:
            self.state = [([value], [value]) for value in self.state]
        self.state = [
            (below + [lax.ppermute(below[-1], "dp", up)], above + [lax.ppermute(above[-1], "dp", down)])
            for below, above in self.state
        ]
        if step == 3:
            z = chip_bits()[0]
            lines = []
            for below, above in self.state:
                blocks = []
                for block in range(4):
                    options = [below[k - block] if k >= block else above[block - k] for k in range(4)]
                    blocks.append(lax.select_n(z, *options))
                lines.append(tuple(jnp.stack([b[side] for b in blocks]) for side in range(2)))
            self.state = lines

    def double(self, step):
        self.state = [(value, exchange(value, 4 * step)) for value in self.state]

    def finish_double(self, step):
        z = chip_bits()[0]
        bit = z % 2 if step == 1 else z // 2
        result = [
            jnp.stack([jnp.where(bit == 0, value, other), jnp.where(bit == 0, other, value)])
            for value, other in self.state
        ]
        if step == 2:
            result = [tuple(value[:, :, side].reshape((4,) + value.shape[3:]) for side in range(2)) for value in result]
        self.state = result

    def pair(self, step):
        masks = (1, 2) if step == 1 else (2, 1)
        self.state = [
            tuple((value, exchange(value, mask)) for value, mask in zip(halves, masks)) for halves in self.state
        ]

    def finish_pair(self, step):
        _, y, x = chip_bits()
        bits = (x, y) if step == 1 else (y, x)
        self.state = [
            tuple(
                jnp.stack([jnp.where(bit == 0, value, other), jnp.where(bit == 0, other, value)])
                for (value, other), bit in zip(halves, bits)
            )
            for halves in self.state
        ]

    def rows(self, index, low, high):
        first, second = [half[..., low:high] for half in self.state[index]]
        first = jnp.moveaxis(first, (0, 1, 2), (1, 2, 0))
        second = jnp.moveaxis(second, (0, 1, 2), (2, 1, 0))
        whole = jnp.stack([first, second], axis=3)
        return whole.reshape(-1, whole.shape[-1])


class Scatter:
    def __init__(self, *values):
        self.state = []
        for value in values:
            grid = value.reshape((4, 2, 2) + value.shape[1:])
            self.state.append((jnp.moveaxis(grid[:, :, :, 0], 2, 0), jnp.moveaxis(grid[:, :, :, 1], 1, 0)))

    def pair(self, step):
        _, y, x = chip_bits()
        order = ((x, 1), (y, 2)) if step == 1 else ((y, 2), (x, 1))
        sums = []
        for halves in self.state:
            result = []
            for value, (bit, mask) in zip(halves, order):
                keep = jnp.where(bit == 0, value[0], value[1])
                give = jnp.where(bit == 0, value[1], value[0])
                total = (keep.astype(jnp.float32) + exchange(give, mask).astype(jnp.float32)).astype(value.dtype)
                result.append(jnp.moveaxis(total, 1, 0) if step == 1 else total)
            sums.append(tuple(result) if step == 1 else (jnp.stack(result, axis=1), None, None))
        self.state = sums

    def line(self, step):
        z = chip_bits()[0]
        offset = 4 - step
        ups = [(i, i + 4) for i in range(12) if i // 4 + offset <= 3]
        downs = [(i + 4, i) for i in range(12) if i // 4 + 1 - offset >= 0]
        sums, self.totals = [], []
        for value, up, down in self.state:

            def block(at):
                options = [value[min(max(k + at, 0), 3)] for k in range(4)]
                return lax.select_n(z, *options).astype(jnp.float32)

            to_above, to_below = block(offset), block(-offset)
            if up is not None:
                to_above = to_above + up.astype(jnp.float32)
                to_below = to_below + down.astype(jnp.float32)
            up = lax.ppermute(to_above.astype(value.dtype), "dp", ups)
            down = lax.ppermute(to_below.astype(value.dtype), "dp", downs)
            sums.append((value, up, down))
            if step == 3:
                self.totals.append(block(0) + up.astype(jnp.float32) + down.astype(jnp.float32))
        self.state = sums


def norm_parts(value):
    average = jnp.mean(value, axis=-1, keepdims=True)
    centred = value - average
    variance = jnp.mean(centred * centred, axis=-1, keepdims=True)
    inverse = lax.rsqrt(variance + eps_norm)
    return centred * inverse, inverse


def norm_back(unit, inverse, gain, grad):
    scaled = grad * gain
    mean_grad = jnp.mean(scaled, axis=-1, keepdims=True)
    mean_along = jnp.mean(scaled * unit, axis=-1, keepdims=True)
    return inverse * (scaled - mean_grad - unit * mean_along)


def head_split(
    hidden_in, prefix, w_qkv, q_bias, v_bias, rel_table, w_posk, w_posq, posq_bias, w_out, out_bias,
    norm1_gain, norm1_bias, w_up, up_bias, w_down, down_bias, norm2_gain, norm2_bias, out_grad,
):
    bf = jnp.bfloat16
    f32 = jnp.float32
    core = lax.axis_index("seq")
    rows = w_qkv.shape[0]
    units = w_down.shape[0]
    table_rows = rel_table.shape[0]
    chips = 16
    half = D // 2
    ff_half = chips * units
    buckets = 2 * SPAN

    last_rows = rows - table_rows
    vectors = (q_bias, v_bias, posq_bias, out_bias, norm1_gain, norm1_bias, down_bias, norm2_gain)
    left = jnp.stack(vectors)
    right = jnp.concatenate(
        [jnp.pad(norm2_bias, (0, units - rows))[None], up_bias[None], jnp.zeros((last_rows - 2, units), bf)], axis=0
    )
    small = jnp.concatenate([jnp.pad(left, ((0, 0), (0, 128 - rows))), jnp.pad(right, ((0, 0), (0, half - 128 - units)))], axis=1)

    def columns(side):
        qkv = w_qkv.reshape(rows, 3, 2, half)[:, :, side].reshape(rows, 3 * half)
        corner = jnp.concatenate([rel_table[:, side * half : (side + 1) * half], small], axis=0)
        cut = slice(side * half, (side + 1) * half)
        up = w_up.reshape(rows, chips, 2, units)[:, :, side].reshape(rows, ff_half)
        return (
            jnp.concatenate([qkv, w_posk[:, cut], w_posq[:, cut], corner], axis=1),
            jnp.concatenate([w_out[:, cut], up], axis=1),
        )

    early0, late0 = columns(0)
    early1, late1 = columns(1)
    early_got = swap(jnp.where(core == 0, early1, early0))
    late_got = swap(jnp.where(core == 0, late1, late0))
    hidden_got = swap(hidden_in)

    def by_core(first, second, got):
        own = jnp.where(core == 0, first, second)
        return jnp.stack([jnp.where(core == 0, own, got), jnp.where(core == 0, got, own)])

    early_chain = Gather(by_core(early0, early1, early_got))
    downs = jnp.concatenate([w_down.reshape(2, 2, rows, D)[:, 0], w_down.reshape(2, 2, rows, D)[:, 1]], axis=-1)
    late_chain = Gather(jnp.concatenate([by_core(late0, late1, late_got), downs], axis=-1))
    for step in (1, 2, 3):
        early_chain.line(step)
    tie((early_chain, late_chain))
    early_chain.pair(1)
    late_chain.double(1)
    tie((early_chain, late_chain))
    early_chain.finish_pair(1)
    late_chain.finish_double(1)
    early_chain.pair(2)
    late_chain.double(2)
    early_chain.finish_pair(2)
    hidden_all = ordered(core, hidden_in, hidden_got)
    w_qkv_own = early_chain.rows(0, 0, 3 * half)
    w_pos_own = early_chain.rows(0, 3 * half, 5 * half)
    corner = early_chain.rows(0, 5 * half, 6 * half).reshape(2 * chips, rows, half)
    table_half = corner[:, :table_rows].reshape(buckets, half)
    small = corner[:, table_rows:]
    table = ordered(core, table_half, swap(table_half), axis=1)

    owner = (lax.broadcasted_iota(jnp.int32, (2 * chips, D), 1) // rows == lax.broadcasted_iota(jnp.int32, (2 * chips, D), 0)).astype(bf)
    inside = lax.broadcasted_iota(jnp.int32, (rows, D), 1) % rows == lax.broadcasted_iota(jnp.int32, (rows, D), 0)
    unit_owner = (
        2 * (lax.broadcasted_iota(jnp.int32, (2 * chips, ff_half), 1) // units) + core
        == lax.broadcasted_iota(jnp.int32, (2 * chips, ff_half), 0)
    ).astype(bf)
    unit_inside = lax.broadcasted_iota(jnp.int32, (units, ff_half), 1) % units == lax.broadcasted_iota(jnp.int32, (units, ff_half), 0)
    spots = jnp.concatenate([small[:, :, :rows], small[:, :, 128 : 128 + rows]], axis=1)
    wide = lax.dot_general(spots, owner, (((0,), (0,)), ((), ())), preferred_element_type=f32)
    lists = jnp.sum(jnp.where(inside, wide, 0.0), axis=1)
    qb, vb, pqb, ob, gain1, shift1, db, gain2, shift2 = [lists[i] for i in range(9)]
    wide = inner_first(small[:, 1, 128 : 128 + units], unit_owner)
    ub = jnp.sum(jnp.where(unit_inside, wide, 0.0), axis=0)

    band = lax.broadcasted_iota(jnp.int32, (BAND, buckets), 0)
    bucket = lax.broadcasted_iota(jnp.int32, (BAND, buckets), 1)
    chosen = (jnp.clip(SPAN + 384 - band, 0, buckets - 1) == bucket).astype(bf)
    pos_shift = jnp.concatenate([jnp.zeros((half,), f32), half_of(core, pqb, 0)])
    pos = (product(table, w_pos_own) + pos_shift).astype(bf)
    pos_band = product(chosen, pos).astype(bf)

    qkv_shift = jnp.concatenate([half_of(core, qb, 0), jnp.zeros((half,), f32), half_of(core, vb, 0)])
    merged = (product(hidden_all, w_qkv_own) + qkv_shift).astype(bf)
    merged, pos_band = tie((late_chain,), (merged, pos_band))
    late_chain.finish_double(2)
    late_chain.pair(1)
    context_parts, prob_parts = [], []
    for pair in range(half // PAIR):
        part, kept = attention_forward(prefix, merged, pos_band, pair, 0)
        prob_parts.append(kept)
        part, kept = attention_forward(prefix, merged, pos_band, pair, 1, (part,))
        prob_parts.append(kept)
        if pair == 0:
            part, merged = tie((late_chain,), (part, merged))
            late_chain.finish_pair(1)
            late_chain.pair(2)
        context_parts.append(part)
    context_parts = tie((late_chain,), context_parts)
    late_chain.finish_pair(2)
    context = jnp.concatenate(context_parts, axis=1)
    out_columns = late_chain.rows(0, 0, half)
    w_out_own = ordered(
        core, half_of(core, out_columns, 0), swap(half_of(1 - core, out_columns, 0)), axis=1
    )
    w_up_own = late_chain.rows(0, half, half + ff_half)
    down_at = half + ff_half
    down_parts = [late_chain.rows(0, at, at + D).reshape(2 * chips, rows, D) for at in (down_at, down_at + D)]
    w_down_own = jnp.stack(down_parts, axis=1).reshape(ff_half, D)

    def summed_rows(left, multiply):
        given = swap(multiply(half_of(1 - core, left, 0)).astype(bf))
        return multiply(half_of(core, left, 0)) + given.astype(f32)

    hidden_f = hidden_in.astype(f32)
    residual1 = hidden_f + summed_rows(context, lambda part: product(part, w_out_own)) + ob
    unit1, inverse1 = norm_parts(residual1)
    normed = unit1 * gain1 + shift1
    normed_low = normed.astype(bf)
    normed_all = ordered(core, normed_low, swap(normed_low))
    expanded = product(normed_all, w_up_own) + ub
    normal_cdf = 0.5 + 0.5 * lax.erf(expanded * math.sqrt(0.5))
    activated = (expanded * normal_cdf).astype(bf)
    slope = (
        normal_cdf + expanded * jnp.exp(-0.5 * expanded * expanded) * (1.0 / math.sqrt(2.0 * math.pi))
    ).astype(bf)
    activated, slope = lax.optimization_barrier((activated, slope))
    residual2 = normed + summed_rows(activated, lambda part: product(part, w_down_own)) + db
    unit2, inverse2 = norm_parts(residual2)
    hidden_out = (unit2 * gain2 + shift2).astype(bf)

    grad = out_grad.astype(f32)
    d_res2 = norm_back(unit2, inverse2, gain2, grad)
    d_gain2 = jnp.sum(grad * unit2, axis=0, keepdims=True)
    d_shift2 = jnp.sum(grad, axis=0, keepdims=True)
    d_reduced = d_res2.astype(bf)
    d_down_bias = column_sums(d_reduced)[None]
    reduced_all = ordered(core, d_reduced, swap(d_reduced))
    d_expanded = (inner_last(reduced_all, w_down_own) * slope.astype(f32)).astype(bf)
    d_normed = summed_rows(d_expanded, lambda part: inner_last(part, w_up_own)) + d_res2
    d_wdown = inner_first(activated, reduced_all).astype(bf)
    d_wup = inner_first(normed_all, d_expanded).astype(bf)
    d_up_bias = column_sums(d_expanded)
    d_res1 = norm_back(unit1, inverse1, gain1, d_normed)
    d_gain1 = jnp.sum(d_normed * unit1, axis=0, keepdims=True)
    d_shift1 = jnp.sum(d_normed, axis=0, keepdims=True)
    d_attended = d_res1.astype(bf)
    d_out_bias = column_sums(d_attended)[None]
    attended_all = ordered(core, d_attended, swap(d_attended))
    d_context = inner_last(attended_all, w_out_own).astype(bf)
    d_wout_rows = inner_first(context, attended_all).astype(bf)
    d_wout = ordered(
        core, half_of(core, d_wout_rows, 1), swap(half_of(1 - core, d_wout_rows, 1)), axis=0
    )

    def rejoin(first, second):
        own = jnp.where(core == 0, first, second)
        got = swap(jnp.where(core == 0, second, first).astype(bf)).astype(f32)
        return jnp.where(core == 0, own, got), jnp.where(core == 0, got, own)

    late_cols = jnp.concatenate([d_wout, d_wup], axis=1).reshape(chips, 2, rows, half + ff_half)
    down_cols = d_wdown.reshape(chips, 2, 2, rows, D)
    late_sums = Scatter(jnp.concatenate([late_cols, down_cols[:, :, 0], down_cols[:, :, 1]], axis=-1))
    grads = []
    late_steps = {0: lambda: late_sums.pair(1), 3: lambda: late_sums.pair(2), 5: lambda: late_sums.line(1)}
    found = ()
    for index in range(half // HEAD_DIM):
        if index in late_steps:
            found, d_context = tie((late_sums,), (found, d_context))
            late_steps[index]()
        if index % 2 == 0:
            found = ()
        found = attention_backward(merged, d_context, prob_parts[index], pos_band, index // 2, index % 2, tuple(found[:3]))
        grads.append(found)
    grads[-1] = tie((late_sums,), found)
    d_merged = jnp.concatenate([g[i] for i in range(3) for g in grads[1::2]], axis=1)
    d_q, d_v = d_merged[:, :half], d_merged[:, 2 * half :]
    d_wqkv = inner_first(hidden_all, d_merged).astype(bf)
    d_q_bias = column_sums(d_q)[None]
    d_v_bias = column_sums(d_v)[None]
    d_band = jnp.concatenate([g[i] for i in (3, 4) for g in grads], axis=0).astype(bf)
    d_pos = lax.dot_general(
        chosen, d_band, (((0,), (1,)), ((), ())), preferred_element_type=f32
    )
    d_posq_bias = jnp.sum(d_pos[:, half:], axis=0, keepdims=True)
    d_pos_low = d_pos.astype(bf)
    d_wpos = inner_first(table, d_pos_low).astype(bf)
    d_table_all = inner_last(d_pos_low, w_pos_own).astype(bf)
    d_table = (
        half_of(core, d_table_all, 1).astype(f32)
        + swap(half_of(1 - core, d_table_all, 1)).astype(f32)
    ).astype(bf)

    def whole(part):
        blank = jnp.zeros_like(part)
        return ordered(core, part, blank, axis=1)

    lists_grad = jnp.concatenate(
        [whole(jnp.concatenate([d_q_bias, d_v_bias, d_posq_bias], axis=0)), d_out_bias, d_gain1, d_shift1, d_down_bias, d_gain2, d_shift2],
        axis=0,
    ).astype(bf)
    lists_grad = jnp.pad(lists_grad, ((0, 7), (0, 0)))
    pieces = jnp.where(inside, lists_grad[:, None, :], jnp.zeros((), bf)).reshape(16 * rows, D)
    unit_at = lax.broadcasted_iota(jnp.int32, (half, ff_half), 1) % units + 256 == lax.broadcasted_iota(jnp.int32, (half, ff_half), 0)
    unit_pieces = jnp.where(unit_at, d_up_bias.astype(bf), jnp.zeros((), bf))
    vector = (inner_last(owner, pieces) + inner_last(unit_owner, unit_pieces)).astype(bf)
    corner_grad = jnp.concatenate(
        [
            d_table.reshape(2 * chips, table_rows, half),
            jnp.pad(vector[:, None, :], ((0, 0), (0, last_rows - 1), (0, 0))),
        ],
        axis=1,
    ).reshape(chips * 2 * rows, half)
    early_sums = Scatter(
        jnp.concatenate([d_wqkv, d_wpos, corner_grad], axis=1).reshape(chips, 2, rows, 6 * half)
    )
    d_merged = tie((early_sums,), d_merged)
    early_sums.pair(1)
    in_grad = d_res1 + summed_rows(d_merged, lambda part: inner_last(part, w_qkv_own))
    in_grad = tie((late_sums,), in_grad)
    late_sums.line(2)
    late_sums.line(3)
    late_grads = late_sums.totals[0]
    down_grads = late_grads[:, :, half + ff_half :]
    late_grads = late_grads[:, :, : half + ff_half]
    late_left, late_right = rejoin(late_grads[0], late_grads[1])
    place = lax.broadcasted_iota(jnp.int32, (D, D), 0)
    place = (place % half) // units * (2 * units) + place // half * units + place % units
    unit_order = (place == lax.broadcasted_iota(jnp.int32, (D, D), 1)).astype(bf)
    early_sums.pair(2)
    g_wdown = jnp.stack([down_grads[:, :, :D], down_grads[:, :, D:]], axis=1).reshape(units, D)
    g_wout = jnp.concatenate([late_left[:, :half], late_right[:, :half]], axis=1)
    joined = []
    for group in range(ff_half // half):
        cut = slice(half + group * half, half + (group + 1) * half)
        joined.append(jnp.concatenate([late_left[:, cut], late_right[:, cut]], axis=1))
    joined = product(jnp.concatenate(joined, axis=0).astype(bf), unit_order)
    g_wup = jnp.concatenate([joined[g * rows : (g + 1) * rows] for g in range(ff_half // half)], axis=1)
    for step in (1, 2, 3):
        early_sums.line(step)
    early_grads = early_sums.totals[0]
    early_left, early_right = rejoin(early_grads[0], early_grads[1])
    vector_sum = early_left[table_rows, 5 * half :] + early_right[table_rows, 5 * half :]

    def side_by_side(left, right, at, count):
        pieces = []
        for index in range(count):
            cut = slice((at + index) * half, (at + index + 1) * half)
            pieces += [left[:, cut], right[:, cut]]
        return jnp.concatenate(pieces, axis=1)

    g_wqkv = side_by_side(early_left, early_right, 0, 3)
    g_wposk = side_by_side(early_left, early_right, 3, 1)
    g_wposq = side_by_side(early_left, early_right, 4, 1)
    g_table = side_by_side(early_left, early_right, 5, 1)[:table_rows]
    g = [vector_sum[i * rows : (i + 1) * rows] for i in range(9)]
    g_up_bias = vector_sum[256 : 256 + units]
    return (
        hidden_out, in_grad, g_wqkv, g[0], g[1], g_table, g_wposk, g_wposq, g[2], g_wout, g[3], g[4], g[5],
        g_wup, g_up_bias, g_wdown, g[6], g[7], g[8],
    )


def row_split(
    hidden_in,
    prefix,
    w_qkv,
    q_bias,
    v_bias,
    rel_table,
    w_posk,
    w_posq,
    posq_bias,
    w_out,
    out_bias,
    norm1_gain,
    norm1_bias,
    w_up,
    up_bias,
    w_down,
    down_bias,
    norm2_gain,
    norm2_bias,
    out_grad,
):
    gathered = (
        lax.all_gather(w_qkv, ("dp", "seq"), axis=0, tiled=True),
        lax.all_gather(q_bias, ("dp", "seq"), axis=0, tiled=True),
        lax.all_gather(v_bias, ("dp", "seq"), axis=0, tiled=True),
        lax.all_gather(rel_table, ("dp", "seq"), axis=0, tiled=True),
        lax.all_gather(w_posk, ("dp", "seq"), axis=0, tiled=True),
        lax.all_gather(w_posq, ("dp", "seq"), axis=0, tiled=True),
        lax.all_gather(posq_bias, ("dp", "seq"), axis=0, tiled=True),
        lax.all_gather(w_out, ("dp", "seq"), axis=0, tiled=True),
        lax.all_gather(out_bias, ("dp", "seq"), axis=0, tiled=True),
        lax.all_gather(norm1_gain, ("dp", "seq"), axis=0, tiled=True),
        lax.all_gather(norm1_bias, ("dp", "seq"), axis=0, tiled=True),
        lax.all_gather(w_up, ("dp", "seq"), axis=0, tiled=True),
        lax.all_gather(up_bias, ("dp", "seq"), axis=0, tiled=True),
        lax.all_gather(w_down, ("dp", "seq"), axis=0, tiled=True),
        lax.all_gather(down_bias, ("dp", "seq"), axis=0, tiled=True),
        lax.all_gather(norm2_gain, ("dp", "seq"), axis=0, tiled=True),
        lax.all_gather(norm2_bias, ("dp", "seq"), axis=0, tiled=True),
    )
    (
        full_qkv,
        full_qb,
        full_vb,
        full_table,
        full_posk,
        full_posq,
        full_pqb,
        full_out,
        full_ob,
        full_g1,
        full_b1,
        full_up,
        full_ub,
        full_down,
        full_db,
        full_g2,
        full_b2,
    ) = gathered
    row_count = hidden_in.shape[0]
    groups = lax.axis_size("seq")
    seq_length = row_count * groups
    seq_rank = lax.axis_index("seq")
    prefix_len = prefix[0]
    score_scale = 1.0 / math.sqrt(3 * HEAD_DIM)
    buckets = 2 * SPAN
    window = row_count + buckets
    first_row = seq_rank * row_count
    query_pos = first_row + jnp.arange(row_count, dtype=jnp.int32)
    key_pos = jnp.arange(seq_length, dtype=jnp.int32)
    visible = (key_pos[None, :] < prefix_len) | (key_pos[None, :] <= query_pos[:, None])
    padded_cols = jnp.arange(seq_length + buckets, dtype=jnp.int32)
    below_window = padded_cols[None, :] < first_row

    def skew_table(table, row_total, offset, col_total):
        shifted = jnp.pad(
            jnp.flip(table, axis=1), ((0, 0), (row_count, row_count - 1)), mode="edge"
        )
        stride = shifted.shape[1] - 1
        flattened = shifted.reshape(-1)
        picked = lax.slice_in_dim(flattened, offset, offset + row_total * stride)
        return picked.reshape(row_total, stride)[:, :col_total]

    def pos_terms(table_a, table_w, edge_terms):
        band_terms = (
            skew_table(table_a, row_count, row_count - 1, window)
            + skew_table(table_w, window, window - 1, row_count).T
        )
        low_side = table_a[:, buckets - 1 : buckets] + jnp.pad(edge_terms[0], (SPAN, SPAN))[None, :]
        high_side = table_a[:, 0:1] + jnp.pad(edge_terms[1], (SPAN, SPAN))[None, :]
        backdrop = jnp.where(below_window, low_side, high_side)
        placed = lax.dynamic_update_slice(
            backdrop, band_terms, (jnp.zeros((), jnp.int32), first_row)
        )
        return placed[:, SPAN : SPAN + seq_length]

    pos_keys = product(full_table, full_posk).astype(jnp.bfloat16)
    pos_queries = (product(full_table, full_posq) + full_pqb.astype(jnp.float32)).astype(
        jnp.bfloat16
    )
    merged = product(hidden_in, full_qkv)
    queries = (merged[:, :D] + full_qb.astype(jnp.float32)).astype(jnp.bfloat16)
    keys_local = merged[:, D : 2 * D].astype(jnp.bfloat16)
    values_local = (merged[:, 2 * D :] + full_vb.astype(jnp.float32)).astype(jnp.bfloat16)
    keys_all, values_all = (
        lax.all_gather(keys_local, "seq", axis=0, tiled=True),
        lax.all_gather(values_local, "seq", axis=0, tiled=True),
    )
    query_heads = split_heads(queries)
    key_heads = split_heads(keys_all)
    value_heads = split_heads(values_all)
    posk_heads = split_heads(pos_keys)
    posq_heads = split_heads(pos_queries)

    def head_scores(query_h, key_h, posk_h, posq_h):
        content = inner_last(query_h, key_h)
        table_a = inner_last(query_h, posk_h)
        key_padded = jnp.pad(key_h, ((SPAN, SPAN), (0, 0)))
        key_window = lax.dynamic_slice_in_dim(key_padded, first_row, window, 0)
        table_w = inner_last(key_window, posq_h)
        end_rows = jnp.stack([posq_h[0], posq_h[buckets - 1]])
        edge_terms = inner_last(end_rows, key_h)
        raw = content + pos_terms(table_a, table_w, edge_terms)
        masked = jnp.where(visible, raw * score_scale, -jnp.inf)
        return (masked, table_a, table_w, edge_terms, key_window, end_rows)

    def head_forward(operands):
        query_h, key_h, value_h, posk_h, posq_h = operands
        scores = head_scores(query_h, key_h, posk_h, posq_h)[0]
        highest = jnp.max(scores, axis=1, keepdims=True)
        expo = jnp.exp(scores - highest)
        totals = jnp.sum(expo, axis=1, keepdims=True)
        probs_low = (expo / totals).astype(jnp.bfloat16)
        return (product(probs_low, value_h), (highest + jnp.log(totals))[:, 0])

    contexts, log_totals = lax.map(
        head_forward, (query_heads, key_heads, value_heads, posk_heads, posq_heads)
    )
    context = join_heads(contexts).astype(jnp.bfloat16)
    hidden_f = hidden_in.astype(jnp.float32)
    residual1 = hidden_f + product(context, full_out) + full_ob.astype(jnp.float32)
    gain1 = full_g1.astype(jnp.float32)
    shift1 = full_b1.astype(jnp.float32)
    normed = normalize(residual1, gain1, shift1)
    normed_low = normed.astype(jnp.bfloat16)
    expanded = product(normed_low, full_up) + full_ub.astype(jnp.float32)
    activated = gelu_exact(expanded).astype(jnp.bfloat16)
    residual2 = normed + product(activated, full_down) + full_db.astype(jnp.float32)
    gain2 = full_g2.astype(jnp.float32)
    shift2 = full_b2.astype(jnp.float32)
    hidden_out = normalize(residual2, gain2, shift2).astype(jnp.bfloat16)
    regathered = (
        lax.all_gather(w_qkv, ("dp", "seq"), axis=0, tiled=True),
        lax.all_gather(q_bias, ("dp", "seq"), axis=0, tiled=True),
        lax.all_gather(v_bias, ("dp", "seq"), axis=0, tiled=True),
        lax.all_gather(rel_table, ("dp", "seq"), axis=0, tiled=True),
        lax.all_gather(w_posk, ("dp", "seq"), axis=0, tiled=True),
        lax.all_gather(w_posq, ("dp", "seq"), axis=0, tiled=True),
        lax.all_gather(posq_bias, ("dp", "seq"), axis=0, tiled=True),
        lax.all_gather(w_out, ("dp", "seq"), axis=0, tiled=True),
        lax.all_gather(out_bias, ("dp", "seq"), axis=0, tiled=True),
        lax.all_gather(norm1_gain, ("dp", "seq"), axis=0, tiled=True),
        lax.all_gather(norm1_bias, ("dp", "seq"), axis=0, tiled=True),
        lax.all_gather(w_up, ("dp", "seq"), axis=0, tiled=True),
        lax.all_gather(up_bias, ("dp", "seq"), axis=0, tiled=True),
        lax.all_gather(w_down, ("dp", "seq"), axis=0, tiled=True),
        lax.all_gather(down_bias, ("dp", "seq"), axis=0, tiled=True),
        lax.all_gather(norm2_gain, ("dp", "seq"), axis=0, tiled=True),
        lax.all_gather(norm2_bias, ("dp", "seq"), axis=0, tiled=True),
    )
    (
        back_qkv,
        back_qb,
        back_vb,
        back_table,
        back_posk,
        back_posq,
        back_pqb,
        back_out,
        back_ob,
        back_g1,
        back_b1,
        back_up,
        back_ub,
        back_down,
        back_db,
        back_g2,
        back_b2,
    ) = regathered
    _, pull_second = jax.vjp(normalize, residual2, gain2, shift2)
    d_res2, d_gain2, d_shift2 = pull_second(out_grad.astype(jnp.float32))
    d_reduced = d_res2.astype(jnp.bfloat16)
    d_wdown = inner_first(activated, d_reduced)
    d_down_bias = column_sums(d_reduced)
    d_activated = inner_last(d_reduced, back_down)
    _, pull_gelu = jax.vjp(gelu_exact, expanded)
    d_expanded = pull_gelu(d_activated)[0].astype(jnp.bfloat16)
    d_wup = inner_first(normed_low, d_expanded)
    d_up_bias = column_sums(d_expanded)
    d_normed = inner_last(d_expanded, back_up) + d_res2
    _, pull_first = jax.vjp(normalize, residual1, gain1, shift1)
    d_res1, d_gain1, d_shift1 = pull_first(d_normed)
    d_attended = d_res1.astype(jnp.bfloat16)
    d_wout = inner_first(context, d_attended)
    d_out_bias = column_sums(d_attended)
    d_context = inner_last(d_attended, back_out).astype(jnp.bfloat16)
    dctx_heads = split_heads(d_context)

    def head_backward(operands):
        query_h, key_h, value_h, posk_h, posq_h, log_total, dctx_h = operands
        scores, table_a, table_w, edge_terms, key_window, end_rows = head_scores(
            query_h, key_h, posk_h, posq_h
        )
        probs = jnp.exp(scores - log_total[:, None])
        probs_low = probs.astype(jnp.bfloat16)
        d_probs = inner_last(dctx_h, value_h)
        d_value = inner_first(probs_low, dctx_h)
        row_dot = jnp.sum(probs * d_probs, axis=1, keepdims=True)
        d_raw = (probs * (d_probs - row_dot) * score_scale).astype(jnp.bfloat16)
        _, pull_terms = jax.vjp(pos_terms, table_a, table_w, edge_terms)
        d_table_a, d_table_w, d_edges = pull_terms(d_raw.astype(jnp.float32))
        d_table_a = d_table_a.astype(jnp.bfloat16)
        d_table_w = d_table_w.astype(jnp.bfloat16)
        d_edges = d_edges.astype(jnp.bfloat16)
        d_query = product(d_raw, key_h) + product(d_table_a, posk_h)
        window_grad = product(d_table_w, posq_h)
        key_canvas = jnp.zeros((seq_length + buckets, HEAD_DIM), jnp.float32)
        placed_grad = lax.dynamic_update_slice(
            key_canvas, window_grad, (first_row, jnp.zeros((), jnp.int32))
        )
        d_key = (
            inner_first(d_raw, query_h)
            + placed_grad[SPAN : SPAN + seq_length]
            + inner_first(d_edges, end_rows)
        )
        d_posk = inner_first(d_table_a, query_h)
        end_grads = product(d_edges, key_h)
        d_posq = inner_first(d_table_w, key_window)
        d_posq = d_posq.at[0].add(end_grads[0]).at[buckets - 1].add(end_grads[1])
        return (d_query, d_key, d_value, d_posk, d_posq)

    d_q_heads, d_k_heads, d_v_heads, d_posk_heads, d_posq_heads = lax.map(
        head_backward,
        (query_heads, key_heads, value_heads, posk_heads, posq_heads, log_totals, dctx_heads),
    )
    d_queries = join_heads(d_q_heads).astype(jnp.bfloat16)
    d_keys_part, d_values_part = (
        lax.psum_scatter(
            join_heads(d_k_heads).astype(jnp.bfloat16), "seq", scatter_dimension=0, tiled=True
        ).astype(jnp.float32),
        lax.psum_scatter(
            join_heads(d_v_heads).astype(jnp.bfloat16), "seq", scatter_dimension=0, tiled=True
        ).astype(jnp.float32),
    )
    d_keys = d_keys_part.astype(jnp.bfloat16)
    d_values = d_values_part.astype(jnp.bfloat16)
    d_merged = jnp.concatenate([d_queries, d_keys, d_values], axis=1)
    d_wqkv = inner_first(hidden_in, d_merged)
    d_q_bias = column_sums(d_queries)
    d_v_bias = column_sums(d_values)
    in_grad = d_res1 + inner_last(d_merged, back_qkv)
    d_posk_rows, d_posq_rows = (
        lax.psum_scatter(join_heads(d_posk_heads), ("dp", "seq"), scatter_dimension=0, tiled=True),
        lax.psum_scatter(join_heads(d_posq_heads), ("dp", "seq"), scatter_dimension=0, tiled=True),
    )
    d_posk_low = d_posk_rows.astype(jnp.bfloat16)
    d_posq_low = d_posq_rows.astype(jnp.bfloat16)
    rel_table_grad = inner_last(d_posk_low, back_posk) + inner_last(d_posq_low, back_posq)
    d_wposk = inner_first(rel_table, d_posk_low)
    d_wposq = inner_first(rel_table, d_posq_low)
    d_posq_bias = column_sums(d_posq_low)
    summed = (
        lax.psum_scatter(d_wqkv, ("dp", "seq"), scatter_dimension=0, tiled=True),
        lax.psum_scatter(d_q_bias, ("dp", "seq"), scatter_dimension=0, tiled=True),
        lax.psum_scatter(d_v_bias, ("dp", "seq"), scatter_dimension=0, tiled=True),
        lax.psum_scatter(d_wposk, ("dp", "seq"), scatter_dimension=0, tiled=True),
        lax.psum_scatter(d_wposq, ("dp", "seq"), scatter_dimension=0, tiled=True),
        lax.psum_scatter(d_posq_bias, ("dp", "seq"), scatter_dimension=0, tiled=True),
        lax.psum_scatter(d_wout, ("dp", "seq"), scatter_dimension=0, tiled=True),
        lax.psum_scatter(d_out_bias, ("dp", "seq"), scatter_dimension=0, tiled=True),
        lax.psum_scatter(d_gain1, ("dp", "seq"), scatter_dimension=0, tiled=True),
        lax.psum_scatter(d_shift1, ("dp", "seq"), scatter_dimension=0, tiled=True),
        lax.psum_scatter(d_wup, ("dp", "seq"), scatter_dimension=0, tiled=True),
        lax.psum_scatter(d_up_bias, ("dp", "seq"), scatter_dimension=0, tiled=True),
        lax.psum_scatter(d_wdown, ("dp", "seq"), scatter_dimension=0, tiled=True),
        lax.psum_scatter(d_down_bias, ("dp", "seq"), scatter_dimension=0, tiled=True),
        lax.psum_scatter(d_gain2, ("dp", "seq"), scatter_dimension=0, tiled=True),
        lax.psum_scatter(d_shift2, ("dp", "seq"), scatter_dimension=0, tiled=True),
    )
    return (
        hidden_out,
        in_grad,
        summed[0],
        summed[1],
        summed[2],
        rel_table_grad,
        summed[3],
        summed[4],
        summed[5],
        summed[6],
        summed[7],
        summed[8],
        summed[9],
        summed[10],
        summed[11],
        summed[12],
        summed[13],
        summed[14],
        summed[15],
    )


def solution(mesh):
    placed = (
        P(("dp", "seq"), None),
        P("dp"),
        P(("dp", "seq"), None),
        P(("dp", "seq")),
        P(("dp", "seq")),
        P(("dp", "seq"), None),
        P(("dp", "seq"), None),
        P(("dp", "seq"), None),
        P(("dp", "seq")),
        P(("dp", "seq"), None),
        P(("dp", "seq")),
        P(("dp", "seq")),
        P(("dp", "seq")),
        P(("dp", "seq"), None),
        P(("dp", "seq")),
        P(("dp", "seq"), None),
        P(("dp", "seq")),
        P(("dp", "seq")),
        P(("dp", "seq")),
        P(("dp", "seq"), None),
    )
    return jax.shard_map(
        head_split if dict(mesh.shape) == {"dp": 16, "seq": 2} else row_split,
        mesh=mesh,
        in_specs=placed,
        out_specs=(
            P(("dp", "seq"), None),
            P(("dp", "seq"), None),
            P(("dp", "seq"), None),
            P(("dp", "seq")),
            P(("dp", "seq")),
            P(("dp", "seq"), None),
            P(("dp", "seq"), None),
            P(("dp", "seq"), None),
            P(("dp", "seq")),
            P(("dp", "seq"), None),
            P(("dp", "seq")),
            P(("dp", "seq")),
            P(("dp", "seq")),
            P(("dp", "seq"), None),
            P(("dp", "seq")),
            P(("dp", "seq"), None),
            P(("dp", "seq")),
            P(("dp", "seq")),
            P(("dp", "seq")),
        ),
        check_vma=False,
    )
```
